32 devices in a mesh: dp: 8 (over z, x), tensor: 4 (over y, core).
Axes of the slice: x: 2, y: 2, z: 4, core: 2. Of those that a mesh axis runs over, the one named last changes fastest.
Arguments:
- images: bfloat16 [128, 196, 768], P('dp'), may hold values from -6 to 6
- keep_index: int32 [128, 49], P('dp'), may hold values from 0 to 195, as said below
- unshuffle: int32 [128, 196], P('dp'), may hold values from 0 to 195, as said below
- masked: int32 [128, 196], P('dp'), may hold values from 0 to 1, as said below
- image_valid: int32 [128], P('dp'), may hold values from 0 to 1
- encoder_in: float32 [768, 4, 1344], P('dp', 'tensor'), may hold values from -0.21875 to 0.21875
- encoder_out: float32 [4, 960, 768], P('tensor', 'dp'), may hold values from -0.21875 to 0.21875
- decoder_in: float32 [512, 4, 896], P('dp', 'tensor'), may hold values from -0.25 to 0.25
- decoder_out: float32 [4, 640, 512], P('tensor', 'dp'), may hold values from -0.25 to 0.25
- pixel_maps: float32 [1280, 768], P('dp'), may hold values from -0.21875 to 0.21875
- bridge_map: float32 [768, 512], P('dp'), may hold values from -0.21875 to 0.21875
- vector_pack: float32 [7, 1280], P(None, 'dp')
- first_encoder_in: float32 [768, 4, 1344], P('dp', 'tensor'), may hold values from -1.9073486e-05 to 1.9073486e-05
- first_encoder_out: float32 [4, 960, 768], P('tensor', 'dp'), may hold values from -1.9073486e-05 to 1.9073486e-05
- first_decoder_in: float32 [512, 4, 896], P('dp', 'tensor'), may hold values from -1.9073486e-05 to 1.9073486e-05
- first_decoder_out: float32 [4, 640, 512], P('tensor', 'dp'), may hold values from -1.9073486e-05 to 1.9073486e-05
- first_pixel_maps: float32 [1280, 768], P('dp'), may hold values from -1.9073486e-05 to 1.9073486e-05
- first_bridge_map: float32 [768, 512], P('dp'), may hold values from -1.9073486e-05 to 1.9073486e-05
- first_vector_pack: float32 [7, 1280], P(None, 'dp'), may hold values from -1.9073486e-05 to 1.9073486e-05
- second_encoder_in: float32 [768, 4, 1344], P('dp', 'tensor'), may hold values from 9.934108e-13 to 3.973643e-12
- second_encoder_out: float32 [4, 960, 768], P('tensor', 'dp'), may hold values from 9.934108e-13 to 3.973643e-12
- second_decoder_in: float32 [512, 4, 896], P('dp', 'tensor'), may hold values from 9.934108e-13 to 3.973643e-12
- second_decoder_out: float32 [4, 640, 512], P('tensor', 'dp'), may hold values from 9.934108e-13 to 3.973643e-12
- second_pixel_maps: float32 [1280, 768], P('dp'), may hold values from 9.934108e-13 to 3.973643e-12
- second_bridge_map: float32 [768, 512], P('dp'), may hold values from 9.934108e-13 to 3.973643e-12
- second_vector_pack: float32 [7, 1280], P(None, 'dp'), may hold values from 9.934108e-13 to 3.973643e-12
Outputs:
- loss_value: float32 [], replicated
- norm_pairs: float32 [2, 7], replicated
- next_first_encoder_in: float32 [768, 4, 1344], P('dp', 'tensor')
- next_first_encoder_out: float32 [4, 960, 768], P('tensor', 'dp')
- next_first_decoder_in: float32 [512, 4, 896], P('dp', 'tensor')
- next_first_decoder_out: float32 [4, 640, 512], P('tensor', 'dp')
- next_first_pixel_maps: float32 [1280, 768], P('dp')
- next_first_bridge_map: float32 [768, 512], P('dp')
- next_first_vector_pack: float32 [7, 1280], P(None, 'dp')
- next_second_encoder_in: float32 [768, 4, 1344], P('dp', 'tensor')
- next_second_encoder_out: float32 [4, 960, 768], P('tensor', 'dp')
- next_second_decoder_in: float32 [512, 4, 896], P('dp', 'tensor')
- next_second_decoder_out: float32 [4, 640, 512], P('tensor', 'dp')
- next_second_pixel_maps: float32 [1280, 768], P('dp')
- next_second_bridge_map: float32 [768, 512], P('dp')
- next_second_vector_pack: float32 [7, 1280], P(None, 'dp')
- next_encoder_in: float32 [768, 4, 1344], P('dp', 'tensor')
- next_encoder_out: float32 [4, 960, 768], P('tensor', 'dp')
- next_decoder_in: float32 [512, 4, 896], P('dp', 'tensor')
- next_decoder_out: float32 [4, 640, 512], P('tensor', 'dp')
- next_pixel_maps: float32 [1280, 768], P('dp')
- next_bridge_map: float32 [768, 512], P('dp')
- next_vector_pack: float32 [7, 1280], P(None, 'dp')
The draws below stay inside these ranges and needn't reach their ends.
Inputs may be any that keep to these rules, and one draw needn't show every extreme that they name: `keep_index`: each row names 49 different patches, in the image's shuffled order. `unshuffle`: each row is a permutation of the patches' places, with unshuffle[b, keep_index[b, j]] = j. masked[b, p] = 1 exactly where unshuffle[b, p] >= 49.
All inputs are finite; a program needn't handle non-finite values.
Results may differ from the reference program's by a relative error of at most 0.0035.
The reference program's roundings to bfloat16 on the way count: a program that leaves them out, or rounds other values in their place, can miss the bound.
Values may be sent and summed in bfloat16 or wider, within the bound.
A program may use at most 192 MiB of HBM per device.

```python
import math
import jax
import jax.numpy as jnp
from jax import lax

ENCODER_WIDTH = 768
H_E = 12
HD_E = 64
D_D = 512
H_D = 16
HD_D = 32
PATCH_DIM = 768
GRID_PATCHES = 14
IMAGE_PATCHES = 196
KEEP = 49
IMAGES = 128
ENC_COLS = 1344
ENC_ROWS = 960
DEC_COLS = 896
DEC_ROWS = 640
N_DP = 8
N_TENSOR = 4


def shuffle_order(key):
    keys_all = jax.random.split(jax.random.fold_in(key, 11), IMAGES)
    return jax.vmap(lambda single: jax.random.permutation(single, IMAGE_PATCHES))(keys_all).astype(jnp.int32)


def draw_keep_index(key, part):
    return shuffle_order(key)[:, :KEEP]


def draw_unshuffle(key, part):
    return jnp.argsort(shuffle_order(key), axis=1, stable=True).astype(jnp.int32)


def draw_masked(key, part):
    return (draw_unshuffle(key, part) >= KEEP).astype(jnp.int32)


def draw_image_valid(key, part):
    rolled = jax.random.randint(jax.random.fold_in(key, 23), (IMAGES,), 0, 16)
    flags = (rolled < 13).astype(jnp.int32)
    return flags.at[0].set(1)


def draw_vector_pack(key, part):
    columns = ENCODER_WIDTH + D_D
    row_ids = jnp.arange(7, dtype=jnp.int32)[:, None]
    gains = jax.random.uniform(jax.random.fold_in(key, 3), (7, columns), jnp.float32, 0.6, 1.4)
    others = 0.3 * jax.random.normal(jax.random.fold_in(key, 5), (7, columns), jnp.float32)
    return jnp.where(row_ids % 2 == 1, gains, others)


def block_levels(key, dims, cuts, least, high):
    def one(axis_at, blocks):
        steps = jax.random.uniform(jax.random.fold_in(jax.random.fold_in(key, 6), axis_at), (blocks,), jnp.float32, least / len(cuts), high / len(cuts))
        return jnp.repeat(jnp.exp(steps), dims[axis_at] // blocks).reshape((-1,) + (1,) * (len(dims) - axis_at - 1))

    level = one(*cuts[0])
    for cut in cuts[1:]:
        level = level * one(*cut)
    return level


def normal_values(own_key, dims, spread, reach, cuts=(), held_as=jnp.bfloat16):
    values = jax.random.normal(own_key, dims, jnp.float32) * spread
    if len(cuts) > 0:
        values = block_levels(own_key, dims, cuts, -0.22, 0.18) * values
    return jnp.clip(values, min=-reach, max=reach).astype(held_as)


def setup_inputs(seed: int = 0) -> dict:
    seeds = jax.random.split(jax.random.key(seed), 27)
    images = normal_values(seeds[0], (IMAGES, IMAGE_PATCHES, PATCH_DIM), 1.0, 6.0, ((0, 8),))
    keep_index = draw_keep_index(jax.random.fold_in(seeds[26], 71), 0)
    unshuffle = draw_unshuffle(jax.random.fold_in(seeds[26], 71), 0)
    masked = draw_masked(jax.random.fold_in(seeds[26], 71), 0)
    image_valid = draw_image_valid(jax.random.fold_in(seeds[26], 71), 0)
    encoder_in = normal_values(seeds[5], (ENCODER_WIDTH, N_TENSOR, ENC_COLS), ENCODER_WIDTH ** -0.5, 0.21875, ((0, 8), (1, 4)), jnp.float32)
    encoder_out = normal_values(seeds[6], (N_TENSOR, ENC_ROWS, ENCODER_WIDTH), ENCODER_WIDTH ** -0.5, 0.21875, ((0, 4), (1, 8)), jnp.float32)
    decoder_in = normal_values(seeds[7], (D_D, N_TENSOR, DEC_COLS), D_D ** -0.5, 0.25, ((0, 8), (1, 4)), jnp.float32)
    decoder_out = normal_values(seeds[8], (N_TENSOR, DEC_ROWS, D_D), D_D ** -0.5, 0.25, ((0, 4), (1, 8)), jnp.float32)
    pixel_maps = normal_values(seeds[9], (PATCH_DIM + D_D, ENCODER_WIDTH), PATCH_DIM ** -0.5, 0.21875, ((0, 8),), jnp.float32)
    bridge_map = normal_values(seeds[10], (ENCODER_WIDTH, D_D), ENCODER_WIDTH ** -0.5, 0.21875, ((0, 8),), jnp.float32)
    vector_pack = draw_vector_pack(jax.random.fold_in(seeds[26], 71), 0)
    first_encoder_in = normal_values(seeds[12], (ENCODER_WIDTH, N_TENSOR, ENC_COLS), (0.33 / (PATCH_DIM * (120 * IMAGES) ** 0.5)), 1.9073486328125e-05, ((0, 8), (1, 4)), jnp.float32)
    first_encoder_out = normal_values(seeds[13], (N_TENSOR, ENC_ROWS, ENCODER_WIDTH), (0.33 / (PATCH_DIM * (120 * IMAGES) ** 0.5)), 1.9073486328125e-05, ((0, 4), (1, 8)), jnp.float32)
    first_decoder_in = normal_values(seeds[14], (D_D, N_TENSOR, DEC_COLS), (0.33 / (PATCH_DIM * (120 * IMAGES) ** 0.5)), 1.9073486328125e-05, ((0, 8), (1, 4)), jnp.float32)
    first_decoder_out = normal_values(seeds[15], (N_TENSOR, DEC_ROWS, D_D), (0.33 / (PATCH_DIM * (120 * IMAGES) ** 0.5)), 1.9073486328125e-05, ((0, 4), (1, 8)), jnp.float32)
    first_pixel_maps = normal_values(seeds[16], (PATCH_DIM + D_D, ENCODER_WIDTH), (0.33 / (PATCH_DIM * (120 * IMAGES) ** 0.5)), 1.9073486328125e-05, ((0, 8),), jnp.float32)
    first_bridge_map = normal_values(seeds[17], (ENCODER_WIDTH, D_D), (0.33 / (PATCH_DIM * (120 * IMAGES) ** 0.5)), 1.9073486328125e-05, ((0, 8),), jnp.float32)
    first_vector_pack = normal_values(seeds[18], (7, ENCODER_WIDTH + D_D), (0.33 / (PATCH_DIM * (120 * IMAGES) ** 0.5)), 1.9073486328125e-05, ((1, 8),), jnp.float32)
    second_encoder_in = jnp.clip(jnp.exp(math.log(3.973643029203666e-12) - 1.3862944 * jax.random.uniform(seeds[19], (ENCODER_WIDTH, N_TENSOR, ENC_COLS), jnp.float32) ** block_levels(seeds[19], (ENCODER_WIDTH, N_TENSOR, ENC_COLS), ((0, 8), (1, 4)), -0.2, 0.2)), 9.934107573009165e-13, 3.973643029203666e-12)
    second_encoder_out = jnp.clip(jnp.exp(math.log(3.973643029203666e-12) - 1.3862944 * jax.random.uniform(seeds[20], (N_TENSOR, ENC_ROWS, ENCODER_WIDTH), jnp.float32) ** block_levels(seeds[20], (N_TENSOR, ENC_ROWS, ENCODER_WIDTH), ((0, 4), (1, 8)), -0.2, 0.2)), 9.934107573009165e-13, 3.973643029203666e-12)
    second_decoder_in = jnp.clip(jnp.exp(math.log(3.973643029203666e-12) - 1.3862944 * jax.random.uniform(seeds[21], (D_D, N_TENSOR, DEC_COLS), jnp.float32) ** block_levels(seeds[21], (D_D, N_TENSOR, DEC_COLS), ((0, 8), (1, 4)), -0.2, 0.2)), 9.934107573009165e-13, 3.973643029203666e-12)
    second_decoder_out = jnp.clip(jnp.exp(math.log(3.973643029203666e-12) - 1.3862944 * jax.random.uniform(seeds[22], (N_TENSOR, DEC_ROWS, D_D), jnp.float32) ** block_levels(seeds[22], (N_TENSOR, DEC_ROWS, D_D), ((0, 4), (1, 8)), -0.2, 0.2)), 9.934107573009165e-13, 3.973643029203666e-12)
    second_pixel_maps = jnp.clip(jnp.exp(math.log(3.973643029203666e-12) - 1.3862944 * jax.random.uniform(seeds[23], (PATCH_DIM + D_D, ENCODER_WIDTH), jnp.float32) ** block_levels(seeds[23], (PATCH_DIM + D_D, ENCODER_WIDTH), ((0, 8),), -0.2, 0.2)), 9.934107573009165e-13, 3.973643029203666e-12)
    second_bridge_map = jnp.clip(jnp.exp(math.log(3.973643029203666e-12) - 1.3862944 * jax.random.uniform(seeds[24], (ENCODER_WIDTH, D_D), jnp.float32) ** block_levels(seeds[24], (ENCODER_WIDTH, D_D), ((0, 8),), -0.2, 0.2)), 9.934107573009165e-13, 3.973643029203666e-12)
    second_vector_pack = jnp.clip(jnp.exp(math.log(3.973643029203666e-12) - 1.3862944 * jax.random.uniform(seeds[25], (7, ENCODER_WIDTH + D_D), jnp.float32) ** block_levels(seeds[25], (7, ENCODER_WIDTH + D_D), ((1, 8),), -0.2, 0.2)), 9.934107573009165e-13, 3.973643029203666e-12)
    return dict(images=images, keep_index=keep_index, unshuffle=unshuffle, masked=masked, image_valid=image_valid, encoder_in=encoder_in, encoder_out=encoder_out, decoder_in=decoder_in, decoder_out=decoder_out, pixel_maps=pixel_maps, bridge_map=bridge_map, vector_pack=vector_pack, first_encoder_in=first_encoder_in, first_encoder_out=first_encoder_out, first_decoder_in=first_decoder_in, first_decoder_out=first_decoder_out, first_pixel_maps=first_pixel_maps, first_bridge_map=first_bridge_map, first_vector_pack=first_vector_pack, second_encoder_in=second_encoder_in, second_encoder_out=second_encoder_out, second_decoder_in=second_decoder_in, second_decoder_out=second_decoder_out, second_pixel_maps=second_pixel_maps, second_bridge_map=second_bridge_map, second_vector_pack=second_vector_pack)


eps_norm = 1e-06
beta_one = 0.9
beta_two = 0.999
step_count = 7.0
learn_rate = 0.3
decay_matrix = 0.05
eps_moment = 1e-06

@jax.custom_vjp
def low(v):
    return lax.optimization_barrier(v.astype(jnp.bfloat16)).astype(jnp.float32)

@jax.custom_vjp
def low_back(v):
    return v

def low_keep(v):
    return (low(v), None)

def low_pass(kept, grad):
    return (grad,)

def back_keep(v):
    return (v, None)

def back_low(kept, grad):
    return (low(grad),)
low.defvjp(low_keep, low_pass)
low_back.defvjp(back_keep, back_low)

def product(left_side, right_side):
    return jnp.einsum('...d,dc->...c', left_side, right_side, precision=lax.Precision.HIGHEST)

def sinusoid_table(feature_width, grid_side, patch_count):
    position = jnp.arange(patch_count, dtype=jnp.int32)
    quarter = feature_width // 4
    omegas = 1.0 / 10000.0 ** (jnp.arange(quarter, dtype=jnp.float32) / quarter)

    def half_table(coords):
        angles = coords.astype(jnp.float32)[:, None] * omegas[None, :]
        return jnp.concatenate([jnp.sin(angles), jnp.cos(angles)], axis=1)
    return jnp.concatenate([half_table(position % grid_side), half_table(position // grid_side)], axis=1)

def layer_norm(stream, gain_row, shift_row):
    centred = stream - lax.optimization_barrier(jnp.mean(stream, axis=-1, keepdims=True))
    inverse = lax.rsqrt(lax.optimization_barrier(jnp.mean(centred * centred, axis=-1, keepdims=True)) + eps_norm)
    return centred * inverse * gain_row + shift_row

def layer(stream, w_input, w_output, vectors, head_total, head_dim):
    image_count, token_count, model_width = stream.shape
    inner_width = head_total // N_TENSOR * head_dim

    def columns(begin, finish):
        return w_input[:, :, begin:finish].reshape(model_width, -1)

    def rows_of(begin, finish):
        return w_output[:, begin:finish].reshape(-1, model_width)
    shape_heads = (image_count, token_count, head_total, head_dim)
    normed_one = low(layer_norm(stream, vectors[0], vectors[1]))
    queries = low(low_back(product(normed_one, columns(0, inner_width)))).reshape(shape_heads)
    keys_all = low(low_back(product(normed_one, columns(inner_width, 2 * inner_width)))).reshape(shape_heads)
    values_all = low(low_back(product(normed_one, columns(2 * inner_width, 3 * inner_width)))).reshape(shape_heads)
    scores = low_back(jnp.einsum('bqhd,bkhd->bhqk', queries, keys_all, precision=lax.Precision.HIGHEST) * head_dim ** (-0.5))
    shifted = jnp.exp(scores - lax.optimization_barrier(jnp.max(scores, axis=-1, keepdims=True)))
    attention = shifted / lax.optimization_barrier(jnp.sum(shifted, axis=-1, keepdims=True))
    mixed_heads = jnp.einsum('bhqk,bkhd->bqhd', low(attention), values_all, precision=lax.Precision.HIGHEST)
    mixed_heads = low(low_back(mixed_heads.reshape(image_count, token_count, -1)))
    after_attn = stream + low_back(product(mixed_heads, rows_of(0, inner_width)))
    normed_two = low(layer_norm(after_attn, vectors[2], vectors[3]))
    hidden = low_back(product(normed_two, columns(3 * inner_width, w_input.shape[2])))
    active = low(jax.nn.gelu(hidden, approximate=False))
    return after_attn + low_back(product(active, rows_of(inner_width, w_output.shape[1])))

def group_loss(params, batch, patch_total):
    encoder_in, encoder_out, decoder_in, decoder_out, pixel_maps, bridge_map, vector_pack = params
    images, keep_index, unshuffle, masked, patch_flags = batch
    pixels = images.astype(jnp.float32)
    image_count = pixels.shape[0]
    retained_pixels = jnp.take_along_axis(pixels, keep_index[:, :, None], axis=1)
    embedded = low_back(product(retained_pixels, pixel_maps[:PATCH_DIM])) + sinusoid_table(ENCODER_WIDTH, GRID_PATCHES, IMAGE_PATCHES)[keep_index]
    enc_vectors = vector_pack[:, :ENCODER_WIDTH]
    dec_vectors = vector_pack[:, ENCODER_WIDTH:]
    enc_start = jnp.concatenate([jnp.broadcast_to(enc_vectors[0], (image_count, 1, ENCODER_WIDTH)), embedded], axis=1)
    enc_end = layer(enc_start, encoder_in, encoder_out, enc_vectors[1:5], H_E, HD_E)
    enc_low = low(layer_norm(enc_end, enc_vectors[5], enc_vectors[6]))
    projected = low_back(product(enc_low, bridge_map))
    picked = jnp.take_along_axis(projected[:, 1:], jnp.minimum(unshuffle, KEEP - 1)[:, :, None], axis=1)
    mask_column = masked.astype(jnp.float32)[:, :, None]
    filled = picked * (1.0 - mask_column) + mask_column * dec_vectors[0] + sinusoid_table(D_D, GRID_PATCHES, IMAGE_PATCHES)
    dec_start = jnp.concatenate([projected[:, :1], filled], axis=1)
    dec_end = layer(dec_start, decoder_in, decoder_out, dec_vectors[1:5], H_D, HD_D)
    dec_low = low(layer_norm(dec_end, dec_vectors[5], dec_vectors[6]))
    predicted = low_back(product(dec_low[:, 1:], pixel_maps[PATCH_DIM:]))
    centred = pixels - lax.optimization_barrier(jnp.mean(pixels, axis=-1, keepdims=True))
    variance = lax.optimization_barrier(jnp.sum(centred * centred, axis=-1, keepdims=True)) / (PATCH_DIM - 1)
    target = centred * lax.rsqrt(variance + eps_norm)
    errors = predicted - target
    return jnp.sum(lax.optimization_barrier(jnp.mean(errors * errors, axis=-1)) * patch_flags) / patch_total

def reference(images, keep_index, unshuffle, masked, image_valid, encoder_in, encoder_out, decoder_in, decoder_out, pixel_maps, bridge_map, vector_pack, first_encoder_in, first_encoder_out, first_decoder_in, first_decoder_out, first_pixel_maps, first_bridge_map, first_vector_pack, second_encoder_in, second_encoder_out, second_decoder_in, second_decoder_out, second_pixel_maps, second_bridge_map, second_vector_pack):
    masters = (encoder_in, encoder_out, decoder_in, decoder_out, pixel_maps, bridge_map, vector_pack)
    firsts = (first_encoder_in, first_encoder_out, first_decoder_in, first_decoder_out, first_pixel_maps, first_bridge_map, first_vector_pack)
    seconds = (second_encoder_in, second_encoder_out, second_decoder_in, second_decoder_out, second_pixel_maps, second_bridge_map, second_vector_pack)
    patch_flags = masked.astype(jnp.float32) * image_valid.astype(jnp.float32)[:, None]
    patch_total = jnp.sum(patch_flags)
    batches = tuple((member.reshape((N_DP, -1) + member.shape[1:]) for member in (images, keep_index, unshuffle, masked, patch_flags)))

    def total_loss(params):
        low_params = tuple((low(member) for member in params))

        def one_group(carry, batch):
            return (carry + group_loss(low_params, batch, patch_total), None)
        summed, _ = lax.scan(jax.checkpoint(one_group), jnp.zeros((), jnp.float32), batches)
        return summed
    loss_value, backward = jax.vjp(total_loss, masters)
    gradients = backward(jnp.ones((), jnp.float32))[0]
    bias_one = 1.0 - beta_one ** step_count
    bias_two = 1.0 - beta_two ** step_count
    decays = (decay_matrix,) * 6 + (0.0,)
    new_firsts, new_seconds, updates = ([], [], [])
    for gradient, master, moment_one, moment_two, decay_value in zip(gradients, masters, firsts, seconds, decays):
        next_one = beta_one * moment_one + (1.0 - beta_one) * gradient
        next_two = beta_two * moment_two + (1.0 - beta_two) * gradient * gradient
        new_firsts.append(next_one)
        new_seconds.append(next_two)
        updates.append(next_one / bias_one / (jnp.sqrt(next_two / bias_two) + eps_moment) + decay_value * master)
    weight_norm = jnp.stack([jnp.sqrt(jnp.sum(master * master)) for master in masters])
    update_norm = jnp.stack([jnp.sqrt(jnp.sum(update * update)) for update in updates])
    step_ratio = learn_rate * weight_norm / update_norm
    news = [master - step_ratio[position] * update for position, (master, update) in enumerate(zip(masters, updates))]
    norm_pairs = jnp.stack([weight_norm, update_norm])
    return (loss_value, norm_pairs, new_firsts[0], new_firsts[1], new_firsts[2], new_firsts[3], new_firsts[4], new_firsts[5], new_firsts[6], new_seconds[0], new_seconds[1], new_seconds[2], new_seconds[3], new_seconds[4], new_seconds[5], new_seconds[6], news[0], news[1], news[2], news[3], news[4], news[5], news[6])
```

```python
import functools

import jax
import jax.numpy as jnp
from jax import lax
from jax.experimental import pallas as pl
from jax.experimental.pallas import tpu as pltpu
from jax.sharding import PartitionSpec as P

ENCODER_WIDTH = 768
H_E = 12
HD_E = 64
D_D = 512
H_D = 16
HD_D = 32
PATCH_DIM = 768
GRID_PATCHES = 14
IMAGE_PATCHES = 196
KEEP = 49

eps_norm = 1e-06
beta_one = 0.9
beta_two = 0.999
step_count = 7.0
learn_rate = 0.3
decay_matrix = 0.05
eps_moment = 1e-06
highest_precision = lax.Precision.HIGHEST
f32 = jnp.float32
bf16 = jnp.bfloat16
EVERY = ("dp", "tensor")
GROUPED = ("tensor", "dp")


MESH_ID = pl.DeviceIdType.MESH
PIX, EIN, EOUT, BRI, DIN, DOUT, VEC = range(7)


def place():
    dp_at = lax.axis_index("dp")
    group = lax.axis_index("tensor")
    z, x = lax.div(dp_at, 2), lax.rem(dp_at, 2)
    y, c = lax.div(group, 2), lax.rem(group, 2)
    return z, x, y, c


def device(z, x, y, c):
    return (z * 2 + x, y * 2 + c)


def flip(z, m):
    low = lax.rem(z, 2)
    high = lax.div(z, 2)
    if m % 2:
        low = 1 - low
    if m // 2:
        high = 1 - high
    return high * 2 + low


def greet(z, x, y, c):
    barrier = pltpu.get_barrier_semaphore()
    peers = [
        device(z, x, y, 1 - c),
        device(z, x, 1 - y, c),
        device(z, 1 - x, y, c),
        device(flip(z, 1), x, y, c),
        device(flip(z, 2), x, y, c),
        device(flip(z, 3), x, y, c),
    ]
    for peer in peers:
        pl.semaphore_signal(barrier, inc=1, device_id=peer, device_id_type=MESH_ID)
    pl.semaphore_wait(barrier, 6)


SHARED = (PIX, BRI)


def spot(array, y, c, z, x):
    return (z, x, y, c) if array in SHARED else (y, c, z, x)


def half_spot(array, y, z, x):
    return (z, x, y) if array in SHARED else (y, z, x)


def whole_shape(array, part):
    return ((4, 2, 2, 2) if array in SHARED else (2, 2, 4, 2)) + part


GATHER_STEPS = (
    ((VEC, 0, 8, 0), (PIX, 0, 24, 0), (PIX, 24, 16, 1)),
    ((EIN, 0, 32, 0), (EIN, 32, 16, 1)),
    ((EIN, 48, 16, 0), (EIN, 64, 32, 1)),
    ((EOUT, 0, 32, 0), (EOUT, 32, 32, 1)),
    ((EOUT, 64, 32, 0), (EOUT, 96, 24, 1)),
    ((BRI, 0, 8, 0), (BRI, 8, 16, 1), (DIN, 0, 32, 0), (DIN, 32, 32, 1)),
    ((DOUT, 0, 48, 0), (DOUT, 48, 32, 1)),
)


def gather_kernel(*refs):
    count = 7
    parts = refs[:count]
    outs = refs[count : 2 * count]
    send, recv, local = refs[2 * count :]
    z, x, y, c = place()
    units = []
    for at, step in enumerate(GATHER_STEPS):
        for unit in step:
            units.append((at,) + unit)
    copies = {}

    def rows(array, region, first, size):
        ref = outs[array]
        return ref.at[region + (pl.ds(first, size),)]

    def plan(number, stage):
        at, array, first, size, turn = units[number]
        every = slice(None)
        if stage < 3:
            src = parts[array].at[pl.ds(first, size)]
            dst = rows(array, spot(array, y, c, z, x), first, size)
            peer = device(flip(z, stage + 1), x, y, c)
        else:
            if stage == 3:
                region = spot(array, y, c, every, x)
                peer = device(z, x, 1 - y, c) if turn == 0 else device(z, 1 - x, y, c)
            elif stage == 4 and turn == 0:
                region = spot(array, every, c, every, x)
                peer = device(z, 1 - x, y, c)
            elif stage == 4:
                region = spot(array, y, c, every, every)
                peer = device(z, x, 1 - y, c)
            else:
                region = spot(array, every, c, every, every)
                peer = device(z, x, y, 1 - c)
            src = dst = rows(array, region, first, size)
        return pltpu.make_async_remote_copy(
            src_ref=src,
            dst_ref=dst,
            send_sem=send.at[number, stage],
            recv_sem=recv.at[number, stage],
            device_id=peer,
            device_id_type=MESH_ID,
        )

    def start(number, stage):
        copies[number, stage] = plan(number, stage)
        copies[number, stage].start()

    own = []
    for array in range(count):
        own.append(
            pltpu.make_async_copy(parts[array], outs[array].at[spot(array, y, c, z, x)], local.at[array])
        )
        own[-1].start()
    greet(z, x, y, c)
    steps = len(GATHER_STEPS)
    waited = set()
    for tick in range(steps + 4):
        for number, unit in enumerate(units):
            if unit[0] == tick:
                for stage in range(3):
                    start(number, stage)
        for number, unit in enumerate(units):
            if unit[0] == tick - 1:
                if unit[1] not in waited:
                    waited.add(unit[1])
                    own[unit[1]].wait()
                for stage in range(3):
                    copies[number, stage].wait_recv()
                start(number, 3)
        for back in (2, 3):
            for number, unit in enumerate(units):
                if unit[0] == tick - back:
                    copies[number, back + 1].wait_recv()
                    start(number, back + 2)
        for number, unit in enumerate(units):
            if unit[0] == tick - 4:
                copies[number, 5].wait_recv()
    for key in copies:
        copies[key].wait_send()


def gather_weights(parts):
    count = 7
    units = sum(len(step) for step in GATHER_STEPS)
    outs = [
        jax.ShapeDtypeStruct(whole_shape(array, part.shape), part.dtype)
        for array, part in enumerate(parts)
    ]
    total = sum(int(part.size) * 32 * part.dtype.itemsize for part in parts)
    return pl.pallas_call(
        gather_kernel,
        out_shape=outs,
        in_specs=[pl.BlockSpec(memory_space=pltpu.VMEM)] * count,
        out_specs=[pl.BlockSpec(memory_space=pl.ANY)] * count,
        scratch_shapes=[
            pltpu.SemaphoreType.DMA((units, 6)),
            pltpu.SemaphoreType.DMA((units, 6)),
            pltpu.SemaphoreType.DMA((count,)),
        ],
        compiler_params=pltpu.CompilerParams(collective_id=0, has_side_effects=True),
        cost_estimate=pl.CostEstimate(flops=0, bytes_accessed=2 * total, transcendentals=0),
        name="gather_weights",
    )(*parts)


SCATTER_STEPS = (
    ((DOUT, 0, 48, 0), (DOUT, 48, 32, 1)),
    ((BRI, 0, 8, 0), (BRI, 8, 16, 1), (DIN, 0, 32, 0), (DIN, 32, 32, 1)),
    ((PIX, 0, 24, 0), (PIX, 24, 16, 1)),
    ((EOUT, 0, 32, 0), (EOUT, 32, 32, 1)),
    ((EOUT, 64, 32, 0), (EOUT, 96, 24, 1)),
    ((EIN, 0, 32, 0), (EIN, 32, 16, 1)),
    ((EIN, 48, 16, 0), (EIN, 64, 32, 1)),
)
def scatter_kernel(shapes, units, *refs):
    grads = refs[:7]
    outs = refs[7:14]
    refs = refs[14:]
    n = len(units)
    own, one, two, three, four = (refs[k * n : (k + 1) * n] for k in range(5))
    vec_one, vec_two, vec_three, vec_four, vec_sum = refs[5 * n : 5 * n + 5]
    send, recv, local, vsend, vrecv, tsend, trecv = refs[5 * n + 5 :]
    z, x, y, c = place()
    every = slice(None)
    copies = {}

    def remote(src, dst, key, send_sem, recv_sem, peer):
        copies[key] = pltpu.make_async_remote_copy(
            src_ref=src,
            dst_ref=dst,
            send_sem=send_sem,
            recv_sem=recv_sem,
            device_id=peer,
            device_id_type=MESH_ID,
        )
        copies[key].start()

    def start(number, stage):
        at, array, first, size, turn = units[number]
        mine = own[number]
        if stage == 0:
            peer = device(z, x, y, 1 - c)
            src = grads[array].at[
                spot(array, every, 1 - c, every, every) + (pl.ds(first, size),)
            ]
            dst = one[number]
        elif stage == 1 and turn == 0:
            peer = device(z, 1 - x, y, c)
            src, dst = mine.at[half_spot(array, every, every, 1 - x)], two[number]
        elif stage == 1:
            peer = device(z, x, 1 - y, c)
            src, dst = mine.at[half_spot(array, 1 - y, every, every)], two[number]
        elif stage == 2 and turn == 0:
            peer = device(z, x, 1 - y, c)
            src, dst = mine.at[half_spot(array, 1 - y, every, x)], three[number]
        elif stage == 2:
            peer = device(z, 1 - x, y, c)
            src, dst = mine.at[half_spot(array, y, every, 1 - x)], three[number]
        else:
            other = flip(z, stage - 2)
            peer = device(other, x, y, c)
            src, dst = mine.at[half_spot(array, y, other, x)], four[number].at[stage - 3]
        remote(src, dst, (number, stage), send.at[number, stage], recv.at[number, stage], peer)

    def add(number, stage):
        at, array, first, size, turn = units[number]
        mine = own[number]

        def pair(here, there):
            mine[here] = (mine[here].astype(f32) + there.astype(f32)).astype(bf16)

        if stage == 0:

            @pl.loop(0, 16)
            def _(k):
                iy, iz, ix = k // 8, (k // 2) % 4, k % 2
                here = half_spot(array, iy, iz, ix)
                pair(here, one[number][here])

        elif stage == 1 and turn == 0:

            @pl.loop(0, 8)
            def _(k):
                iy, iz = k // 4, k % 4
                there = (iz, iy) if array in SHARED else (iy, iz)
                pair(half_spot(array, iy, iz, x), two[number][there])

        elif stage == 1:

            @pl.loop(0, 8)
            def _(k):
                iz, ix = k // 2, k % 2
                pair(half_spot(array, y, iz, ix), two[number][iz, ix])

        elif stage == 2:

            @pl.loop(0, 4)
            def _(k):
                pair(half_spot(array, y, k, x), three[number][k])

        else:
            total = mine[half_spot(array, y, z, x)].astype(f32)
            for slot in range(3):
                total = total + four[number][slot].astype(f32)
            if array in SHARED:
                outs[array][y * 2 + c, pl.ds(first, size)] = total
            else:
                outs[array][pl.ds(first, size)] = total

    loads = []
    for number, (at, array, first, size, turn) in enumerate(units):
        loads.append(
            pltpu.make_async_copy(
                grads[array].at[spot(array, every, c, every, every) + (pl.ds(first, size),)],
                own[number],
                local.at[number],
            )
        )
    greet(z, x, y, c)
    steps = units[-1][0] + 1

    def step_units(tick):
        return [number for number in range(n) if units[number][0] == tick]

    vec_dst = (vec_one, vec_two, vec_three)
    vec_peer = (device(z, x, y, 1 - c), device(z, 1 - x, y, c), device(z, x, 1 - y, c))

    for tick in range(steps + 4):
        for number in step_units(tick):
            loads[number].start()
            start(number, 0)
        for number in step_units(tick - 1):
            loads[number].wait()
            copies[number, 0].wait_recv()
            add(number, 0)
            start(number, 1)
        for number in step_units(tick - 2):
            copies[number, 1].wait()
            add(number, 1)
            start(number, 2)
        for number in step_units(tick - 3):
            copies[number, 2].wait()
            add(number, 2)
            for stage in (3, 4, 5):
                start(number, stage)
        for number in step_units(tick - 4):
            for stage in (3, 4, 5):
                copies[number, stage].wait()
            add(number, 3)
        if tick < 4:
            if tick == 0:
                vec_sum[...] = grads[6][...]
            if tick < 3:
                remote(vec_sum.at[...], vec_dst[tick], ("v", tick), vsend.at[tick], vrecv.at[tick], vec_peer[tick])
            else:
                vec_four[z] = vec_sum[...]
                for m in (1, 2, 3):
                    remote(vec_sum.at[...], vec_four.at[z], ("v", 2 + m), vsend.at[2 + m], vrecv.at[2 + m], device(flip(z, m), x, y, c))
        if 1 <= tick <= 3:
            pass
        if tick < 3:
            copies["v", tick].wait()
            vec_sum[...] = vec_sum[...] + vec_dst[tick][...]
        if tick == 4:
            for m in (1, 2, 3):
                copies["v", 2 + m].wait()
            outs[6][...] = ((vec_four[0] + vec_four[1]) + (vec_four[2] + vec_four[3]))
        for array in SHARED:
            last = max(units[number][0] for number in range(n) if units[number][1] == array)
            if tick == last + 4:
                here = y * 2 + c
                for k, peer in enumerate((device(z, x, y, 1 - c), device(z, x, 1 - y, c), device(z, x, 1 - y, 1 - c))):
                    slot = SHARED.index(array) * 3 + k
                    remote(outs[array].at[here], outs[array].at[here], ("t", slot), tsend.at[slot], trecv.at[slot], peer)
    for slot in range(6):
        copies["t", slot].wait()
    for number in range(n):
        copies[number, 0].wait_send()


def scatter_gradients(grads):
    units = [(at,) + unit for at, step in enumerate(SCATTER_STEPS) for unit in step]
    n = len(units)
    shapes = [grad.shape for grad in grads]
    outs = []
    for array in range(6):
        rows, columns = shapes[array][4:]
        if array in SHARED:
            outs.append(jax.ShapeDtypeStruct((4, rows, columns), f32))
        else:
            outs.append(jax.ShapeDtypeStruct((rows, columns), f32))
    outs.append(jax.ShapeDtypeStruct(grads[6].shape, f32))
    scratch = []
    for stage in range(5):
        for at, array, first, size, turn in units:
            shared = array in SHARED
            lead = ((4, 2, 2) if shared else (2, 4, 2), (4,), (3,))
            if stage < 2:
                lead = lead[0]
            elif stage == 2:
                lead = ((4, 2) if shared else (2, 4)) if turn == 0 else (4, 2)
            else:
                lead = lead[stage - 2]
            scratch.append(pltpu.VMEM(lead + (size, shapes[array][5]), bf16))
    vec = grads[6].shape
    scratch += [pltpu.VMEM(vec, f32)] * 3 + [pltpu.VMEM((4,) + vec, f32), pltpu.VMEM(vec, f32)]
    scratch += [
        pltpu.SemaphoreType.DMA((n, 6)),
        pltpu.SemaphoreType.DMA((n, 6)),
        pltpu.SemaphoreType.DMA((n,)),
        pltpu.SemaphoreType.DMA((6,)),
        pltpu.SemaphoreType.DMA((6,)),
        pltpu.SemaphoreType.DMA((6,)),
        pltpu.SemaphoreType.DMA((6,)),
    ]
    total = sum(int(grad.size) * grad.dtype.itemsize for grad in grads)
    return pl.pallas_call(
        functools.partial(scatter_kernel, shapes, units),
        out_shape=outs,
        in_specs=[pl.BlockSpec(memory_space=pl.ANY)] * 6 + [pl.BlockSpec(memory_space=pltpu.VMEM)],
        out_specs=[pl.BlockSpec(memory_space=pltpu.VMEM)] * 7,
        scratch_shapes=scratch,
        compiler_params=pltpu.CompilerParams(
            collective_id=1, has_side_effects=True, vmem_limit_bytes=60 * 1024 * 1024
        ),
        cost_estimate=pl.CostEstimate(flops=0, bytes_accessed=2 * total, transcendentals=0),
        name="scatter_gradients",
    )(*grads)


def mm(spec, left, right):
    return jnp.einsum(spec, left, right, preferred_element_type=f32)


def sinusoid_table(feature_width, grid_side, patch_count):
    position = jnp.arange(patch_count, dtype=jnp.int32)
    quarter = feature_width // 4
    omegas = 1.0 / 10000.0 ** (jnp.arange(quarter, dtype=f32) / quarter)

    def half_table(coords):
        angles = coords.astype(f32)[:, None] * omegas[None, :]
        return jnp.concatenate([jnp.sin(angles), jnp.cos(angles)], axis=1)

    return jnp.concatenate(
        [half_table(position % grid_side), half_table(position // grid_side)], axis=1
    )


def norm_forward(stream, gain_row, shift_row):
    centred = stream - jnp.mean(stream, axis=-1, keepdims=True)
    inverse = lax.rsqrt(jnp.mean(centred * centred, axis=-1, keepdims=True) + eps_norm)
    unit_values = centred * inverse
    return (unit_values * gain_row + shift_row, unit_values, inverse)


def norm_backward(incoming, unit_values, inverse, gain_row):
    scaled = incoming * gain_row
    inner_part = (
        scaled
        - jnp.mean(scaled, axis=-1, keepdims=True)
        - unit_values * jnp.mean(scaled * unit_values, axis=-1, keepdims=True)
    )
    width = incoming.shape[-1]
    gain_grad = jnp.sum((incoming * unit_values).reshape(-1, width), axis=0)
    shift_grad = jnp.sum(incoming.reshape(-1, width), axis=0)
    return (inverse * inner_part, gain_grad, shift_grad)


def layer_forward(stream, w_input, w_output, vectors, group_heads, head_dim):
    image_count, token_count, model_width = stream.shape
    groups = w_input.shape[0]
    inner = group_heads * head_dim
    normed_one, unit_one, inverse_one = norm_forward(stream, vectors[0], vectors[1])
    input_one = normed_one.astype(bf16)
    raw_heads = mm("bsd,tdc->btsc", input_one, w_input[:, :, : 3 * inner]).astype(bf16)
    triple = raw_heads.reshape(image_count, groups, token_count, 3, group_heads, head_dim)
    scores = mm("btqhd,btkhd->bthqk", triple[:, :, :, 0], triple[:, :, :, 1]) * head_dim ** (-0.5)
    shifted = jnp.exp(scores - jnp.max(scores, axis=-1, keepdims=True))
    attention = shifted / jnp.sum(shifted, axis=-1, keepdims=True)
    mixed = mm("bthqk,btkhd->btqhd", attention.astype(bf16), triple[:, :, :, 2])
    mixed_low = mixed.reshape(image_count, groups, token_count, inner).astype(bf16)
    after_attn = stream + mm("btsc,tcd->bsd", mixed_low, w_output[:, :inner])
    normed_two, unit_two, inverse_two = norm_forward(after_attn, vectors[2], vectors[3])
    input_two = normed_two.astype(bf16)
    hidden = mm("bsd,tdc->btsc", input_two, w_input[:, :, 3 * inner :])
    active = jax.nn.gelu(hidden, approximate=False).astype(bf16)
    result = after_attn + mm("btsc,tcd->bsd", active, w_output[:, inner:])
    saved_state = (
        unit_one,
        inverse_one,
        input_one,
        triple,
        attention,
        mixed_low,
        unit_two,
        inverse_two,
        input_two,
        hidden,
        active,
    )
    return (result, saved_state)


def layer_backward(stream_grad, saved_state, w_input, w_output, vectors, group_heads, head_dim):
    (
        unit_one,
        inverse_one,
        input_one,
        triple,
        attention,
        mixed_low,
        unit_two,
        inverse_two,
        input_two,
        hidden,
        active,
    ) = saved_state
    image_count, token_count, model_width = stream_grad.shape
    groups = w_input.shape[0]
    inner = group_heads * head_dim
    score_scale = head_dim ** (-0.5)
    grad_low = stream_grad.astype(bf16)
    grad_down = mm("btsc,bsd->tcd", active, grad_low)
    grad_active = mm("bsd,tcd->btsc", grad_low, w_output[:, inner:])
    gelu_back = jax.vjp(lambda values: jax.nn.gelu(values, approximate=False), hidden)[1]
    grad_hidden = gelu_back(grad_active)[0].astype(bf16)
    grad_up = mm("bsd,btsc->tdc", input_two, grad_hidden)
    grad_two = mm("btsc,tdc->bsd", grad_hidden, w_input[:, :, 3 * inner :])
    grad_mid, gain_two, shift_two = norm_backward(grad_two, unit_two, inverse_two, vectors[2])
    grad_mid = grad_mid + stream_grad
    mid_low = grad_mid.astype(bf16)
    grad_attn_rows = mm("btsc,bsd->tcd", mixed_low, mid_low)
    grad_mixed = mm("bsd,tcd->btsc", mid_low, w_output[:, :inner]).astype(bf16)
    grad_mixed = grad_mixed.reshape(image_count, groups, token_count, group_heads, head_dim)
    grad_values = mm("bthqk,btqhd->btkhd", attention.astype(bf16), grad_mixed)
    grad_attention = mm("btqhd,btkhd->bthqk", grad_mixed, triple[:, :, :, 2])
    grad_scores = attention * (
        grad_attention - jnp.sum(attention * grad_attention, axis=-1, keepdims=True)
    )
    scores_low = grad_scores.astype(bf16)
    grad_queries = mm("bthqk,btkhd->btqhd", scores_low, triple[:, :, :, 1]) * score_scale
    grad_keys = mm("bthqk,btqhd->btkhd", scores_low, triple[:, :, :, 0]) * score_scale
    grad_raw = (
        jnp.stack([grad_queries, grad_keys, grad_values], axis=3)
        .reshape(image_count, groups, token_count, 3 * inner)
        .astype(bf16)
    )
    grad_triple = mm("bsd,btsc->tdc", input_one, grad_raw)
    grad_one = mm("btsc,tdc->bsd", grad_raw, w_input[:, :, : 3 * inner])
    grad_stream, gain_one, shift_one = norm_backward(grad_one, unit_one, inverse_one, vectors[0])
    grad_in_cols = jnp.concatenate([grad_triple, grad_up], axis=2)
    grad_out_rows = jnp.concatenate([grad_attn_rows, grad_down], axis=1)
    return (
        grad_stream + grad_mid,
        grad_in_cols,
        grad_out_rows,
        jnp.stack([gain_one, shift_one, gain_two, shift_two]),
    )


def gather_grouped(part, groups):
    whole = lax.all_gather(part, GROUPED, axis=0, tiled=True)
    return whole.reshape(groups, -1, whole.shape[-1])


def scatter_grouped(gradient):
    flat = gradient.reshape(-1, gradient.shape[-1])
    return lax.psum_scatter(flat, GROUPED, scatter_dimension=0, tiled=True)


def ringed(tensor_count):
    return tensor_count == 4 and lax.axis_size("dp") == 8


def gather_all(masters, counted):
    tensor_count = lax.axis_size("tensor")
    columns = masters[6].shape[1]
    flat = [
        master.reshape(-1, master.shape[-1]).astype(bf16) for master in masters[:4]
    ]
    vectors_low = masters[6].astype(bf16).astype(f32)
    if ringed(tensor_count):
        at = lax.axis_index("tensor")
        quarters = [
            lax.dynamic_slice_in_dim(
                master, at * (master.shape[0] // tensor_count), master.shape[0] // tensor_count
            ).astype(bf16)
            for master in masters[4:6]
        ]
        lanes = 256
        vec_part = jnp.concatenate(
            [
                jnp.pad(vectors_low, ((0, 0), (0, lanes - columns))),
                jnp.broadcast_to(counted, (1, lanes)),
            ],
            axis=0,
        )
        wholes = gather_weights([quarters[0], flat[0], flat[1], quarters[1], flat[2], flat[3], vec_part])
        grouped = [
            wholes[k].reshape(tensor_count, -1, wholes[k].shape[-1]) for k in (EIN, EOUT, DIN, DOUT)
        ]
        pixel_w = wholes[PIX].reshape(-1, wholes[PIX].shape[-1])
        bridge_w = wholes[BRI].reshape(-1, wholes[BRI].shape[-1])
        vec_parts = wholes[VEC][0, 0].reshape(8, 8, lanes)
        vectors_all = vec_parts[:, :7, :columns].transpose(1, 0, 2).reshape(7, -1)
        patch_total = jnp.sum(vec_parts[:, 7, 0])
        return grouped, pixel_w, bridge_w, vectors_all, patch_total
    grouped = [gather_grouped(part, tensor_count) for part in flat]
    pixel_w = lax.all_gather(masters[4].astype(bf16), "dp", axis=0, tiled=True)
    bridge_w = lax.all_gather(masters[5].astype(bf16), "dp", axis=0, tiled=True)
    vectors_all = lax.all_gather(vectors_low, "dp", axis=1, tiled=True)
    return grouped, pixel_w, bridge_w, vectors_all, lax.psum(counted, "dp")


def reduce_all(gradients, loss_part, masters):
    tensor_count = lax.axis_size("tensor")
    columns = masters[6].shape[1]
    dp_at = lax.axis_index("dp")
    grouped, grad_pixel, grad_bridge, grad_vectors = gradients
    packed = jnp.concatenate(
        [grad_vectors, jnp.broadcast_to(loss_part, (1, grad_vectors.shape[1]))], axis=0
    )
    if ringed(tensor_count):
        shapes = {
            EIN: masters[0].reshape(-1, masters[0].shape[-1]).shape,
            EOUT: masters[1].reshape(-1, masters[1].shape[-1]).shape,
            DIN: masters[2].reshape(-1, masters[2].shape[-1]).shape,
            DOUT: masters[3].reshape(-1, masters[3].shape[-1]).shape,
            PIX: (masters[4].shape[0] // tensor_count, masters[4].shape[1]),
            BRI: (masters[5].shape[0] // tensor_count, masters[5].shape[1]),
        }
        sources = {PIX: grad_pixel, EIN: grouped[0], EOUT: grouped[1], BRI: grad_bridge, DIN: grouped[2], DOUT: grouped[3]}
        operands = [
            sources[array].astype(bf16).reshape(whole_shape(array, shapes[array]))
            for array in range(6)
        ]
        sums = scatter_gradients(operands + [packed])
        reduced = [sums[EIN], sums[EOUT], sums[DIN], sums[DOUT], sums[PIX], sums[BRI]]
        vector_sum = sums[VEC]
    else:

        def scatter_shared(gradient):
            part = lax.psum_scatter(gradient, EVERY, scatter_dimension=0, tiled=True)
            return lax.all_gather(part, "tensor", axis=0, tiled=True)

        reduced = [scatter_grouped(gradient) for gradient in grouped]
        reduced += [scatter_shared(grad_pixel), scatter_shared(grad_bridge)]
        vector_sum = lax.psum(packed, EVERY)
    own = lax.dynamic_slice_in_dim(vector_sum[:7], dp_at * columns, columns, axis=1)
    reduced = [gradient.reshape(master.shape) for gradient, master in zip(reduced + [own], masters)]
    return reduced, vector_sum[7, 0]


def shards(
    images,
    keep_index,
    unshuffle,
    masked,
    image_valid,
    *state,
):
    masters, firsts, seconds = state[:7], state[7:14], state[14:21]
    encoder_in, encoder_out, decoder_in, decoder_out, pixel_maps, bridge_map, vector_pack = masters
    tensor_count = lax.axis_size("tensor")
    tensor_at = lax.axis_index("tensor")
    counted = jnp.sum(masked.astype(f32) * image_valid.astype(f32)[:, None])
    grouped_w, pixel_w, bridge_w, vectors_all, patch_total = gather_all(masters, counted)
    enc_in_w, enc_out_w, dec_in_w, dec_out_w = grouped_w
    embedding_weight = pixel_w[:PATCH_DIM]
    head_w = pixel_w[PATCH_DIM:]
    enc_vectors = vectors_all[:, :ENCODER_WIDTH]
    dec_vectors = vectors_all[:, ENCODER_WIDTH:]
    enc_heads = H_E // tensor_count
    dec_heads = H_D // tensor_count
    image_count = images.shape[0] // tensor_count

    def own(member):
        return lax.dynamic_slice_in_dim(member, tensor_at * image_count, image_count, axis=0)

    images, keep_index, unshuffle, masked, image_valid = map(
        own, (images, keep_index, unshuffle, masked, image_valid)
    )
    patch_flags = masked.astype(f32) * image_valid.astype(f32)[:, None]
    patch_ids = jnp.arange(IMAGE_PATCHES, dtype=jnp.int32)
    selection_matrix = (keep_index[:, :, None] == patch_ids[None, None, :]).astype(f32)
    retained_pixels = mm("bkp,bpc->bkc", selection_matrix.astype(bf16), images).astype(bf16)
    kept_pos = jnp.einsum(
        "nau,uc->nac",
        selection_matrix,
        sinusoid_table(ENCODER_WIDTH, GRID_PATCHES, IMAGE_PATCHES),
        precision=highest_precision,
    )
    embedded = mm("fzh,hg->fzg", retained_pixels, embedding_weight) + kept_pos
    enc_start = jnp.concatenate(
        [jnp.broadcast_to(enc_vectors[0], (image_count, 1, ENCODER_WIDTH)), embedded], axis=1
    )
    enc_end, enc_saved = layer_forward(
        enc_start, enc_in_w, enc_out_w, enc_vectors[1:5], enc_heads, HD_E
    )
    enc_normed, enc_unit, enc_inverse = norm_forward(enc_end, enc_vectors[5], enc_vectors[6])
    enc_low = enc_normed.astype(bf16)
    projected = mm("bsd,de->bse", enc_low, bridge_w)
    placer = (unshuffle[:, :, None] == jnp.arange(KEEP, dtype=jnp.int32)[None, None, :]).astype(f32)
    mask_column = masked.astype(f32)[:, :, None]
    filled = (
        jnp.einsum("bpk,bke->bpe", placer, projected[:, 1:], precision=highest_precision)
        + mask_column * dec_vectors[0]
        + sinusoid_table(D_D, GRID_PATCHES, IMAGE_PATCHES)
    )
    dec_start = jnp.concatenate([projected[:, :1], filled], axis=1)
    dec_end, dec_saved = layer_forward(
        dec_start, dec_in_w, dec_out_w, dec_vectors[1:5], dec_heads, HD_D
    )
    dec_normed, dec_unit, dec_inverse = norm_forward(dec_end, dec_vectors[5], dec_vectors[6])
    dec_low = dec_normed.astype(bf16)
    predicted = mm("bpe,ec->bpc", dec_low[:, 1:], head_w)
    pixels = images.astype(f32)
    pix_centred = pixels - jnp.mean(pixels, axis=-1, keepdims=True)
    variance = jnp.sum(pix_centred * pix_centred, axis=-1, keepdims=True) / (PATCH_DIM - 1)
    target = pix_centred * lax.rsqrt(variance + eps_norm)
    errors = predicted - target
    patch_weight = patch_flags / patch_total
    loss_part = jnp.sum(jnp.mean(errors * errors, axis=-1) * patch_weight)
    grad_pred = (errors * (2.0 / PATCH_DIM) * patch_weight[:, :, None]).astype(bf16)
    grad_head = mm("bpe,bpc->ec", dec_low[:, 1:], grad_pred)
    grad_dec_rows = mm("bpc,ec->bpe", grad_pred, head_w)
    grad_dec_norm = jnp.concatenate([jnp.zeros((image_count, 1, D_D), f32), grad_dec_rows], axis=1)
    grad_dec_end, dec_gain, dec_shift = norm_backward(
        grad_dec_norm, dec_unit, dec_inverse, dec_vectors[5]
    )
    grad_dec_start, grad_dec_in, grad_dec_out, grad_dec_vectors = layer_backward(
        grad_dec_end, dec_saved, dec_in_w, dec_out_w, dec_vectors[1:5], dec_heads, HD_D
    )
    grad_mask = jnp.sum(grad_dec_start[:, 1:] * mask_column, axis=(0, 1))
    grad_rest = jnp.einsum(
        "bpk,bpe->bke", placer, grad_dec_start[:, 1:], precision=highest_precision
    )
    grad_projected = jnp.concatenate([grad_dec_start[:, :1], grad_rest], axis=1).astype(bf16)
    grad_bridge = mm("bsd,bse->de", enc_low, grad_projected)
    grad_enc_norm = mm("bse,de->bsd", grad_projected, bridge_w)
    grad_enc_end, enc_gain, enc_shift = norm_backward(
        grad_enc_norm, enc_unit, enc_inverse, enc_vectors[5]
    )
    grad_enc_start, grad_enc_in, grad_enc_out, grad_enc_vectors = layer_backward(
        grad_enc_end, enc_saved, enc_in_w, enc_out_w, enc_vectors[1:5], enc_heads, HD_E
    )
    grad_class = jnp.sum(grad_enc_start[:, 0], axis=0)
    grad_embed = mm("wmx,wmg->xg", retained_pixels, grad_enc_start[:, 1:].astype(bf16))
    grad_vectors = jnp.concatenate(
        [
            jnp.concatenate(
                [grad_class[None], grad_enc_vectors, enc_gain[None], enc_shift[None]], axis=0
            ),
            jnp.concatenate(
                [grad_mask[None], grad_dec_vectors, dec_gain[None], dec_shift[None]], axis=0
            ),
        ],
        axis=1,
    )
    grad_pixel = jnp.concatenate([grad_embed, grad_head], axis=0)

    reduced, loss_value = reduce_all(
        ([grad_enc_in, grad_enc_out, grad_dec_in, grad_dec_out], grad_pixel, grad_bridge, grad_vectors),
        loss_part,
        masters,
    )
    decays = (decay_matrix,) * 6 + (0.0,)
    share_counts = (1.0,) * 4 + (float(tensor_count),) * 3
    bias_one = 1.0 - beta_one**step_count
    bias_two = 1.0 - beta_two**step_count
    new_firsts, new_seconds, updates = ([], [], [])
    for gradient, master, moment_one, moment_two, decay_value in zip(
        reduced, masters, firsts, seconds, decays
    ):
        next_one = beta_one * moment_one + (1.0 - beta_one) * gradient
        next_two = beta_two * moment_two + (1.0 - beta_two) * gradient * gradient
        new_firsts.append(next_one)
        new_seconds.append(next_two)
        updates.append(
            next_one / bias_one / (jnp.sqrt(next_two / bias_two) + eps_moment)
            + decay_value * master
        )

    def squares(members):
        return jnp.stack(
            [jnp.sum(member * member) / count for member, count in zip(members, share_counts)]
        )

    totals = lax.psum((squares(masters), squares(updates)), EVERY)
    weight_norm = jnp.sqrt(totals[0])
    update_norm = jnp.sqrt(totals[1])
    step_ratio = learn_rate * weight_norm / update_norm
    news = [
        master - step_ratio[position] * update
        for position, (master, update) in enumerate(zip(masters, updates))
    ]
    return tuple(
        [loss_value, jnp.stack([weight_norm, update_norm])] + new_firsts + new_seconds + news
    )


def solution(mesh):
    state_specs = (
        P("dp", "tensor", None),
        P("tensor", "dp", None),
        P("dp", "tensor", None),
        P("tensor", "dp", None),
        P("dp", None),
        P("dp", None),
        P(None, "dp"),
    )
    in_specs = (
        P("dp", None, None),
        P("dp", None),
        P("dp", None),
        P("dp", None),
        P("dp"),
    ) + state_specs * 3
    out_specs = (P(), P()) + state_specs * 3
    return jax.shard_map(shards, mesh=mesh, in_specs=in_specs, out_specs=out_specs, check_vma=False)
```

```python
import functools

import jax
import jax.numpy as jnp
from jax import lax
from jax.experimental import pallas as pl
from jax.experimental.pallas import tpu as pltpu
from jax.sharding import PartitionSpec as P
import numpy as np

ENCODER_WIDTH = 768
H_E = 12
HD_E = 64
D_D = 512
H_D = 16
HD_D = 32
PATCH_DIM = 768
GRID_PATCHES = 14
IMAGE_PATCHES = 196
KEEP = 49

eps_norm = 1e-06
beta_one = 0.9
beta_two = 0.999
step_count = 7.0
learn_rate = 0.3
decay_matrix = 0.05
eps_moment = 1e-06
f32 = jnp.float32
bf16 = jnp.bfloat16
EVERY = ("dp", "tensor")
GROUPED = ("tensor", "dp")


MESH_ID = pl.DeviceIdType.MESH
PIX, EIN, EOUT, BRI, DIN, DOUT, VEC = range(7)


def place():
    dp_at = lax.axis_index("dp")
    group = lax.axis_index("tensor")
    z, x = lax.div(dp_at, 2), lax.rem(dp_at, 2)
    y, c = lax.div(group, 2), lax.rem(group, 2)
    return z, x, y, c


def device(z, x, y, c):
    return (z * 2 + x, y * 2 + c)


def flip(z, m):
    low = lax.rem(z, 2)
    high = lax.div(z, 2)
    if m % 2:
        low = 1 - low
    if m // 2:
        high = 1 - high
    return high * 2 + low


def greet(z, x, y, c):
    barrier = pltpu.get_barrier_semaphore()
    peers = [
        device(z, x, y, 1 - c),
        device(z, x, 1 - y, c),
        device(z, 1 - x, y, c),
        device(flip(z, 1), x, y, c),
        device(flip(z, 2), x, y, c),
        device(flip(z, 3), x, y, c),
    ]
    for peer in peers:
        pl.semaphore_signal(barrier, inc=1, device_id=peer, device_id_type=MESH_ID)
    pl.semaphore_wait(barrier, 6)


SHARED = (PIX, BRI)


def spot(array, y, c, z, x):
    return (z, x, y, c) if array in SHARED else (y, c, z, x)


def half_spot(array, y, z, x):
    return (z, x, y) if array in SHARED else (y, z, x)


def whole_shape(array, part):
    return ((4, 2, 2, 2) if array in SHARED else (2, 2, 4, 2)) + part


GATHER_STEPS = (
    ((VEC, 0, 8, 0), (PIX, 0, 24, 0), (PIX, 24, 16, 1)),
    ((EIN, 0, 32, 0), (EIN, 32, 16, 1)),
    ((EIN, 48, 16, 0), (EIN, 64, 32, 1)),
    ((EOUT, 0, 32, 0), (EOUT, 32, 32, 1)),
    ((EOUT, 64, 32, 0), (EOUT, 96, 24, 1)),
    ((BRI, 0, 8, 0), (BRI, 8, 16, 1), (DIN, 0, 32, 0), (DIN, 32, 32, 1)),
    ((DOUT, 0, 48, 0), (DOUT, 48, 32, 1)),
)


def gather_kernel(*refs):
    count = 7
    parts = refs[:count]
    outs = refs[count : 2 * count]
    send, recv, local = refs[2 * count :]
    z, x, y, c = place()
    units = []
    for at, step in enumerate(GATHER_STEPS):
        for unit in step:
            units.append((at,) + unit)
    copies = {}

    def rows(array, region, first, size):
        ref = outs[array]
        return ref.at[region + (pl.ds(first, size),)]

    def plan(number, stage):
        at, array, first, size, turn = units[number]
        every = slice(None)
        if stage < 3:
            src = parts[array].at[pl.ds(first, size)]
            dst = rows(array, spot(array, y, c, z, x), first, size)
            peer = device(flip(z, stage + 1), x, y, c)
        else:
            if stage == 3:
                region = spot(array, y, c, every, x)
                peer = device(z, x, 1 - y, c) if turn == 0 else device(z, 1 - x, y, c)
            elif stage == 4 and turn == 0:
                region = spot(array, every, c, every, x)
                peer = device(z, 1 - x, y, c)
            elif stage == 4:
                region = spot(array, y, c, every, every)
                peer = device(z, x, 1 - y, c)
            else:
                region = spot(array, every, c, every, every)
                peer = device(z, x, y, 1 - c)
            src = dst = rows(array, region, first, size)
        return pltpu.make_async_remote_copy(
            src_ref=src,
            dst_ref=dst,
            send_sem=send.at[number, stage],
            recv_sem=recv.at[number, stage],
            device_id=peer,
            device_id_type=MESH_ID,
        )

    def start(number, stage):
        copies[number, stage] = plan(number, stage)
        copies[number, stage].start()

    own = []
    for array in range(count):
        own.append(
            pltpu.make_async_copy(parts[array], outs[array].at[spot(array, y, c, z, x)], local.at[array])
        )
        own[-1].start()
    greet(z, x, y, c)
    steps = len(GATHER_STEPS)
    waited = set()
    for tick in range(steps + 4):
        for number, unit in enumerate(units):
            if unit[0] == tick:
                for stage in range(3):
                    start(number, stage)
        for number, unit in enumerate(units):
            if unit[0] == tick - 1:
                if unit[1] not in waited:
                    waited.add(unit[1])
                    own[unit[1]].wait()
                for stage in range(3):
                    copies[number, stage].wait_recv()
                start(number, 3)
        for back in (2, 3):
            for number, unit in enumerate(units):
                if unit[0] == tick - back:
                    copies[number, back + 1].wait_recv()
                    start(number, back + 2)
        for number, unit in enumerate(units):
            if unit[0] == tick - 4:
                copies[number, 5].wait_recv()
    for key in copies:
        copies[key].wait_send()


def gather_weights(parts):
    count = 7
    units = sum(len(step) for step in GATHER_STEPS)
    outs = [
        jax.ShapeDtypeStruct(whole_shape(array, part.shape), part.dtype)
        for array, part in enumerate(parts)
    ]
    total = sum(int(part.size) * 32 * part.dtype.itemsize for part in parts)
    return pl.pallas_call(
        gather_kernel,
        out_shape=outs,
        in_specs=[pl.BlockSpec(memory_space=pltpu.VMEM)] * count,
        out_specs=[pl.BlockSpec(memory_space=pl.ANY)] * count,
        scratch_shapes=[
            pltpu.SemaphoreType.DMA((units, 6)),
            pltpu.SemaphoreType.DMA((units, 6)),
            pltpu.SemaphoreType.DMA((count,)),
        ],
        compiler_params=pltpu.CompilerParams(collective_id=0, has_side_effects=True),
        cost_estimate=pl.CostEstimate(flops=0, bytes_accessed=2 * total, transcendentals=0),
        name="gather_weights",
    )(*parts)


SCATTER_STEPS = (
    ((DOUT, 0, 48, 0), (DOUT, 48, 32, 1)),
    ((BRI, 0, 8, 0), (BRI, 8, 16, 1), (DIN, 0, 32, 0), (DIN, 32, 32, 1)),
    ((PIX, 0, 24, 0), (PIX, 24, 16, 1)),
    ((EOUT, 0, 32, 0), (EOUT, 32, 32, 1)),
    ((EOUT, 64, 32, 0), (EOUT, 96, 24, 1)),
    ((EIN, 0, 32, 0), (EIN, 32, 16, 1)),
    ((EIN, 48, 16, 0), (EIN, 64, 32, 1)),
)
def scatter_kernel(shapes, units, *refs):
    grads = refs[:7]
    outs = refs[7:14]
    refs = refs[14:]
    n = len(units)
    own, one, two, three, four = (refs[k * n : (k + 1) * n] for k in range(5))
    vec_one, vec_two, vec_three, vec_four, vec_sum = refs[5 * n : 5 * n + 5]
    send, recv, local, vsend, vrecv, tsend, trecv = refs[5 * n + 5 :]
    z, x, y, c = place()
    every = slice(None)
    copies = {}

    def remote(src, dst, key, send_sem, recv_sem, peer):
        copies[key] = pltpu.make_async_remote_copy(
            src_ref=src,
            dst_ref=dst,
            send_sem=send_sem,
            recv_sem=recv_sem,
            device_id=peer,
            device_id_type=MESH_ID,
        )
        copies[key].start()

    def start(number, stage):
        at, array, first, size, turn = units[number]
        mine = own[number]
        if stage == 0:
            peer = device(z, x, y, 1 - c)
            src = grads[array].at[
                spot(array, every, 1 - c, every, every) + (pl.ds(first, size),)
            ]
            dst = one[number]
        elif stage == 1 and turn == 0:
            peer = device(z, 1 - x, y, c)
            src, dst = mine.at[half_spot(array, every, every, 1 - x)], two[number]
        elif stage == 1:
            peer = device(z, x, 1 - y, c)
            src, dst = mine.at[half_spot(array, 1 - y, every, every)], two[number]
        elif stage == 2 and turn == 0:
            peer = device(z, x, 1 - y, c)
            src, dst = mine.at[half_spot(array, 1 - y, every, x)], three[number]
        elif stage == 2:
            peer = device(z, 1 - x, y, c)
            src, dst = mine.at[half_spot(array, y, every, 1 - x)], three[number]
        else:
            other = flip(z, stage - 2)
            peer = device(other, x, y, c)
            src, dst = mine.at[half_spot(array, y, other, x)], four[number].at[stage - 3]
        remote(src, dst, (number, stage), send.at[number, stage], recv.at[number, stage], peer)

    def add(number, stage):
        at, array, first, size, turn = units[number]
        mine = own[number]

        def pair(here, there):
            mine[here] = (mine[here].astype(f32) + there.astype(f32)).astype(bf16)

        if stage == 0:

            @pl.loop(0, 16)
            def _(k):
                iy, iz, ix = k // 8, (k // 2) % 4, k % 2
                here = half_spot(array, iy, iz, ix)
                pair(here, one[number][here])

        elif stage == 1 and turn == 0:

            @pl.loop(0, 8)
            def _(k):
                iy, iz = k // 4, k % 4
                there = (iz, iy) if array in SHARED else (iy, iz)
                pair(half_spot(array, iy, iz, x), two[number][there])

        elif stage == 1:

            @pl.loop(0, 8)
            def _(k):
                iz, ix = k // 2, k % 2
                pair(half_spot(array, y, iz, ix), two[number][iz, ix])

        elif stage == 2:

            @pl.loop(0, 4)
            def _(k):
                pair(half_spot(array, y, k, x), three[number][k])

        else:
            total = mine[half_spot(array, y, z, x)].astype(f32)
            for slot in range(3):
                total = total + four[number][slot].astype(f32)
            if array in SHARED:
                outs[array][y * 2 + c, pl.ds(first, size)] = total
            else:
                outs[array][pl.ds(first, size)] = total

    loads = []
    for number, (at, array, first, size, turn) in enumerate(units):
        loads.append(
            pltpu.make_async_copy(
                grads[array].at[spot(array, every, c, every, every) + (pl.ds(first, size),)],
                own[number],
                local.at[number],
            )
        )
    greet(z, x, y, c)
    steps = units[-1][0] + 1

    def step_units(tick):
        return [number for number in range(n) if units[number][0] == tick]

    vec_dst = (vec_one, vec_two, vec_three)
    vec_peer = (device(z, x, y, 1 - c), device(z, 1 - x, y, c), device(z, x, 1 - y, c))

    for tick in range(steps + 4):
        for number in step_units(tick):
            loads[number].start()
            start(number, 0)
        for number in step_units(tick - 1):
            loads[number].wait()
            copies[number, 0].wait_recv()
            add(number, 0)
            start(number, 1)
        for number in step_units(tick - 2):
            copies[number, 1].wait()
            add(number, 1)
            start(number, 2)
        for number in step_units(tick - 3):
            copies[number, 2].wait()
            add(number, 2)
            for stage in (3, 4, 5):
                start(number, stage)
        for number in step_units(tick - 4):
            for stage in (3, 4, 5):
                copies[number, stage].wait()
            add(number, 3)
        if tick < 4:
            if tick == 0:
                vec_sum[...] = grads[6][...]
            if tick < 3:
                remote(vec_sum.at[...], vec_dst[tick], ("v", tick), vsend.at[tick], vrecv.at[tick], vec_peer[tick])
            else:
                vec_four[z] = vec_sum[...]
                for m in (1, 2, 3):
                    remote(vec_sum.at[...], vec_four.at[z], ("v", 2 + m), vsend.at[2 + m], vrecv.at[2 + m], device(flip(z, m), x, y, c))
        if 1 <= tick <= 3:
            pass
        if tick < 3:
            copies["v", tick].wait()
            vec_sum[...] = vec_sum[...] + vec_dst[tick][...]
        if tick == 4:
            for m in (1, 2, 3):
                copies["v", 2 + m].wait()
            outs[6][...] = ((vec_four[0] + vec_four[1]) + (vec_four[2] + vec_four[3]))
        for array in SHARED:
            last = max(units[number][0] for number in range(n) if units[number][1] == array)
            if tick == last + 4:
                here = y * 2 + c
                for k, peer in enumerate((device(z, x, y, 1 - c), device(z, x, 1 - y, c), device(z, x, 1 - y, 1 - c))):
                    slot = SHARED.index(array) * 3 + k
                    remote(outs[array].at[here], outs[array].at[here], ("t", slot), tsend.at[slot], trecv.at[slot], peer)
    for slot in range(6):
        copies["t", slot].wait()
    for number in range(n):
        copies[number, 0].wait_send()


def scatter_gradients(grads):
    units = [(at,) + unit for at, step in enumerate(SCATTER_STEPS) for unit in step]
    n = len(units)
    shapes = [grad.shape for grad in grads]
    outs = []
    for array in range(6):
        rows, columns = shapes[array][4:]
        if array in SHARED:
            outs.append(jax.ShapeDtypeStruct((4, rows, columns), f32))
        else:
            outs.append(jax.ShapeDtypeStruct((rows, columns), f32))
    outs.append(jax.ShapeDtypeStruct(grads[6].shape, f32))
    scratch = []
    for stage in range(5):
        for at, array, first, size, turn in units:
            shared = array in SHARED
            lead = ((4, 2, 2) if shared else (2, 4, 2), (4,), (3,))
            if stage < 2:
                lead = lead[0]
            elif stage == 2:
                lead = ((4, 2) if shared else (2, 4)) if turn == 0 else (4, 2)
            else:
                lead = lead[stage - 2]
            scratch.append(pltpu.VMEM(lead + (size, shapes[array][5]), bf16))
    vec = grads[6].shape
    scratch += [pltpu.VMEM(vec, f32)] * 3 + [pltpu.VMEM((4,) + vec, f32), pltpu.VMEM(vec, f32)]
    scratch += [
        pltpu.SemaphoreType.DMA((n, 6)),
        pltpu.SemaphoreType.DMA((n, 6)),
        pltpu.SemaphoreType.DMA((n,)),
        pltpu.SemaphoreType.DMA((6,)),
        pltpu.SemaphoreType.DMA((6,)),
        pltpu.SemaphoreType.DMA((6,)),
        pltpu.SemaphoreType.DMA((6,)),
    ]
    total = sum(int(grad.size) * grad.dtype.itemsize for grad in grads)
    return pl.pallas_call(
        functools.partial(scatter_kernel, shapes, units),
        out_shape=outs,
        in_specs=[pl.BlockSpec(memory_space=pl.ANY)] * 6 + [pl.BlockSpec(memory_space=pltpu.VMEM)],
        out_specs=[pl.BlockSpec(memory_space=pltpu.VMEM)] * 7,
        scratch_shapes=scratch,
        compiler_params=pltpu.CompilerParams(
            collective_id=1, has_side_effects=True, vmem_limit_bytes=60 * 1024 * 1024
        ),
        cost_estimate=pl.CostEstimate(flops=0, bytes_accessed=2 * total, transcendentals=0),
        name="scatter_gradients",
    )(*grads)


def sinusoid_table(feature_width, grid_side, patch_count, padded):
    position = np.arange(patch_count)
    quarter = feature_width // 4
    omegas = 1.0 / 10000.0 ** (np.arange(quarter) / quarter)
    parts = []
    for coords in (position % grid_side, position // grid_side):
        angles = coords[:, None] * omegas[None, :]
        parts += [np.sin(angles), np.cos(angles)]
    table = np.concatenate(parts, axis=1).astype(np.float32)
    return jnp.asarray(np.pad(table, ((0, padded - patch_count), (0, 0))))


GROUPS = 4
ENC = dict(step=128, images=4, block=64, tokens=50, width=768, heads=3, head=64, hidden=768, spans=1)
DEC = dict(step=208, images=4, block=208, tokens=197, width=512, heads=4, head=32, hidden=512, spans=4)
CLASS_ROW = 49
MASK_ROW = 50


def dot(left, right, dims=((1,), (0,)), precision=None):
    return lax.dot_general(
        left, right, (dims, ((), ())), preferred_element_type=f32, precision=precision
    )


def dot_t(left, right):
    return dot(left, right, ((0,), (0,)))


def dot_nt(left, right):
    return dot(left, right, ((1,), (1,)))


def exact_dot(left, right, dims):
    return dot(left, right, dims, lax.Precision.HIGHEST)


def row_loop(count, step, body):
    @pl.loop(0, count // step)
    def _(k):
        body(pl.ds(pl.multiple_of(k * step, step), step))


def fold(values):
    step, width = values.shape
    return jnp.sum(values.reshape(step // 8, 8, width), axis=0)


def norm_rows(source, gain, shift, unit, inverse, low, step):
    def body(rows):
        values = source[rows]
        centred = values - jnp.mean(values, axis=-1, keepdims=True)
        scale = lax.rsqrt(jnp.mean(centred * centred, axis=-1, keepdims=True) + eps_norm)
        normed = centred * scale
        unit[rows] = normed
        inverse[rows] = scale
        low[rows] = (normed * gain + shift).astype(bf16)

    row_loop(source.shape[0], step, body)


def norm_back_rows(incoming, unit, inverse, gain, result, residual, sums, at, step):
    width = incoming.shape[-1]

    def body(rows):
        given = incoming[rows]
        normed = unit[rows]
        scaled = given * gain
        inner = (
            scaled
            - jnp.mean(scaled, axis=-1, keepdims=True)
            - normed * jnp.mean(scaled * normed, axis=-1, keepdims=True)
        )
        value = inverse[rows] * inner
        if residual is not None:
            value = value + residual[rows]
        sums[at] = sums[at] + fold(given * normed)
        sums[at + 1] = sums[at + 1] + fold(given)
        result[rows] = value

    row_loop(incoming.shape[0], step, body)


def attend_mask(dims):
    size = dims["block"] * dims["images"] // dims["spans"]
    key = lax.broadcasted_iota(jnp.int32, (size, size), 1)
    if dims["spans"] == 1:
        query = lax.broadcasted_iota(jnp.int32, (size, size), 0)
        return ((key // dims["block"]) == (query // dims["block"])) & (
            (key % dims["block"]) < dims["tokens"]
        )
    return key < dims["tokens"]


def layer_forward_rows(dims, stream, w_in, w_out, vectors, saved):
    unit_one, inv_one, low_one, qkv, probs, mixed, unit_two, inv_two, low_two, active, slope = saved
    count, width = stream.shape
    inner = dims["heads"] * dims["head"]
    span = count // dims["spans"]
    norm_rows(stream, vectors[1:2, :], vectors[2:3, :], unit_one, inv_one, low_one, dims["step"])

    @pl.loop(0, GROUPS)
    def _(t):
        weights = w_in[t, :, : 3 * inner] if inner % 128 == 0 else w_in[t][:, : 3 * inner]

        def body(rows):
            qkv[t, rows] = dot(low_one[rows], weights).astype(bf16)

        body(slice(None))

    scale = dims["head"] ** (-0.5)

    @pl.loop(0, GROUPS * dims["spans"])
    def _(k):
        t = k // dims["spans"]
        b = k % dims["spans"]
        rows = pl.ds(pl.multiple_of(b * span, span), span)
        triple = qkv[t, rows]
        allowed = attend_mask(dims)
        results = []
        for head in range(dims["heads"]):
            q, key, v = (
                triple[:, part * inner + head * dims["head"] : part * inner + (head + 1) * dims["head"]]
                for part in range(3)
            )
            scores = jnp.where(allowed, dot_nt(q, key) * scale, -1e30)
            shifted = jnp.exp(scores - jnp.max(scores, axis=-1, keepdims=True))
            share = shifted / jnp.sum(shifted, axis=-1, keepdims=True)
            probs[k * dims["heads"] + head] = share
            results.append(dot(share.astype(bf16), v))
        mixed[t, rows] = jnp.concatenate(results, axis=1).astype(bf16)

    @pl.loop(0, GROUPS)
    def _(t):
        weights = w_out[t, :inner]

        def body(rows):
            stream[rows] = stream[rows] + dot(mixed[t, rows], weights)

        body(slice(None))

    norm_rows(stream, vectors[3:4, :], vectors[4:5, :], unit_two, inv_two, low_two, dims["step"])

    @pl.loop(0, GROUPS)
    def _(t):
        up = w_in[t, :, 3 * inner :] if inner % 128 == 0 else w_in[t][:, 3 * inner :]
        down = w_out[t, inner:]

        def body(rows):
            slope[t, rows] = dot(low_two[rows], up)

        body(slice(None))

        def bend(rows):
            hidden = slope[t, rows]
            level = 0.5 + 0.5 * lax.erf(hidden * (0.5**0.5))
            active[t, rows] = (hidden * level).astype(bf16)
            slope[t, rows] = level + hidden * (
                jnp.exp(-0.5 * hidden * hidden) * (0.5 / np.pi) ** 0.5
            )

        row_loop(count, 32, bend)

        def body_two(rows):
            stream[rows] = stream[rows] + dot(active[t, rows], down)

        body_two(slice(None))


def layer_backward_rows(dims, given, spare, w_in, w_out, vectors, saved, low, flow, grad_in, grad_out, sums):
    unit_one, inv_one, low_one, qkv, probs, mixed, unit_two, inv_two, low_two, active, slope = saved
    count, width = given.shape
    inner = dims["heads"] * dims["head"]
    span = count // dims["spans"]
    aligned = inner % 128 == 0

    def lower(rows):
        low[rows] = given[rows].astype(bf16)
        spare[rows] = jnp.zeros_like(spare[rows])

    row_loop(count, 32, lower)

    @pl.loop(0, GROUPS)
    def _(t):
        down = w_out[t, inner:]
        up = w_in[t, :, 3 * inner :] if aligned else w_in[t][:, 3 * inner :]
        grad_out[t, inner:] = dot_t(active[t], low[...]).astype(bf16)

        def body(rows):
            flow[rows] = (slope[t, rows] * dot_nt(low[rows], down)).astype(bf16)
            spare[rows] = spare[rows] + dot_nt(flow[rows], up)

        body(slice(None))
        grad_up = dot_t(low_two[...], flow[...]).astype(bf16)
        if aligned:
            grad_in[t, :, 3 * inner :] = grad_up
        else:
            grad_in[t] = jnp.concatenate([jnp.zeros((width, 3 * inner), bf16), grad_up], axis=1)

    norm_back_rows(spare, unit_two, inv_two, vectors[3:4, :], given, given, sums, 3, dims["step"])
    row_loop(count, 32, lower)

    @pl.loop(0, GROUPS)
    def _(t):
        weights = w_out[t, :inner]
        grad_out[t, :inner] = dot_t(mixed[t], low[...]).astype(bf16)

        def body(rows):
            mixed[t, rows] = dot_nt(low[rows], weights).astype(bf16)

        body(slice(None))

    scale = dims["head"] ** (-0.5)

    @pl.loop(0, GROUPS * dims["spans"])
    def _(k):
        t = k // dims["spans"]
        b = k % dims["spans"]
        rows = pl.ds(pl.multiple_of(b * span, span), span)
        triple = qkv[t, rows]
        back = mixed[t, rows]
        parts = ([], [], [])
        for head in range(dims["heads"]):
            q, key, v = (
                triple[:, part * inner + head * dims["head"] : part * inner + (head + 1) * dims["head"]]
                for part in range(3)
            )
            grad_o = back[:, head * dims["head"] : (head + 1) * dims["head"]]
            share = probs[k * dims["heads"] + head]
            grad_p = dot_nt(grad_o, v)
            grad_s = share * (grad_p - jnp.sum(share * grad_p, axis=-1, keepdims=True))
            low_s = grad_s.astype(bf16)
            parts[0].append(dot(low_s, key) * scale)
            parts[1].append(dot_t(low_s, q) * scale)
            parts[2].append(dot_t(share.astype(bf16), grad_o))
        qkv[t, rows] = jnp.concatenate(parts[0] + parts[1] + parts[2], axis=1).astype(bf16)

    @pl.loop(0, GROUPS)
    def _(t):
        weights = w_in[t, :, : 3 * inner] if aligned else w_in[t][:, : 3 * inner]
        grad_triple = dot_t(low_one[...], qkv[t]).astype(bf16)
        if aligned:
            grad_in[t, :, : 3 * inner] = grad_triple
        else:
            grad_in[t] = jnp.concatenate([grad_triple, grad_in[t][:, 3 * inner :]], axis=1)

        def body(rows):
            spare[rows] = spare[rows] + dot_nt(qkv[t, rows], weights)

        body(slice(None))

    norm_back_rows(spare, unit_one, inv_one, vectors[1:2, :], given, given, sums, 1, dims["step"])


def saved_shapes(dims):
    count = dims["images"] * dims["block"]
    width, inner = dims["width"], dims["heads"] * dims["head"]
    span = count // dims["spans"]
    return [
        ((count, width), f32),
        ((count, 1), f32),
        ((count, width), bf16),
        ((GROUPS, count, 3 * inner), bf16),
        ((GROUPS * dims["spans"] * dims["heads"], span, span), f32),
        ((GROUPS, count, inner), bf16),
        ((count, width), f32),
        ((count, 1), f32),
        ((count, width), bf16),
        ((GROUPS, count, dims["hidden"]), bf16),
        ((GROUPS, count, dims["hidden"]), f32),
    ]


def decoder_kernel(*refs):
    projected, codes, weight_rows, images, table, w_in, w_out, head, vectors = refs[:9]
    grad_in, grad_out, grad_head, grad_projected, vec_out = refs[9:14]
    stream, given, unit, inverse, low, flow, sums, loss = refs[14:22]
    saved = refs[22:]
    dims = DEC
    count, width = stream.shape
    block = dims["block"]
    sums[...] = jnp.zeros_like(sums)
    loss[...] = jnp.zeros_like(loss)

    def placer(b):
        return (
            lax.broadcasted_iota(jnp.int32, (64, block), 0) == codes[b][:, :block]
        ).astype(f32)

    def block_rows(b):
        return pl.ds(pl.multiple_of(b * block, block), block)

    @pl.loop(0, dims["images"])
    def _(b):
        at = lax.broadcasted_iota(jnp.int32, (64, width), 0)
        source = jnp.where(at == MASK_ROW, vectors[0:1, :], projected[b])
        source = jnp.where(at > MASK_ROW, 0.0, source)
        stream[block_rows(b)] = exact_dot(placer(b), source, ((0,), (0,))) + table[...]

    layer_forward_rows(dims, stream, w_in, w_out, vectors, saved)
    norm_rows(stream, vectors[5:6, :], vectors[6:7, :], unit, inverse, low, dims["step"])
    grad_head[...] = jnp.zeros_like(grad_head)
    pixels_wide = images.shape[-1]

    @pl.loop(0, dims["images"])
    def _(b):
        rows = block_rows(b)
        predicted = dot(low[rows], head[...])
        pixels = images[b].astype(f32)
        centred = pixels - jnp.mean(pixels, axis=-1, keepdims=True)
        variance = jnp.sum(centred * centred, axis=-1, keepdims=True) / (pixels_wide - 1)
        errors = predicted - centred * lax.rsqrt(variance + eps_norm)
        at = lax.broadcasted_iota(jnp.int32, (64, 128), 0)
        spread = jnp.where(at == MASK_ROW, weight_rows[b], 0.0)
        weight = exact_dot(placer(b), spread, ((0,), (0,)))[:, :1]
        loss[...] = loss[...] + fold(errors * errors * weight)
        grad_low = (errors * (2.0 / pixels_wide) * weight).astype(bf16)
        grad_head[...] = grad_head[...] + dot_t(low[rows], grad_low)
        given[rows] = dot_nt(grad_low, head[...])

    norm_back_rows(given, unit, inverse, vectors[5:6, :], given, None, sums, 5, dims["step"])
    layer_backward_rows(
        dims, given, stream, w_in, w_out, vectors, saved, low, flow, grad_in, grad_out, sums
    )

    @pl.loop(0, dims["images"])
    def _(b):
        back = exact_dot(placer(b), given[block_rows(b)], ((1,), (0,)))
        at = lax.broadcasted_iota(jnp.int32, (64, width), 0)
        grad_projected[b] = jnp.where(at < MASK_ROW, back, 0.0).astype(bf16)
        sums[0] = sums[0] + fold(jnp.where(at == MASK_ROW, back, 0.0))

    for row in range(7):
        vec_out[row : row + 1, :] = jnp.sum(sums[row], axis=0, keepdims=True)
    total = jnp.sum(jnp.sum(loss[...], axis=0, keepdims=True), axis=1, keepdims=True)
    vec_out[7:8, :] = jnp.broadcast_to(total / pixels_wide, (1, width))


def decoder_step(projected, codes, weight_rows, images, table, w_in, w_out, head, vectors):
    dims = DEC
    count, width = dims["images"] * dims["block"], dims["width"]
    outs = [
        jax.ShapeDtypeStruct(w_in.shape, bf16),
        jax.ShapeDtypeStruct(w_out.shape, bf16),
        jax.ShapeDtypeStruct(head.shape, f32),
        jax.ShapeDtypeStruct(projected.shape, bf16),
        jax.ShapeDtypeStruct((8, width), f32),
    ]
    scratch = [
        ((count, width), f32),
        ((count, width), f32),
        ((count, width), f32),
        ((count, 1), f32),
        ((count, width), bf16),
        ((count, dims["hidden"]), bf16),
        ((7, 8, width), f32),
        ((8, images.shape[-1]), f32),
    ] + saved_shapes(dims)
    return pl.pallas_call(
        decoder_kernel,
        out_shape=outs,
        scratch_shapes=[pltpu.VMEM(shape, dtype) for shape, dtype in scratch],
        compiler_params=pltpu.CompilerParams(vmem_limit_bytes=62 * 1024 * 1024),
        name="decoder_step",
    )(projected, codes, weight_rows, images, table, w_in, w_out, head, vectors)


def encoder_forward_kernel(*refs):
    kept, images, table, w_in, w_out, embed, bridge, vectors = refs[:8]
    projected, retained, unit, inverse, low = refs[8:13]
    saved = refs[13:24]
    (stream,) = refs[24:]
    dims = ENC
    count, width = stream.shape
    block = dims["block"]

    @pl.loop(0, dims["images"])
    def _(b):
        rows = pl.ds(pl.multiple_of(b * block, block), block)
        choice = (
            lax.broadcasted_iota(jnp.int32, (table.shape[0], block), 0) == kept[b][:, :block]
        )
        retained[rows] = dot_t(choice.astype(bf16), images[b]).astype(bf16)
        places = exact_dot(choice.astype(f32), table[...], ((0,), (0,)))
        at = lax.broadcasted_iota(jnp.int32, (block, width), 0)
        start = dot(retained[rows], embed[...]) + places
        stream[rows] = jnp.where(at == CLASS_ROW, vectors[0:1, :], start)

    layer_forward_rows(dims, stream, w_in, w_out, vectors, saved)
    norm_rows(stream, vectors[5:6, :], vectors[6:7, :], unit, inverse, low, dims["step"])

    @pl.loop(0, dims["images"])
    def _(b):
        rows = pl.ds(pl.multiple_of(b * block, block), block)
        projected[b] = dot(low[rows], bridge[...])


def encoder_forward(kept, images, table, w_in, w_out, embed, bridge, vectors):
    dims = ENC
    count, width = dims["images"] * dims["block"], dims["width"]
    outs = [
        ((dims["images"], dims["block"], bridge.shape[1]), f32),
        ((count, images.shape[-1]), bf16),
        ((count, width), f32),
        ((count, 1), f32),
        ((count, width), bf16),
    ] + saved_shapes(dims)
    return pl.pallas_call(
        encoder_forward_kernel,
        out_shape=[jax.ShapeDtypeStruct(shape, dtype) for shape, dtype in outs],
        scratch_shapes=[pltpu.VMEM((count, width), f32)],
        compiler_params=pltpu.CompilerParams(vmem_limit_bytes=62 * 1024 * 1024),
        name="encoder_forward",
    )(kept, images, table, w_in, w_out, embed, bridge, vectors)


def encoder_backward_kernel(*refs):
    grad_projected, retained, unit, inverse, low_end = refs[:5]
    saved = list(refs[5:16])
    w_in, w_out, bridge, vectors = refs[16:20]
    grad_in, grad_out, grad_bridge, grad_embed, vec_out = refs[20:25]
    given, spare, low, flow, sums, qkv, mixed = refs[25:]
    dims = ENC
    count, width = given.shape
    block = dims["block"]
    sums[...] = jnp.zeros_like(sums)
    qkv[...] = saved[3][...]
    mixed[...] = saved[5][...]
    saved[3], saved[5] = qkv, mixed

    flat = grad_projected[...].reshape(count, grad_projected.shape[-1])
    grad_bridge[...] = dot_t(low_end[...], flat).astype(bf16)
    given[...] = dot_nt(flat, bridge[...])
    norm_back_rows(given, unit, inverse, vectors[5:6, :], given, None, sums, 5, dims["step"])
    layer_backward_rows(
        dims, given, spare, w_in, w_out, vectors, saved, low, flow, grad_in, grad_out, sums
    )
    grad_embed[...] = dot_t(retained[...], given[...].astype(bf16)).astype(bf16)

    def tokens(rows):
        at = lax.broadcasted_iota(jnp.int32, (block, width), 0)
        sums[0] = sums[0] + fold(jnp.where(at == CLASS_ROW, given[rows], 0.0))

    row_loop(count, block, tokens)
    for row in range(7):
        vec_out[row : row + 1, :] = jnp.sum(sums[row], axis=0, keepdims=True)
    vec_out[7:8, :] = jnp.zeros((1, width), f32)


def encoder_backward(grad_projected, kept_state, w_in, w_out, bridge, vectors):
    dims = ENC
    count, width = dims["images"] * dims["block"], dims["width"]
    shapes = saved_shapes(dims)
    pixels_wide = kept_state[0].shape[1]
    outs = [
        jax.ShapeDtypeStruct(w_in.shape, bf16),
        jax.ShapeDtypeStruct(w_out.shape, bf16),
        jax.ShapeDtypeStruct(bridge.shape, bf16),
        jax.ShapeDtypeStruct((pixels_wide, width), bf16),
        jax.ShapeDtypeStruct((8, width), f32),
    ]
    scratch = [
        ((count, width), f32),
        ((count, width), f32),
        ((count, width), bf16),
        ((count, dims["hidden"]), bf16),
        ((7, 8, width), f32),
        shapes[3],
        shapes[5],
    ]
    return pl.pallas_call(
        encoder_backward_kernel,
        out_shape=outs,
        scratch_shapes=[pltpu.VMEM(shape, dtype) for shape, dtype in scratch],
        compiler_params=pltpu.CompilerParams(vmem_limit_bytes=62 * 1024 * 1024),
        name="encoder_backward",
    )(grad_projected, *kept_state, w_in, w_out, bridge, vectors)


def gather_grouped(part, groups):
    whole = lax.all_gather(part, GROUPED, axis=0, tiled=True)
    return whole.reshape(groups, -1, whole.shape[-1])


def scatter_grouped(gradient):
    flat = gradient.astype(f32).reshape(-1, gradient.shape[-1])
    return lax.psum_scatter(flat, GROUPED, scatter_dimension=0, tiled=True)


def ringed(tensor_count):
    return tensor_count == 4 and lax.axis_size("dp") == 8


def gather_all(masters, counted):
    tensor_count = lax.axis_size("tensor")
    columns = masters[6].shape[1]
    flat = [
        master.reshape(-1, master.shape[-1]).astype(bf16) for master in masters[:4]
    ]
    vectors_low = masters[6].astype(bf16).astype(f32)
    if ringed(tensor_count):
        at = lax.axis_index("tensor")
        quarters = [
            lax.dynamic_slice_in_dim(
                master, at * (master.shape[0] // tensor_count), master.shape[0] // tensor_count
            ).astype(bf16)
            for master in masters[4:6]
        ]
        lanes = 256
        vec_part = jnp.concatenate(
            [
                jnp.pad(vectors_low, ((0, 0), (0, lanes - columns))),
                jnp.broadcast_to(counted, (1, lanes)),
            ],
            axis=0,
        )
        wholes = gather_weights([quarters[0], flat[0], flat[1], quarters[1], flat[2], flat[3], vec_part])
        grouped = [
            wholes[k].reshape(tensor_count, -1, wholes[k].shape[-1]) for k in (EIN, EOUT, DIN, DOUT)
        ]
        pixel_w = wholes[PIX].reshape(-1, wholes[PIX].shape[-1])
        bridge_w = wholes[BRI].reshape(-1, wholes[BRI].shape[-1])
        vec_parts = wholes[VEC][0, 0].reshape(8, 8, lanes)
        vectors_all = vec_parts[:, :7, :columns].transpose(1, 0, 2).reshape(7, -1)
        patch_total = jnp.sum(vec_parts[:, 7, 0])
        return grouped, pixel_w, bridge_w, vectors_all, patch_total
    grouped = [gather_grouped(part, tensor_count) for part in flat]
    pixel_w = lax.all_gather(masters[4].astype(bf16), "dp", axis=0, tiled=True)
    bridge_w = lax.all_gather(masters[5].astype(bf16), "dp", axis=0, tiled=True)
    vectors_all = lax.all_gather(vectors_low, "dp", axis=1, tiled=True)
    return grouped, pixel_w, bridge_w, vectors_all, lax.psum(counted, "dp")


def reduce_all(gradients, masters):
    tensor_count = lax.axis_size("tensor")
    columns = masters[6].shape[1]
    dp_at = lax.axis_index("dp")
    grouped, grad_pixel, grad_bridge, packed = gradients
    if ringed(tensor_count):
        shapes = {
            EIN: masters[0].reshape(-1, masters[0].shape[-1]).shape,
            EOUT: masters[1].reshape(-1, masters[1].shape[-1]).shape,
            DIN: masters[2].reshape(-1, masters[2].shape[-1]).shape,
            DOUT: masters[3].reshape(-1, masters[3].shape[-1]).shape,
            PIX: (masters[4].shape[0] // tensor_count, masters[4].shape[1]),
            BRI: (masters[5].shape[0] // tensor_count, masters[5].shape[1]),
        }
        sources = {PIX: grad_pixel, EIN: grouped[0], EOUT: grouped[1], BRI: grad_bridge, DIN: grouped[2], DOUT: grouped[3]}
        operands = [
            sources[array].reshape(whole_shape(array, shapes[array]))
            for array in range(6)
        ]
        sums = scatter_gradients(operands + [packed])
        reduced = [sums[EIN], sums[EOUT], sums[DIN], sums[DOUT], sums[PIX], sums[BRI]]
        vector_sum = sums[VEC]
    else:

        def scatter_shared(gradient):
            part = lax.psum_scatter(gradient.astype(f32), EVERY, scatter_dimension=0, tiled=True)
            return lax.all_gather(part, "tensor", axis=0, tiled=True)

        reduced = [scatter_grouped(gradient) for gradient in grouped]
        reduced += [scatter_shared(grad_pixel), scatter_shared(grad_bridge)]
        vector_sum = lax.psum(packed, EVERY)
    own = lax.dynamic_slice_in_dim(vector_sum[:7], dp_at * columns, columns, axis=1)
    reduced = [gradient.reshape(master.shape) for gradient, master in zip(reduced + [own], masters)]
    return reduced, vector_sum[7, -1]


def shards(
    images,
    keep_index,
    unshuffle,
    masked,
    image_valid,
    *state,
):
    masters, firsts, seconds = state[:7], state[7:14], state[14:21]
    encoder_in, encoder_out, decoder_in, decoder_out, pixel_maps, bridge_map, vector_pack = masters
    tensor_count = lax.axis_size("tensor")
    tensor_at = lax.axis_index("tensor")
    counted = jnp.sum(masked.astype(f32) * image_valid.astype(f32)[:, None])
    grouped_w, pixel_w, bridge_w, vectors_all, patch_total = gather_all(masters, counted)
    enc_in_w, enc_out_w, dec_in_w, dec_out_w = grouped_w
    enc_vectors = vectors_all[:, :ENCODER_WIDTH]
    dec_vectors = vectors_all[:, ENCODER_WIDTH:]
    image_count = images.shape[0] // tensor_count

    def own(member):
        return lax.dynamic_slice_in_dim(member, tensor_at * image_count, image_count, axis=0)

    images, keep_index, unshuffle, masked, image_valid = map(
        own, (images, keep_index, unshuffle, masked, image_valid)
    )
    block = DEC["block"]
    images = jnp.pad(images, ((0, 0), (0, block - IMAGE_PATCHES), (0, 0)))
    lanes = 256
    codes = jnp.pad(
        jnp.where(masked == 1, MASK_ROW, unshuffle),
        ((0, 0), (0, lanes - IMAGE_PATCHES)),
        constant_values=-1,
    )
    codes = jnp.where(jnp.arange(lanes) == IMAGE_PATCHES, CLASS_ROW, codes)[:, None, :]
    kept = jnp.pad(keep_index, ((0, 0), (0, 128 - KEEP)), constant_values=-1)[:, None, :]
    weight_rows = jnp.broadcast_to(
        (image_valid.astype(f32) / patch_total)[:, None, None], (image_count, 1, 128)
    )
    enc_state = encoder_forward(
        kept,
        images,
        sinusoid_table(ENCODER_WIDTH, GRID_PATCHES, IMAGE_PATCHES, block),
        enc_in_w,
        enc_out_w,
        pixel_w[:PATCH_DIM],
        bridge_w,
        enc_vectors,
    )
    grad_dec_in, grad_dec_out, grad_head, grad_projected, dec_sums = decoder_step(
        enc_state[0],
        codes,
        weight_rows,
        images,
        sinusoid_table(D_D, GRID_PATCHES, IMAGE_PATCHES, block),
        dec_in_w,
        dec_out_w,
        pixel_w[PATCH_DIM:],
        dec_vectors,
    )
    grad_enc_in, grad_enc_out, grad_bridge, grad_embed, enc_sums = encoder_backward(
        grad_projected, enc_state[1:], enc_in_w, enc_out_w, bridge_w, enc_vectors
    )
    grad_pixel = jnp.concatenate([grad_embed, grad_head.astype(bf16)], axis=0)
    packed = jnp.concatenate([enc_sums, dec_sums], axis=1)
    reduced, loss_value = reduce_all(
        ([grad_enc_in, grad_enc_out, grad_dec_in, grad_dec_out], grad_pixel, grad_bridge, packed),
        masters,
    )
    decays = (decay_matrix,) * 6 + (0.0,)
    share_counts = (1.0,) * 4 + (float(tensor_count),) * 3
    bias_one = 1.0 - beta_one**step_count
    bias_two = 1.0 - beta_two**step_count
    new_firsts, new_seconds, updates = ([], [], [])
    for gradient, master, moment_one, moment_two, decay_value in zip(
        reduced, masters, firsts, seconds, decays
    ):
        next_one = beta_one * moment_one + (1.0 - beta_one) * gradient
        next_two = beta_two * moment_two + (1.0 - beta_two) * gradient * gradient
        new_firsts.append(next_one)
        new_seconds.append(next_two)
        updates.append(
            next_one / bias_one / (jnp.sqrt(next_two / bias_two) + eps_moment)
            + decay_value * master
        )

    def squares(members):
        return jnp.stack(
            [jnp.sum(member * member) / count for member, count in zip(members, share_counts)]
        )

    totals = lax.psum((squares(masters), squares(updates)), EVERY)
    weight_norm = jnp.sqrt(totals[0])
    update_norm = jnp.sqrt(totals[1])
    step_ratio = learn_rate * weight_norm / update_norm
    news = [
        master - step_ratio[position] * update
        for position, (master, update) in enumerate(zip(masters, updates))
    ]
    return tuple(
        [loss_value, jnp.stack([weight_norm, update_norm])] + new_firsts + new_seconds + news
    )


def solution(mesh):
    state_specs = (
        P("dp", "tensor", None),
        P("tensor", "dp", None),
        P("dp", "tensor", None),
        P("tensor", "dp", None),
        P("dp", None),
        P("dp", None),
        P(None, "dp"),
    )
    in_specs = (
        P("dp", None, None),
        P("dp", None),
        P("dp", None),
        P("dp", None),
        P("dp"),
    ) + state_specs * 3
    out_specs = (P(), P()) + state_specs * 3
    return jax.shard_map(shards, mesh=mesh, in_specs=in_specs, out_specs=out_specs, check_vma=False)
```

```python
import functools

import jax
import jax.numpy as jnp
from jax import lax
from jax.experimental import pallas as pl
from jax.experimental.pallas import tpu as pltpu
from jax.sharding import PartitionSpec as P
import numpy as np

ENCODER_WIDTH = 768
H_E = 12
HD_E = 64
D_D = 512
H_D = 16
HD_D = 32
PATCH_DIM = 768
GRID_PATCHES = 14
IMAGE_PATCHES = 196
KEEP = 49

eps_norm = 1e-06
beta_one = 0.9
beta_two = 0.999
step_count = 7.0
learn_rate = 0.3
decay_matrix = 0.05
eps_moment = 1e-06
f32 = jnp.float32
bf16 = jnp.bfloat16
EVERY = ("dp", "tensor")
GROUPED = ("tensor", "dp")


MESH_ID = pl.DeviceIdType.MESH
PIX, EIN, EOUT, BRI, DIN, DOUT, VEC = range(7)


def place():
    dp_at = lax.axis_index("dp")
    group = lax.axis_index("tensor")
    z, x = lax.div(dp_at, 2), lax.rem(dp_at, 2)
    y, c = lax.div(group, 2), lax.rem(group, 2)
    return z, x, y, c


def device(z, x, y, c):
    return (z * 2 + x, y * 2 + c)


def flip(z, m):
    low = lax.rem(z, 2)
    high = lax.div(z, 2)
    if m % 2:
        low = 1 - low
    if m // 2:
        high = 1 - high
    return high * 2 + low


def greet(z, x, y, c):
    barrier = pltpu.get_barrier_semaphore()
    peers = [
        device(z, x, y, 1 - c),
        device(z, x, 1 - y, c),
        device(z, 1 - x, y, c),
        device(flip(z, 1), x, y, c),
        device(flip(z, 2), x, y, c),
        device(flip(z, 3), x, y, c),
    ]
    for peer in peers:
        pl.semaphore_signal(barrier, inc=1, device_id=peer, device_id_type=MESH_ID)
    pl.semaphore_wait(barrier, 6)


SHARED = (PIX, BRI)


def spot(array, y, c, z, x):
    return (z, x, y, c) if array in SHARED else (y, c, z, x)


def half_spot(array, y, z, x):
    return (z, x, y) if array in SHARED else (y, z, x)


def whole_shape(array, part):
    return ((4, 2, 2, 2) if array in SHARED else (2, 2, 4, 2)) + part


GATHER_STEPS = (
    ((VEC, 0, 8, 0), (PIX, 0, 24, 0), (PIX, 24, 16, 1)),
    ((EIN, 0, 32, 0), (EIN, 32, 16, 1)),
    ((EIN, 48, 16, 0), (EIN, 64, 32, 1)),
    ((EOUT, 0, 32, 0), (EOUT, 32, 32, 1)),
    ((EOUT, 64, 32, 0), (EOUT, 96, 24, 1)),
    ((BRI, 0, 8, 0), (BRI, 8, 16, 1), (DIN, 0, 32, 0), (DIN, 32, 32, 1)),
    ((DOUT, 0, 48, 0), (DOUT, 48, 32, 1)),
)


def gather_kernel(*refs):
    count = 7
    parts = refs[:count]
    outs = refs[count : 2 * count]
    send, recv, local = refs[2 * count :]
    z, x, y, c = place()
    units = []
    for at, step in enumerate(GATHER_STEPS):
        for unit in step:
            units.append((at,) + unit)
    copies = {}

    def rows(array, region, first, size):
        ref = outs[array]
        return ref.at[region + (pl.ds(first, size),)]

    def plan(number, stage):
        at, array, first, size, turn = units[number]
        every = slice(None)
        if stage < 3:
            src = parts[array].at[pl.ds(first, size)]
            dst = rows(array, spot(array, y, c, z, x), first, size)
            peer = device(flip(z, stage + 1), x, y, c)
        else:
            if stage == 3:
                region = spot(array, y, c, every, x)
                peer = device(z, x, 1 - y, c) if turn == 0 else device(z, 1 - x, y, c)
            elif stage == 4 and turn == 0:
                region = spot(array, every, c, every, x)
                peer = device(z, 1 - x, y, c)
            elif stage == 4:
                region = spot(array, y, c, every, every)
                peer = device(z, x, 1 - y, c)
            else:
                region = spot(array, every, c, every, every)
                peer = device(z, x, y, 1 - c)
            src = dst = rows(array, region, first, size)
        return pltpu.make_async_remote_copy(
            src_ref=src,
            dst_ref=dst,
            send_sem=send.at[number, stage],
            recv_sem=recv.at[number, stage],
            device_id=peer,
            device_id_type=MESH_ID,
        )

    def start(number, stage):
        copies[number, stage] = plan(number, stage)
        copies[number, stage].start()

    own = []
    for array in range(count):
        own.append(
            pltpu.make_async_copy(parts[array], outs[array].at[spot(array, y, c, z, x)], local.at[array])
        )
        own[-1].start()
    greet(z, x, y, c)
    steps = len(GATHER_STEPS)
    waited = set()
    for tick in range(steps + 4):
        for number, unit in enumerate(units):
            if unit[0] == tick:
                for stage in range(3):
                    start(number, stage)
        for number, unit in enumerate(units):
            if unit[0] == tick - 1:
                if unit[1] not in waited:
                    waited.add(unit[1])
                    own[unit[1]].wait()
                for stage in range(3):
                    copies[number, stage].wait_recv()
                start(number, 3)
        for back in (2, 3):
            for number, unit in enumerate(units):
                if unit[0] == tick - back:
                    copies[number, back + 1].wait_recv()
                    start(number, back + 2)
        for number, unit in enumerate(units):
            if unit[0] == tick - 4:
                copies[number, 5].wait_recv()
    for key in copies:
        copies[key].wait_send()


def gather_weights(parts):
    count = 7
    units = sum(len(step) for step in GATHER_STEPS)
    outs = [
        jax.ShapeDtypeStruct(whole_shape(array, part.shape), part.dtype)
        for array, part in enumerate(parts)
    ]
    total = sum(int(part.size) * 32 * part.dtype.itemsize for part in parts)
    return pl.pallas_call(
        gather_kernel,
        out_shape=outs,
        in_specs=[pl.BlockSpec(memory_space=pltpu.VMEM)] * count,
        out_specs=[pl.BlockSpec(memory_space=pl.ANY)] * count,
        scratch_shapes=[
            pltpu.SemaphoreType.DMA((units, 6)),
            pltpu.SemaphoreType.DMA((units, 6)),
            pltpu.SemaphoreType.DMA((count,)),
        ],
        compiler_params=pltpu.CompilerParams(collective_id=0, has_side_effects=True),
        cost_estimate=pl.CostEstimate(flops=0, bytes_accessed=2 * total, transcendentals=0),
        name="gather_weights",
    )(*parts)


SCATTER_STEPS = (
    ((DOUT, 0, 48, 0), (DOUT, 48, 32, 1)),
    ((BRI, 0, 8, 0), (BRI, 8, 16, 1), (DIN, 0, 32, 0), (DIN, 32, 32, 1)),
    ((PIX, 0, 24, 0), (PIX, 24, 16, 1)),
    ((EOUT, 0, 32, 0), (EOUT, 32, 32, 1)),
    ((EOUT, 64, 32, 0), (EOUT, 96, 24, 1)),
    ((EIN, 0, 32, 0), (EIN, 32, 16, 1)),
    ((EIN, 48, 16, 0), (EIN, 64, 32, 1)),
)
STAT_LANES = {EIN: 0, EOUT: 1, DIN: 2, DOUT: 3, PIX: 4, BRI: 5, VEC: 6}


def state_rows(ref, rows):
    if len(ref.shape) == 2:
        return ref[rows]
    return ref[rows, 0, :] if ref.shape[1] == 1 else ref[0, rows, :]


def put_rows(ref, rows, values):
    if len(ref.shape) == 2:
        ref[rows] = values
    elif ref.shape[1] == 1:
        ref[rows, 0, :] = values
    else:
        ref[0, rows, :] = values


def moments(gradient, moment_one, moment_two, master, decay):
    next_one = beta_one * moment_one + (1.0 - beta_one) * gradient
    next_two = beta_two * moment_two + (1.0 - beta_two) * gradient * gradient
    bias_one = 1.0 - beta_one**step_count
    bias_two = 1.0 - beta_two**step_count
    update = next_one / bias_one / (jnp.sqrt(next_two / bias_two) + eps_moment) + decay * master
    return next_one, next_two, update


def state_step(rows):
    return next(step for step in (32, 40, rows) if rows % step == 0)


def scatter_kernel(shapes, units, *refs):
    grads = refs[:7]
    masters, firsts, seconds = refs[7:14], refs[14:21], refs[21:28]
    outs = refs[28:36]
    refs = refs[36:]
    n = len(units)
    own, one, two, three, four = (refs[k * n : (k + 1) * n] for k in range(5))
    vec_one, vec_two, vec_three, vec_four, vec_sum = refs[5 * n : 5 * n + 5]
    stats, stat_one, stat_two, stat_three, stat_four = refs[5 * n + 5 : 5 * n + 10]
    send, recv, local, vsend, vrecv, tsend, trecv, ssend, srecv = refs[5 * n + 10 :]
    z, x, y, c = place()
    every = slice(None)
    copies = {}
    stat_row = lax.broadcasted_iota(jnp.int32, (8, 128), 0)
    stat_lane = lax.broadcasted_iota(jnp.int32, (8, 128), 1)

    def tally(array):
        if array == VEC:
            gradient = outs[VEC][:7, : masters[VEC].shape[1]]
            update = moments(
                gradient, firsts[VEC][...], seconds[VEC][...], masters[VEC][...], 0.0
            )[2]
            squares = [jnp.sum(v * v, axis=0, keepdims=True) for v in (masters[VEC][...], update)]
        else:
            flat = (array in SHARED) and outs[array].shape[0] == 4
            count = outs[array].shape[0] * outs[array].shape[1] if flat else outs[array].shape[0]
            columns = outs[array].shape[-1]
            step = outs[array].shape[1] if flat else state_step(count)

            def body(k, carry):
                rows = pl.ds(pl.multiple_of(k * step, 8), step)
                gradient = outs[array][k] if flat else outs[array][rows]
                master = state_rows(masters[array], rows)
                update = moments(
                    gradient,
                    state_rows(firsts[array], rows),
                    state_rows(seconds[array], rows),
                    master,
                    decay_matrix,
                )[2]
                return tuple(
                    total + jnp.sum((v * v).reshape(step // 8, 8, columns), axis=0)
                    for total, v in zip(carry, (master, update))
                )

            start = (jnp.zeros((8, columns), f32),) * 2
            squares = [
                jnp.sum(v, axis=0, keepdims=True)
                for v in lax.fori_loop(0, count // step, body, start)
            ]
        share = 0.25 if array in SHARED + (VEC,) else 1.0
        total = stats[...]
        for row, square in enumerate(squares):
            value = jnp.sum(square, axis=1, keepdims=True) * share
            total = total + jnp.where((stat_row == row) & (stat_lane == STAT_LANES[array]), value, 0.0)
        stats[...] = total

    def remote(src, dst, key, send_sem, recv_sem, peer):
        copies[key] = pltpu.make_async_remote_copy(
            src_ref=src,
            dst_ref=dst,
            send_sem=send_sem,
            recv_sem=recv_sem,
            device_id=peer,
            device_id_type=MESH_ID,
        )
        copies[key].start()

    def start(number, stage):
        at, array, first, size, turn = units[number]
        mine = own[number]
        if stage == 0:
            peer = device(z, x, y, 1 - c)
            src = grads[array].at[
                spot(array, every, 1 - c, every, every) + (pl.ds(first, size),)
            ]
            dst = one[number]
        elif stage == 1 and turn == 0:
            peer = device(z, 1 - x, y, c)
            src, dst = mine.at[half_spot(array, every, every, 1 - x)], two[number]
        elif stage == 1:
            peer = device(z, x, 1 - y, c)
            src, dst = mine.at[half_spot(array, 1 - y, every, every)], two[number]
        elif stage == 2 and turn == 0:
            peer = device(z, x, 1 - y, c)
            src, dst = mine.at[half_spot(array, 1 - y, every, x)], three[number]
        elif stage == 2:
            peer = device(z, 1 - x, y, c)
            src, dst = mine.at[half_spot(array, y, every, 1 - x)], three[number]
        else:
            other = flip(z, stage - 2)
            peer = device(other, x, y, c)
            src, dst = mine.at[half_spot(array, y, other, x)], four[number].at[stage - 3]
        remote(src, dst, (number, stage), send.at[number, stage], recv.at[number, stage], peer)

    def add(number, stage):
        at, array, first, size, turn = units[number]
        mine = own[number]

        def pair(here, there):
            mine[here] = (mine[here].astype(f32) + there.astype(f32)).astype(bf16)

        if stage == 0:

            @pl.loop(0, 16)
            def _(k):
                iy, iz, ix = k // 8, (k // 2) % 4, k % 2
                here = half_spot(array, iy, iz, ix)
                pair(here, one[number][here])

        elif stage == 1 and turn == 0:

            @pl.loop(0, 8)
            def _(k):
                iy, iz = k // 4, k % 4
                there = (iz, iy) if array in SHARED else (iy, iz)
                pair(half_spot(array, iy, iz, x), two[number][there])

        elif stage == 1:

            @pl.loop(0, 8)
            def _(k):
                iz, ix = k // 2, k % 2
                pair(half_spot(array, y, iz, ix), two[number][iz, ix])

        elif stage == 2:

            @pl.loop(0, 4)
            def _(k):
                pair(half_spot(array, y, k, x), three[number][k])

        else:
            total = mine[half_spot(array, y, z, x)].astype(f32)
            for slot in range(3):
                total = total + four[number][slot].astype(f32)
            if array in SHARED:
                outs[array][y * 2 + c, pl.ds(first, size)] = total
            else:
                outs[array][pl.ds(first, size)] = total

    loads = []
    for number, (at, array, first, size, turn) in enumerate(units):
        loads.append(
            pltpu.make_async_copy(
                grads[array].at[spot(array, every, c, every, every) + (pl.ds(first, size),)],
                own[number],
                local.at[number],
            )
        )
    stats[...] = jnp.zeros_like(stats)
    greet(z, x, y, c)
    steps = units[-1][0] + 1

    def step_units(tick):
        return [number for number in range(n) if units[number][0] == tick]

    vec_dst = (vec_one, vec_two, vec_three)
    vec_peer = (device(z, x, y, 1 - c), device(z, 1 - x, y, c), device(z, x, 1 - y, c))

    for tick in range(steps + 4):
        for number in step_units(tick):
            loads[number].start()
            start(number, 0)
        for number in step_units(tick - 1):
            loads[number].wait()
            copies[number, 0].wait_recv()
            add(number, 0)
            start(number, 1)
        for number in step_units(tick - 2):
            copies[number, 1].wait()
            add(number, 1)
            start(number, 2)
        for number in step_units(tick - 3):
            copies[number, 2].wait()
            add(number, 2)
            for stage in (3, 4, 5):
                start(number, stage)
        for number in step_units(tick - 4):
            for stage in (3, 4, 5):
                copies[number, stage].wait()
            add(number, 3)
        if tick < 4:
            if tick == 0:
                vec_sum[...] = grads[6][...]
            if tick < 3:
                remote(vec_sum.at[...], vec_dst[tick], ("v", tick), vsend.at[tick], vrecv.at[tick], vec_peer[tick])
            else:
                vec_four[z] = vec_sum[...]
                for m in (1, 2, 3):
                    remote(vec_sum.at[...], vec_four.at[z], ("v", 2 + m), vsend.at[2 + m], vrecv.at[2 + m], device(flip(z, m), x, y, c))
        if tick < 3:
            copies["v", tick].wait()
            vec_sum[...] = vec_sum[...] + vec_dst[tick][...]
        if tick == 4:
            for m in (1, 2, 3):
                copies["v", 2 + m].wait()
            vec_sum[...] = (vec_four[0] + vec_four[1]) + (vec_four[2] + vec_four[3])
            outs[VEC][...] = vec_sum[z * 2 + x]
            tally(VEC)
        for array in range(6):
            last = max(units[number][0] for number in range(n) if units[number][1] == array)
            if array in SHARED and tick == last + 4:
                here = y * 2 + c
                peers = (
                    device(z, x, y, 1 - c),
                    device(z, x, 1 - y, c),
                    device(z, x, 1 - y, 1 - c),
                )
                for k, peer in enumerate(peers):
                    slot = SHARED.index(array) * 3 + k
                    piece = outs[array].at[here]
                    remote(piece, piece, ("t", slot), tsend.at[slot], trecv.at[slot], peer)
            elif array in SHARED and tick == last + 5:
                for k in range(3):
                    copies["t", SHARED.index(array) * 3 + k].wait()
                tally(array)
            elif array not in SHARED and tick == last + 4:
                tally(array)
    stat_peers = (device(z, x, y, 1 - c), device(z, 1 - x, y, c), device(z, x, 1 - y, c))
    for stage, (held, peer) in enumerate(zip((stat_one, stat_two, stat_three), stat_peers)):
        remote(stats, held, ("s", stage), ssend.at[stage], srecv.at[stage], peer)
        copies["s", stage].wait()
        stats[...] = stats[...] + held[...]
    stat_four[z] = stats[...]
    for m in (1, 2, 3):
        remote(
            stats,
            stat_four.at[z],
            ("s", 2 + m),
            ssend.at[2 + m],
            srecv.at[2 + m],
            device(flip(z, m), x, y, c),
        )
    for m in (1, 2, 3):
        copies["s", 2 + m].wait()
    norms = jnp.sqrt((stat_four[0] + stat_four[1]) + (stat_four[2] + stat_four[3]))
    loss = vec_sum[7, 7:8, 128:256][:, 31:32]
    outs[7][...] = jnp.where(stat_row == 2, loss, norms)
    for number in range(n):
        copies[number, 0].wait_send()


def scatter_gradients(grads, masters, firsts, seconds):
    units = [(at,) + unit for at, step in enumerate(SCATTER_STEPS) for unit in step]
    n = len(units)
    shapes = [grad.shape for grad in grads]
    outs = []
    for array in range(6):
        rows, columns = shapes[array][4:]
        if array in SHARED:
            outs.append(jax.ShapeDtypeStruct((4, rows, columns), f32))
        else:
            outs.append(jax.ShapeDtypeStruct((rows, columns), f32))
    outs.append(jax.ShapeDtypeStruct(grads[6].shape[1:], f32))
    outs.append(jax.ShapeDtypeStruct((8, 128), f32))
    scratch = []
    for stage in range(5):
        for at, array, first, size, turn in units:
            shared = array in SHARED
            lead = ((4, 2, 2) if shared else (2, 4, 2), (4,), (3,))
            if stage < 2:
                lead = lead[0]
            elif stage == 2:
                lead = ((4, 2) if shared else (2, 4)) if turn == 0 else (4, 2)
            else:
                lead = lead[stage - 2]
            scratch.append(pltpu.VMEM(lead + (size, shapes[array][5]), bf16))
    vec = grads[6].shape
    scratch += [pltpu.VMEM(vec, f32)] * 3 + [pltpu.VMEM((4,) + vec, f32), pltpu.VMEM(vec, f32)]
    scratch += [pltpu.VMEM((8, 128), f32)] * 4 + [pltpu.VMEM((4, 8, 128), f32)]
    scratch += [
        pltpu.SemaphoreType.DMA((n, 6)),
        pltpu.SemaphoreType.DMA((n, 6)),
        pltpu.SemaphoreType.DMA((n,)),
        pltpu.SemaphoreType.DMA((6,)),
        pltpu.SemaphoreType.DMA((6,)),
        pltpu.SemaphoreType.DMA((6,)),
        pltpu.SemaphoreType.DMA((6,)),
        pltpu.SemaphoreType.DMA((6,)),
        pltpu.SemaphoreType.DMA((6,)),
    ]
    total = sum(int(grad.size) * grad.dtype.itemsize for grad in grads)
    return pl.pallas_call(
        functools.partial(scatter_kernel, shapes, units),
        out_shape=outs,
        in_specs=[pl.BlockSpec(memory_space=pl.ANY)] * 6
        + [pl.BlockSpec(memory_space=pltpu.VMEM)] * 22,
        out_specs=[pl.BlockSpec(memory_space=pltpu.VMEM)] * 8,
        scratch_shapes=scratch,
        compiler_params=pltpu.CompilerParams(
            collective_id=1, has_side_effects=True, vmem_limit_bytes=60 * 1024 * 1024
        ),
        cost_estimate=pl.CostEstimate(flops=0, bytes_accessed=2 * total, transcendentals=0),
        name="scatter_gradients",
    )(*grads, *masters, *firsts, *seconds)


def apply_kernel(*refs):
    grads, masters, firsts, seconds = (refs[7 * k : 7 * k + 7] for k in range(4))
    stats = refs[28]
    next_firsts, next_seconds, news = (refs[29 + 7 * k : 36 + 7 * k] for k in range(3))
    loss, pairs = refs[50:]
    for array in range(7):
        lane = STAT_LANES[array]
        norms = [stats[row : row + 1, :][:, lane : lane + 1] for row in range(2)]
        ratio = learn_rate * norms[0] / norms[1]
        count = masters[array].shape[0]
        if len(masters[array].shape) == 3:
            count = count * masters[array].shape[1]
        decay = 0.0 if array == VEC else decay_matrix

        def body(rows, array=array, ratio=ratio, decay=decay):
            if array == VEC:
                gradient = grads[VEC][:7, : masters[VEC].shape[1]]
            else:
                gradient = grads[array][rows]
            master = state_rows(masters[array], rows)
            next_one, next_two, update = moments(
                gradient,
                state_rows(firsts[array], rows),
                state_rows(seconds[array], rows),
                master,
                decay,
            )
            put_rows(next_firsts[array], rows, next_one)
            put_rows(next_seconds[array], rows, next_two)
            put_rows(news[array], rows, master - ratio * update)

        if array == VEC:
            body(slice(None))
        else:
            row_loop(count, state_step(count), body)
    pairs[...] = stats[:2, :][:, :7]
    loss[...] = stats[2:3, :][:, :1]


def apply_update(reduced, masters, firsts, seconds, stats):
    shapes = [jax.ShapeDtypeStruct(master.shape, f32) for master in masters]
    results = pl.pallas_call(
        apply_kernel,
        out_shape=shapes * 3
        + [jax.ShapeDtypeStruct((1, 1), f32), jax.ShapeDtypeStruct((2, 7), f32)],
        compiler_params=pltpu.CompilerParams(vmem_limit_bytes=48 * 1024 * 1024),
        name="apply_update",
    )(*reduced, *masters, *firsts, *seconds, stats)
    return results[:7], results[7:14], results[14:21], results[21].reshape(()), results[22]


def sinusoid_table(feature_width, grid_side, patch_count, padded):
    position = np.arange(patch_count)
    quarter = feature_width // 4
    omegas = 1.0 / 10000.0 ** (np.arange(quarter) / quarter)
    parts = []
    for coords in (position % grid_side, position // grid_side):
        angles = coords[:, None] * omegas[None, :]
        parts += [np.sin(angles), np.cos(angles)]
    table = np.concatenate(parts, axis=1).astype(np.float32)
    return jnp.asarray(np.pad(table, ((0, padded - patch_count), (0, 0))))


GROUPS = 4
ENC = dict(step=128, images=4, block=64, tokens=50, width=768, heads=3, head=64, hidden=768, spans=1)
DEC = dict(step=208, images=4, block=208, tokens=197, width=512, heads=4, head=32, hidden=512, spans=4)
CLASS_ROW = 49
MASK_ROW = 50


def dot(left, right, dims=((1,), (0,)), precision=None):
    return lax.dot_general(
        left, right, (dims, ((), ())), preferred_element_type=f32, precision=precision
    )


def dot_t(left, right):
    return dot(left, right, ((0,), (0,)))


def dot_nt(left, right):
    return dot(left, right, ((1,), (1,)))


def exact_dot(left, right, dims):
    return dot(left, right, dims, lax.Precision.HIGHEST)


def row_loop(count, step, body):
    @pl.loop(0, count // step)
    def _(k):
        body(pl.ds(pl.multiple_of(k * step, step), step))


def fold(values):
    step, width = values.shape
    return jnp.sum(values.reshape(step // 8, 8, width), axis=0)


def norm_rows(source, gain, shift, unit, inverse, low, step):
    def body(rows):
        values = source[rows]
        centred = values - jnp.mean(values, axis=-1, keepdims=True)
        scale = lax.rsqrt(jnp.mean(centred * centred, axis=-1, keepdims=True) + eps_norm)
        normed = centred * scale
        unit[rows] = normed
        inverse[rows] = scale
        low[rows] = (normed * gain + shift).astype(bf16)

    row_loop(source.shape[0], step, body)


def norm_back_rows(incoming, unit, inverse, gain, result, residual, sums, at, step):
    width = incoming.shape[-1]

    def body(rows):
        given = incoming[rows]
        normed = unit[rows]
        scaled = given * gain
        inner = (
            scaled
            - jnp.mean(scaled, axis=-1, keepdims=True)
            - normed * jnp.mean(scaled * normed, axis=-1, keepdims=True)
        )
        value = inverse[rows] * inner
        if residual is not None:
            value = value + residual[rows]
        sums[at] = sums[at] + fold(given * normed)
        sums[at + 1] = sums[at + 1] + fold(given)
        result[rows] = value

    row_loop(incoming.shape[0], step, body)


def attend_mask(dims):
    size = dims["block"] * dims["images"] // dims["spans"]
    key = lax.broadcasted_iota(jnp.int32, (size, size), 1)
    if dims["spans"] == 1:
        query = lax.broadcasted_iota(jnp.int32, (size, size), 0)
        return ((key // dims["block"]) == (query // dims["block"])) & (
            (key % dims["block"]) < dims["tokens"]
        )
    return key < dims["tokens"]


def layer_forward_rows(dims, stream, w_in, w_out, vectors, saved):
    unit_one, inv_one, low_one, qkv, probs, mixed, unit_two, inv_two, low_two, active, slope = saved
    count, width = stream.shape
    inner = dims["heads"] * dims["head"]
    span = count // dims["spans"]
    norm_rows(stream, vectors[1:2, :], vectors[2:3, :], unit_one, inv_one, low_one, dims["step"])

    @pl.loop(0, GROUPS)
    def _(t):
        weights = w_in[t, :, : 3 * inner] if inner % 128 == 0 else w_in[t][:, : 3 * inner]

        def body(rows):
            qkv[t, rows] = dot(low_one[rows], weights).astype(bf16)

        body(slice(None))

    scale = dims["head"] ** (-0.5)

    @pl.loop(0, GROUPS * dims["spans"])
    def _(k):
        t = k // dims["spans"]
        b = k % dims["spans"]
        rows = pl.ds(pl.multiple_of(b * span, span), span)
        triple = qkv[t, rows]
        allowed = attend_mask(dims)
        results = []
        for head in range(dims["heads"]):
            q, key, v = (
                triple[:, part * inner + head * dims["head"] : part * inner + (head + 1) * dims["head"]]
                for part in range(3)
            )
            scores = jnp.where(allowed, dot_nt(q, key) * scale, -1e30)
            shifted = jnp.exp(scores - jnp.max(scores, axis=-1, keepdims=True))
            share = shifted / jnp.sum(shifted, axis=-1, keepdims=True)
            probs[k * dims["heads"] + head] = share
            results.append(dot(share.astype(bf16), v))
        mixed[t, rows] = jnp.concatenate(results, axis=1).astype(bf16)

    @pl.loop(0, GROUPS)
    def _(t):
        weights = w_out[t, :inner]

        def body(rows):
            stream[rows] = stream[rows] + dot(mixed[t, rows], weights)

        body(slice(None))

    norm_rows(stream, vectors[3:4, :], vectors[4:5, :], unit_two, inv_two, low_two, dims["step"])

    @pl.loop(0, GROUPS)
    def _(t):
        up = w_in[t, :, 3 * inner :] if inner % 128 == 0 else w_in[t][:, 3 * inner :]
        down = w_out[t, inner:]

        def body(rows):
            slope[t, rows] = dot(low_two[rows], up)

        body(slice(None))

        def bend(rows):
            hidden = slope[t, rows]
            level = 0.5 + 0.5 * lax.erf(hidden * (0.5**0.5))
            active[t, rows] = (hidden * level).astype(bf16)
            slope[t, rows] = level + hidden * (
                jnp.exp(-0.5 * hidden * hidden) * (0.5 / np.pi) ** 0.5
            )

        row_loop(count, 32, bend)

        def body_two(rows):
            stream[rows] = stream[rows] + dot(active[t, rows], down)

        body_two(slice(None))


def layer_backward_rows(dims, given, spare, w_in, w_out, vectors, saved, low, flow, grad_in, grad_out, sums):
    unit_one, inv_one, low_one, qkv, probs, mixed, unit_two, inv_two, low_two, active, slope = saved
    count, width = given.shape
    inner = dims["heads"] * dims["head"]
    span = count // dims["spans"]
    aligned = inner % 128 == 0

    def lower(rows):
        low[rows] = given[rows].astype(bf16)
        spare[rows] = jnp.zeros_like(spare[rows])

    row_loop(count, 32, lower)

    @pl.loop(0, GROUPS)
    def _(t):
        down = w_out[t, inner:]
        up = w_in[t, :, 3 * inner :] if aligned else w_in[t][:, 3 * inner :]
        grad_out[t, inner:] = dot_t(active[t], low[...]).astype(bf16)

        def body(rows):
            flow[rows] = (slope[t, rows] * dot_nt(low[rows], down)).astype(bf16)
            spare[rows] = spare[rows] + dot_nt(flow[rows], up)

        body(slice(None))
        grad_up = dot_t(low_two[...], flow[...]).astype(bf16)
        if aligned:
            grad_in[t, :, 3 * inner :] = grad_up
        else:
            grad_in[t] = jnp.concatenate([jnp.zeros((width, 3 * inner), bf16), grad_up], axis=1)

    norm_back_rows(spare, unit_two, inv_two, vectors[3:4, :], given, given, sums, 3, dims["step"])
    row_loop(count, 32, lower)

    @pl.loop(0, GROUPS)
    def _(t):
        weights = w_out[t, :inner]
        grad_out[t, :inner] = dot_t(mixed[t], low[...]).astype(bf16)

        def body(rows):
            mixed[t, rows] = dot_nt(low[rows], weights).astype(bf16)

        body(slice(None))

    scale = dims["head"] ** (-0.5)

    @pl.loop(0, GROUPS * dims["spans"])
    def _(k):
        t = k // dims["spans"]
        b = k % dims["spans"]
        rows = pl.ds(pl.multiple_of(b * span, span), span)
        triple = qkv[t, rows]
        back = mixed[t, rows]
        parts = ([], [], [])
        for head in range(dims["heads"]):
            q, key, v = (
                triple[:, part * inner + head * dims["head"] : part * inner + (head + 1) * dims["head"]]
                for part in range(3)
            )
            grad_o = back[:, head * dims["head"] : (head + 1) * dims["head"]]
            share = probs[k * dims["heads"] + head]
            grad_p = dot_nt(grad_o, v)
            grad_s = share * (grad_p - jnp.sum(share * grad_p, axis=-1, keepdims=True))
            low_s = grad_s.astype(bf16)
            parts[0].append(dot(low_s, key) * scale)
            parts[1].append(dot_t(low_s, q) * scale)
            parts[2].append(dot_t(share.astype(bf16), grad_o))
        qkv[t, rows] = jnp.concatenate(parts[0] + parts[1] + parts[2], axis=1).astype(bf16)

    @pl.loop(0, GROUPS)
    def _(t):
        weights = w_in[t, :, : 3 * inner] if aligned else w_in[t][:, : 3 * inner]
        grad_triple = dot_t(low_one[...], qkv[t]).astype(bf16)
        if aligned:
            grad_in[t, :, : 3 * inner] = grad_triple
        else:
            grad_in[t] = jnp.concatenate([grad_triple, grad_in[t][:, 3 * inner :]], axis=1)

        def body(rows):
            spare[rows] = spare[rows] + dot_nt(qkv[t, rows], weights)

        body(slice(None))

    norm_back_rows(spare, unit_one, inv_one, vectors[1:2, :], given, given, sums, 1, dims["step"])


def saved_shapes(dims):
    count = dims["images"] * dims["block"]
    width, inner = dims["width"], dims["heads"] * dims["head"]
    span = count // dims["spans"]
    return [
        ((count, width), f32),
        ((count, 1), f32),
        ((count, width), bf16),
        ((GROUPS, count, 3 * inner), bf16),
        ((GROUPS * dims["spans"] * dims["heads"], span, span), f32),
        ((GROUPS, count, inner), bf16),
        ((count, width), f32),
        ((count, 1), f32),
        ((count, width), bf16),
        ((GROUPS, count, dims["hidden"]), bf16),
        ((GROUPS, count, dims["hidden"]), f32),
    ]


def decoder_kernel(*refs):
    projected, codes, weight_rows, images, table, w_in, w_out, head, vectors = refs[:9]
    grad_in, grad_out, grad_head, grad_projected, vec_out = refs[9:14]
    stream, given, unit, inverse, low, flow, sums, loss = refs[14:22]
    saved = refs[22:]
    dims = DEC
    count, width = stream.shape
    block = dims["block"]
    sums[...] = jnp.zeros_like(sums)
    loss[...] = jnp.zeros_like(loss)

    def placer(b):
        return (
            lax.broadcasted_iota(jnp.int32, (64, block), 0) == codes[b][:, :block]
        ).astype(f32)

    def block_rows(b):
        return pl.ds(pl.multiple_of(b * block, block), block)

    @pl.loop(0, dims["images"])
    def _(b):
        at = lax.broadcasted_iota(jnp.int32, (64, width), 0)
        source = jnp.where(at == MASK_ROW, vectors[0:1, :], projected[b])
        source = jnp.where(at > MASK_ROW, 0.0, source)
        stream[block_rows(b)] = exact_dot(placer(b), source, ((0,), (0,))) + table[...]

    layer_forward_rows(dims, stream, w_in, w_out, vectors, saved)
    norm_rows(stream, vectors[5:6, :], vectors[6:7, :], unit, inverse, low, dims["step"])
    grad_head[...] = jnp.zeros_like(grad_head)
    pixels_wide = images.shape[-1]

    @pl.loop(0, dims["images"])
    def _(b):
        rows = block_rows(b)
        predicted = dot(low[rows], head[...])
        pixels = images[b].astype(f32)
        centred = pixels - jnp.mean(pixels, axis=-1, keepdims=True)
        variance = jnp.sum(centred * centred, axis=-1, keepdims=True) / (pixels_wide - 1)
        errors = predicted - centred * lax.rsqrt(variance + eps_norm)
        at = lax.broadcasted_iota(jnp.int32, (64, 128), 0)
        spread = jnp.where(at == MASK_ROW, weight_rows[b], 0.0)
        weight = exact_dot(placer(b), spread, ((0,), (0,)))[:, :1]
        loss[...] = loss[...] + fold(errors * errors * weight)
        grad_low = (errors * (2.0 / pixels_wide) * weight).astype(bf16)
        grad_head[...] = grad_head[...] + dot_t(low[rows], grad_low)
        given[rows] = dot_nt(grad_low, head[...])

    norm_back_rows(given, unit, inverse, vectors[5:6, :], given, None, sums, 5, dims["step"])
    layer_backward_rows(
        dims, given, stream, w_in, w_out, vectors, saved, low, flow, grad_in, grad_out, sums
    )

    @pl.loop(0, dims["images"])
    def _(b):
        back = exact_dot(placer(b), given[block_rows(b)], ((1,), (0,)))
        at = lax.broadcasted_iota(jnp.int32, (64, width), 0)
        grad_projected[b] = jnp.where(at < MASK_ROW, back, 0.0).astype(bf16)
        sums[0] = sums[0] + fold(jnp.where(at == MASK_ROW, back, 0.0))

    for row in range(7):
        vec_out[row : row + 1, :] = jnp.sum(sums[row], axis=0, keepdims=True)
    total = jnp.sum(jnp.sum(loss[...], axis=0, keepdims=True), axis=1, keepdims=True)
    vec_out[7:8, :] = jnp.broadcast_to(total / pixels_wide, (1, width))


def decoder_step(projected, codes, weight_rows, images, table, w_in, w_out, head, vectors):
    dims = DEC
    count, width = dims["images"] * dims["block"], dims["width"]
    outs = [
        jax.ShapeDtypeStruct(w_in.shape, bf16),
        jax.ShapeDtypeStruct(w_out.shape, bf16),
        jax.ShapeDtypeStruct(head.shape, f32),
        jax.ShapeDtypeStruct(projected.shape, bf16),
        jax.ShapeDtypeStruct((8, width), f32),
    ]
    scratch = [
        ((count, width), f32),
        ((count, width), f32),
        ((count, width), f32),
        ((count, 1), f32),
        ((count, width), bf16),
        ((count, dims["hidden"]), bf16),
        ((7, 8, width), f32),
        ((8, images.shape[-1]), f32),
    ] + saved_shapes(dims)
    return pl.pallas_call(
        decoder_kernel,
        out_shape=outs,
        scratch_shapes=[pltpu.VMEM(shape, dtype) for shape, dtype in scratch],
        compiler_params=pltpu.CompilerParams(vmem_limit_bytes=62 * 1024 * 1024),
        name="decoder_step",
    )(projected, codes, weight_rows, images, table, w_in, w_out, head, vectors)


def encoder_forward_kernel(*refs):
    kept, images, table, w_in, w_out, embed, bridge, vectors = refs[:8]
    projected, retained, unit, inverse, low = refs[8:13]
    saved = refs[13:24]
    (stream,) = refs[24:]
    dims = ENC
    count, width = stream.shape
    block = dims["block"]

    @pl.loop(0, dims["images"])
    def _(b):
        rows = pl.ds(pl.multiple_of(b * block, block), block)
        choice = (
            lax.broadcasted_iota(jnp.int32, (table.shape[0], block), 0) == kept[b][:, :block]
        )
        retained[rows] = dot_t(choice.astype(bf16), images[b]).astype(bf16)
        places = exact_dot(choice.astype(f32), table[...], ((0,), (0,)))
        at = lax.broadcasted_iota(jnp.int32, (block, width), 0)
        start = dot(retained[rows], embed[...]) + places
        stream[rows] = jnp.where(at == CLASS_ROW, vectors[0:1, :], start)

    layer_forward_rows(dims, stream, w_in, w_out, vectors, saved)
    norm_rows(stream, vectors[5:6, :], vectors[6:7, :], unit, inverse, low, dims["step"])

    @pl.loop(0, dims["images"])
    def _(b):
        rows = pl.ds(pl.multiple_of(b * block, block), block)
        projected[b] = dot(low[rows], bridge[...])


def encoder_forward(kept, images, table, w_in, w_out, embed, bridge, vectors):
    dims = ENC
    count, width = dims["images"] * dims["block"], dims["width"]
    outs = [
        ((dims["images"], dims["block"], bridge.shape[1]), f32),
        ((count, images.shape[-1]), bf16),
        ((count, width), f32),
        ((count, 1), f32),
        ((count, width), bf16),
    ] + saved_shapes(dims)
    return pl.pallas_call(
        encoder_forward_kernel,
        out_shape=[jax.ShapeDtypeStruct(shape, dtype) for shape, dtype in outs],
        scratch_shapes=[pltpu.VMEM((count, width), f32)],
        compiler_params=pltpu.CompilerParams(vmem_limit_bytes=62 * 1024 * 1024),
        name="encoder_forward",
    )(kept, images, table, w_in, w_out, embed, bridge, vectors)


def encoder_backward_kernel(*refs):
    grad_projected, retained, unit, inverse, low_end = refs[:5]
    saved = list(refs[5:16])
    w_in, w_out, bridge, vectors = refs[16:20]
    grad_in, grad_out, grad_bridge, grad_embed, vec_out = refs[20:25]
    given, spare, low, flow, sums, qkv, mixed = refs[25:]
    dims = ENC
    count, width = given.shape
    block = dims["block"]
    sums[...] = jnp.zeros_like(sums)
    qkv[...] = saved[3][...]
    mixed[...] = saved[5][...]
    saved[3], saved[5] = qkv, mixed

    flat = grad_projected[...].reshape(count, grad_projected.shape[-1])
    grad_bridge[...] = dot_t(low_end[...], flat).astype(bf16)
    given[...] = dot_nt(flat, bridge[...])
    norm_back_rows(given, unit, inverse, vectors[5:6, :], given, None, sums, 5, dims["step"])
    layer_backward_rows(
        dims, given, spare, w_in, w_out, vectors, saved, low, flow, grad_in, grad_out, sums
    )
    grad_embed[...] = dot_t(retained[...], given[...].astype(bf16)).astype(bf16)

    def tokens(rows):
        at = lax.broadcasted_iota(jnp.int32, (block, width), 0)
        sums[0] = sums[0] + fold(jnp.where(at == CLASS_ROW, given[rows], 0.0))

    row_loop(count, block, tokens)
    for row in range(7):
        vec_out[row : row + 1, :] = jnp.sum(sums[row], axis=0, keepdims=True)
    vec_out[7:8, :] = jnp.zeros((1, width), f32)


def encoder_backward(grad_projected, kept_state, w_in, w_out, bridge, vectors):
    dims = ENC
    count, width = dims["images"] * dims["block"], dims["width"]
    shapes = saved_shapes(dims)
    pixels_wide = kept_state[0].shape[1]
    outs = [
        jax.ShapeDtypeStruct(w_in.shape, bf16),
        jax.ShapeDtypeStruct(w_out.shape, bf16),
        jax.ShapeDtypeStruct(bridge.shape, bf16),
        jax.ShapeDtypeStruct((pixels_wide, width), bf16),
        jax.ShapeDtypeStruct((8, width), f32),
    ]
    scratch = [
        ((count, width), f32),
        ((count, width), f32),
        ((count, width), bf16),
        ((count, dims["hidden"]), bf16),
        ((7, 8, width), f32),
        shapes[3],
        shapes[5],
    ]
    return pl.pallas_call(
        encoder_backward_kernel,
        out_shape=outs,
        scratch_shapes=[pltpu.VMEM(shape, dtype) for shape, dtype in scratch],
        compiler_params=pltpu.CompilerParams(vmem_limit_bytes=62 * 1024 * 1024),
        name="encoder_backward",
    )(grad_projected, *kept_state, w_in, w_out, bridge, vectors)


def gather_grouped(part, groups):
    whole = lax.all_gather(part, GROUPED, axis=0, tiled=True)
    return whole.reshape(groups, -1, whole.shape[-1])


def scatter_grouped(gradient):
    flat = gradient.astype(f32).reshape(-1, gradient.shape[-1])
    return lax.psum_scatter(flat, GROUPED, scatter_dimension=0, tiled=True)


def ringed(tensor_count):
    return tensor_count == 4 and lax.axis_size("dp") == 8


def gather_all(masters, counted):
    tensor_count = lax.axis_size("tensor")
    columns = masters[6].shape[1]
    flat = [
        master.reshape(-1, master.shape[-1]).astype(bf16) for master in masters[:4]
    ]
    vectors_low = masters[6].astype(bf16).astype(f32)
    if ringed(tensor_count):
        at = lax.axis_index("tensor")
        quarters = [
            lax.dynamic_slice_in_dim(
                master, at * (master.shape[0] // tensor_count), master.shape[0] // tensor_count
            ).astype(bf16)
            for master in masters[4:6]
        ]
        lanes = 256
        vec_part = jnp.concatenate(
            [
                jnp.pad(vectors_low, ((0, 0), (0, lanes - columns))),
                jnp.broadcast_to(counted, (1, lanes)),
            ],
            axis=0,
        )
        wholes = gather_weights([quarters[0], flat[0], flat[1], quarters[1], flat[2], flat[3], vec_part])
        grouped = [
            wholes[k].reshape(tensor_count, -1, wholes[k].shape[-1]) for k in (EIN, EOUT, DIN, DOUT)
        ]
        pixel_w = wholes[PIX].reshape(-1, wholes[PIX].shape[-1])
        bridge_w = wholes[BRI].reshape(-1, wholes[BRI].shape[-1])
        vec_parts = wholes[VEC][0, 0].reshape(8, 8, lanes)
        vectors_all = vec_parts[:, :7, :columns].transpose(1, 0, 2).reshape(7, -1)
        patch_total = jnp.sum(vec_parts[:, 7, 0])
        return grouped, pixel_w, bridge_w, vectors_all, patch_total
    grouped = [gather_grouped(part, tensor_count) for part in flat]
    pixel_w = lax.all_gather(masters[4].astype(bf16), "dp", axis=0, tiled=True)
    bridge_w = lax.all_gather(masters[5].astype(bf16), "dp", axis=0, tiled=True)
    vectors_all = lax.all_gather(vectors_low, "dp", axis=1, tiled=True)
    return grouped, pixel_w, bridge_w, vectors_all, lax.psum(counted, "dp")


def ring_finish(gradients, masters, firsts, seconds):
    grouped, grad_pixel, grad_bridge, packed = gradients
    tensor_count = lax.axis_size("tensor")
    columns = masters[6].shape[1]
    order = (4, 0, 1, 5, 2, 3, 6)
    sources = (grad_pixel, grouped[0], grouped[1], grad_bridge, grouped[2], grouped[3])
    operands = []
    for array, source in enumerate(sources):
        master = masters[order[array]]
        rows, wide = master.size // master.shape[-1], master.shape[-1]
        if array in SHARED:
            rows = rows // tensor_count
        operands.append(source.reshape(whole_shape(array, (rows, wide))))
    packed = packed.reshape(8, -1, columns).transpose(1, 0, 2)
    operands.append(jnp.pad(packed, ((0, 0), (0, 0), (0, 256 - columns))))
    states = [[members[k] for k in order] for members in (masters, firsts, seconds)]
    *sums, stats = scatter_gradients(operands, *states)
    for array in SHARED:
        sums[array] = sums[array].reshape(-1, sums[array].shape[-1])
    *results, loss_value, pairs = apply_update(sums, *states, stats)
    place_of = {k: at for at, k in enumerate(order)}
    results = [[members[place_of[k]] for k in range(7)] for members in results]
    return (loss_value, pairs, *results[0], *results[1], *results[2])


def plain_finish(gradients, masters, firsts, seconds):
    grouped, grad_pixel, grad_bridge, packed = gradients
    tensor_count = lax.axis_size("tensor")
    columns = masters[6].shape[1]

    def scatter_shared(gradient):
        part = lax.psum_scatter(gradient.astype(f32), EVERY, scatter_dimension=0, tiled=True)
        return lax.all_gather(part, "tensor", axis=0, tiled=True)

    reduced = [scatter_grouped(gradient) for gradient in grouped]
    reduced += [scatter_shared(grad_pixel), scatter_shared(grad_bridge)]
    vector_sum = lax.psum(packed, EVERY)
    own = lax.dynamic_slice_in_dim(
        vector_sum[:7], lax.axis_index("dp") * columns, columns, axis=1
    )
    reduced = [gradient.reshape(master.shape) for gradient, master in zip(reduced + [own], masters)]
    decays = (decay_matrix,) * 6 + (0.0,)
    share_counts = (1.0,) * 4 + (float(tensor_count),) * 3
    steps = [moments(*member) for member in zip(reduced, firsts, seconds, masters, decays)]
    new_firsts, new_seconds, updates = zip(*steps)

    def squares(members):
        return jnp.stack(
            [jnp.sum(member * member) / count for member, count in zip(members, share_counts)]
        )

    weight_norm, update_norm = map(
        jnp.sqrt, lax.psum((squares(masters), squares(updates)), EVERY)
    )
    ratio = learn_rate * weight_norm / update_norm
    news = [
        master - ratio[position] * update
        for position, (master, update) in enumerate(zip(masters, updates))
    ]
    return (vector_sum[7, -1], jnp.stack([weight_norm, update_norm]), *new_firsts, *new_seconds, *news)


def shards(
    images,
    keep_index,
    unshuffle,
    masked,
    image_valid,
    *state,
):
    masters, firsts, seconds = state[:7], state[7:14], state[14:21]
    encoder_in, encoder_out, decoder_in, decoder_out, pixel_maps, bridge_map, vector_pack = masters
    tensor_count = lax.axis_size("tensor")
    tensor_at = lax.axis_index("tensor")
    counted = jnp.sum(masked.astype(f32) * image_valid.astype(f32)[:, None])
    grouped_w, pixel_w, bridge_w, vectors_all, patch_total = gather_all(masters, counted)
    enc_in_w, enc_out_w, dec_in_w, dec_out_w = grouped_w
    enc_vectors = vectors_all[:, :ENCODER_WIDTH]
    dec_vectors = vectors_all[:, ENCODER_WIDTH:]
    image_count = images.shape[0] // tensor_count

    def own(member):
        return lax.dynamic_slice_in_dim(member, tensor_at * image_count, image_count, axis=0)

    images, keep_index, unshuffle, masked, image_valid = map(
        own, (images, keep_index, unshuffle, masked, image_valid)
    )
    block = DEC["block"]
    images = jnp.pad(images, ((0, 0), (0, block - IMAGE_PATCHES), (0, 0)))
    lanes = 256
    codes = jnp.pad(
        jnp.where(masked == 1, MASK_ROW, unshuffle),
        ((0, 0), (0, lanes - IMAGE_PATCHES)),
        constant_values=-1,
    )
    codes = jnp.where(jnp.arange(lanes) == IMAGE_PATCHES, CLASS_ROW, codes)[:, None, :]
    kept = jnp.pad(keep_index, ((0, 0), (0, 128 - KEEP)), constant_values=-1)[:, None, :]
    weight_rows = jnp.broadcast_to(
        (image_valid.astype(f32) / patch_total)[:, None, None], (image_count, 1, 128)
    )
    enc_state = encoder_forward(
        kept,
        images,
        sinusoid_table(ENCODER_WIDTH, GRID_PATCHES, IMAGE_PATCHES, block),
        enc_in_w,
        enc_out_w,
        pixel_w[:PATCH_DIM],
        bridge_w,
        enc_vectors,
    )
    grad_dec_in, grad_dec_out, grad_head, grad_projected, dec_sums = decoder_step(
        enc_state[0],
        codes,
        weight_rows,
        images,
        sinusoid_table(D_D, GRID_PATCHES, IMAGE_PATCHES, block),
        dec_in_w,
        dec_out_w,
        pixel_w[PATCH_DIM:],
        dec_vectors,
    )
    grad_enc_in, grad_enc_out, grad_bridge, grad_embed, enc_sums = encoder_backward(
        grad_projected, enc_state[1:], enc_in_w, enc_out_w, bridge_w, enc_vectors
    )
    grad_pixel = jnp.concatenate([grad_embed, grad_head.astype(bf16)], axis=0)
    packed = jnp.concatenate([enc_sums, dec_sums], axis=1)
    finish = ring_finish if ringed(tensor_count) else plain_finish
    return finish(
        ([grad_enc_in, grad_enc_out, grad_dec_in, grad_dec_out], grad_pixel, grad_bridge, packed),
        masters,
        firsts,
        seconds,
    )


def solution(mesh):
    state_specs = (
        P("dp", "tensor", None),
        P("tensor", "dp", None),
        P("dp", "tensor", None),
        P("tensor", "dp", None),
        P("dp", None),
        P("dp", None),
        P(None, "dp"),
    )
    in_specs = (
        P("dp", None, None),
        P("dp", None),
        P("dp", None),
        P("dp", None),
        P("dp"),
    ) + state_specs * 3
    out_specs = (P(), P()) + state_specs * 3
    return jax.shard_map(shards, mesh=mesh, in_specs=in_specs, out_specs=out_specs, check_vma=False)
```

```python
import functools

import jax
import jax.numpy as jnp
from jax import lax
from jax.experimental import pallas as pl
from jax.experimental.pallas import tpu as pltpu
from jax.sharding import PartitionSpec as P
import numpy as np

ENCODER_WIDTH = 768
H_E = 12
HD_E = 64
D_D = 512
H_D = 16
HD_D = 32
PATCH_DIM = 768
GRID_PATCHES = 14
IMAGE_PATCHES = 196
KEEP = 49

eps_norm = 1e-06
beta_one = 0.9
beta_two = 0.999
step_count = 7.0
learn_rate = 0.3
decay_matrix = 0.05
eps_moment = 1e-06
f32 = jnp.float32
bf16 = jnp.bfloat16
EVERY = ("dp", "tensor")
GROUPED = ("tensor", "dp")


MESH_ID = pl.DeviceIdType.MESH
PIX, EIN, EOUT, BRI, DIN, DOUT, VEC = range(7)


def place():
    dp_at = lax.axis_index("dp")
    group = lax.axis_index("tensor")
    z, x = lax.div(dp_at, 2), lax.rem(dp_at, 2)
    y, c = lax.div(group, 2), lax.rem(group, 2)
    return z, x, y, c


def device(z, x, y, c):
    return (z * 2 + x, y * 2 + c)


def flip(z, m):
    low = lax.rem(z, 2)
    high = lax.div(z, 2)
    if m % 2:
        low = 1 - low
    if m // 2:
        high = 1 - high
    return high * 2 + low


def greet(z, x, y, c):
    barrier = pltpu.get_barrier_semaphore()
    peers = [
        device(z, x, y, 1 - c),
        device(z, x, 1 - y, c),
        device(z, 1 - x, y, c),
        device(flip(z, 1), x, y, c),
        device(flip(z, 2), x, y, c),
        device(flip(z, 3), x, y, c),
    ]
    for peer in peers:
        pl.semaphore_signal(barrier, inc=1, device_id=peer, device_id_type=MESH_ID)
    pl.semaphore_wait(barrier, 6)


SHARED = (PIX, BRI)


def spot(array, y, c, z, x):
    return (z, x, y, c) if array in SHARED else (y, c, z, x)


def half_spot(array, y, z, x):
    return (z, x, y) if array in SHARED else (y, z, x)


def whole_shape(array, part):
    return ((4, 2, 2, 2) if array in SHARED else (2, 2, 4, 2)) + part


GATHER_STEPS = (
    ((VEC, 0, 8, 0), (PIX, 0, 24, 0), (PIX, 24, 16, 1)),
    ((EIN, 0, 32, 0), (EIN, 32, 16, 1)),
    ((EIN, 48, 16, 0), (EIN, 64, 32, 1)),
    ((EOUT, 0, 32, 0), (EOUT, 32, 32, 1)),
    ((EOUT, 64, 32, 0), (EOUT, 96, 24, 1), (BRI, 0, 16, 1), (BRI, 16, 8, 0)),
    ((DIN, 0, 32, 0), (DIN, 32, 32, 1)),
    ((DOUT, 0, 48, 0), (DOUT, 48, 32, 1)),
)


def gather_ticks(parts, outs, send, recv, local):
    count = 7
    z, x, y, c = place()
    units = []
    for at, step in enumerate(GATHER_STEPS):
        for unit in step:
            units.append((at,) + unit)
    copies = {}

    def rows(array, region, first, size):
        ref = outs[array]
        return ref.at[region + (pl.ds(first, size),)]

    def plan(number, stage):
        at, array, first, size, turn = units[number]
        every = slice(None)
        if stage < 3:
            src = parts[array].at[pl.ds(first, size)]
            dst = rows(array, spot(array, y, c, z, x), first, size)
            peer = device(flip(z, stage + 1), x, y, c)
        else:
            if stage == 3:
                region = spot(array, y, c, every, x)
                peer = device(z, x, 1 - y, c) if turn == 0 else device(z, 1 - x, y, c)
            elif stage == 4 and turn == 0:
                region = spot(array, every, c, every, x)
                peer = device(z, 1 - x, y, c)
            elif stage == 4:
                region = spot(array, y, c, every, every)
                peer = device(z, x, 1 - y, c)
            else:
                region = spot(array, every, c, every, every)
                peer = device(z, x, y, 1 - c)
            src = dst = rows(array, region, first, size)
        return pltpu.make_async_remote_copy(
            src_ref=src,
            dst_ref=dst,
            send_sem=send.at[number, stage],
            recv_sem=recv.at[number, stage],
            device_id=peer,
            device_id_type=MESH_ID,
        )

    def start(number, stage):
        copies[number, stage] = plan(number, stage)
        copies[number, stage].start()

    own = []
    for array in range(count):
        own.append(
            pltpu.make_async_copy(parts[array], outs[array].at[spot(array, y, c, z, x)], local.at[array])
        )
        own[-1].start()
    greet(z, x, y, c)
    steps = len(GATHER_STEPS)
    waited = set()
    for tick in range(steps + 4):
        for number, unit in enumerate(units):
            if unit[0] == tick:
                for stage in range(3):
                    start(number, stage)
        for number, unit in enumerate(units):
            if unit[0] == tick - 1:
                if unit[1] not in waited:
                    waited.add(unit[1])
                    own[unit[1]].wait()
                for stage in range(3):
                    copies[number, stage].wait_recv()
                start(number, 3)
        for back in (2, 3):
            for number, unit in enumerate(units):
                if unit[0] == tick - back:
                    copies[number, back + 1].wait_recv()
                    start(number, back + 2)
        for number, unit in enumerate(units):
            if unit[0] == tick - 4:
                copies[number, 5].wait_recv()
        if tick < steps + 3:
            yield tick
    for key in copies:
        copies[key].wait_send()
    yield steps + 3
    yield None


SCATTER_STEPS = (
    ((DOUT, 0, 48, 0), (DOUT, 48, 32, 1)),
    ((BRI, 0, 8, 0), (BRI, 8, 16, 1), (DIN, 0, 32, 0), (DIN, 32, 32, 1)),
    ((PIX, 0, 24, 0), (PIX, 24, 16, 1)),
    ((EOUT, 0, 32, 0), (EOUT, 32, 32, 1)),
    ((EOUT, 64, 32, 0), (EOUT, 96, 24, 1)),
    ((EIN, 0, 32, 0), (EIN, 32, 16, 1)),
    ((EIN, 48, 16, 0), (EIN, 64, 32, 1)),
)
STAT_LANES = {EIN: 0, EOUT: 1, DIN: 2, DOUT: 3, PIX: 4, BRI: 5, VEC: 6}


def state_rows(ref, rows):
    if len(ref.shape) == 2:
        return ref[rows]
    return ref[rows, 0, :] if ref.shape[1] == 1 else ref[0, rows, :]


def put_rows(ref, rows, values):
    if len(ref.shape) == 2:
        ref[rows] = values
    elif ref.shape[1] == 1:
        ref[rows, 0, :] = values
    else:
        ref[0, rows, :] = values


def moments(gradient, moment_one, moment_two, master, decay):
    next_one = beta_one * moment_one + (1.0 - beta_one) * gradient
    next_two = beta_two * moment_two + (1.0 - beta_two) * gradient * gradient
    bias_one = 1.0 - beta_one**step_count
    bias_two = 1.0 - beta_two**step_count
    update = next_one / bias_one / (jnp.sqrt(next_two / bias_two) + eps_moment) + decay * master
    return next_one, next_two, update


def state_step(rows):
    return next(step for step in (32, 40, rows) if rows % step == 0)


def scatter_kernel(shapes, units, *refs):
    grads = refs[:7]
    masters, firsts, seconds = refs[7:14], refs[14:21], refs[21:28]
    outs = refs[28:36]
    refs = refs[36:]
    n = len(units)
    own, one, two, three, four = (refs[k * n : (k + 1) * n] for k in range(5))
    vec_one, vec_two, vec_three, vec_four, vec_sum = refs[5 * n : 5 * n + 5]
    stats, stat_one, stat_two, stat_three, stat_four = refs[5 * n + 5 : 5 * n + 10]
    send, recv, local, vsend, vrecv, tsend, trecv, ssend, srecv = refs[5 * n + 10 :]
    z, x, y, c = place()
    every = slice(None)
    copies = {}
    stat_row = lax.broadcasted_iota(jnp.int32, (8, 128), 0)
    stat_lane = lax.broadcasted_iota(jnp.int32, (8, 128), 1)

    def tally(array):
        if array == VEC:
            gradient = outs[VEC][:7, : masters[VEC].shape[1]]
            update = moments(
                gradient, firsts[VEC][...], seconds[VEC][...], masters[VEC][...], 0.0
            )[2]
            squares = [jnp.sum(v * v, axis=0, keepdims=True) for v in (masters[VEC][...], update)]
        else:
            flat = (array in SHARED) and outs[array].shape[0] == 4
            count = outs[array].shape[0] * outs[array].shape[1] if flat else outs[array].shape[0]
            columns = outs[array].shape[-1]
            step = outs[array].shape[1] if flat else state_step(count)

            def body(k, carry):
                rows = pl.ds(pl.multiple_of(k * step, 8), step)
                gradient = outs[array][k] if flat else outs[array][rows]
                master = state_rows(masters[array], rows)
                update = moments(
                    gradient,
                    state_rows(firsts[array], rows),
                    state_rows(seconds[array], rows),
                    master,
                    decay_matrix,
                )[2]
                return tuple(
                    total + jnp.sum((v * v).reshape(step // 8, 8, columns), axis=0)
                    for total, v in zip(carry, (master, update))
                )

            start = (jnp.zeros((8, columns), f32),) * 2
            squares = [
                jnp.sum(v, axis=0, keepdims=True)
                for v in lax.fori_loop(0, count // step, body, start)
            ]
        share = 0.25 if array in SHARED + (VEC,) else 1.0
        total = stats[...]
        for row, square in enumerate(squares):
            value = jnp.sum(square, axis=1, keepdims=True) * share
            total = total + jnp.where((stat_row == row) & (stat_lane == STAT_LANES[array]), value, 0.0)
        stats[...] = total

    def remote(src, dst, key, send_sem, recv_sem, peer):
        copies[key] = pltpu.make_async_remote_copy(
            src_ref=src,
            dst_ref=dst,
            send_sem=send_sem,
            recv_sem=recv_sem,
            device_id=peer,
            device_id_type=MESH_ID,
        )
        copies[key].start()

    def start(number, stage):
        at, array, first, size, turn = units[number]
        mine = own[number]
        if stage == 0:
            peer = device(z, x, y, 1 - c)
            src = grads[array].at[
                spot(array, every, 1 - c, every, every) + (pl.ds(first, size),)
            ]
            dst = one[number]
        elif stage == 1 and turn == 0:
            peer = device(z, 1 - x, y, c)
            src, dst = mine.at[half_spot(array, every, every, 1 - x)], two[number]
        elif stage == 1:
            peer = device(z, x, 1 - y, c)
            src, dst = mine.at[half_spot(array, 1 - y, every, every)], two[number]
        elif stage == 2 and turn == 0:
            peer = device(z, x, 1 - y, c)
            src, dst = mine.at[half_spot(array, 1 - y, every, x)], three[number]
        elif stage == 2:
            peer = device(z, 1 - x, y, c)
            src, dst = mine.at[half_spot(array, y, every, 1 - x)], three[number]
        else:
            other = flip(z, stage - 2)
            peer = device(other, x, y, c)
            src, dst = mine.at[half_spot(array, y, other, x)], four[number].at[stage - 3]
        remote(src, dst, (number, stage), send.at[number, stage], recv.at[number, stage], peer)

    def add(number, stage):
        at, array, first, size, turn = units[number]
        mine = own[number]

        def pair(here, there):
            mine[here] = (mine[here].astype(f32) + there.astype(f32)).astype(bf16)

        if stage == 0:

            @pl.loop(0, 16)
            def _(k):
                iy, iz, ix = k // 8, (k // 2) % 4, k % 2
                here = half_spot(array, iy, iz, ix)
                pair(here, one[number][here])

        elif stage == 1 and turn == 0:

            @pl.loop(0, 8)
            def _(k):
                iy, iz = k // 4, k % 4
                there = (iz, iy) if array in SHARED else (iy, iz)
                pair(half_spot(array, iy, iz, x), two[number][there])

        elif stage == 1:

            @pl.loop(0, 8)
            def _(k):
                iz, ix = k // 2, k % 2
                pair(half_spot(array, y, iz, ix), two[number][iz, ix])

        elif stage == 2:

            @pl.loop(0, 4)
            def _(k):
                pair(half_spot(array, y, k, x), three[number][k])

        else:
            total = mine[half_spot(array, y, z, x)].astype(f32)
            for slot in range(3):
                total = total + four[number][slot].astype(f32)
            if array in SHARED:
                outs[array][y * 2 + c, pl.ds(first, size)] = total
            else:
                outs[array][pl.ds(first, size)] = total

    loads = []
    for number, (at, array, first, size, turn) in enumerate(units):
        loads.append(
            pltpu.make_async_copy(
                grads[array].at[spot(array, every, c, every, every) + (pl.ds(first, size),)],
                own[number],
                local.at[number],
            )
        )
    stats[...] = jnp.zeros_like(stats)
    greet(z, x, y, c)
    steps = units[-1][0] + 1

    def step_units(tick):
        return [number for number in range(n) if units[number][0] == tick]

    vec_dst = (vec_one, vec_two, vec_three)
    vec_peer = (device(z, x, y, 1 - c), device(z, 1 - x, y, c), device(z, x, 1 - y, c))

    for tick in range(steps + 4):
        for number in step_units(tick):
            loads[number].start()
            start(number, 0)
        for number in step_units(tick - 1):
            loads[number].wait()
            copies[number, 0].wait_recv()
            add(number, 0)
            start(number, 1)
        for number in step_units(tick - 2):
            copies[number, 1].wait()
            add(number, 1)
            start(number, 2)
        for number in step_units(tick - 3):
            copies[number, 2].wait()
            add(number, 2)
            for stage in (3, 4, 5):
                start(number, stage)
        for number in step_units(tick - 4):
            for stage in (3, 4, 5):
                copies[number, stage].wait()
            add(number, 3)
        if tick < 4:
            if tick == 0:
                vec_sum[...] = grads[6][...]
            if tick < 3:
                remote(vec_sum.at[...], vec_dst[tick], ("v", tick), vsend.at[tick], vrecv.at[tick], vec_peer[tick])
            else:
                vec_four[z] = vec_sum[...]
                for m in (1, 2, 3):
                    remote(vec_sum.at[...], vec_four.at[z], ("v", 2 + m), vsend.at[2 + m], vrecv.at[2 + m], device(flip(z, m), x, y, c))
        if tick < 3:
            copies["v", tick].wait()
            vec_sum[...] = vec_sum[...] + vec_dst[tick][...]
        if tick == 4:
            for m in (1, 2, 3):
                copies["v", 2 + m].wait()
            vec_sum[...] = (vec_four[0] + vec_four[1]) + (vec_four[2] + vec_four[3])
            outs[VEC][...] = vec_sum[z * 2 + x]
            tally(VEC)
        for array in range(6):
            last = max(units[number][0] for number in range(n) if units[number][1] == array)
            if array in SHARED and tick == last + 4:
                here = y * 2 + c
                peers = (
                    device(z, x, y, 1 - c),
                    device(z, x, 1 - y, c),
                    device(z, x, 1 - y, 1 - c),
                )
                for k, peer in enumerate(peers):
                    slot = SHARED.index(array) * 3 + k
                    piece = outs[array].at[here]
                    remote(piece, piece, ("t", slot), tsend.at[slot], trecv.at[slot], peer)
            elif array in SHARED and tick == last + 5:
                for k in range(3):
                    copies["t", SHARED.index(array) * 3 + k].wait()
                tally(array)
            elif array not in SHARED and tick == last + 4:
                tally(array)
    stat_peers = (device(z, x, y, 1 - c), device(z, 1 - x, y, c), device(z, x, 1 - y, c))
    for stage, (held, peer) in enumerate(zip((stat_one, stat_two, stat_three), stat_peers)):
        remote(stats, held, ("s", stage), ssend.at[stage], srecv.at[stage], peer)
        copies["s", stage].wait()
        stats[...] = stats[...] + held[...]
    stat_four[z] = stats[...]
    for m in (1, 2, 3):
        remote(
            stats,
            stat_four.at[z],
            ("s", 2 + m),
            ssend.at[2 + m],
            srecv.at[2 + m],
            device(flip(z, m), x, y, c),
        )
    for m in (1, 2, 3):
        copies["s", 2 + m].wait()
    norms = jnp.sqrt((stat_four[0] + stat_four[1]) + (stat_four[2] + stat_four[3]))
    loss = vec_sum[7, 7:8, 128:256][:, 31:32]
    outs[7][...] = jnp.where(stat_row == 2, loss, norms)
    for number in range(n):
        copies[number, 0].wait_send()


def scatter_gradients(grads, masters, firsts, seconds):
    units = [(at,) + unit for at, step in enumerate(SCATTER_STEPS) for unit in step]
    n = len(units)
    shapes = [grad.shape for grad in grads]
    outs = []
    for array in range(6):
        rows, columns = shapes[array][4:]
        if array in SHARED:
            outs.append(jax.ShapeDtypeStruct((4, rows, columns), f32))
        else:
            outs.append(jax.ShapeDtypeStruct((rows, columns), f32))
    outs.append(jax.ShapeDtypeStruct(grads[6].shape[1:], f32))
    outs.append(jax.ShapeDtypeStruct((8, 128), f32))
    scratch = []
    for stage in range(5):
        for at, array, first, size, turn in units:
            shared = array in SHARED
            lead = ((4, 2, 2) if shared else (2, 4, 2), (4,), (3,))
            if stage < 2:
                lead = lead[0]
            elif stage == 2:
                lead = ((4, 2) if shared else (2, 4)) if turn == 0 else (4, 2)
            else:
                lead = lead[stage - 2]
            scratch.append(pltpu.VMEM(lead + (size, shapes[array][5]), bf16))
    vec = grads[6].shape
    scratch += [pltpu.VMEM(vec, f32)] * 3 + [pltpu.VMEM((4,) + vec, f32), pltpu.VMEM(vec, f32)]
    scratch += [pltpu.VMEM((8, 128), f32)] * 4 + [pltpu.VMEM((4, 8, 128), f32)]
    scratch += [
        pltpu.SemaphoreType.DMA((n, 6)),
        pltpu.SemaphoreType.DMA((n, 6)),
        pltpu.SemaphoreType.DMA((n,)),
        pltpu.SemaphoreType.DMA((6,)),
        pltpu.SemaphoreType.DMA((6,)),
        pltpu.SemaphoreType.DMA((6,)),
        pltpu.SemaphoreType.DMA((6,)),
        pltpu.SemaphoreType.DMA((6,)),
        pltpu.SemaphoreType.DMA((6,)),
    ]
    total = sum(int(grad.size) * grad.dtype.itemsize for grad in grads)
    return pl.pallas_call(
        functools.partial(scatter_kernel, shapes, units),
        out_shape=outs,
        in_specs=[pl.BlockSpec(memory_space=pl.ANY)] * 6
        + [pl.BlockSpec(memory_space=pltpu.VMEM)] * 22,
        out_specs=[pl.BlockSpec(memory_space=pltpu.VMEM)] * 8,
        scratch_shapes=scratch,
        compiler_params=pltpu.CompilerParams(
            collective_id=1, has_side_effects=True, vmem_limit_bytes=60 * 1024 * 1024
        ),
        cost_estimate=pl.CostEstimate(flops=0, bytes_accessed=2 * total, transcendentals=0),
        name="scatter_gradients",
    )(*grads, *masters, *firsts, *seconds)


def apply_kernel(*refs):
    grads, masters, firsts, seconds = (refs[7 * k : 7 * k + 7] for k in range(4))
    stats = refs[28]
    next_firsts, next_seconds, news = (refs[29 + 7 * k : 36 + 7 * k] for k in range(3))
    loss, pairs = refs[50:]
    for array in range(7):
        lane = STAT_LANES[array]
        norms = [stats[row : row + 1, :][:, lane : lane + 1] for row in range(2)]
        ratio = learn_rate * norms[0] / norms[1]
        count = masters[array].shape[0]
        if len(masters[array].shape) == 3:
            count = count * masters[array].shape[1]
        decay = 0.0 if array == VEC else decay_matrix

        def body(rows, array=array, ratio=ratio, decay=decay):
            if array == VEC:
                gradient = grads[VEC][:7, : masters[VEC].shape[1]]
            else:
                gradient = grads[array][rows]
            master = state_rows(masters[array], rows)
            next_one, next_two, update = moments(
                gradient,
                state_rows(firsts[array], rows),
                state_rows(seconds[array], rows),
                master,
                decay,
            )
            put_rows(next_firsts[array], rows, next_one)
            put_rows(next_seconds[array], rows, next_two)
            put_rows(news[array], rows, master - ratio * update)

        if array == VEC:
            body(slice(None))
        else:
            row_loop(count, state_step(count), body)
    pairs[...] = stats[:2, :][:, :7]
    loss[...] = stats[2:3, :][:, :1]


def apply_update(reduced, masters, firsts, seconds, stats):
    shapes = [jax.ShapeDtypeStruct(master.shape, f32) for master in masters]
    results = pl.pallas_call(
        apply_kernel,
        out_shape=shapes * 3
        + [jax.ShapeDtypeStruct((1, 1), f32), jax.ShapeDtypeStruct((2, 7), f32)],
        compiler_params=pltpu.CompilerParams(vmem_limit_bytes=48 * 1024 * 1024),
        name="apply_update",
    )(*reduced, *masters, *firsts, *seconds, stats)
    return results[:7], results[7:14], results[14:21], results[21].reshape(()), results[22]


def sinusoid_table(feature_width, grid_side, patch_count, padded):
    position = np.arange(patch_count)
    quarter = feature_width // 4
    omegas = 1.0 / 10000.0 ** (np.arange(quarter) / quarter)
    parts = []
    for coords in (position % grid_side, position // grid_side):
        angles = coords[:, None] * omegas[None, :]
        parts += [np.sin(angles), np.cos(angles)]
    table = np.concatenate(parts, axis=1).astype(np.float32)
    return jnp.asarray(np.pad(table, ((0, padded - patch_count), (0, 0))))


GROUPS = 4
ENC = dict(step=128, first=0, images=4, block=64, tokens=50, width=768, heads=3, head=64, hidden=768, spans=1)
DEC = dict(step=208, first=768, images=4, block=208, tokens=197, width=512, heads=4, head=32, hidden=512, spans=4)
CLASS_ROW = 49
MASK_ROW = 50


def dot(left, right, dims=((1,), (0,)), precision=None):
    return lax.dot_general(
        left, right, (dims, ((), ())), preferred_element_type=f32, precision=precision
    )


def dot_t(left, right):
    return dot(left, right, ((0,), (0,)))


def dot_nt(left, right):
    return dot(left, right, ((1,), (1,)))


def exact_dot(left, right, dims):
    return dot(left, right, dims, lax.Precision.HIGHEST)


def row_loop(count, step, body):
    @pl.loop(0, count // step)
    def _(k):
        body(pl.ds(pl.multiple_of(k * step, step), step))


def fold(values):
    step, width = values.shape
    return jnp.sum(values.reshape(step // 8, 8, width), axis=0)


def norm_rows(source, gain, shift, unit, inverse, low, step):
    def body(rows):
        values = source[rows]
        centred = values - jnp.mean(values, axis=-1, keepdims=True)
        scale = lax.rsqrt(jnp.mean(centred * centred, axis=-1, keepdims=True) + eps_norm)
        normed = centred * scale
        unit[rows] = normed
        inverse[rows] = scale
        low[rows] = (normed * gain + shift).astype(bf16)

    row_loop(source.shape[0], step, body)


def norm_back_rows(incoming, unit, inverse, gain, result, residual, sums, at, step):
    width = incoming.shape[-1]

    def body(rows):
        given = incoming[rows]
        normed = unit[rows]
        scaled = given * gain
        inner = (
            scaled
            - jnp.mean(scaled, axis=-1, keepdims=True)
            - normed * jnp.mean(scaled * normed, axis=-1, keepdims=True)
        )
        value = inverse[rows] * inner
        if residual is not None:
            value = value + residual[rows]
        sums[at] = sums[at] + fold(given * normed)
        sums[at + 1] = sums[at + 1] + fold(given)
        result[rows] = value

    row_loop(incoming.shape[0], step, body)


def lane_chunks(size):
    return [slice(at, min(at + 128, size)) for at in range(0, size, 128)]


def attend_mask(dims, scores, start):
    if dims["spans"] == 1:
        key = lax.broadcasted_iota(jnp.int32, scores.shape, 0)
        query = lax.broadcasted_iota(jnp.int32, scores.shape, 1) + start
        allowed = ((key // dims["block"]) == (query // dims["block"])) & (
            (key % dims["block"]) < dims["tokens"]
        )
        return jnp.where(allowed, scores, -1e30)
    first = dims["tokens"] // 16 * 16
    tail = scores[first:]
    key = lax.broadcasted_iota(jnp.int32, tail.shape, 0) + first
    return jnp.concatenate([scores[:first], jnp.where(key < dims["tokens"], tail, -1e30)], axis=0)


def layer_forward_rows(dims, stream, w_in, w_out, vectors, saved):
    unit_one, inv_one, low_one, qkv, probs, mixed, unit_two, inv_two, low_two, active, slope, work, low_work, low_more = saved
    count, width = stream.shape
    inner = dims["heads"] * dims["head"]
    span = count // dims["spans"]
    norm_rows(stream, vectors[1:2, :], vectors[2:3, :], unit_one, inv_one, low_one, dims["step"])

    @pl.loop(0, GROUPS)
    def _(t):
        weights = w_in[t, :, : 3 * inner] if inner % 128 == 0 else w_in[t][:, : 3 * inner]

        def body(rows):
            qkv[t, rows] = dot(low_one[rows], weights).astype(bf16)

        body(slice(None))

    scale = dims["head"] ** (-0.5)

    @pl.loop(0, GROUPS * dims["spans"])
    def _(k):
        t = k // dims["spans"]
        b = k % dims["spans"]
        rows = pl.ds(pl.multiple_of(b * span, span), span)
        triple = qkv[t, rows]
        query_t = triple[:, :inner].T
        value_t = triple[:, 2 * inner :].T
        heads = range(dims["heads"])
        lanes = [slice(head * dims["head"], (head + 1) * dims["head"]) for head in heads]
        for head in heads:
            key = triple[:, inner : 2 * inner][:, lanes[head]]
            work[head] = dot(key, query_t[lanes[head]])
        for head in heads:
            for columns in lane_chunks(span):
                scores = attend_mask(dims, work[head, :, columns] * scale, columns.start)
                shifted = jnp.exp(scores - jnp.max(scores, axis=0, keepdims=True))
                share = shifted * (1.0 / jnp.sum(shifted, axis=0, keepdims=True))
                probs[k * dims["heads"] + head, :, columns] = share
                low_work[head, :, columns] = share.astype(bf16)
        results = [dot(value_t[lanes[head]], low_work[head]) for head in heads]
        mixed[t, rows] = jnp.concatenate(results, axis=0).T.astype(bf16)

    yield "attended"

    @pl.loop(0, GROUPS)
    def _(t):
        weights = w_out[t, :inner]

        def body(rows):
            stream[rows] = stream[rows] + dot(mixed[t, rows], weights)

        body(slice(None))

    norm_rows(stream, vectors[3:4, :], vectors[4:5, :], unit_two, inv_two, low_two, dims["step"])

    def feed(t):
        up = w_in[t, :, 3 * inner :] if inner % 128 == 0 else w_in[t][:, 3 * inner :]
        down = w_out[t, inner:]
        slope[t] = dot(low_two[...], up)

        def bend(rows):
            hidden = slope[t, rows]
            level = 0.5 + 0.5 * lax.erf(hidden * (0.5**0.5))
            active[t, rows] = (hidden * level).astype(bf16)
            slope[t, rows] = level + hidden * (
                jnp.exp(-0.5 * hidden * hidden) * (0.5 / np.pi) ** 0.5
            )

        row_loop(count, 32, bend)
        stream[...] = stream[...] + dot(active[t], down)

    half = GROUPS // 2 if dims["spans"] == 1 else GROUPS
    pl.loop(0, half)(feed)
    if half < GROUPS:
        yield "halfway"
        pl.loop(half, GROUPS)(feed)


def layer_backward_rows(dims, given, spare, w_in, w_out, vectors, saved, low, flow, grad_in, grad_out, sums):
    unit_one, inv_one, low_one, qkv, probs, mixed, unit_two, inv_two, low_two, active, slope, work, low_work, low_more = saved
    count, width = given.shape
    inner = dims["heads"] * dims["head"]
    span = count // dims["spans"]
    aligned = inner % 128 == 0

    def lower(rows):
        low[rows] = given[rows].astype(bf16)
        spare[rows] = jnp.zeros_like(spare[rows])

    row_loop(count, 32, lower)

    @pl.loop(0, GROUPS)
    def _(t):
        down = w_out[t, inner:]
        up = w_in[t, :, 3 * inner :] if aligned else w_in[t][:, 3 * inner :]
        grad_out[t, inner:] = dot_t(active[t], low[...]).astype(bf16)

        def body(rows):
            flow[rows] = (slope[t, rows] * dot_nt(low[rows], down)).astype(bf16)
            spare[rows] = spare[rows] + dot_nt(flow[rows], up)

        body(slice(None))
        grad_up = dot_t(low_two[...], flow[...]).astype(bf16)
        if aligned:
            grad_in[t, :, 3 * inner :] = grad_up
        else:
            grad_in[t] = jnp.concatenate([jnp.zeros((width, 3 * inner), bf16), grad_up], axis=1)

    norm_back_rows(spare, unit_two, inv_two, vectors[3:4, :], given, given, sums, 3, dims["step"])
    row_loop(count, 32, lower)

    @pl.loop(0, GROUPS)
    def _(t):
        weights = w_out[t, :inner]
        grad_out[t, :inner] = dot_t(mixed[t], low[...]).astype(bf16)

        def body(rows):
            mixed[t, rows] = dot_nt(low[rows], weights).astype(bf16)

        body(slice(None))

    scale = dims["head"] ** (-0.5)

    @pl.loop(0, GROUPS * dims["spans"])
    def _(k):
        t = k // dims["spans"]
        b = k % dims["spans"]
        rows = pl.ds(pl.multiple_of(b * span, span), span)
        triple = qkv[t, rows]
        back = mixed[t, rows]
        key_t = triple[:, inner : 2 * inner].T
        back_t = back.T
        heads = range(dims["heads"])
        lanes = [slice(head * dims["head"], (head + 1) * dims["head"]) for head in heads]
        for head in heads:
            work[head] = dot(triple[:, 2 * inner :][:, lanes[head]], back_t[lanes[head]])
        for head in heads:
            for columns in lane_chunks(span):
                share = probs[k * dims["heads"] + head, :, columns]
                grad_p = work[head, :, columns]
                grad_s = share * (grad_p - jnp.sum(share * grad_p, axis=0, keepdims=True))
                low_work[head, :, columns] = grad_s.astype(bf16)
                low_more[head, :, columns] = share.astype(bf16)
        parts = ([], [], [])
        for head in heads:
            parts[0].append(dot(key_t[lanes[head]], low_work[head]) * scale)
            parts[1].append(dot(low_work[head], triple[:, :inner][:, lanes[head]]) * scale)
            parts[2].append(dot(low_more[head], back[:, lanes[head]]))
        grad_query = jnp.concatenate(parts[0], axis=0).T
        qkv[t, rows] = jnp.concatenate([grad_query] + parts[1] + parts[2], axis=1).astype(bf16)

    @pl.loop(0, GROUPS)
    def _(t):
        weights = w_in[t, :, : 3 * inner] if aligned else w_in[t][:, : 3 * inner]
        grad_triple = dot_t(low_one[...], qkv[t]).astype(bf16)
        if aligned:
            grad_in[t, :, : 3 * inner] = grad_triple
        else:
            grad_in[t] = jnp.concatenate([grad_triple, grad_in[t][:, 3 * inner :]], axis=1)

        def body(rows):
            spare[rows] = spare[rows] + dot_nt(qkv[t, rows], weights)

        body(slice(None))

    norm_back_rows(spare, unit_one, inv_one, vectors[1:2, :], given, given, sums, 1, dims["step"])


def saved_shapes(dims):
    count = dims["images"] * dims["block"]
    width, inner = dims["width"], dims["heads"] * dims["head"]
    span = count // dims["spans"]
    return [
        ((count, width), f32),
        ((count, 1), f32),
        ((count, width), bf16),
        ((GROUPS, count, 3 * inner), bf16),
        ((GROUPS * dims["spans"] * dims["heads"], span, span), f32),
        ((GROUPS, count, inner), bf16),
        ((count, width), f32),
        ((count, 1), f32),
        ((count, width), bf16),
        ((GROUPS, count, dims["hidden"]), bf16),
        ((GROUPS, count, dims["hidden"]), f32),
    ]


def work_shapes(dims):
    span = dims["images"] * dims["block"] // dims["spans"]
    shape = (dims["heads"], span, span)
    return [(shape, f32), (shape, bf16), (shape, bf16)]


def token_gain(vectors, dims):
    return vectors.at[:, pl.ds(dims["first"], dims["width"])]


def decoder_kernel(*refs):
    projected, codes, images, table, w_in, w_out, pixel_w, vectors_all = refs[:8]
    grad_in, grad_out, grad_head, grad_projected, vec_out = refs[8:13]
    stream, given, unit, inverse, low, flow, sums, loss, head, pixels_here, head_sum, loaded = refs[13:25]
    saved = refs[25:]
    dims = DEC
    vectors = token_gain(vectors_all, dims)
    count, width = stream.shape
    block = dims["block"]
    copies = [pltpu.make_async_copy(pixel_w.at[pl.ds(PATCH_DIM, width)], head, loaded.at[0])]
    for b in range(dims["images"]):
        copies.append(
            pltpu.make_async_copy(
                images.at[b], pixels_here.at[b], loaded.at[1 + b]
            )
        )
    for copy in copies:
        copy.start()
    sums[...] = jnp.zeros_like(sums)
    loss[...] = jnp.zeros_like(loss)

    def placer(b):
        return (
            lax.broadcasted_iota(jnp.int32, (64, block), 0) == codes[b][:1, :block]
        ).astype(f32)

    def block_rows(b):
        return pl.ds(pl.multiple_of(b * block, block), block)

    @pl.loop(0, dims["images"])
    def _(b):
        at = lax.broadcasted_iota(jnp.int32, (64, width), 0)
        source = jnp.where(at == MASK_ROW, vectors[0:1, :], projected[b])
        source = jnp.where(at > MASK_ROW, 0.0, source)
        stream[block_rows(b)] = exact_dot(placer(b), source, ((0,), (0,))) + table[...]

    for _ in layer_forward_rows(dims, stream, w_in, w_out, vectors, saved):
        pass
    norm_rows(stream, vectors[5:6, :], vectors[6:7, :], unit, inverse, low, dims["step"])
    for copy in copies:
        copy.wait()
    head_sum[...] = jnp.zeros_like(head_sum)
    pixels_wide = pixels_here.shape[-1]
    counted = vectors_all[7:8, :]
    patch_total = jnp.sum(counted, axis=1, keepdims=True) / (counted.shape[1] // 8)

    @pl.loop(0, dims["images"])
    def _(b):
        rows = block_rows(b)
        predicted = dot(low[rows], head[...])
        pixels = jnp.concatenate(
            [pixels_here[b], jnp.zeros((block - IMAGE_PATCHES, pixels_wide), bf16)], axis=0
        ).astype(f32)
        centred = pixels - jnp.mean(pixels, axis=-1, keepdims=True)
        variance = jnp.sum(centred * centred, axis=-1, keepdims=True) / (pixels_wide - 1)
        errors = predicted - centred * lax.rsqrt(variance + eps_norm)
        at = lax.broadcasted_iota(jnp.int32, (64, 128), 0)
        share = codes[b][2:3, :128].astype(f32) / patch_total
        spread = jnp.where(at == MASK_ROW, share, 0.0)
        weight = exact_dot(placer(b), spread, ((0,), (0,)))[:, :1]
        loss[...] = loss[...] + fold(errors * errors * weight)
        grad_low = (errors * (2.0 / pixels_wide) * weight).astype(bf16)
        head_sum[...] = head_sum[...] + dot_t(low[rows], grad_low)
        given[rows] = dot_nt(grad_low, head[...])

    grad_head[...] = head_sum[...].astype(bf16)
    norm_back_rows(given, unit, inverse, vectors[5:6, :], given, None, sums, 5, dims["step"])
    layer_backward_rows(
        dims, given, stream, w_in, w_out, vectors, saved, low, flow, grad_in, grad_out, sums
    )

    @pl.loop(0, dims["images"])
    def _(b):
        back = exact_dot(placer(b), given[block_rows(b)], ((1,), (0,)))
        at = lax.broadcasted_iota(jnp.int32, (64, width), 0)
        grad_projected[b] = jnp.where(at < MASK_ROW, back, 0.0).astype(bf16)
        sums[0] = sums[0] + fold(jnp.where(at == MASK_ROW, back, 0.0))

    for row in range(7):
        vec_out[row : row + 1, :] = jnp.sum(sums[row], axis=0, keepdims=True)
    total = jnp.sum(jnp.sum(loss[...], axis=0, keepdims=True), axis=1, keepdims=True)
    vec_out[7:8, :] = jnp.broadcast_to(total / pixels_wide, (1, width))


def decoder_step(projected, codes, images, table, w_in, w_out, pixel_w, vectors):
    dims = DEC
    count, width = dims["images"] * dims["block"], dims["width"]
    wide = images.shape[-1]
    outs = [
        jax.ShapeDtypeStruct(w_in.shape, bf16),
        jax.ShapeDtypeStruct(w_out.shape, bf16),
        jax.ShapeDtypeStruct((width, wide), bf16),
        jax.ShapeDtypeStruct(projected.shape, bf16),
        jax.ShapeDtypeStruct((8, width), f32),
    ]
    scratch = [
        ((count, width), f32),
        ((count, width), f32),
        ((count, width), f32),
        ((count, 1), f32),
        ((count, width), bf16),
        ((count, dims["hidden"]), bf16),
        ((7, 8, width), f32),
        ((8, wide), f32),
        ((width, wide), bf16),
        ((dims["images"],) + images.shape[1:], bf16),
        ((width, wide), f32),
        None,
    ]
    scratch += saved_shapes(dims) + work_shapes(dims)
    in_vmem = pl.BlockSpec(memory_space=pltpu.VMEM)
    anywhere = pl.BlockSpec(memory_space=pl.ANY)
    return pl.pallas_call(
        decoder_kernel,
        out_shape=outs,
        in_specs=[in_vmem, in_vmem, anywhere, in_vmem, in_vmem, in_vmem, anywhere, in_vmem],
        scratch_shapes=[
            pltpu.SemaphoreType.DMA((5,)) if shape is None else pltpu.VMEM(*shape)
            for shape in scratch
        ],
        compiler_params=pltpu.CompilerParams(vmem_limit_bytes=62 * 1024 * 1024),
        name="decoder_step",
    )(projected, codes, images, table, w_in, w_out, pixel_w, vectors)


def encode_kernel(ring, *refs):
    dims = ENC
    images, codes, table = refs[:3]
    refs = refs[3:]
    group = lax.axis_index("tensor")
    if ring:
        masters, count_row, refs = refs[:7], refs[7], refs[8:]
        wholes, vectors_all, projected, kept_state = refs[:7], refs[7], refs[8], refs[9:24]
        refs = refs[24:]
        parts, send, recv, local, vec_parts = refs[:7], *refs[7:11]
        raw = dict(zip((PIX, EOUT, BRI), refs[11:14]))
        refs = refs[14:]
    else:
        wholes, vectors_all = refs[:4], refs[4]
        projected, kept_state = refs[5], refs[6:21]
        refs = refs[21:]
        wholes = dict(zip((PIX, EIN, EOUT, BRI), wholes))
    loaded, flushed = refs[:2]
    pixels_here, stream, w_in, w_out, embed, bridge = refs[2:8]
    retained, unit, inverse, low = refs[8:12]
    saved = refs[12:23]
    work = refs[23:]
    held = (retained, unit, inverse, low) + tuple(saved)
    vectors = token_gain(vectors_all, dims)
    count, width = stream.shape
    block = dims["block"]

    picture_copies = [
        pltpu.make_async_copy(
            images.at[b], pixels_here.at[b], loaded.at[4 + b]
        )
        for b in range(dims["images"])
    ]
    for copy in picture_copies:
        copy.start()

    def load(slot, array, target):
        if not ring:
            source = wholes[array]
            if array == PIX:
                source = source.at[pl.ds(0, PATCH_DIM)]
            pltpu.make_async_copy(source, target, loaded.at[slot]).start()
            return pltpu.make_async_copy(source, target, loaded.at[slot])
        if array != EIN:
            pltpu.make_async_copy(wholes[array], raw[array], loaded.at[slot]).start()
            return pltpu.make_async_copy(wholes[array], raw[array], loaded.at[slot])
        rows = wholes[array].shape[4]

        @pl.loop(0, 32)
        def _(k):
            pltpu.make_async_copy(
                wholes[array].at[k // 16, (k // 8) % 2, (k // 2) % 4, k % 2],
                target.at[k // 8, pl.ds(pl.multiple_of((k % 8) * rows, rows), rows)],
                loaded.at[slot],
            ).start()

        return pltpu.make_async_copy(target, target, loaded.at[slot])

    def assemble(array, target):
        if ring and array in SHARED:
            count = -(-target.shape[0] // raw[array].shape[4])
            pieces = [
                raw[array][k // 8, (k // 4) % 2, (k // 2) % 2, k % 2] for k in range(count)
            ]
            target[...] = jnp.concatenate(pieces, axis=0)[: target.shape[0]]
        elif ring:

            @pl.loop(0, GROUPS)
            def _(t):
                pieces = [raw[array][t // 2, t % 2, k // 2, k % 2] for k in range(8)]
                target[t] = jnp.concatenate(pieces, axis=0)

    flushes = []

    def flush(*members):
        for member in members:
            copy = pltpu.make_async_copy(held[member], kept_state[member], flushed.at[member])
            copy.start()
            flushes.append(copy)

    if ring:
        for array in range(6):
            if array in SHARED:
                rows = masters[array].shape[0] // 4
                rows = pl.ds(pl.multiple_of(group * rows, 8), rows)
                parts[array][...] = masters[array][rows].astype(bf16)
            else:
                parts[array][...] = state_rows(masters[array], slice(None)).astype(bf16)
        columns = masters[VEC].shape[1]
        parts[VEC][...] = jnp.zeros_like(parts[VEC])
        parts[VEC][:7, :columns] = masters[VEC][...].astype(bf16).astype(f32)
        parts[VEC][7:8, :] = count_row[...]
        ticks = gather_ticks(parts, wholes, send, recv, local)

    def advance(times):
        if ring:
            for _ in range(times):
                next(ticks)

    advance(5)
    embed_copy = load(0, PIX, embed)
    if ring:
        vec_copy = pltpu.make_async_copy(wholes[VEC], vec_parts, loaded.at[1])
        vec_copy.start()
        vec_copy.wait()
        vectors_all[...] = jnp.concatenate(
            [vec_parts[0, 0, k // 2, k % 2][:, :columns] for k in range(8)], axis=1
        )
    for copy in picture_copies:
        copy.wait()
    embed_copy.wait()
    assemble(PIX, embed)

    @pl.loop(0, dims["images"])
    def _(b):
        rows = pl.ds(pl.multiple_of(b * block, block), block)
        choice = (
            lax.broadcasted_iota(jnp.int32, (IMAGE_PATCHES, block), 0) == codes[b][1:2, :block]
        )
        retained[rows] = dot_t(choice.astype(bf16), pixels_here[b]).astype(bf16)
        places = exact_dot(choice.astype(f32), table[...], ((0,), (0,)))
        at = lax.broadcasted_iota(jnp.int32, (block, width), 0)
        start = dot(retained[rows], embed[...]) + places
        stream[rows] = jnp.where(at == CLASS_ROW, vectors[0:1, :], start)

    flush(0)
    advance(2)
    load(2, EIN, w_in).wait()
    layer = layer_forward_rows(dims, stream, w_in, w_out, vectors, saved + work)
    next(layer)
    flush(4, 5, 6, 7, 8, 9)
    advance(2)
    bridge_copy = load(1, BRI, bridge)
    load(3, EOUT, w_out).wait()
    assemble(EOUT, w_out)
    next(layer)
    flush(10, 11, 12)
    advance(1)
    for _ in layer:
        pass
    flush(13, 14)
    norm_rows(stream, vectors[5:6, :], vectors[6:7, :], unit, inverse, low, dims["step"])
    flush(1, 2, 3)
    bridge_copy.wait()
    assemble(BRI, bridge)

    @pl.loop(0, dims["images"])
    def _(b):
        rows = pl.ds(pl.multiple_of(b * block, block), block)
        projected[b] = dot(low[rows], bridge[...])

    advance(2)
    for copy in flushes:
        copy.wait()


def encode(images, codes, table, weights, count_row=None, vectors=None):
    dims = ENC
    ring = vectors is None
    count, width = dims["images"] * dims["block"], dims["width"]
    bridge_wide = weights[BRI].shape[-1]
    in_vmem = pl.BlockSpec(memory_space=pltpu.VMEM)
    anywhere = pl.BlockSpec(memory_space=pl.ANY)
    kept_shapes = [
        ((count, images.shape[-1]), bf16),
        ((count, width), f32),
        ((count, 1), f32),
        ((count, width), bf16),
    ] + saved_shapes(dims)
    outs = [((dims["images"], dims["block"], bridge_wide), f32)] + kept_shapes
    out_specs = [in_vmem] + [anywhere] * len(kept_shapes)
    in_specs = [anywhere, in_vmem, in_vmem]
    scratch = []
    if ring:
        shapes = []
        for array in range(6):
            rows, wide = weights[array].size // weights[array].shape[-1], weights[array].shape[-1]
            shapes.append((rows // 4 if array in SHARED else rows, wide))
        shapes.append((8, 256))
        types = [bf16] * 6 + [f32]
        operands = [images, codes, table, *weights, count_row]
        in_specs += [in_vmem] * 8
        gathered = [(whole_shape(k, shape), types[k]) for k, shape in enumerate(shapes)]
        outs = gathered + [((8, shapes_total(weights[VEC])), f32)] + outs
        out_specs = [anywhere] * 7 + [in_vmem] + out_specs
        units = sum(len(step) for step in GATHER_STEPS)
        scratch += [pltpu.VMEM(shape, kind) for shape, kind in zip(shapes, types)]
        scratch += [
            pltpu.SemaphoreType.DMA((units, 6)),
            pltpu.SemaphoreType.DMA((units, 6)),
            pltpu.SemaphoreType.DMA((7,)),
            pltpu.VMEM(whole_shape(VEC, shapes[VEC]), f32),
        ]
        scratch += [
            pltpu.VMEM(whole_shape(array, shapes[array]), bf16) for array in (PIX, EOUT, BRI)
        ]
        params = dict(collective_id=0, has_side_effects=True)
        w_shapes = [
            (GROUPS, 8 * shapes[EIN][0], shapes[EIN][1]),
            (GROUPS, 8 * shapes[EOUT][0], shapes[EOUT][1]),
        ]
    else:
        operands = [images, codes, table] + [weights[k] for k in (PIX, EIN, EOUT, BRI)] + [vectors]
        in_specs += [anywhere] * 4 + [in_vmem]
        params = {}
        w_shapes = [weights[EIN].shape, weights[EOUT].shape]
    scratch += [pltpu.SemaphoreType.DMA((8,)), pltpu.SemaphoreType.DMA((15,))]
    buffers = [
        ((dims["images"],) + images.shape[1:], bf16),
        ((count, width), f32),
        (w_shapes[0], bf16),
        (w_shapes[1], bf16),
        ((PATCH_DIM, width), bf16),
        ((width, bridge_wide), bf16),
    ]
    buffers += kept_shapes + work_shapes(dims)
    scratch += [pltpu.VMEM(*buffer) for buffer in buffers]
    return pl.pallas_call(
        functools.partial(encode_kernel, ring),
        out_shape=[jax.ShapeDtypeStruct(shape, kind) for shape, kind in outs],
        in_specs=in_specs,
        out_specs=out_specs,
        scratch_shapes=scratch,
        compiler_params=pltpu.CompilerParams(vmem_limit_bytes=62 * 1024 * 1024, **params),
        name="gather_encode" if ring else "encode",
    )(*operands)


def shapes_total(vector_shard):
    return 8 * vector_shard.shape[1]


def encoder_backward_kernel(*refs):
    grad_projected, retained, unit, inverse, low_end = refs[:5]
    saved = list(refs[5:16])
    w_in, w_out, bridge, vectors_all, grad_head, dec_sums = refs[16:22]
    grad_in, grad_out, grad_bridge, grad_pixel, packed = refs[22:27]
    given, spare, low, flow, sums, qkv, mixed, vec_all = refs[27:35]
    dims = ENC
    vectors = token_gain(vectors_all, dims)
    count, width = given.shape
    block = dims["block"]
    sums[...] = jnp.zeros_like(sums)
    qkv[...] = saved[3][...]
    mixed[...] = saved[5][...]
    saved[3], saved[5] = qkv, mixed
    saved += refs[35:]

    flat = grad_projected[...].reshape(count, grad_projected.shape[-1])
    grad_bridge[...] = dot_t(low_end[...], flat).astype(bf16)
    given[...] = dot_nt(flat, bridge[...])
    norm_back_rows(given, unit, inverse, vectors[5:6, :], given, None, sums, 5, dims["step"])
    layer_backward_rows(
        dims, given, spare, w_in, w_out, vectors, saved, low, flow, grad_in, grad_out, sums
    )
    grad_pixel[:PATCH_DIM] = dot_t(retained[...], given[...].astype(bf16)).astype(bf16)
    grad_pixel[PATCH_DIM:] = grad_head[...]

    def tokens(rows):
        at = lax.broadcasted_iota(jnp.int32, (block, width), 0)
        sums[0] = sums[0] + fold(jnp.where(at == CLASS_ROW, given[rows], 0.0))

    row_loop(count, block, tokens)
    for row in range(7):
        vec_all[row : row + 1, :width] = jnp.sum(sums[row], axis=0, keepdims=True)
    vec_all[7:8, :width] = jnp.zeros((1, width), f32)
    vec_all[:, width:] = dec_sums[...]
    columns = vec_all.shape[1] // 8
    packed[...] = jnp.zeros_like(packed)
    for k in range(8):
        packed[k, :, :columns] = vec_all[:, k * columns : (k + 1) * columns]


def encoder_backward(grad_projected, kept_state, w_in, w_out, bridge, vectors, grad_head, dec_sums):
    dims = ENC
    count, width = dims["images"] * dims["block"], dims["width"]
    shapes = saved_shapes(dims)
    pixels_wide = kept_state[0].shape[1]
    outs = [
        jax.ShapeDtypeStruct(w_in.shape, bf16),
        jax.ShapeDtypeStruct(w_out.shape, bf16),
        jax.ShapeDtypeStruct(bridge.shape, bf16),
        jax.ShapeDtypeStruct((pixels_wide + grad_head.shape[0], width), bf16),
        jax.ShapeDtypeStruct((8, 8, 256), f32),
    ]
    scratch = [
        ((count, width), f32),
        ((count, width), f32),
        ((count, width), bf16),
        ((count, dims["hidden"]), bf16),
        ((7, 8, width), f32),
        shapes[3],
        shapes[5],
        (vectors.shape, f32),
    ] + work_shapes(dims)
    return pl.pallas_call(
        encoder_backward_kernel,
        out_shape=outs,
        scratch_shapes=[pltpu.VMEM(shape, dtype) for shape, dtype in scratch],
        compiler_params=pltpu.CompilerParams(vmem_limit_bytes=62 * 1024 * 1024),
        name="encoder_backward",
    )(grad_projected, *kept_state, w_in, w_out, bridge, vectors, grad_head, dec_sums)


def gather_grouped(part, groups):
    whole = lax.all_gather(part, GROUPED, axis=0, tiled=True)
    return whole.reshape(groups, -1, whole.shape[-1])


def scatter_grouped(gradient):
    flat = gradient.astype(f32).reshape(-1, gradient.shape[-1])
    return lax.psum_scatter(flat, GROUPED, scatter_dimension=0, tiled=True)


def ringed(tensor_count):
    return tensor_count == 4 and lax.axis_size("dp") == 8


def plain_gather(masters, counted):
    groups = lax.axis_size("tensor")
    wholes = {}
    for array, k in ((EIN, 0), (EOUT, 1), (DIN, 2), (DOUT, 3)):
        flat = masters[k].reshape(-1, masters[k].shape[-1]).astype(bf16)
        wholes[array] = gather_grouped(flat, groups)
    for array, k in ((PIX, 4), (BRI, 5)):
        wholes[array] = lax.all_gather(masters[k].astype(bf16), "dp", axis=0, tiled=True)
    low = masters[6].astype(bf16).astype(f32)
    vectors = lax.all_gather(low, "dp", axis=1, tiled=True)
    eighth = jnp.broadcast_to(lax.psum(counted, "dp") / 8, (1, vectors.shape[1]))
    return wholes, jnp.concatenate([vectors, eighth], axis=0)


def ring_finish(gradients, masters, firsts, seconds):
    grouped, grad_pixel, grad_bridge, packed = gradients
    tensor_count = lax.axis_size("tensor")
    order = (4, 0, 1, 5, 2, 3, 6)
    sources = (grad_pixel, grouped[0], grouped[1], grad_bridge, grouped[2], grouped[3])
    operands = []
    for array, source in enumerate(sources):
        master = masters[order[array]]
        rows, wide = master.size // master.shape[-1], master.shape[-1]
        if array in SHARED:
            rows = rows // tensor_count
        operands.append(source.reshape(whole_shape(array, (rows, wide))))
    operands.append(packed)
    states = [[members[k] for k in order] for members in (masters, firsts, seconds)]
    *sums, stats = scatter_gradients(operands, *states)
    for array in SHARED:
        sums[array] = sums[array].reshape(-1, sums[array].shape[-1])
    *results, loss_value, pairs = apply_update(sums, *states, stats)
    place_of = {k: at for at, k in enumerate(order)}
    results = [[members[place_of[k]] for k in range(7)] for members in results]
    return (loss_value, pairs, *results[0], *results[1], *results[2])


def plain_finish(gradients, masters, firsts, seconds):
    grouped, grad_pixel, grad_bridge, packed = gradients
    tensor_count = lax.axis_size("tensor")
    columns = masters[6].shape[1]

    def scatter_shared(gradient):
        part = lax.psum_scatter(gradient.astype(f32), EVERY, scatter_dimension=0, tiled=True)
        return lax.all_gather(part, "tensor", axis=0, tiled=True)

    reduced = [scatter_grouped(gradient) for gradient in grouped]
    reduced += [scatter_shared(grad_pixel), scatter_shared(grad_bridge)]
    whole = packed.shape[0] * (ENCODER_WIDTH + D_D) // 8
    packed = packed[:, :, : whole // packed.shape[0]].transpose(1, 0, 2).reshape(8, -1)
    vector_sum = lax.psum(packed, EVERY)
    own = lax.dynamic_slice_in_dim(
        vector_sum[:7], lax.axis_index("dp") * columns, columns, axis=1
    )
    reduced = [gradient.reshape(master.shape) for gradient, master in zip(reduced + [own], masters)]
    decays = (decay_matrix,) * 6 + (0.0,)
    share_counts = (1.0,) * 4 + (float(tensor_count),) * 3
    steps = [moments(*member) for member in zip(reduced, firsts, seconds, masters, decays)]
    new_firsts, new_seconds, updates = zip(*steps)

    def squares(members):
        return jnp.stack(
            [jnp.sum(member * member) / count for member, count in zip(members, share_counts)]
        )

    weight_norm, update_norm = map(
        jnp.sqrt, lax.psum((squares(masters), squares(updates)), EVERY)
    )
    ratio = learn_rate * weight_norm / update_norm
    news = [
        master - ratio[position] * update
        for position, (master, update) in enumerate(zip(masters, updates))
    ]
    return (vector_sum[7, -1], jnp.stack([weight_norm, update_norm]), *new_firsts, *new_seconds, *news)


def shards(
    images,
    keep_index,
    unshuffle,
    masked,
    image_valid,
    *state,
):
    masters, firsts, seconds = state[:7], state[7:14], state[14:21]
    tensor_count = lax.axis_size("tensor")
    tensor_at = lax.axis_index("tensor")
    counted = jnp.sum(masked.astype(f32) * image_valid.astype(f32)[:, None])
    image_count = images.shape[0] // tensor_count
    lanes = 256
    codes = jnp.pad(
        jnp.where(masked == 1, MASK_ROW, unshuffle),
        ((0, 0), (0, lanes - IMAGE_PATCHES)),
        constant_values=-1,
    )
    codes = jnp.where(jnp.arange(lanes) == IMAGE_PATCHES, CLASS_ROW, codes)
    kept = jnp.pad(keep_index, ((0, 0), (0, lanes - KEEP)), constant_values=-1)
    valid = jnp.broadcast_to(image_valid[:, None], codes.shape)
    codes = jnp.stack([codes, kept, valid], axis=1)
    images = lax.dynamic_slice_in_dim(images, tensor_at * image_count, image_count, axis=0)
    codes = lax.dynamic_slice_in_dim(codes, tensor_at * image_count, image_count, axis=0)
    enc_table = sinusoid_table(ENCODER_WIDTH, GRID_PATCHES, IMAGE_PATCHES, IMAGE_PATCHES)
    dec_table = sinusoid_table(D_D, GRID_PATCHES, IMAGE_PATCHES, DEC["block"])
    if ringed(tensor_count):
        order = (4, 0, 1, 5, 2, 3, 6)
        results = encode(
            images,
            codes,
            enc_table,
            [masters[k] for k in order],
            jnp.broadcast_to(counted, (1, lanes)),
        )
        wholes, vectors, projected, enc_state = results[:7], results[7], results[8], results[9:]
        wholes = [
            whole.reshape(-1, whole.shape[-1])
            if array in SHARED
            else whole.reshape(tensor_count, -1, whole.shape[-1])
            for array, whole in enumerate(wholes)
        ]
    else:
        wholes, vectors = plain_gather(masters, counted)
        projected, *enc_state = encode(images, codes, enc_table, wholes, vectors=vectors)
    grad_dec_in, grad_dec_out, grad_head, grad_projected, dec_sums = decoder_step(
        projected, codes, images, dec_table, wholes[DIN], wholes[DOUT], wholes[PIX], vectors
    )
    grad_enc_in, grad_enc_out, grad_bridge, grad_pixel, packed = encoder_backward(
        grad_projected,
        enc_state,
        wholes[EIN],
        wholes[EOUT],
        wholes[BRI],
        vectors,
        grad_head,
        dec_sums,
    )
    finish = ring_finish if ringed(tensor_count) else plain_finish
    return finish(
        ([grad_enc_in, grad_enc_out, grad_dec_in, grad_dec_out], grad_pixel, grad_bridge, packed),
        masters,
        firsts,
        seconds,
    )


def solution(mesh):
    state_specs = (
        P("dp", "tensor", None),
        P("tensor", "dp", None),
        P("dp", "tensor", None),
        P("tensor", "dp", None),
        P("dp", None),
        P("dp", None),
        P(None, "dp"),
    )
    in_specs = (
        P("dp", None, None),
        P("dp", None),
        P("dp", None),
        P("dp", None),
        P("dp"),
    ) + state_specs * 3
    out_specs = (P(), P()) + state_specs * 3
    return jax.shard_map(shards, mesh=mesh, in_specs=in_specs, out_specs=out_specs, check_vma=False)
```

```python
import functools

import jax
import jax.numpy as jnp
from jax import lax
from jax.experimental import pallas as pl
from jax.experimental.pallas import tpu as pltpu
from jax.sharding import PartitionSpec as P
import numpy as np

ENCODER_WIDTH = 768
H_E = 12
HD_E = 64
D_D = 512
H_D = 16
HD_D = 32
PATCH_DIM = 768
GRID_PATCHES = 14
IMAGE_PATCHES = 196
KEEP = 49

eps_norm = 1e-06
beta_one = 0.9
beta_two = 0.999
step_count = 7.0
learn_rate = 0.3
decay_matrix = 0.05
eps_moment = 1e-06
f32 = jnp.float32
bf16 = jnp.bfloat16
EVERY = ("dp", "tensor")
GROUPED = ("tensor", "dp")


MESH_ID = pl.DeviceIdType.MESH
PIX, EIN, EOUT, BRI, DIN, DOUT, VEC = range(7)


def place():
    dp_at = lax.axis_index("dp")
    group = lax.axis_index("tensor")
    z, x = lax.div(dp_at, 2), lax.rem(dp_at, 2)
    y, c = lax.div(group, 2), lax.rem(group, 2)
    return z, x, y, c


def device(z, x, y, c):
    return (z * 2 + x, y * 2 + c)


def flip(z, m):
    low = lax.rem(z, 2)
    high = lax.div(z, 2)
    if m % 2:
        low = 1 - low
    if m // 2:
        high = 1 - high
    return high * 2 + low


def greet(z, x, y, c):
    barrier = pltpu.get_barrier_semaphore()
    peers = [device(flip(z, m), x, y, c) for m in (1, 2, 3)]
    for m in range(1, 8):
        peers.append(
            device(
                z,
                1 - x if m // 4 else x,
                1 - y if (m // 2) % 2 else y,
                1 - c if m % 2 else c,
            )
        )
    for peer in peers:
        pl.semaphore_signal(barrier, inc=1, device_id=peer, device_id_type=MESH_ID)
    pl.semaphore_wait(barrier, len(peers))


SHARED = (PIX, BRI)


def spot(array, y, c, z, x):
    return (z, x, y, c) if array in SHARED else (y, c, z, x)


def half_spot(array, y, z, x):
    return (z, x, y) if array in SHARED else (y, z, x)


def whole_shape(array, part):
    return ((4, 2, 2, 2) if array in SHARED else (2, 2, 4, 2)) + part


GATHER_STEPS = (
    ((VEC, 0, 8, 0), (PIX, 0, 24, 0), (PIX, 24, 16, 1)),
    ((EIN, 0, 16, 0), (EIN, 16, 16, 1)),
    ((EIN, 32, 16, 0), (EIN, 48, 16, 1)),
    ((EIN, 64, 16, 0), (EIN, 80, 16, 1)),
    ((EOUT, 0, 24, 0), (EOUT, 24, 24, 1)),
    ((EOUT, 48, 24, 0), (EOUT, 72, 24, 1)),
    ((EOUT, 96, 8, 0), (EOUT, 104, 16, 1), (BRI, 0, 16, 0), (BRI, 16, 8, 1)),
    ((DIN, 0, 16, 0), (DIN, 16, 16, 1)),
    ((DIN, 32, 16, 0), (DIN, 48, 16, 1)),
    ((DOUT, 0, 16, 0), (DOUT, 16, 32, 1)),
    ((DOUT, 48, 16, 0), (DOUT, 64, 16, 1)),
)
DEPTH = 4


def last_step(steps, array):
    return max(at for at, step in enumerate(steps) for unit in step if unit[0] == array)


def gather_ticks(parts, outs, send, recv, local):
    count = 7
    z, x, y, c = place()
    units = []
    for at, step in enumerate(GATHER_STEPS):
        for unit in step:
            units.append((at,) + unit)
    copies = {}

    def rows(array, region, first, size):
        ref = outs[array]
        return ref.at[region + (pl.ds(first, size),)]

    def plan(number, stage):
        at, array, first, size, turn = units[number]
        every = slice(None)
        if stage < 3:
            src = parts[array].at[pl.ds(first, size)]
            dst = rows(array, spot(array, y, c, z, x), first, size)
            peer = device(flip(z, stage + 1), x, y, c)
        else:
            if stage == 3:
                region = spot(array, y, c, every, x)
                peer = device(z, x, 1 - y, c) if turn == 0 else device(z, 1 - x, y, c)
            elif stage == 4 and turn == 0:
                region = spot(array, every, c, every, x)
                peer = device(z, 1 - x, y, c)
            elif stage == 4:
                region = spot(array, y, c, every, every)
                peer = device(z, x, 1 - y, c)
            else:
                region = spot(array, every, c, every, every)
                peer = device(z, x, y, 1 - c)
            src = dst = rows(array, region, first, size)
        return pltpu.make_async_remote_copy(
            src_ref=src,
            dst_ref=dst,
            send_sem=send.at[number, stage],
            recv_sem=recv.at[number, stage],
            device_id=peer,
            device_id_type=MESH_ID,
        )

    def start(number, stage):
        copies[number, stage] = plan(number, stage)
        copies[number, stage].start()

    own = []
    for array in range(count):
        own.append(
            pltpu.make_async_copy(parts[array], outs[array].at[spot(array, y, c, z, x)], local.at[array])
        )
        own[-1].start()
    greet(z, x, y, c)
    steps = len(GATHER_STEPS)
    waited = set()
    for tick in range(steps + 4):
        for number, unit in enumerate(units):
            if unit[0] == tick:
                for stage in range(3):
                    start(number, stage)
        for number, unit in enumerate(units):
            if unit[0] == tick - 1:
                if unit[1] not in waited:
                    waited.add(unit[1])
                    own[unit[1]].wait()
                for stage in range(3):
                    copies[number, stage].wait_recv()
                start(number, 3)
        for back in (2, 3):
            for number, unit in enumerate(units):
                if unit[0] == tick - back:
                    copies[number, back + 1].wait_recv()
                    start(number, back + 2)
        for number, unit in enumerate(units):
            if unit[0] == tick - 4:
                copies[number, 5].wait_recv()
        if tick < steps + 3:
            yield tick
    for key in copies:
        copies[key].wait_send()
    yield steps + 3
    yield None


SCATTER_STEPS = (
    ((BRI, 0, 8, 0), (BRI, 8, 16, 1)),
    ((PIX, 0, 24, 0), (PIX, 24, 16, 1)),
    ((EIN, 0, 16, 0), (EIN, 16, 16, 1)),
    ((EIN, 32, 16, 0), (EIN, 48, 16, 1)),
    ((EIN, 64, 16, 0), (EIN, 80, 16, 1)),
    ((EOUT, 0, 24, 0), (EOUT, 24, 24, 1)),
    ((EOUT, 48, 24, 0), (EOUT, 72, 24, 1)),
    ((EOUT, 96, 8, 0), (EOUT, 104, 16, 1)),
    ((DIN, 0, 16, 0), (DIN, 16, 16, 1)),
    ((DIN, 32, 16, 0), (DIN, 48, 16, 1)),
    ((DOUT, 0, 24, 0), (DOUT, 24, 24, 1)),
    ((DOUT, 48, 16, 0), (DOUT, 64, 16, 1)),
)


STAT_LANES = {EIN: 0, EOUT: 1, DIN: 2, DOUT: 3, PIX: 4, BRI: 5, VEC: 6}


def state_rows(ref, rows):
    if len(ref.shape) == 2:
        return ref[rows]
    return ref[rows, 0, :] if ref.shape[1] == 1 else ref[0, rows, :]


def put_rows(ref, rows, values):
    if len(ref.shape) == 2:
        ref[rows] = values
    elif ref.shape[1] == 1:
        ref[rows, 0, :] = values
    else:
        ref[0, rows, :] = values


def moments(gradient, moment_one, moment_two, master, decay):
    next_one = beta_one * moment_one + (1.0 - beta_one) * gradient
    next_two = beta_two * moment_two + (1.0 - beta_two) * gradient * gradient
    bias_one = 1.0 - beta_one**step_count
    bias_two = 1.0 - beta_two**step_count
    update = next_one / bias_one / (jnp.sqrt(next_two / bias_two) + eps_moment) + decay * master
    return next_one, next_two, update


def state_step(rows):
    return next(step for step in (32, 40, rows) if rows % step == 0)


def scatter_kernel(shapes, units, *refs):
    grads = refs[:7]
    masters, firsts, seconds = refs[7:14], refs[14:21], refs[21:28]
    outs = refs[28:36]
    refs = refs[36:]
    n = len(units)
    own, one, two, three, four = (refs[k * n : (k + 1) * n] for k in range(5))
    vec_one, vec_two, vec_three, vec_four, vec_sum = refs[5 * n : 5 * n + 5]
    stats, stat_one, stat_four = refs[5 * n + 5 : 5 * n + 8]
    send, recv, local, vsend, vrecv, tsend, trecv, ssend, srecv = refs[5 * n + 8 :]
    z, x, y, c = place()
    every = slice(None)
    copies = {}
    stat_row = lax.broadcasted_iota(jnp.int32, (8, 128), 0)
    stat_lane = lax.broadcasted_iota(jnp.int32, (8, 128), 1)

    def tally(array):
        if array == VEC:
            gradient = outs[VEC][:7, : masters[VEC].shape[1]]
            update = moments(
                gradient, firsts[VEC][...], seconds[VEC][...], masters[VEC][...], 0.0
            )[2]
            squares = [jnp.sum(v * v, axis=0, keepdims=True) for v in (masters[VEC][...], update)]
        else:
            flat = (array in SHARED) and outs[array].shape[0] == 4
            count = outs[array].shape[0] * outs[array].shape[1] if flat else outs[array].shape[0]
            columns = outs[array].shape[-1]
            step = outs[array].shape[1] if flat else state_step(count)

            def body(k, carry):
                rows = pl.ds(pl.multiple_of(k * step, 8), step)
                gradient = outs[array][k] if flat else outs[array][rows]
                master = state_rows(masters[array], rows)
                update = moments(
                    gradient,
                    state_rows(firsts[array], rows),
                    state_rows(seconds[array], rows),
                    master,
                    decay_matrix,
                )[2]
                return tuple(
                    total + jnp.sum((v * v).reshape(step // 8, 8, columns), axis=0)
                    for total, v in zip(carry, (master, update))
                )

            start = (jnp.zeros((8, columns), f32),) * 2
            squares = [
                jnp.sum(v, axis=0, keepdims=True)
                for v in lax.fori_loop(0, count // step, body, start)
            ]
        share = 0.25 if array in SHARED + (VEC,) else 1.0
        total = stats[...]
        for row, square in enumerate(squares):
            value = jnp.sum(square, axis=1, keepdims=True) * share
            total = total + jnp.where((stat_row == row) & (stat_lane == STAT_LANES[array]), value, 0.0)
        stats[...] = total

    def remote(src, dst, key, send_sem, recv_sem, peer):
        copies[key] = pltpu.make_async_remote_copy(
            src_ref=src,
            dst_ref=dst,
            send_sem=send_sem,
            recv_sem=recv_sem,
            device_id=peer,
            device_id_type=MESH_ID,
        )
        copies[key].start()

    def start(number, stage):
        at, array, first, size, turn = units[number]
        mine = own[number]
        if stage == 0:
            peer = device(z, x, y, 1 - c)
            src = grads[array].at[
                spot(array, every, 1 - c, every, every) + (pl.ds(first, size),)
            ]
            dst = one[number]
        elif stage == 1 and turn == 0:
            peer = device(z, 1 - x, y, c)
            src, dst = mine.at[half_spot(array, every, every, 1 - x)], two[number]
        elif stage == 1:
            peer = device(z, x, 1 - y, c)
            src, dst = mine.at[half_spot(array, 1 - y, every, every)], two[number]
        elif stage == 2 and turn == 0:
            peer = device(z, x, 1 - y, c)
            src, dst = mine.at[half_spot(array, 1 - y, every, x)], three[number]
        elif stage == 2:
            peer = device(z, 1 - x, y, c)
            src, dst = mine.at[half_spot(array, y, every, 1 - x)], three[number]
        else:
            other = flip(z, stage - 2)
            peer = device(other, x, y, c)
            src, dst = mine.at[half_spot(array, y, other, x)], four[number].at[stage - 3]
        remote(src, dst, (number, stage), send.at[number, stage], recv.at[number, stage], peer)

    def add(number, stage):
        at, array, first, size, turn = units[number]
        mine = own[number]

        def pair(here, there):
            mine[here] = (mine[here].astype(f32) + there.astype(f32)).astype(bf16)

        if stage == 0:

            @pl.loop(0, 16)
            def _(k):
                iy, iz, ix = k // 8, (k // 2) % 4, k % 2
                here = half_spot(array, iy, iz, ix)
                pair(here, one[number][here])

        elif stage == 1 and turn == 0:

            @pl.loop(0, 8)
            def _(k):
                iy, iz = k // 4, k % 4
                there = (iz, iy) if array in SHARED else (iy, iz)
                pair(half_spot(array, iy, iz, x), two[number][there])

        elif stage == 1:

            @pl.loop(0, 8)
            def _(k):
                iz, ix = k // 2, k % 2
                pair(half_spot(array, y, iz, ix), two[number][iz, ix])

        elif stage == 2:

            @pl.loop(0, 4)
            def _(k):
                pair(half_spot(array, y, k, x), three[number][k])

        else:
            total = mine[half_spot(array, y, z, x)].astype(f32)
            for slot in range(3):
                total = total + four[number][slot].astype(f32)
            if array in SHARED:
                outs[array][y * 2 + c, pl.ds(first, size)] = total
            else:
                outs[array][pl.ds(first, size)] = total

    loads = []
    for number, (at, array, first, size, turn) in enumerate(units):
        loads.append(
            pltpu.make_async_copy(
                grads[array].at[spot(array, every, c, every, every) + (pl.ds(first, size),)],
                own[number],
                local.at[number],
            )
        )
    stats[...] = jnp.zeros_like(stats)
    greet(z, x, y, c)
    steps = units[-1][0] + 1

    def step_units(tick):
        return [number for number in range(n) if units[number][0] == tick]

    vec_dst = (vec_one, vec_two, vec_three)
    vec_peer = (device(z, x, y, 1 - c), device(z, 1 - x, y, c), device(z, x, 1 - y, c))

    for tick in range(steps + 4):
        for number in step_units(tick):
            loads[number].start()
            start(number, 0)
        for number in step_units(tick - 1):
            loads[number].wait()
            copies[number, 0].wait_recv()
            add(number, 0)
            start(number, 1)
        for number in step_units(tick - 2):
            copies[number, 1].wait()
            add(number, 1)
            start(number, 2)
        for number in step_units(tick - 3):
            copies[number, 2].wait()
            add(number, 2)
            for stage in (3, 4, 5):
                start(number, stage)
        for number in step_units(tick - 4):
            for stage in (3, 4, 5):
                copies[number, stage].wait()
            add(number, 3)
        if tick < 4:
            if tick == 0:
                vec_sum[...] = grads[6][...]
            if tick < 3:
                remote(vec_sum.at[...], vec_dst[tick], ("v", tick), vsend.at[tick], vrecv.at[tick], vec_peer[tick])
            else:
                vec_four[z] = vec_sum[...]
                for m in (1, 2, 3):
                    remote(vec_sum.at[...], vec_four.at[z], ("v", 2 + m), vsend.at[2 + m], vrecv.at[2 + m], device(flip(z, m), x, y, c))
        if tick < 3:
            copies["v", tick].wait()
            vec_sum[...] = vec_sum[...] + vec_dst[tick][...]
        if tick == 4:
            for m in (1, 2, 3):
                copies["v", 2 + m].wait()
            vec_sum[...] = (vec_four[0] + vec_four[1]) + (vec_four[2] + vec_four[3])
            outs[VEC][...] = vec_sum[z * 2 + x]
            tally(VEC)
        for array in range(6):
            last = max(units[number][0] for number in range(n) if units[number][1] == array)
            if array in SHARED and tick == last + 4:
                here = y * 2 + c
                peers = (
                    device(z, x, y, 1 - c),
                    device(z, x, 1 - y, c),
                    device(z, x, 1 - y, 1 - c),
                )
                for k, peer in enumerate(peers):
                    slot = SHARED.index(array) * 3 + k
                    piece = outs[array].at[here]
                    remote(piece, piece, ("t", slot), tsend.at[slot], trecv.at[slot], peer)
            elif array in SHARED and tick == last + 5:
                for k in range(3):
                    copies["t", SHARED.index(array) * 3 + k].wait()
                tally(array)
            elif array not in SHARED and tick == last + 4:
                tally(array)
    here = (x * 2 + y) * 2 + c
    stat_one[here] = stats[...]
    for m in range(1, 8):
        peer = device(
            z,
            1 - x if m // 4 else x,
            1 - y if (m // 2) % 2 else y,
            1 - c if m % 2 else c,
        )
        remote(stats, stat_one.at[here], ("p", m), ssend.at[m], srecv.at[m], peer)
    for m in range(1, 8):
        copies["p", m].wait()
    total = stat_one[0]
    for slot in range(1, 8):
        total = total + stat_one[slot]
    stats[...] = total
    stat_four[z] = total
    for m in (1, 2, 3):
        remote(
            stats,
            stat_four.at[z],
            ("s", 2 + m),
            ssend.at[7 + m],
            srecv.at[7 + m],
            device(flip(z, m), x, y, c),
        )
    for m in (1, 2, 3):
        copies["s", 2 + m].wait()
    norms = jnp.sqrt((stat_four[0] + stat_four[1]) + (stat_four[2] + stat_four[3]))
    loss = vec_sum[7, 7:8, 128:256][:, 31:32]
    outs[7][...] = jnp.where(stat_row == 2, loss, norms)
    for number in range(n):
        copies[number, 0].wait_send()


def scatter_gradients(grads, masters, firsts, seconds):
    units = [(at,) + unit for at, step in enumerate(SCATTER_STEPS) for unit in step]
    n = len(units)
    shapes = [grad.shape for grad in grads]
    outs = []
    for array in range(6):
        rows, columns = shapes[array][4:]
        if array in SHARED:
            outs.append(jax.ShapeDtypeStruct((4, rows, columns), f32))
        else:
            outs.append(jax.ShapeDtypeStruct((rows, columns), f32))
    outs.append(jax.ShapeDtypeStruct(grads[6].shape[1:], f32))
    outs.append(jax.ShapeDtypeStruct((8, 128), f32))
    scratch = []
    for stage in range(5):
        for at, array, first, size, turn in units:
            shared = array in SHARED
            lead = ((4, 2, 2) if shared else (2, 4, 2), (4,), (3,))
            if stage < 2:
                lead = lead[0]
            elif stage == 2:
                lead = ((4, 2) if shared else (2, 4)) if turn == 0 else (4, 2)
            else:
                lead = lead[stage - 2]
            scratch.append(pltpu.VMEM(lead + (size, shapes[array][5]), bf16))
    vec = grads[6].shape
    scratch += [pltpu.VMEM(vec, f32)] * 3 + [pltpu.VMEM((4,) + vec, f32), pltpu.VMEM(vec, f32)]
    scratch += [pltpu.VMEM(lead + (8, 128), f32) for lead in ((), (8,), (4,))]
    scratch += [
        pltpu.SemaphoreType.DMA((n, 6)),
        pltpu.SemaphoreType.DMA((n, 6)),
        pltpu.SemaphoreType.DMA((n,)),
        pltpu.SemaphoreType.DMA((6,)),
        pltpu.SemaphoreType.DMA((6,)),
        pltpu.SemaphoreType.DMA((6,)),
        pltpu.SemaphoreType.DMA((6,)),
        pltpu.SemaphoreType.DMA((11,)),
        pltpu.SemaphoreType.DMA((11,)),
    ]
    total = sum(int(grad.size) * grad.dtype.itemsize for grad in grads)
    return pl.pallas_call(
        functools.partial(scatter_kernel, shapes, units),
        out_shape=outs,
        in_specs=[pl.BlockSpec(memory_space=pl.ANY)] * 6
        + [pl.BlockSpec(memory_space=pltpu.VMEM)] * 22,
        out_specs=[pl.BlockSpec(memory_space=pltpu.VMEM)] * 8,
        scratch_shapes=scratch,
        compiler_params=pltpu.CompilerParams(
            collective_id=1, has_side_effects=True, vmem_limit_bytes=60 * 1024 * 1024
        ),
        cost_estimate=pl.CostEstimate(flops=0, bytes_accessed=2 * total, transcendentals=0),
        name="scatter_gradients",
    )(*grads, *masters, *firsts, *seconds)


def apply_kernel(*refs):
    sources, stats = refs[:28], refs[28]
    targets = refs[29:50]
    loss, pairs = refs[50:52]
    held = refs[52:80]
    results = refs[80:101]
    loaded, stored = refs[101:]
    loads = [
        pltpu.make_async_copy(source, target, loaded.at[at])
        for at, (source, target) in enumerate(zip(sources, held))
    ]
    order = (EIN, EOUT, DIN, DOUT, PIX, BRI, VEC)
    for array in order:
        for kind in range(4):
            loads[7 * kind + array].start()
    grads, masters, firsts, seconds = (held[7 * k : 7 * k + 7] for k in range(4))
    next_firsts, next_seconds, news = (results[7 * k : 7 * k + 7] for k in range(3))
    stores = [
        pltpu.make_async_copy(source, target, stored.at[at])
        for at, (source, target) in enumerate(zip(results, targets))
    ]
    for array in order:
        lane = STAT_LANES[array]
        norms = [stats[row : row + 1, :][:, lane : lane + 1] for row in range(2)]
        ratio = learn_rate * norms[0] / norms[1]
        count = masters[array].shape[0]
        if len(masters[array].shape) == 3:
            count = count * masters[array].shape[1]
        decay = 0.0 if array == VEC else decay_matrix

        def body(rows, array=array, ratio=ratio, decay=decay):
            if array == VEC:
                gradient = grads[VEC][:7, : masters[VEC].shape[1]]
            else:
                gradient = grads[array][rows]
            master = state_rows(masters[array], rows)
            next_one, next_two, update = moments(
                gradient,
                state_rows(firsts[array], rows),
                state_rows(seconds[array], rows),
                master,
                decay,
            )
            put_rows(next_firsts[array], rows, next_one)
            put_rows(next_seconds[array], rows, next_two)
            put_rows(news[array], rows, master - ratio * update)

        for kind in range(4):
            loads[7 * kind + array].wait()
        if array == VEC:
            body(slice(None))
        else:
            row_loop(count, state_step(count), body)
        for kind in range(3):
            stores[7 * kind + array].start()
    pairs[...] = stats[:2, :][:, :7]
    loss[...] = stats[2:3, :][:, :1]
    for store in stores:
        store.wait()


def apply_update(reduced, masters, firsts, seconds, stats):
    shapes = [jax.ShapeDtypeStruct(master.shape, f32) for master in masters]
    operands = [*reduced, *masters, *firsts, *seconds]
    in_vmem = pl.BlockSpec(memory_space=pltpu.VMEM)
    anywhere = pl.BlockSpec(memory_space=pl.ANY)
    results = pl.pallas_call(
        apply_kernel,
        out_shape=shapes * 3
        + [jax.ShapeDtypeStruct((1, 1), f32), jax.ShapeDtypeStruct((2, 7), f32)],
        in_specs=[anywhere] * 28 + [in_vmem],
        out_specs=[anywhere] * 21 + [in_vmem] * 2,
        scratch_shapes=[pltpu.VMEM(member.shape, f32) for member in operands]
        + [pltpu.VMEM(master.shape, f32) for master in masters] * 3
        + [pltpu.SemaphoreType.DMA((28,)), pltpu.SemaphoreType.DMA((21,))],
        compiler_params=pltpu.CompilerParams(vmem_limit_bytes=60 * 1024 * 1024),
        name="apply_update",
    )(*operands, stats)
    return results[:7], results[7:14], results[14:21], results[21].reshape(()), results[22]


def sinusoid_table(feature_width, grid_side, patch_count, padded):
    position = np.arange(patch_count)
    quarter = feature_width // 4
    omegas = 1.0 / 10000.0 ** (np.arange(quarter) / quarter)
    parts = []
    for coords in (position % grid_side, position // grid_side):
        angles = coords[:, None] * omegas[None, :]
        parts += [np.sin(angles), np.cos(angles)]
    table = np.concatenate(parts, axis=1).astype(np.float32)
    return jnp.asarray(np.pad(table, ((0, padded - patch_count), (0, 0))))


GROUPS = 4
ENC = dict(step=128, first=0, images=4, block=64, tokens=50, width=768, heads=3, head=64, hidden=768, spans=1)
DEC = dict(step=208, first=768, images=4, block=208, tokens=197, width=512, heads=4, head=32, hidden=512, spans=4)
CLASS_ROW = 49
MASK_ROW = 50


def dot(left, right, dims=((1,), (0,)), precision=None):
    return lax.dot_general(
        left, right, (dims, ((), ())), preferred_element_type=f32, precision=precision
    )


def dot_t(left, right):
    return dot(left, right, ((0,), (0,)))


def dot_nt(left, right):
    return dot(left, right, ((1,), (1,)))


def exact_dot(left, right, dims):
    return dot(left, right, dims, lax.Precision.HIGHEST)


def row_loop(count, step, body):
    @pl.loop(0, count // step)
    def _(k):
        body(pl.ds(pl.multiple_of(k * step, step), step))


def fold(values):
    step, width = values.shape
    return jnp.sum(values.reshape(step // 8, 8, width), axis=0)


def norm_rows(source, gain, shift, unit, inverse, low, step):
    def body(rows):
        values = source[rows]
        centred = values - jnp.mean(values, axis=-1, keepdims=True)
        scale = lax.rsqrt(jnp.mean(centred * centred, axis=-1, keepdims=True) + eps_norm)
        normed = centred * scale
        unit[rows] = normed
        inverse[rows] = scale
        low[rows] = (normed * gain + shift).astype(bf16)

    row_loop(source.shape[0], step, body)


def norm_back_rows(incoming, unit, inverse, gain, result, residual, sums, at, step):
    width = incoming.shape[-1]

    def body(rows):
        given = incoming[rows]
        normed = unit[rows]
        scaled = given * gain
        inner = (
            scaled
            - jnp.mean(scaled, axis=-1, keepdims=True)
            - normed * jnp.mean(scaled * normed, axis=-1, keepdims=True)
        )
        value = inverse[rows] * inner
        if residual is not None:
            value = value + residual[rows]
        sums[at] = sums[at] + fold(given * normed)
        sums[at + 1] = sums[at + 1] + fold(given)
        result[rows] = value

    row_loop(incoming.shape[0], step, body)


def lane_chunks(size):
    return [slice(at, min(at + 128, size)) for at in range(0, size, 128)]


def attend_mask(dims, scores, start):
    if dims["spans"] == 1:
        key = lax.broadcasted_iota(jnp.int32, scores.shape, 0)
        query = lax.broadcasted_iota(jnp.int32, scores.shape, 1) + start
        allowed = ((key // dims["block"]) == (query // dims["block"])) & (
            (key % dims["block"]) < dims["tokens"]
        )
        return jnp.where(allowed, scores, -1e30)
    first = dims["tokens"] // 16 * 16
    tail = scores[first:]
    key = lax.broadcasted_iota(jnp.int32, tail.shape, 0) + first
    return jnp.concatenate([scores[:first], jnp.where(key < dims["tokens"], tail, -1e30)], axis=0)


def layer_forward_rows(dims, stream, w_in, w_out, vectors, saved):
    unit_one, inv_one, low_one, qkv, probs, mixed, unit_two, inv_two, low_two, active, slope, work, low_work, low_more = saved
    count, width = stream.shape
    inner = dims["heads"] * dims["head"]
    span = count // dims["spans"]
    norm_rows(stream, vectors[1:2, :], vectors[2:3, :], unit_one, inv_one, low_one, dims["step"])

    @pl.loop(0, GROUPS)
    def _(t):
        weights = w_in[t, :, : 3 * inner] if inner % 128 == 0 else w_in[t][:, : 3 * inner]

        def body(rows):
            qkv[t, rows] = dot(low_one[rows], weights).astype(bf16)

        body(slice(None))

    yield "projected"
    scale = dims["head"] ** (-0.5)

    @pl.loop(0, GROUPS * dims["spans"])
    def _(k):
        t = k // dims["spans"]
        b = k % dims["spans"]
        rows = pl.ds(pl.multiple_of(b * span, span), span)
        triple = qkv[t, rows]
        query_t = triple[:, :inner].T
        value_t = triple[:, 2 * inner :].T
        heads = range(dims["heads"])
        lanes = [slice(head * dims["head"], (head + 1) * dims["head"]) for head in heads]
        for head in heads:
            key = triple[:, inner : 2 * inner][:, lanes[head]]
            work[head] = dot(key, query_t[lanes[head]])
        for head in heads:
            for columns in lane_chunks(span):
                scores = attend_mask(dims, work[head, :, columns] * scale, columns.start)
                shifted = jnp.exp(scores - jnp.max(scores, axis=0, keepdims=True))
                share = shifted * (1.0 / jnp.sum(shifted, axis=0, keepdims=True))
                probs[k * dims["heads"] + head, :, columns] = share
                low_work[head, :, columns] = share.astype(bf16)
        results = [dot(value_t[lanes[head]], low_work[head]) for head in heads]
        mixed[t, rows] = jnp.concatenate(results, axis=0).T.astype(bf16)

    yield "attended"

    @pl.loop(0, GROUPS)
    def _(t):
        weights = w_out[t, :inner]

        def body(rows):
            stream[rows] = stream[rows] + dot(mixed[t, rows], weights)

        body(slice(None))

    norm_rows(stream, vectors[3:4, :], vectors[4:5, :], unit_two, inv_two, low_two, dims["step"])

    def feed(t):
        up = w_in[t, :, 3 * inner :] if inner % 128 == 0 else w_in[t][:, 3 * inner :]
        down = w_out[t, inner:]
        slope[t] = dot(low_two[...], up)

        def bend(rows):
            hidden = slope[t, rows]
            level = 0.5 + 0.5 * lax.erf(hidden * (0.5**0.5))
            active[t, rows] = (hidden * level).astype(bf16)
            slope[t, rows] = level + hidden * (
                jnp.exp(-0.5 * hidden * hidden) * (0.5 / np.pi) ** 0.5
            )

        row_loop(count, 32, bend)
        stream[...] = stream[...] + dot(active[t], down)

    half = GROUPS // 2 if dims["spans"] == 1 else GROUPS
    pl.loop(0, half)(feed)
    if half < GROUPS:
        yield "halfway"
        pl.loop(half, GROUPS)(feed)


def layer_backward_rows(dims, given, spare, w_in, w_out, vectors, saved, low, flow, grad_in, grad_out, sums):
    unit_one, inv_one, low_one, qkv, probs, mixed, unit_two, inv_two, low_two, active, slope, work, low_work, low_more = saved
    count, width = given.shape
    inner = dims["heads"] * dims["head"]
    span = count // dims["spans"]
    aligned = inner % 128 == 0

    def lower(rows):
        low[rows] = given[rows].astype(bf16)
        spare[rows] = jnp.zeros_like(spare[rows])

    row_loop(count, 32, lower)

    @pl.loop(0, GROUPS)
    def _(t):
        down = w_out[t, inner:]
        up = w_in[t, :, 3 * inner :] if aligned else w_in[t][:, 3 * inner :]
        grad_out[t, inner:] = dot_t(active[t], low[...]).astype(bf16)

        def body(rows):
            flow[rows] = (slope[t, rows] * dot_nt(low[rows], down)).astype(bf16)
            spare[rows] = spare[rows] + dot_nt(flow[rows], up)

        body(slice(None))
        grad_up = dot_t(low_two[...], flow[...]).astype(bf16)
        if aligned:
            grad_in[t, :, 3 * inner :] = grad_up
        else:
            grad_in[t] = jnp.concatenate([jnp.zeros((width, 3 * inner), bf16), grad_up], axis=1)

    norm_back_rows(spare, unit_two, inv_two, vectors[3:4, :], given, given, sums, 3, dims["step"])
    row_loop(count, 32, lower)

    @pl.loop(0, GROUPS)
    def _(t):
        weights = w_out[t, :inner]
        grad_out[t, :inner] = dot_t(mixed[t], low[...]).astype(bf16)

        def body(rows):
            mixed[t, rows] = dot_nt(low[rows], weights).astype(bf16)

        body(slice(None))

    scale = dims["head"] ** (-0.5)

    @pl.loop(0, GROUPS * dims["spans"])
    def _(k):
        t = k // dims["spans"]
        b = k % dims["spans"]
        rows = pl.ds(pl.multiple_of(b * span, span), span)
        triple = qkv[t, rows]
        back = mixed[t, rows]
        key_t = triple[:, inner : 2 * inner].T
        back_t = back.T
        heads = range(dims["heads"])
        lanes = [slice(head * dims["head"], (head + 1) * dims["head"]) for head in heads]
        for head in heads:
            work[head] = dot(triple[:, 2 * inner :][:, lanes[head]], back_t[lanes[head]])
        for head in heads:
            for columns in lane_chunks(span):
                share = probs[k * dims["heads"] + head, :, columns]
                grad_p = work[head, :, columns]
                grad_s = share * (grad_p - jnp.sum(share * grad_p, axis=0, keepdims=True))
                low_work[head, :, columns] = grad_s.astype(bf16)
                low_more[head, :, columns] = share.astype(bf16)
        parts = ([], [], [])
        for head in heads:
            parts[0].append(dot(key_t[lanes[head]], low_work[head]) * scale)
            parts[1].append(dot(low_work[head], triple[:, :inner][:, lanes[head]]) * scale)
            parts[2].append(dot(low_more[head], back[:, lanes[head]]))
        grad_query = jnp.concatenate(parts[0], axis=0).T
        qkv[t, rows] = jnp.concatenate([grad_query] + parts[1] + parts[2], axis=1).astype(bf16)

    @pl.loop(0, GROUPS)
    def _(t):
        weights = w_in[t, :, : 3 * inner] if aligned else w_in[t][:, : 3 * inner]
        grad_triple = dot_t(low_one[...], qkv[t]).astype(bf16)
        if aligned:
            grad_in[t, :, : 3 * inner] = grad_triple
        else:
            grad_in[t] = jnp.concatenate([grad_triple, grad_in[t][:, 3 * inner :]], axis=1)

        def body(rows):
            spare[rows] = spare[rows] + dot_nt(qkv[t, rows], weights)

        body(slice(None))

    norm_back_rows(spare, unit_one, inv_one, vectors[1:2, :], given, given, sums, 1, dims["step"])


def saved_shapes(dims):
    count = dims["images"] * dims["block"]
    width, inner = dims["width"], dims["heads"] * dims["head"]
    span = count // dims["spans"]
    return [
        ((count, width), f32),
        ((count, 1), f32),
        ((count, width), bf16),
        ((GROUPS, count, 3 * inner), bf16),
        ((GROUPS * dims["spans"] * dims["heads"], span, span), f32),
        ((GROUPS, count, inner), bf16),
        ((count, width), f32),
        ((count, 1), f32),
        ((count, width), bf16),
        ((GROUPS, count, dims["hidden"]), bf16),
        ((GROUPS, count, dims["hidden"]), f32),
    ]


def work_shapes(dims):
    span = dims["images"] * dims["block"] // dims["spans"]
    shape = (dims["heads"], span, span)
    return [(shape, f32), (shape, bf16), (shape, bf16)]


def token_gain(vectors, dims):
    return vectors.at[:, pl.ds(dims["first"], dims["width"])]


def decoder_kernel(*refs):
    projected, codes, images, table, w_in, w_out, pixel_w, vectors_all = refs[:8]
    grad_in, grad_out, grad_head, grad_projected, vec_out = refs[8:13]
    stream, given, unit, inverse, low, flow, sums, loss, head, pixels_here, head_sum, loaded = refs[13:25]
    saved = refs[25:]
    dims = DEC
    vectors = token_gain(vectors_all, dims)
    count, width = stream.shape
    block = dims["block"]
    copies = [pltpu.make_async_copy(pixel_w.at[pl.ds(PATCH_DIM, width)], head, loaded.at[0])]
    for b in range(dims["images"]):
        copies.append(
            pltpu.make_async_copy(
                images.at[b], pixels_here.at[b], loaded.at[1 + b]
            )
        )
    for copy in copies:
        copy.start()
    sums[...] = jnp.zeros_like(sums)
    loss[...] = jnp.zeros_like(loss)

    def placer(b):
        return (
            lax.broadcasted_iota(jnp.int32, (64, block), 0) == codes[b][:1, :block]
        ).astype(f32)

    def block_rows(b):
        return pl.ds(pl.multiple_of(b * block, block), block)

    @pl.loop(0, dims["images"])
    def _(b):
        at = lax.broadcasted_iota(jnp.int32, (64, width), 0)
        source = jnp.where(at == MASK_ROW, vectors[0:1, :], projected[b])
        source = jnp.where(at > MASK_ROW, 0.0, source)
        stream[block_rows(b)] = exact_dot(placer(b), source, ((0,), (0,))) + table[...]

    for _ in layer_forward_rows(dims, stream, w_in, w_out, vectors, saved):
        pass
    norm_rows(stream, vectors[5:6, :], vectors[6:7, :], unit, inverse, low, dims["step"])
    for copy in copies:
        copy.wait()
    head_sum[...] = jnp.zeros_like(head_sum)
    pixels_wide = pixels_here.shape[-1]
    counted = vectors_all[7:8, :]
    patch_total = jnp.sum(counted, axis=1, keepdims=True) / (counted.shape[1] // 8)

    @pl.loop(0, dims["images"])
    def _(b):
        rows = block_rows(b)
        predicted = dot(low[rows], head[...])
        pixels = jnp.concatenate(
            [pixels_here[b], jnp.zeros((block - IMAGE_PATCHES, pixels_wide), bf16)], axis=0
        ).astype(f32)
        centred = pixels - jnp.mean(pixels, axis=-1, keepdims=True)
        variance = jnp.sum(centred * centred, axis=-1, keepdims=True) / (pixels_wide - 1)
        errors = predicted - centred * lax.rsqrt(variance + eps_norm)
        at = lax.broadcasted_iota(jnp.int32, (64, 128), 0)
        share = codes[b][2:3, :128].astype(f32) / patch_total
        spread = jnp.where(at == MASK_ROW, share, 0.0)
        weight = exact_dot(placer(b), spread, ((0,), (0,)))[:, :1]
        loss[...] = loss[...] + fold(errors * errors * weight)
        grad_low = (errors * (2.0 / pixels_wide) * weight).astype(bf16)
        head_sum[...] = head_sum[...] + dot_t(low[rows], grad_low)
        given[rows] = dot_nt(grad_low, head[...])

    grad_head[...] = head_sum[...].astype(bf16)
    norm_back_rows(given, unit, inverse, vectors[5:6, :], given, None, sums, 5, dims["step"])
    layer_backward_rows(
        dims, given, stream, w_in, w_out, vectors, saved, low, flow, grad_in, grad_out, sums
    )

    @pl.loop(0, dims["images"])
    def _(b):
        back = exact_dot(placer(b), given[block_rows(b)], ((1,), (0,)))
        at = lax.broadcasted_iota(jnp.int32, (64, width), 0)
        grad_projected[b] = jnp.where(at < MASK_ROW, back, 0.0).astype(bf16)
        sums[0] = sums[0] + fold(jnp.where(at == MASK_ROW, back, 0.0))

    for row in range(7):
        vec_out[row : row + 1, :] = jnp.sum(sums[row], axis=0, keepdims=True)
    total = jnp.sum(jnp.sum(loss[...], axis=0, keepdims=True), axis=1, keepdims=True)
    vec_out[7:8, :] = jnp.broadcast_to(total / pixels_wide, (1, width))


def decoder_step(projected, codes, images, table, w_in, w_out, pixel_w, vectors):
    dims = DEC
    count, width = dims["images"] * dims["block"], dims["width"]
    wide = images.shape[-1]
    outs = [
        jax.ShapeDtypeStruct(w_in.shape, bf16),
        jax.ShapeDtypeStruct(w_out.shape, bf16),
        jax.ShapeDtypeStruct((width, wide), bf16),
        jax.ShapeDtypeStruct(projected.shape, bf16),
        jax.ShapeDtypeStruct((8, width), f32),
    ]
    scratch = [
        ((count, width), f32),
        ((count, width), f32),
        ((count, width), f32),
        ((count, 1), f32),
        ((count, width), bf16),
        ((count, dims["hidden"]), bf16),
        ((7, 8, width), f32),
        ((8, wide), f32),
        ((width, wide), bf16),
        ((dims["images"],) + images.shape[1:], bf16),
        ((width, wide), f32),
        None,
    ]
    scratch += saved_shapes(dims) + work_shapes(dims)
    in_vmem = pl.BlockSpec(memory_space=pltpu.VMEM)
    anywhere = pl.BlockSpec(memory_space=pl.ANY)
    return pl.pallas_call(
        decoder_kernel,
        out_shape=outs,
        in_specs=[in_vmem, in_vmem, anywhere, in_vmem, in_vmem, in_vmem, anywhere, in_vmem],
        scratch_shapes=[
            pltpu.SemaphoreType.DMA((5,)) if shape is None else pltpu.VMEM(*shape)
            for shape in scratch
        ],
        compiler_params=pltpu.CompilerParams(vmem_limit_bytes=62 * 1024 * 1024),
        name="decoder_step",
    )(projected, codes, images, table, w_in, w_out, pixel_w, vectors)


def encode_kernel(ring, *refs):
    dims = ENC
    images, codes, table = refs[:3]
    refs = refs[3:]
    group = lax.axis_index("tensor")
    if ring:
        masters, count_row, refs = refs[:7], refs[7], refs[8:]
        wholes, vectors_all, projected, kept_state = refs[:7], refs[7], refs[8], refs[9:24]
        refs = refs[24:]
        parts, send, recv, local, vec_parts = refs[:7], *refs[7:11]
        raw = dict(zip((PIX, EOUT, BRI), refs[11:14]))
        refs = refs[14:]
    else:
        wholes, vectors_all = refs[:4], refs[4]
        projected, kept_state = refs[5], refs[6:21]
        refs = refs[21:]
        wholes = dict(zip((PIX, EIN, EOUT, BRI), wholes))
    loaded, flushed = refs[:2]
    pixels_here, stream, w_in, w_out, embed, bridge = refs[2:8]
    retained, unit, inverse, low = refs[8:12]
    saved = refs[12:23]
    work = refs[23:]
    held = (retained, unit, inverse, low) + tuple(saved)
    vectors = token_gain(vectors_all, dims)
    count, width = stream.shape
    block = dims["block"]

    picture_copies = [
        pltpu.make_async_copy(
            images.at[b], pixels_here.at[b], loaded.at[4 + b]
        )
        for b in range(dims["images"])
    ]
    for copy in picture_copies:
        copy.start()

    def load(slot, array, target):
        if not ring:
            source = wholes[array]
            if array == PIX:
                source = source.at[pl.ds(0, PATCH_DIM)]
            pltpu.make_async_copy(source, target, loaded.at[slot]).start()
            return pltpu.make_async_copy(source, target, loaded.at[slot])
        if array != EIN:
            pltpu.make_async_copy(wholes[array], raw[array], loaded.at[slot]).start()
            return pltpu.make_async_copy(wholes[array], raw[array], loaded.at[slot])
        rows = wholes[array].shape[4]

        @pl.loop(0, 32)
        def _(k):
            pltpu.make_async_copy(
                wholes[array].at[k // 16, (k // 8) % 2, (k // 2) % 4, k % 2],
                target.at[k // 8, pl.ds(pl.multiple_of((k % 8) * rows, rows), rows)],
                loaded.at[slot],
            ).start()

        return pltpu.make_async_copy(target, target, loaded.at[slot])

    def assemble(array, target):
        if ring and array in SHARED:
            count = -(-target.shape[0] // raw[array].shape[4])
            pieces = [
                raw[array][k // 8, (k // 4) % 2, (k // 2) % 2, k % 2] for k in range(count)
            ]
            target[...] = jnp.concatenate(pieces, axis=0)[: target.shape[0]]
        elif ring:

            @pl.loop(0, GROUPS)
            def _(t):
                pieces = [raw[array][t // 2, t % 2, k // 2, k % 2] for k in range(8)]
                target[t] = jnp.concatenate(pieces, axis=0)

    flushes = []

    def flush(*members):
        for member in members:
            copy = pltpu.make_async_copy(held[member], kept_state[member], flushed.at[member])
            copy.start()
            flushes.append(copy)

    if ring:
        for array in range(6):
            if array in SHARED:
                rows = masters[array].shape[0] // 4
                rows = pl.ds(pl.multiple_of(group * rows, 8), rows)
                parts[array][...] = masters[array][rows].astype(bf16)
            else:
                parts[array][...] = state_rows(masters[array], slice(None)).astype(bf16)
        columns = masters[VEC].shape[1]
        parts[VEC][...] = jnp.zeros_like(parts[VEC])
        parts[VEC][:7, :columns] = masters[VEC][...].astype(bf16).astype(f32)
        parts[VEC][7:8, :] = count_row[...]
        ticks = gather_ticks(parts, wholes, send, recv, local)

    done = [-1]

    def until(tick):
        while ring and done[0] < tick:
            next(ticks)
            done[0] += 1

    at_embed, at_in, at_out = (
        last_step(GATHER_STEPS, array) + DEPTH for array in (PIX, EIN, EOUT)
    )
    at_end = len(GATHER_STEPS) - 1 + DEPTH
    until(at_embed)
    embed_copy = load(0, PIX, embed)
    if ring:
        vec_copy = pltpu.make_async_copy(wholes[VEC], vec_parts, loaded.at[1])
        vec_copy.start()
        vec_copy.wait()
        vectors_all[...] = jnp.concatenate(
            [vec_parts[0, 0, k // 2, k % 2][:, :columns] for k in range(8)], axis=1
        )
    for copy in picture_copies:
        copy.wait()
    embed_copy.wait()
    assemble(PIX, embed)

    @pl.loop(0, dims["images"])
    def _(b):
        rows = pl.ds(pl.multiple_of(b * block, block), block)
        choice = (
            lax.broadcasted_iota(jnp.int32, (IMAGE_PATCHES, block), 0) == codes[b][1:2, :block]
        )
        retained[rows] = dot_t(choice.astype(bf16), pixels_here[b]).astype(bf16)
        places = exact_dot(choice.astype(f32), table[...], ((0,), (0,)))
        at = lax.broadcasted_iota(jnp.int32, (block, width), 0)
        start = dot(retained[rows], embed[...]) + places
        stream[rows] = jnp.where(at == CLASS_ROW, vectors[0:1, :], start)

    flush(0)
    until(at_in)
    load(2, EIN, w_in).wait()
    layer = layer_forward_rows(dims, stream, w_in, w_out, vectors, saved + work)
    next(layer)
    until(at_in + 1)
    next(layer)
    flush(4, 5, 6, 7, 8, 9)
    until(at_out)
    bridge_copy = load(1, BRI, bridge)
    load(3, EOUT, w_out).wait()
    assemble(EOUT, w_out)
    next(layer)
    flush(10, 11, 12)
    until(at_out + 1)
    for _ in layer:
        pass
    flush(13, 14)
    until(at_out + 2)
    norm_rows(stream, vectors[5:6, :], vectors[6:7, :], unit, inverse, low, dims["step"])
    flush(1, 2, 3)
    bridge_copy.wait()
    assemble(BRI, bridge)

    @pl.loop(0, dims["images"])
    def _(b):
        rows = pl.ds(pl.multiple_of(b * block, block), block)
        projected[b] = dot(low[rows], bridge[...])

    until(at_end + 1)
    for copy in flushes:
        copy.wait()


def encode(images, codes, table, weights, count_row=None, vectors=None):
    dims = ENC
    ring = vectors is None
    count, width = dims["images"] * dims["block"], dims["width"]
    bridge_wide = weights[BRI].shape[-1]
    in_vmem = pl.BlockSpec(memory_space=pltpu.VMEM)
    anywhere = pl.BlockSpec(memory_space=pl.ANY)
    kept_shapes = [
        ((count, images.shape[-1]), bf16),
        ((count, width), f32),
        ((count, 1), f32),
        ((count, width), bf16),
    ] + saved_shapes(dims)
    outs = [((dims["images"], dims["block"], bridge_wide), f32)] + kept_shapes
    out_specs = [in_vmem] + [anywhere] * len(kept_shapes)
    in_specs = [anywhere, in_vmem, in_vmem]
    scratch = []
    if ring:
        shapes = []
        for array in range(6):
            rows, wide = weights[array].size // weights[array].shape[-1], weights[array].shape[-1]
            shapes.append((rows // 4 if array in SHARED else rows, wide))
        shapes.append((8, 256))
        types = [bf16] * 6 + [f32]
        operands = [images, codes, table, *weights, count_row]
        in_specs += [in_vmem] * 8
        gathered = [(whole_shape(k, shape), types[k]) for k, shape in enumerate(shapes)]
        outs = gathered + [((8, shapes_total(weights[VEC])), f32)] + outs
        out_specs = [anywhere] * 7 + [in_vmem] + out_specs
        units = sum(len(step) for step in GATHER_STEPS)
        scratch += [pltpu.VMEM(shape, kind) for shape, kind in zip(shapes, types)]
        scratch += [
            pltpu.SemaphoreType.DMA((units, 6)),
            pltpu.SemaphoreType.DMA((units, 6)),
            pltpu.SemaphoreType.DMA((7,)),
            pltpu.VMEM(whole_shape(VEC, shapes[VEC]), f32),
        ]
        scratch += [
            pltpu.VMEM(whole_shape(array, shapes[array]), bf16) for array in (PIX, EOUT, BRI)
        ]
        params = dict(collective_id=0, has_side_effects=True)
        w_shapes = [
            (GROUPS, 8 * shapes[EIN][0], shapes[EIN][1]),
            (GROUPS, 8 * shapes[EOUT][0], shapes[EOUT][1]),
        ]
    else:
        operands = [images, codes, table] + [weights[k] for k in (PIX, EIN, EOUT, BRI)] + [vectors]
        in_specs += [anywhere] * 4 + [in_vmem]
        params = {}
        w_shapes = [weights[EIN].shape, weights[EOUT].shape]
    scratch += [pltpu.SemaphoreType.DMA((8,)), pltpu.SemaphoreType.DMA((15,))]
    buffers = [
        ((dims["images"],) + images.shape[1:], bf16),
        ((count, width), f32),
        (w_shapes[0], bf16),
        (w_shapes[1], bf16),
        ((PATCH_DIM, width), bf16),
        ((width, bridge_wide), bf16),
    ]
    buffers += kept_shapes + work_shapes(dims)
    scratch += [pltpu.VMEM(*buffer) for buffer in buffers]
    return pl.pallas_call(
        functools.partial(encode_kernel, ring),
        out_shape=[jax.ShapeDtypeStruct(shape, kind) for shape, kind in outs],
        in_specs=in_specs,
        out_specs=out_specs,
        scratch_shapes=scratch,
        compiler_params=pltpu.CompilerParams(vmem_limit_bytes=62 * 1024 * 1024, **params),
        name="gather_encode" if ring else "encode",
    )(*operands)


def shapes_total(vector_shard):
    return 8 * vector_shard.shape[1]


def encoder_backward_kernel(*refs):
    grad_projected, retained, unit, inverse, low_end = refs[:5]
    saved = list(refs[5:16])
    w_in, w_out, bridge, vectors_all, grad_head, dec_sums = refs[16:22]
    grad_in, grad_out, grad_bridge, grad_pixel, packed = refs[22:27]
    given, spare, low, flow, sums, qkv, mixed, vec_all = refs[27:35]
    dims = ENC
    vectors = token_gain(vectors_all, dims)
    count, width = given.shape
    block = dims["block"]
    sums[...] = jnp.zeros_like(sums)
    qkv[...] = saved[3][...]
    mixed[...] = saved[5][...]
    saved[3], saved[5] = qkv, mixed
    saved += refs[35:]

    flat = grad_projected[...].reshape(count, grad_projected.shape[-1])
    grad_bridge[...] = dot_t(low_end[...], flat).astype(bf16)
    given[...] = dot_nt(flat, bridge[...])
    norm_back_rows(given, unit, inverse, vectors[5:6, :], given, None, sums, 5, dims["step"])
    layer_backward_rows(
        dims, given, spare, w_in, w_out, vectors, saved, low, flow, grad_in, grad_out, sums
    )
    grad_pixel[:PATCH_DIM] = dot_t(retained[...], given[...].astype(bf16)).astype(bf16)
    grad_pixel[PATCH_DIM:] = grad_head[...]

    def tokens(rows):
        at = lax.broadcasted_iota(jnp.int32, (block, width), 0)
        sums[0] = sums[0] + fold(jnp.where(at == CLASS_ROW, given[rows], 0.0))

    row_loop(count, block, tokens)
    for row in range(7):
        vec_all[row : row + 1, :width] = jnp.sum(sums[row], axis=0, keepdims=True)
    vec_all[7:8, :width] = jnp.zeros((1, width), f32)
    vec_all[:, width:] = dec_sums[...]
    columns = vec_all.shape[1] // 8
    packed[...] = jnp.zeros_like(packed)
    for k in range(8):
        packed[k, :, :columns] = vec_all[:, k * columns : (k + 1) * columns]


def encoder_backward(grad_projected, kept_state, w_in, w_out, bridge, vectors, grad_head, dec_sums):
    dims = ENC
    count, width = dims["images"] * dims["block"], dims["width"]
    shapes = saved_shapes(dims)
    pixels_wide = kept_state[0].shape[1]
    outs = [
        jax.ShapeDtypeStruct(w_in.shape, bf16),
        jax.ShapeDtypeStruct(w_out.shape, bf16),
        jax.ShapeDtypeStruct(bridge.shape, bf16),
        jax.ShapeDtypeStruct((pixels_wide + grad_head.shape[0], width), bf16),
        jax.ShapeDtypeStruct((8, 8, 256), f32),
    ]
    scratch = [
        ((count, width), f32),
        ((count, width), f32),
        ((count, width), bf16),
        ((count, dims["hidden"]), bf16),
        ((7, 8, width), f32),
        shapes[3],
        shapes[5],
        (vectors.shape, f32),
    ] + work_shapes(dims)
    return pl.pallas_call(
        encoder_backward_kernel,
        out_shape=outs,
        scratch_shapes=[pltpu.VMEM(shape, dtype) for shape, dtype in scratch],
        compiler_params=pltpu.CompilerParams(vmem_limit_bytes=62 * 1024 * 1024),
        name="encoder_backward",
    )(grad_projected, *kept_state, w_in, w_out, bridge, vectors, grad_head, dec_sums)


def gather_grouped(part, groups):
    whole = lax.all_gather(part, GROUPED, axis=0, tiled=True)
    return whole.reshape(groups, -1, whole.shape[-1])


def scatter_grouped(gradient):
    flat = gradient.astype(f32).reshape(-1, gradient.shape[-1])
    return lax.psum_scatter(flat, GROUPED, scatter_dimension=0, tiled=True)


def ringed(tensor_count):
    return tensor_count == 4 and lax.axis_size("dp") == 8


def plain_gather(masters, counted):
    groups = lax.axis_size("tensor")
    wholes = {}
    for array, k in ((EIN, 0), (EOUT, 1), (DIN, 2), (DOUT, 3)):
        flat = masters[k].reshape(-1, masters[k].shape[-1]).astype(bf16)
        wholes[array] = gather_grouped(flat, groups)
    for array, k in ((PIX, 4), (BRI, 5)):
        wholes[array] = lax.all_gather(masters[k].astype(bf16), "dp", axis=0, tiled=True)
    low = masters[6].astype(bf16).astype(f32)
    vectors = lax.all_gather(low, "dp", axis=1, tiled=True)
    eighth = jnp.broadcast_to(lax.psum(counted, "dp") / 8, (1, vectors.shape[1]))
    return wholes, jnp.concatenate([vectors, eighth], axis=0)


def ring_finish(gradients, masters, firsts, seconds):
    grouped, grad_pixel, grad_bridge, packed = gradients
    tensor_count = lax.axis_size("tensor")
    order = (4, 0, 1, 5, 2, 3, 6)
    sources = (grad_pixel, grouped[0], grouped[1], grad_bridge, grouped[2], grouped[3])
    operands = []
    for array, source in enumerate(sources):
        master = masters[order[array]]
        rows, wide = master.size // master.shape[-1], master.shape[-1]
        if array in SHARED:
            rows = rows // tensor_count
        operands.append(source.reshape(whole_shape(array, (rows, wide))))
    operands.append(packed)
    states = [[members[k] for k in order] for members in (masters, firsts, seconds)]
    *sums, stats = scatter_gradients(operands, *states)
    for array in SHARED:
        sums[array] = sums[array].reshape(-1, sums[array].shape[-1])
    *results, loss_value, pairs = apply_update(sums, *states, stats)
    place_of = {k: at for at, k in enumerate(order)}
    results = [[members[place_of[k]] for k in range(7)] for members in results]
    return (loss_value, pairs, *results[0], *results[1], *results[2])


def plain_finish(gradients, masters, firsts, seconds):
    grouped, grad_pixel, grad_bridge, packed = gradients
    tensor_count = lax.axis_size("tensor")
    columns = masters[6].shape[1]

    def scatter_shared(gradient):
        part = lax.psum_scatter(gradient.astype(f32), EVERY, scatter_dimension=0, tiled=True)
        return lax.all_gather(part, "tensor", axis=0, tiled=True)

    reduced = [scatter_grouped(gradient) for gradient in grouped]
    reduced += [scatter_shared(grad_pixel), scatter_shared(grad_bridge)]
    whole = packed.shape[0] * (ENCODER_WIDTH + D_D) // 8
    packed = packed[:, :, : whole // packed.shape[0]].transpose(1, 0, 2).reshape(8, -1)
    vector_sum = lax.psum(packed, EVERY)
    own = lax.dynamic_slice_in_dim(
        vector_sum[:7], lax.axis_index("dp") * columns, columns, axis=1
    )
    reduced = [gradient.reshape(master.shape) for gradient, master in zip(reduced + [own], masters)]
    decays = (decay_matrix,) * 6 + (0.0,)
    share_counts = (1.0,) * 4 + (float(tensor_count),) * 3
    steps = [moments(*member) for member in zip(reduced, firsts, seconds, masters, decays)]
    new_firsts, new_seconds, updates = zip(*steps)

    def squares(members):
        return jnp.stack(
            [jnp.sum(member * member) / count for member, count in zip(members, share_counts)]
        )

    weight_norm, update_norm = map(
        jnp.sqrt, lax.psum((squares(masters), squares(updates)), EVERY)
    )
    ratio = learn_rate * weight_norm / update_norm
    news = [
        master - ratio[position] * update
        for position, (master, update) in enumerate(zip(masters, updates))
    ]
    return (vector_sum[7, -1], jnp.stack([weight_norm, update_norm]), *new_firsts, *new_seconds, *news)


def shards(
    images,
    keep_index,
    unshuffle,
    masked,
    image_valid,
    *state,
):
    masters, firsts, seconds = state[:7], state[7:14], state[14:21]
    tensor_count = lax.axis_size("tensor")
    tensor_at = lax.axis_index("tensor")
    counted = jnp.sum(masked.astype(f32) * image_valid.astype(f32)[:, None])
    image_count = images.shape[0] // tensor_count
    lanes = 256
    codes = jnp.pad(
        jnp.where(masked == 1, MASK_ROW, unshuffle),
        ((0, 0), (0, lanes - IMAGE_PATCHES)),
        constant_values=-1,
    )
    codes = jnp.where(jnp.arange(lanes) == IMAGE_PATCHES, CLASS_ROW, codes)
    kept = jnp.pad(keep_index, ((0, 0), (0, lanes - KEEP)), constant_values=-1)
    valid = jnp.broadcast_to(image_valid[:, None], codes.shape)
    codes = jnp.stack([codes, kept, valid], axis=1)
    images = lax.dynamic_slice_in_dim(images, tensor_at * image_count, image_count, axis=0)
    codes = lax.dynamic_slice_in_dim(codes, tensor_at * image_count, image_count, axis=0)
    enc_table = sinusoid_table(ENCODER_WIDTH, GRID_PATCHES, IMAGE_PATCHES, IMAGE_PATCHES)
    dec_table = sinusoid_table(D_D, GRID_PATCHES, IMAGE_PATCHES, DEC["block"])
    if ringed(tensor_count):
        order = (4, 0, 1, 5, 2, 3, 6)
        results = encode(
            images,
            codes,
            enc_table,
            [masters[k] for k in order],
            jnp.broadcast_to(counted, (1, lanes)),
        )
        wholes, vectors, projected, enc_state = results[:7], results[7], results[8], results[9:]
        wholes = [
            whole.reshape(-1, whole.shape[-1])
            if array in SHARED
            else whole.reshape(tensor_count, -1, whole.shape[-1])
            for array, whole in enumerate(wholes)
        ]
    else:
        wholes, vectors = plain_gather(masters, counted)
        projected, *enc_state = encode(images, codes, enc_table, wholes, vectors=vectors)
    grad_dec_in, grad_dec_out, grad_head, grad_projected, dec_sums = decoder_step(
        projected, codes, images, dec_table, wholes[DIN], wholes[DOUT], wholes[PIX], vectors
    )
    grad_enc_in, grad_enc_out, grad_bridge, grad_pixel, packed = encoder_backward(
        grad_projected,
        enc_state,
        wholes[EIN],
        wholes[EOUT],
        wholes[BRI],
        vectors,
        grad_head,
        dec_sums,
    )
    finish = ring_finish if ringed(tensor_count) else plain_finish
    return finish(
        ([grad_enc_in, grad_enc_out, grad_dec_in, grad_dec_out], grad_pixel, grad_bridge, packed),
        masters,
        firsts,
        seconds,
    )


def solution(mesh):
    state_specs = (
        P("dp", "tensor", None),
        P("tensor", "dp", None),
        P("dp", "tensor", None),
        P("tensor", "dp", None),
        P("dp", None),
        P("dp", None),
        P(None, "dp"),
    )
    in_specs = (
        P("dp", None, None),
        P("dp", None),
        P("dp", None),
        P("dp", None),
        P("dp"),
    ) + state_specs * 3
    out_specs = (P(), P()) + state_specs * 3
    return jax.shard_map(shards, mesh=mesh, in_specs=in_specs, out_specs=out_specs, check_vma=False)
```

```python
import functools

import jax
import jax.numpy as jnp
from jax import lax
from jax.experimental import pallas as pl
from jax.experimental.pallas import tpu as pltpu
from jax.sharding import PartitionSpec as P
import numpy as np

ENCODER_WIDTH = 768
H_E = 12
HD_E = 64
D_D = 512
H_D = 16
HD_D = 32
PATCH_DIM = 768
GRID_PATCHES = 14
IMAGE_PATCHES = 196
KEEP = 49

eps_norm = 1e-06
beta_one = 0.9
beta_two = 0.999
step_count = 7.0
learn_rate = 0.3
decay_matrix = 0.05
eps_moment = 1e-06
f32 = jnp.float32
bf16 = jnp.bfloat16
EVERY = ("dp", "tensor")
GROUPED = ("tensor", "dp")


MESH_ID = pl.DeviceIdType.MESH
PIX, EIN, EOUT, BRI, DIN, DOUT, VEC = range(7)


def place():
    dp_at = lax.axis_index("dp")
    group = lax.axis_index("tensor")
    z, x = lax.div(dp_at, 2), lax.rem(dp_at, 2)
    y, c = lax.div(group, 2), lax.rem(group, 2)
    return z, x, y, c


def device(z, x, y, c):
    return (z * 2 + x, y * 2 + c)


def flip(z, m):
    low = lax.rem(z, 2)
    high = lax.div(z, 2)
    if m % 2:
        low = 1 - low
    if m // 2:
        high = 1 - high
    return high * 2 + low


def greet(z, x, y, c):
    barrier = pltpu.get_barrier_semaphore()
    peers = [device(flip(z, m), x, y, c) for m in (1, 2, 3)]
    for m in range(1, 8):
        peers.append(
            device(
                z,
                1 - x if m // 4 else x,
                1 - y if (m // 2) % 2 else y,
                1 - c if m % 2 else c,
            )
        )
    for peer in peers:
        pl.semaphore_signal(barrier, inc=1, device_id=peer, device_id_type=MESH_ID)
    pl.semaphore_wait(barrier, len(peers))


SHARED = (PIX, BRI)


def spot(array, y, c, z, x):
    return (z, x, y, c) if array in SHARED else (y, c, z, x)


def half_spot(array, y, z, x):
    return (z, x, y) if array in SHARED else (y, z, x)


def whole_shape(array, part):
    return ((4, 2, 2, 2) if array in SHARED else (2, 2, 4, 2)) + part


GATHER_STEPS = (
    ((VEC, 0, 8, 0), (PIX, 0, 24, 0), (PIX, 24, 16, 1)),
    ((EIN, 0, 16, 0), (EIN, 16, 16, 1)),
    ((EIN, 32, 16, 0), (EIN, 48, 16, 1)),
    ((EIN, 64, 16, 0), (EIN, 80, 16, 1)),
    ((EOUT, 0, 24, 0), (EOUT, 24, 24, 1)),
    ((EOUT, 48, 24, 0), (EOUT, 72, 24, 1)),
    ((EOUT, 96, 8, 0), (EOUT, 104, 16, 1), (BRI, 0, 16, 0), (BRI, 16, 8, 1)),
    ((DIN, 0, 16, 0), (DIN, 16, 16, 1)),
    ((DIN, 32, 16, 0), (DIN, 48, 16, 1)),
    ((DOUT, 0, 16, 0), (DOUT, 16, 32, 1)),
    ((DOUT, 48, 16, 0), (DOUT, 64, 16, 1)),
)
DEPTH = 4


def last_step(steps, array):
    return max(at for at, step in enumerate(steps) for unit in step if unit[0] == array)


def gather_ticks(parts, outs, send, recv, local):
    count = 7
    z, x, y, c = place()
    units = []
    for at, step in enumerate(GATHER_STEPS):
        for unit in step:
            units.append((at,) + unit)
    copies = {}

    def rows(array, region, first, size):
        ref = outs[array]
        return ref.at[region + (pl.ds(first, size),)]

    def plan(number, stage):
        at, array, first, size, turn = units[number]
        every = slice(None)
        if stage < 3:
            src = parts[array].at[pl.ds(first, size)]
            dst = rows(array, spot(array, y, c, z, x), first, size)
            peer = device(flip(z, stage + 1), x, y, c)
        else:
            if stage == 3:
                region = spot(array, y, c, every, x)
                peer = device(z, x, 1 - y, c) if turn == 0 else device(z, 1 - x, y, c)
            elif stage == 4 and turn == 0:
                region = spot(array, every, c, every, x)
                peer = device(z, 1 - x, y, c)
            elif stage == 4:
                region = spot(array, y, c, every, every)
                peer = device(z, x, 1 - y, c)
            else:
                region = spot(array, every, c, every, every)
                peer = device(z, x, y, 1 - c)
            src = dst = rows(array, region, first, size)
        return pltpu.make_async_remote_copy(
            src_ref=src,
            dst_ref=dst,
            send_sem=send.at[number, stage],
            recv_sem=recv.at[number, stage],
            device_id=peer,
            device_id_type=MESH_ID,
        )

    def start(number, stage):
        copies[number, stage] = plan(number, stage)
        copies[number, stage].start()

    own = []
    for array in range(count):
        own.append(
            pltpu.make_async_copy(parts[array], outs[array].at[spot(array, y, c, z, x)], local.at[array])
        )
        own[-1].start()
    greet(z, x, y, c)
    steps = len(GATHER_STEPS)
    waited = set()
    for tick in range(steps + 4):
        for number, unit in enumerate(units):
            if unit[0] == tick:
                for stage in range(3):
                    start(number, stage)
        for number, unit in enumerate(units):
            if unit[0] == tick - 1:
                if unit[1] not in waited:
                    waited.add(unit[1])
                    own[unit[1]].wait()
                for stage in range(3):
                    copies[number, stage].wait_recv()
                start(number, 3)
        for back in (2, 3):
            for number, unit in enumerate(units):
                if unit[0] == tick - back:
                    copies[number, back + 1].wait_recv()
                    start(number, back + 2)
        for number, unit in enumerate(units):
            if unit[0] == tick - 4:
                copies[number, 5].wait_recv()
        if tick < steps + 3:
            yield tick
    for key in copies:
        copies[key].wait_send()
    yield steps + 3
    yield None


SCATTER_STEPS = (
    ((BRI, 0, 8, 0), (BRI, 8, 16, 1)),
    ((PIX, 0, 24, 0), (PIX, 24, 16, 1)),
    ((EIN, 0, 16, 0), (EIN, 16, 16, 1)),
    ((EIN, 32, 16, 0), (EIN, 48, 16, 1)),
    ((EIN, 64, 16, 0), (EIN, 80, 16, 1)),
    ((EOUT, 0, 24, 0), (EOUT, 24, 24, 1)),
    ((EOUT, 48, 24, 0), (EOUT, 72, 24, 1)),
    ((EOUT, 96, 8, 0), (EOUT, 104, 16, 1)),
    ((DIN, 0, 16, 0), (DIN, 16, 16, 1)),
    ((DIN, 32, 16, 0), (DIN, 48, 16, 1)),
    ((DOUT, 0, 24, 0), (DOUT, 24, 24, 1)),
    ((DOUT, 48, 16, 0), (DOUT, 64, 16, 1)),
)


STAT_LANES = {EIN: 0, EOUT: 1, DIN: 2, DOUT: 3, PIX: 4, BRI: 5, VEC: 6}


def state_rows(ref, rows):
    if len(ref.shape) == 2:
        return ref[rows]
    return ref[rows, 0, :] if ref.shape[1] == 1 else ref[0, rows, :]


def put_rows(ref, rows, values):
    if len(ref.shape) == 2:
        ref[rows] = values
    elif ref.shape[1] == 1:
        ref[rows, 0, :] = values
    else:
        ref[0, rows, :] = values


def moments(gradient, moment_one, moment_two, master, decay):
    next_one = beta_one * moment_one + (1.0 - beta_one) * gradient
    next_two = beta_two * moment_two + (1.0 - beta_two) * gradient * gradient
    bias_one = 1.0 - beta_one**step_count
    bias_two = 1.0 - beta_two**step_count
    update = next_one / bias_one / (jnp.sqrt(next_two / bias_two) + eps_moment) + decay * master
    return next_one, next_two, update


def state_step(rows):
    return next(step for step in (32, 40, rows) if rows % step == 0)


def scatter_kernel(shapes, units, *refs):
    grads = refs[:7]
    masters, firsts, seconds = refs[7:14], refs[14:21], refs[21:28]
    outs = refs[28:36]
    refs = refs[36:]
    n = len(units)
    own, one, two, three, four = (refs[k * n : (k + 1) * n] for k in range(5))
    vec_one, vec_two, vec_three, vec_four, vec_sum = refs[5 * n : 5 * n + 5]
    stats, stat_one, stat_four = refs[5 * n + 5 : 5 * n + 8]
    send, recv, local, vsend, vrecv, tsend, trecv, ssend, srecv = refs[5 * n + 8 :]
    z, x, y, c = place()
    every = slice(None)
    copies = {}
    stat_row = lax.broadcasted_iota(jnp.int32, (8, 128), 0)
    stat_lane = lax.broadcasted_iota(jnp.int32, (8, 128), 1)

    def tally(array):
        if array == VEC:
            gradient = outs[VEC][:7, : masters[VEC].shape[1]]
            update = moments(
                gradient, firsts[VEC][...], seconds[VEC][...], masters[VEC][...], 0.0
            )[2]
            squares = [jnp.sum(v * v, axis=0, keepdims=True) for v in (masters[VEC][...], update)]
        else:
            flat = (array in SHARED) and outs[array].shape[0] == 4
            count = outs[array].shape[0] * outs[array].shape[1] if flat else outs[array].shape[0]
            columns = outs[array].shape[-1]
            step = outs[array].shape[1] if flat else state_step(count)

            def body(k, carry):
                rows = pl.ds(pl.multiple_of(k * step, 8), step)
                gradient = outs[array][k] if flat else outs[array][rows]
                master = state_rows(masters[array], rows)
                update = moments(
                    gradient,
                    state_rows(firsts[array], rows),
                    state_rows(seconds[array], rows),
                    master,
                    decay_matrix,
                )[2]
                return tuple(
                    total + jnp.sum((v * v).reshape(step // 8, 8, columns), axis=0)
                    for total, v in zip(carry, (master, update))
                )

            start = (jnp.zeros((8, columns), f32),) * 2
            squares = [
                jnp.sum(v, axis=0, keepdims=True)
                for v in lax.fori_loop(0, count // step, body, start)
            ]
        share = 0.25 if array in SHARED + (VEC,) else 1.0
        total = stats[...]
        for row, square in enumerate(squares):
            value = jnp.sum(square, axis=1, keepdims=True) * share
            total = total + jnp.where((stat_row == row) & (stat_lane == STAT_LANES[array]), value, 0.0)
        stats[...] = total

    def remote(src, dst, key, send_sem, recv_sem, peer):
        copies[key] = pltpu.make_async_remote_copy(
            src_ref=src,
            dst_ref=dst,
            send_sem=send_sem,
            recv_sem=recv_sem,
            device_id=peer,
            device_id_type=MESH_ID,
        )
        copies[key].start()

    def start(number, stage):
        at, array, first, size, turn = units[number]
        mine = own[number]
        if stage == 0:
            peer = device(z, x, y, 1 - c)
            src = grads[array].at[
                spot(array, every, 1 - c, every, every) + (pl.ds(first, size),)
            ]
            dst = one[number]
        elif stage == 1 and turn == 0:
            peer = device(z, 1 - x, y, c)
            src, dst = mine.at[half_spot(array, every, every, 1 - x)], two[number]
        elif stage == 1:
            peer = device(z, x, 1 - y, c)
            src, dst = mine.at[half_spot(array, 1 - y, every, every)], two[number]
        elif stage == 2 and turn == 0:
            peer = device(z, x, 1 - y, c)
            src, dst = mine.at[half_spot(array, 1 - y, every, x)], three[number]
        elif stage == 2:
            peer = device(z, 1 - x, y, c)
            src, dst = mine.at[half_spot(array, y, every, 1 - x)], three[number]
        else:
            other = flip(z, stage - 2)
            peer = device(other, x, y, c)
            src, dst = mine.at[half_spot(array, y, other, x)], four[number].at[stage - 3]
        remote(src, dst, (number, stage), send.at[number, stage], recv.at[number, stage], peer)

    def add(number, stage):
        at, array, first, size, turn = units[number]
        mine = own[number]

        def pair(here, there):
            mine[here] = (mine[here].astype(f32) + there.astype(f32)).astype(bf16)

        if stage == 0:

            @pl.loop(0, 16)
            def _(k):
                iy, iz, ix = k // 8, (k // 2) % 4, k % 2
                here = half_spot(array, iy, iz, ix)
                pair(here, one[number][here])

        elif stage == 1 and turn == 0:

            @pl.loop(0, 8)
            def _(k):
                iy, iz = k // 4, k % 4
                there = (iz, iy) if array in SHARED else (iy, iz)
                pair(half_spot(array, iy, iz, x), two[number][there])

        elif stage == 1:

            @pl.loop(0, 8)
            def _(k):
                iz, ix = k // 2, k % 2
                pair(half_spot(array, y, iz, ix), two[number][iz, ix])

        elif stage == 2:

            @pl.loop(0, 4)
            def _(k):
                pair(half_spot(array, y, k, x), three[number][k])

        else:
            total = mine[half_spot(array, y, z, x)].astype(f32)
            for slot in range(3):
                total = total + four[number][slot].astype(f32)
            if array in SHARED:
                outs[array][y * 2 + c, pl.ds(first, size)] = total
            else:
                outs[array][pl.ds(first, size)] = total

    loads = []
    for number, (at, array, first, size, turn) in enumerate(units):
        loads.append(
            pltpu.make_async_copy(
                grads[array].at[spot(array, every, c, every, every) + (pl.ds(first, size),)],
                own[number],
                local.at[number],
            )
        )
    stats[...] = jnp.zeros_like(stats)
    greet(z, x, y, c)
    steps = units[-1][0] + 1

    def step_units(tick):
        return [number for number in range(n) if units[number][0] == tick]

    vec_dst = (vec_one, vec_two, vec_three)
    vec_peer = (device(z, x, y, 1 - c), device(z, 1 - x, y, c), device(z, x, 1 - y, c))

    for tick in range(steps + 4):
        for number in step_units(tick):
            loads[number].start()
            start(number, 0)
        for number in step_units(tick - 1):
            loads[number].wait()
            copies[number, 0].wait_recv()
            add(number, 0)
            start(number, 1)
        for number in step_units(tick - 2):
            copies[number, 1].wait()
            add(number, 1)
            start(number, 2)
        for number in step_units(tick - 3):
            copies[number, 2].wait()
            add(number, 2)
            for stage in (3, 4, 5):
                start(number, stage)
        for number in step_units(tick - 4):
            for stage in (3, 4, 5):
                copies[number, stage].wait()
            add(number, 3)
        if tick < 4:
            if tick == 0:
                vec_sum[...] = grads[6][...]
            if tick < 3:
                remote(vec_sum.at[...], vec_dst[tick], ("v", tick), vsend.at[tick], vrecv.at[tick], vec_peer[tick])
            else:
                vec_four[z] = vec_sum[...]
                for m in (1, 2, 3):
                    remote(vec_sum.at[...], vec_four.at[z], ("v", 2 + m), vsend.at[2 + m], vrecv.at[2 + m], device(flip(z, m), x, y, c))
        if tick < 3:
            copies["v", tick].wait()
            vec_sum[...] = vec_sum[...] + vec_dst[tick][...]
        if tick == 4:
            for m in (1, 2, 3):
                copies["v", 2 + m].wait()
            vec_sum[...] = (vec_four[0] + vec_four[1]) + (vec_four[2] + vec_four[3])
            outs[VEC][...] = vec_sum[z * 2 + x]
            tally(VEC)
        for array in range(6):
            last = max(units[number][0] for number in range(n) if units[number][1] == array)
            if array in SHARED and tick == last + 4:
                here = y * 2 + c
                peers = (
                    device(z, x, y, 1 - c),
                    device(z, x, 1 - y, c),
                    device(z, x, 1 - y, 1 - c),
                )
                for k, peer in enumerate(peers):
                    slot = SHARED.index(array) * 3 + k
                    piece = outs[array].at[here]
                    remote(piece, piece, ("t", slot), tsend.at[slot], trecv.at[slot], peer)
            elif array in SHARED and tick == last + 5:
                for k in range(3):
                    copies["t", SHARED.index(array) * 3 + k].wait()
                tally(array)
            elif array not in SHARED and tick == last + 4:
                tally(array)
    here = (x * 2 + y) * 2 + c
    stat_one[here] = stats[...]
    for m in range(1, 8):
        peer = device(
            z,
            1 - x if m // 4 else x,
            1 - y if (m // 2) % 2 else y,
            1 - c if m % 2 else c,
        )
        remote(stats, stat_one.at[here], ("p", m), ssend.at[m], srecv.at[m], peer)
    for m in range(1, 8):
        copies["p", m].wait()
    total = stat_one[0]
    for slot in range(1, 8):
        total = total + stat_one[slot]
    stats[...] = total
    stat_four[z] = total
    for m in (1, 2, 3):
        remote(
            stats,
            stat_four.at[z],
            ("s", 2 + m),
            ssend.at[7 + m],
            srecv.at[7 + m],
            device(flip(z, m), x, y, c),
        )
    for m in (1, 2, 3):
        copies["s", 2 + m].wait()
    norms = jnp.sqrt((stat_four[0] + stat_four[1]) + (stat_four[2] + stat_four[3]))
    loss = vec_sum[7, 7:8, 128:256][:, 31:32]
    outs[7][...] = jnp.where(stat_row == 2, loss, norms)
    for number in range(n):
        copies[number, 0].wait_send()


def scatter_gradients(grads, masters, firsts, seconds):
    units = [(at,) + unit for at, step in enumerate(SCATTER_STEPS) for unit in step]
    n = len(units)
    shapes = [grad.shape for grad in grads]
    outs = []
    for array in range(6):
        rows, columns = shapes[array][4:]
        if array in SHARED:
            outs.append(jax.ShapeDtypeStruct((4, rows, columns), f32))
        else:
            outs.append(jax.ShapeDtypeStruct((rows, columns), f32))
    outs.append(jax.ShapeDtypeStruct(grads[6].shape[1:], f32))
    outs.append(jax.ShapeDtypeStruct((8, 128), f32))
    scratch = []
    for stage in range(5):
        for at, array, first, size, turn in units:
            shared = array in SHARED
            lead = ((4, 2, 2) if shared else (2, 4, 2), (4,), (3,))
            if stage < 2:
                lead = lead[0]
            elif stage == 2:
                lead = ((4, 2) if shared else (2, 4)) if turn == 0 else (4, 2)
            else:
                lead = lead[stage - 2]
            scratch.append(pltpu.VMEM(lead + (size, shapes[array][5]), bf16))
    vec = grads[6].shape
    scratch += [pltpu.VMEM(vec, f32)] * 3 + [pltpu.VMEM((4,) + vec, f32), pltpu.VMEM(vec, f32)]
    scratch += [pltpu.VMEM(lead + (8, 128), f32) for lead in ((), (8,), (4,))]
    scratch += [
        pltpu.SemaphoreType.DMA((n, 6)),
        pltpu.SemaphoreType.DMA((n, 6)),
        pltpu.SemaphoreType.DMA((n,)),
        pltpu.SemaphoreType.DMA((6,)),
        pltpu.SemaphoreType.DMA((6,)),
        pltpu.SemaphoreType.DMA((6,)),
        pltpu.SemaphoreType.DMA((6,)),
        pltpu.SemaphoreType.DMA((11,)),
        pltpu.SemaphoreType.DMA((11,)),
    ]
    total = sum(int(grad.size) * grad.dtype.itemsize for grad in grads)
    return pl.pallas_call(
        functools.partial(scatter_kernel, shapes, units),
        out_shape=outs,
        in_specs=[pl.BlockSpec(memory_space=pl.ANY)] * 6
        + [pl.BlockSpec(memory_space=pltpu.VMEM)] * 22,
        out_specs=[pl.BlockSpec(memory_space=pltpu.VMEM)] * 8,
        scratch_shapes=scratch,
        compiler_params=pltpu.CompilerParams(
            collective_id=1, has_side_effects=True, vmem_limit_bytes=60 * 1024 * 1024
        ),
        cost_estimate=pl.CostEstimate(flops=0, bytes_accessed=2 * total, transcendentals=0),
        name="scatter_gradients",
    )(*grads, *masters, *firsts, *seconds)


def apply_kernel(*refs):
    sources, stats = refs[:28], refs[28]
    targets = refs[29:50]
    loss, pairs = refs[50:52]
    held = refs[52:80]
    results = refs[80:101]
    loaded, stored = refs[101:]
    loads = [
        pltpu.make_async_copy(source, target, loaded.at[at])
        for at, (source, target) in enumerate(zip(sources, held))
    ]
    order = (EIN, EOUT, DIN, DOUT, PIX, BRI, VEC)
    for array in order:
        for kind in range(4):
            loads[7 * kind + array].start()
    grads, masters, firsts, seconds = (held[7 * k : 7 * k + 7] for k in range(4))
    next_firsts, next_seconds, news = (results[7 * k : 7 * k + 7] for k in range(3))
    stores = [
        pltpu.make_async_copy(source, target, stored.at[at])
        for at, (source, target) in enumerate(zip(results, targets))
    ]
    for array in order:
        lane = STAT_LANES[array]
        norms = [stats[row : row + 1, :][:, lane : lane + 1] for row in range(2)]
        ratio = learn_rate * norms[0] / norms[1]
        count = masters[array].shape[0]
        if len(masters[array].shape) == 3:
            count = count * masters[array].shape[1]
        decay = 0.0 if array == VEC else decay_matrix

        def body(rows, array=array, ratio=ratio, decay=decay):
            if array == VEC:
                gradient = grads[VEC][:7, : masters[VEC].shape[1]]
            else:
                gradient = grads[array][rows]
            master = state_rows(masters[array], rows)
            next_one, next_two, update = moments(
                gradient,
                state_rows(firsts[array], rows),
                state_rows(seconds[array], rows),
                master,
                decay,
            )
            put_rows(next_firsts[array], rows, next_one)
            put_rows(next_seconds[array], rows, next_two)
            put_rows(news[array], rows, master - ratio * update)

        for kind in range(4):
            loads[7 * kind + array].wait()
        if array == VEC:
            body(slice(None))
        else:
            row_loop(count, state_step(count), body)
        for kind in range(3):
            stores[7 * kind + array].start()
    pairs[...] = stats[:2, :][:, :7]
    loss[...] = stats[2:3, :][:, :1]
    for store in stores:
        store.wait()


def apply_update(reduced, masters, firsts, seconds, stats):
    shapes = [jax.ShapeDtypeStruct(master.shape, f32) for master in masters]
    operands = [*reduced, *masters, *firsts, *seconds]
    in_vmem = pl.BlockSpec(memory_space=pltpu.VMEM)
    anywhere = pl.BlockSpec(memory_space=pl.ANY)
    results = pl.pallas_call(
        apply_kernel,
        out_shape=shapes * 3
        + [jax.ShapeDtypeStruct((1, 1), f32), jax.ShapeDtypeStruct((2, 7), f32)],
        in_specs=[anywhere] * 28 + [in_vmem],
        out_specs=[anywhere] * 21 + [in_vmem] * 2,
        scratch_shapes=[pltpu.VMEM(member.shape, f32) for member in operands]
        + [pltpu.VMEM(master.shape, f32) for master in masters] * 3
        + [pltpu.SemaphoreType.DMA((28,)), pltpu.SemaphoreType.DMA((21,))],
        compiler_params=pltpu.CompilerParams(vmem_limit_bytes=60 * 1024 * 1024),
        name="apply_update",
    )(*operands, stats)
    return results[:7], results[7:14], results[14:21], results[21].reshape(()), results[22]


def sinusoid_table(feature_width, grid_side, patch_count, padded):
    position = np.arange(patch_count)
    quarter = feature_width // 4
    omegas = 1.0 / 10000.0 ** (np.arange(quarter) / quarter)
    parts = []
    for coords in (position % grid_side, position // grid_side):
        angles = coords[:, None] * omegas[None, :]
        parts += [np.sin(angles), np.cos(angles)]
    table = np.concatenate(parts, axis=1).astype(np.float32)
    return jnp.asarray(np.pad(table, ((0, padded - patch_count), (0, 0))))


GROUPS = 4
ENC = dict(step=128, first=0, images=4, block=64, tokens=50, width=768, heads=3, head=64, hidden=768, spans=1)
DEC = dict(step=208, first=768, images=4, block=208, tokens=197, width=512, heads=4, head=32, hidden=512, spans=4)
CLASS_ROW = 49
MASK_ROW = 50


def dot(left, right, dims=((1,), (0,)), precision=None):
    return lax.dot_general(
        left, right, (dims, ((), ())), preferred_element_type=f32, precision=precision
    )


def dot_t(left, right):
    return dot(left, right, ((0,), (0,)))


def dot_nt(left, right):
    return dot(left, right, ((1,), (1,)))


def exact_pick(choice, values, dims):
    total = None
    for _ in range(3):
        part = values.astype(bf16)
        values = values - part.astype(f32)
        product = dot(choice, part, dims)
        total = product if total is None else total + product
    return total


def row_loop(count, step, body):
    @pl.loop(0, count // step)
    def _(k):
        body(pl.ds(pl.multiple_of(k * step, step), step))


def fold(values):
    step, width = values.shape
    return jnp.sum(values.reshape(step // 8, 8, width), axis=0)


def norm_rows(source, gain, shift, unit, inverse, low, step):
    def body(rows):
        values = source[rows]
        centred = values - jnp.mean(values, axis=-1, keepdims=True)
        scale = lax.rsqrt(jnp.mean(centred * centred, axis=-1, keepdims=True) + eps_norm)
        normed = centred * scale
        unit[rows] = normed
        inverse[rows] = scale
        low[rows] = (normed * gain + shift).astype(bf16)

    row_loop(source.shape[0], step, body)


def norm_back_rows(incoming, unit, inverse, gain, result, residual, sums, at, step):
    width = incoming.shape[-1]

    def body(rows):
        given = incoming[rows]
        normed = unit[rows]
        scaled = given * gain
        inner = (
            scaled
            - jnp.mean(scaled, axis=-1, keepdims=True)
            - normed * jnp.mean(scaled * normed, axis=-1, keepdims=True)
        )
        value = inverse[rows] * inner
        if residual is not None:
            value = value + residual[rows]
        sums[at] = sums[at] + fold(given * normed)
        sums[at + 1] = sums[at + 1] + fold(given)
        result[rows] = value

    row_loop(incoming.shape[0], step, body)


def lane_chunks(size):
    return [slice(at, min(at + 128, size)) for at in range(0, size, 128)]


def attend_mask(dims, scores, start):
    if dims["spans"] == 1:
        key = lax.broadcasted_iota(jnp.int32, scores.shape, 0)
        query = lax.broadcasted_iota(jnp.int32, scores.shape, 1) + start
        allowed = ((key // dims["block"]) == (query // dims["block"])) & (
            (key % dims["block"]) < dims["tokens"]
        )
        return jnp.where(allowed, scores, -1e30)
    first = dims["tokens"] // 16 * 16
    tail = scores[first:]
    key = lax.broadcasted_iota(jnp.int32, tail.shape, 0) + first
    return jnp.concatenate([scores[:first], jnp.where(key < dims["tokens"], tail, -1e30)], axis=0)


def layer_forward_rows(dims, stream, w_in, w_out, vectors, saved):
    unit_one, inv_one, low_one, qkv, probs, mixed, unit_two, inv_two, low_two, active, slope, work, low_work, low_more = saved
    count, width = stream.shape
    inner = dims["heads"] * dims["head"]
    span = count // dims["spans"]
    norm_rows(stream, vectors[1:2, :], vectors[2:3, :], unit_one, inv_one, low_one, dims["step"])

    @pl.loop(0, GROUPS)
    def _(t):
        weights = w_in[t, :, : 3 * inner] if inner % 128 == 0 else w_in[t][:, : 3 * inner]

        def body(rows):
            qkv[t, rows] = dot(low_one[rows], weights).astype(bf16)

        body(slice(None))

    yield "projected"
    scale = dims["head"] ** (-0.5)

    @pl.loop(0, GROUPS * dims["spans"])
    def _(k):
        t = k // dims["spans"]
        b = k % dims["spans"]
        rows = pl.ds(pl.multiple_of(b * span, span), span)
        triple = qkv[t, rows]
        query_t = triple[:, :inner].T
        value_t = triple[:, 2 * inner :].T
        heads = range(dims["heads"])
        lanes = [slice(head * dims["head"], (head + 1) * dims["head"]) for head in heads]
        for head in heads:
            key = triple[:, inner : 2 * inner][:, lanes[head]]
            work[head] = dot(key, query_t[lanes[head]])
        for head in heads:
            for columns in lane_chunks(span):
                scores = attend_mask(dims, work[head, :, columns] * scale, columns.start)
                shifted = jnp.exp(scores - jnp.max(scores, axis=0, keepdims=True))
                share = shifted * (1.0 / jnp.sum(shifted, axis=0, keepdims=True))
                probs[k * dims["heads"] + head, :, columns] = share
                low_work[head, :, columns] = share.astype(bf16)
        results = [dot(value_t[lanes[head]], low_work[head]) for head in heads]
        mixed[t, rows] = jnp.concatenate(results, axis=0).T.astype(bf16)

    yield "attended"

    @pl.loop(0, GROUPS)
    def _(t):
        weights = w_out[t, :inner]

        def body(rows):
            stream[rows] = stream[rows] + dot(mixed[t, rows], weights)

        body(slice(None))

    norm_rows(stream, vectors[3:4, :], vectors[4:5, :], unit_two, inv_two, low_two, dims["step"])

    def feed(t):
        up = w_in[t, :, 3 * inner :] if inner % 128 == 0 else w_in[t][:, 3 * inner :]
        down = w_out[t, inner:]
        slope[t] = dot(low_two[...], up)

        def bend(rows):
            hidden = slope[t, rows]
            level = 0.5 + 0.5 * lax.erf(hidden * (0.5**0.5))
            active[t, rows] = (hidden * level).astype(bf16)
            slope[t, rows] = level + hidden * (
                jnp.exp(-0.5 * hidden * hidden) * (0.5 / np.pi) ** 0.5
            )

        row_loop(count, 32, bend)
        stream[...] = stream[...] + dot(active[t], down)

    half = GROUPS // 2 if dims["spans"] == 1 else GROUPS
    pl.loop(0, half)(feed)
    if half < GROUPS:
        yield "halfway"
        pl.loop(half, GROUPS)(feed)


def layer_backward_rows(
    dims, given, spare, w_in, w_out, vectors, saved, low, flow, turned, grad_in, grad_out, sums, need, ready
):
    unit_one, inv_one, low_one, qkv, probs, mixed, unit_two, inv_two, low_two, active, slope, work, low_work, low_more = saved
    count, width = given.shape
    inner = dims["heads"] * dims["head"]
    span = count // dims["spans"]
    aligned = inner % 128 == 0

    def lower(rows):
        low[rows] = given[rows].astype(bf16)
        spare[rows] = jnp.zeros_like(spare[rows])

    row_loop(count, 32, lower)
    need("low_two", "active", "slope", "w_out", "w_in")
    turned[...] = low_two[...].T

    @pl.loop(0, GROUPS)
    def _(t):
        down = w_out[t, inner:]
        up = w_in[t, :, 3 * inner :] if aligned else w_in[t][:, 3 * inner :]
        grad_out[t, inner:] = dot_t(active[t], low[...]).astype(bf16)

        def body(rows):
            flow[rows] = (slope[t, rows] * dot_nt(low[rows], down)).astype(bf16)
            spare[rows] = spare[rows] + dot_nt(flow[rows], up)

        body(slice(None))
        grad_up = dot(turned[...], flow[...]).astype(bf16)
        if aligned:
            grad_in[t, :, 3 * inner :] = grad_up
        else:
            grad_in[t] = jnp.concatenate([jnp.zeros((width, 3 * inner), bf16), grad_up], axis=1)

    need("unit_two", "inv_two", "mixed")
    norm_back_rows(spare, unit_two, inv_two, vectors[3:4, :], given, given, sums, 3, dims["step"])
    row_loop(count, 32, lower)

    @pl.loop(0, GROUPS)
    def _(t):
        weights = w_out[t, :inner]
        grad_out[t, :inner] = dot_t(mixed[t], low[...]).astype(bf16)

        mixed[t] = dot_nt(low[...], weights).astype(bf16)
        ready("out", t)

    need("qkv", "probs")

    scale = dims["head"] ** (-0.5)

    @pl.loop(0, GROUPS * dims["spans"])
    def _(k):
        t = k // dims["spans"]
        b = k % dims["spans"]
        rows = pl.ds(pl.multiple_of(b * span, span), span)
        triple = qkv[t, rows]
        back = mixed[t, rows]
        key_t = triple[:, inner : 2 * inner].T
        back_t = back.T
        heads = range(dims["heads"])
        lanes = [slice(head * dims["head"], (head + 1) * dims["head"]) for head in heads]
        for head in heads:
            work[head] = dot(triple[:, 2 * inner :][:, lanes[head]], back_t[lanes[head]])
        for head in heads:
            for columns in lane_chunks(span):
                share = probs[k * dims["heads"] + head, :, columns]
                grad_p = work[head, :, columns]
                grad_s = share * (grad_p - jnp.sum(share * grad_p, axis=0, keepdims=True))
                low_work[head, :, columns] = grad_s.astype(bf16)
                low_more[head, :, columns] = share.astype(bf16)
        parts = ([], [], [])
        for head in heads:
            parts[0].append(dot(key_t[lanes[head]], low_work[head]) * scale)
            parts[1].append(dot(low_work[head], triple[:, :inner][:, lanes[head]]) * scale)
            parts[2].append(dot(low_more[head], back[:, lanes[head]]))
        grad_query = jnp.concatenate(parts[0], axis=0).T
        qkv[t, rows] = jnp.concatenate([grad_query] + parts[1] + parts[2], axis=1).astype(bf16)

    need("low_one", "unit_one", "inv_one")
    turned[...] = low_one[...].T

    @pl.loop(0, GROUPS)
    def _(t):
        weights = w_in[t, :, : 3 * inner] if aligned else w_in[t][:, : 3 * inner]
        grad_triple = dot(turned[...], qkv[t]).astype(bf16)
        if aligned:
            grad_in[t, :, : 3 * inner] = grad_triple
        else:
            grad_in[t] = jnp.concatenate([grad_triple, grad_in[t][:, 3 * inner :]], axis=1)

        ready("in", t)
        spare[...] = spare[...] + dot_nt(qkv[t], weights)

    norm_back_rows(spare, unit_one, inv_one, vectors[1:2, :], given, given, sums, 1, dims["step"])


def saved_shapes(dims):
    count = dims["images"] * dims["block"]
    width, inner = dims["width"], dims["heads"] * dims["head"]
    span = count // dims["spans"]
    return [
        ((count, width), f32),
        ((count, 1), f32),
        ((count, width), bf16),
        ((GROUPS, count, 3 * inner), bf16),
        ((GROUPS * dims["spans"] * dims["heads"], span, span), f32),
        ((GROUPS, count, inner), bf16),
        ((count, width), f32),
        ((count, 1), f32),
        ((count, width), bf16),
        ((GROUPS, count, dims["hidden"]), bf16),
        ((GROUPS, count, dims["hidden"]), f32),
    ]


def work_shapes(dims):
    span = dims["images"] * dims["block"] // dims["spans"]
    shape = (dims["heads"], span, span)
    return [(shape, f32), (shape, bf16), (shape, bf16)]


SAVED = (
    "unit_one", "inv_one", "low_one", "qkv", "probs", "mixed",
    "unit_two", "inv_two", "low_two", "active", "slope",
)


def loader(names, sources, targets, semaphores):
    copies = {}
    for at, (name, source, target) in enumerate(zip(names, sources, targets)):
        copies[name] = pltpu.make_async_copy(source, target, semaphores.at[at])
        copies[name].start()

    def need(*wanted):
        for name in wanted:
            if name in copies:
                copies.pop(name).wait()

    return need


def storer(held, outs, semaphores):
    def ready(kind, t):
        at = ("in", "out").index(kind)
        pltpu.make_async_copy(held[at].at[t], outs[at].at[t], semaphores.at[at]).start()

    def finish():
        for at in range(2):
            pltpu.make_async_copy(held[at], outs[at], semaphores.at[at]).wait()

    return ready, finish


def token_gain(vectors, dims):
    return vectors.at[:, pl.ds(dims["first"], dims["width"])]


def decoder_kernel(*refs):
    projected, codes, images, table, w_in_all, w_out_all, pixel_w, vectors_all = refs[:8]
    grad_in_all, grad_out_all, grad_head, grad_projected, vec_out = refs[8:13]
    stream, given, unit, inverse, low, flow, sums, loss, head, pixels_here, head_sum = refs[13:24]
    w_in, w_out, grad_in, grad_out, turned, loaded, stored = refs[24:31]
    saved = refs[31:]
    dims = DEC
    vectors = token_gain(vectors_all, dims)
    count, width = stream.shape
    block = dims["block"]
    need = loader(
        ("w_in", "w_out", "head", "images"),
        (w_in_all, w_out_all, pixel_w.at[pl.ds(PATCH_DIM, width)], images),
        (w_in, w_out, head, pixels_here),
        loaded,
    )
    ready, finish = storer((grad_in, grad_out), (grad_in_all, grad_out_all), stored)
    sums[...] = jnp.zeros_like(sums)
    loss[...] = jnp.zeros_like(loss)

    def placer(b):
        return (
            lax.broadcasted_iota(jnp.int32, (64, block), 0) == codes[b][:1, :block]
        ).astype(bf16)

    def block_rows(b):
        return pl.ds(pl.multiple_of(b * block, block), block)

    @pl.loop(0, dims["images"])
    def _(b):
        at = lax.broadcasted_iota(jnp.int32, (64, width), 0)
        source = jnp.where(at == MASK_ROW, vectors[0:1, :], projected[b])
        source = jnp.where(at > MASK_ROW, 0.0, source)
        stream[block_rows(b)] = exact_pick(placer(b), source, ((0,), (0,))) + table[...]

    need("w_in", "w_out")
    for _ in layer_forward_rows(dims, stream, w_in, w_out, vectors, saved):
        pass
    norm_rows(stream, vectors[5:6, :], vectors[6:7, :], unit, inverse, low, dims["step"])
    need("head", "images")
    head_sum[...] = jnp.zeros_like(head_sum)
    pixels_wide = pixels_here.shape[-1]
    counted = vectors_all[7:8, :]
    patch_total = jnp.sum(counted, axis=1, keepdims=True) / (counted.shape[1] // 8)

    @pl.loop(0, dims["images"])
    def _(b):
        rows = block_rows(b)
        predicted = dot(low[rows], head[...])
        pixels = pixels_here[b].astype(f32)
        centred = pixels - jnp.mean(pixels, axis=-1, keepdims=True)
        variance = jnp.sum(centred * centred, axis=-1, keepdims=True) / (pixels_wide - 1)
        errors = predicted - centred * lax.rsqrt(variance + eps_norm)
        at = lax.broadcasted_iota(jnp.int32, (64, 128), 0)
        spread = jnp.where(at == MASK_ROW, codes[b][2:3, :128].astype(f32), 0.0)
        weight = dot_t(placer(b), spread.astype(bf16))[:, :1] / patch_total
        loss[...] = loss[...] + fold(errors * errors * weight)
        grad_low = (errors * (2.0 / pixels_wide) * weight).astype(bf16)
        head_sum[...] = head_sum[...] + dot_t(low[rows], grad_low)
        given[rows] = dot_nt(grad_low, head[...])

    grad_head[...] = head_sum[...].astype(bf16)
    norm_back_rows(given, unit, inverse, vectors[5:6, :], given, None, sums, 5, dims["step"])
    layer_backward_rows(
        dims, given, stream, w_in, w_out, vectors, saved, low, flow, turned, grad_in, grad_out, sums, need, ready
    )

    @pl.loop(0, dims["images"])
    def _(b):
        back = exact_pick(placer(b), given[block_rows(b)], ((1,), (0,)))
        at = lax.broadcasted_iota(jnp.int32, (64, width), 0)
        grad_projected[b] = jnp.where(at < MASK_ROW, back, 0.0).astype(bf16)
        sums[0] = sums[0] + fold(jnp.where(at == MASK_ROW, back, 0.0))

    for row in range(7):
        vec_out[row : row + 1, :] = jnp.sum(sums[row], axis=0, keepdims=True)
    total = jnp.sum(jnp.sum(loss[...], axis=0, keepdims=True), axis=1, keepdims=True)
    vec_out[7:8, :] = jnp.broadcast_to(total / pixels_wide, (1, width))
    finish()


def decoder_step(projected, codes, images, table, w_in, w_out, pixel_w, vectors):
    dims = DEC
    count, width = dims["images"] * dims["block"], dims["width"]
    wide = images.shape[-1]
    outs = [
        jax.ShapeDtypeStruct(w_in.shape, bf16),
        jax.ShapeDtypeStruct(w_out.shape, bf16),
        jax.ShapeDtypeStruct((width, wide), bf16),
        jax.ShapeDtypeStruct(projected.shape, bf16),
        jax.ShapeDtypeStruct((8, width), f32),
    ]
    scratch = [
        ((count, width), f32),
        ((count, width), f32),
        ((count, width), f32),
        ((count, 1), f32),
        ((count, width), bf16),
        ((count, dims["hidden"]), bf16),
        ((7, 8, width), f32),
        ((8, wide), f32),
        ((width, wide), bf16),
        (images.shape, bf16),
        ((width, wide), f32),
        (w_in.shape, bf16),
        (w_out.shape, bf16),
        (w_in.shape, bf16),
        (w_out.shape, bf16),
        ((width, count), bf16),
        4,
        2,
    ]
    scratch += saved_shapes(dims) + work_shapes(dims)
    in_vmem = pl.BlockSpec(memory_space=pltpu.VMEM)
    anywhere = pl.BlockSpec(memory_space=pl.ANY)
    return pl.pallas_call(
        decoder_kernel,
        out_shape=outs,
        in_specs=[in_vmem, in_vmem, anywhere, in_vmem, anywhere, anywhere, anywhere, in_vmem],
        out_specs=[anywhere, anywhere, in_vmem, in_vmem, in_vmem],
        scratch_shapes=[
            pltpu.SemaphoreType.DMA((shape,)) if isinstance(shape, int) else pltpu.VMEM(*shape)
            for shape in scratch
        ],
        compiler_params=pltpu.CompilerParams(vmem_limit_bytes=62 * 1024 * 1024),
        name="decoder_step",
    )(projected, codes, images, table, w_in, w_out, pixel_w, vectors)


def encode_kernel(ring, *refs):
    dims = ENC
    images, keep_index, unshuffle, masked, image_valid, table = refs[:6]
    refs = refs[6:]
    group = lax.axis_index("tensor")
    if ring:
        masters, refs = refs[:7], refs[7:]
        wholes, vectors_all, codes, pictures, projected = refs[:7], *refs[7:11]
        kept_state, refs = refs[11:26], refs[26:]
        parts, send, recv, local, vec_parts = refs[:7], *refs[7:11]
        raw = dict(zip((PIX, EOUT, BRI), refs[11:14]))
        refs = refs[14:]
    else:
        wholes, vectors_all = refs[:4], refs[4]
        codes, pictures, projected, kept_state = refs[5], refs[6], refs[7], refs[8:23]
        refs = refs[23:]
        wholes = dict(zip((PIX, EIN, EOUT, BRI), wholes))
    loaded, flushed = refs[:2]
    eight, pixels_here, stream, w_in, w_out, embed, bridge = refs[2:9]
    retained, unit, inverse, low = refs[9:13]
    saved = refs[13:24]
    work = refs[24:]
    held = (retained, unit, inverse, low) + tuple(saved)
    vectors = token_gain(vectors_all, dims)
    count, width = stream.shape
    block = dims["block"]

    first = pl.multiple_of((group // 2) * 8, 8)
    eight_copy = pltpu.make_async_copy(images.at[:, pl.ds(first, 8)], eight, loaded.at[4])
    eight_copy.start()
    lane = lax.broadcasted_iota(jnp.int32, (1, codes.shape[2]), 1)
    valid = image_valid[...]
    image_at = lax.broadcasted_iota(jnp.int32, valid.shape, 1)
    codes[...] = jnp.full(codes.shape, -1, jnp.int32)
    for b in range(dims["images"]):
        mine = group * dims["images"] + b
        row = pl.ds(mine, 1)
        codes[b, 0:1, :] = jnp.where(lane == IMAGE_PATCHES, CLASS_ROW, -1)
        codes[b, 0:1, :IMAGE_PATCHES] = jnp.where(masked[row] == 1, MASK_ROW, unshuffle[row])
        codes[b, 1:2, :KEEP] = keep_index[row]
        own_valid = jnp.sum(
            jnp.where(image_at == mine, valid, 0).astype(f32), axis=1, keepdims=True
        )
        codes[b, 2:3, :] = jnp.broadcast_to(own_valid, (1, codes.shape[2])).astype(jnp.int32)

    def load(slot, array, target):
        if not ring:
            source = wholes[array]
            if array == PIX:
                source = source.at[pl.ds(0, PATCH_DIM)]
            pltpu.make_async_copy(source, target, loaded.at[slot]).start()
            return pltpu.make_async_copy(source, target, loaded.at[slot])
        if array != EIN:
            pltpu.make_async_copy(wholes[array], raw[array], loaded.at[slot]).start()
            return pltpu.make_async_copy(wholes[array], raw[array], loaded.at[slot])
        rows = wholes[array].shape[4]

        @pl.loop(0, 32)
        def _(k):
            pltpu.make_async_copy(
                wholes[array].at[k // 16, (k // 8) % 2, (k // 2) % 4, k % 2],
                target.at[k // 8, pl.ds(pl.multiple_of((k % 8) * rows, rows), rows)],
                loaded.at[slot],
            ).start()

        return pltpu.make_async_copy(target, target, loaded.at[slot])

    def assemble(array, target):
        if ring and array in SHARED:
            count = -(-target.shape[0] // raw[array].shape[4])
            pieces = [
                raw[array][k // 8, (k // 4) % 2, (k // 2) % 2, k % 2] for k in range(count)
            ]
            target[...] = jnp.concatenate(pieces, axis=0)[: target.shape[0]]
        elif ring:

            @pl.loop(0, GROUPS)
            def _(t):
                pieces = [raw[array][t // 2, t % 2, k // 2, k % 2] for k in range(8)]
                target[t] = jnp.concatenate(pieces, axis=0)

    flushes = []

    def flush(*members):
        for member in members:
            copy = pltpu.make_async_copy(held[member], kept_state[member], flushed.at[member])
            copy.start()
            flushes.append(copy)

    if ring:
        for array in range(6):
            if array in SHARED:
                rows = masters[array].shape[0] // 4
                rows = pl.ds(pl.multiple_of(group * rows, 8), rows)
                parts[array][...] = masters[array][rows].astype(bf16)
            else:
                parts[array][...] = state_rows(masters[array], slice(None)).astype(bf16)
        columns = masters[VEC].shape[1]
        parts[VEC][...] = jnp.zeros_like(parts[VEC])
        parts[VEC][:7, :columns] = masters[VEC][...].astype(bf16).astype(f32)
        counts = dot(valid.astype(bf16), masked[...].astype(f32).astype(bf16))
        counted = jnp.sum(counts, axis=1, keepdims=True)
        parts[VEC][7:8, :] = jnp.broadcast_to(counted, (1, parts[VEC].shape[1]))
        ticks = gather_ticks(parts, wholes, send, recv, local)

    done = [-1]

    def until(tick):
        while ring and done[0] < tick:
            next(ticks)
            done[0] += 1

    at_embed, at_in, at_out = (
        last_step(GATHER_STEPS, array) + DEPTH for array in (PIX, EIN, EOUT)
    )
    at_end = len(GATHER_STEPS) - 1 + DEPTH
    until(0)
    eight_copy.wait()
    pixels_wide = eight.shape[2]

    @pl.loop(0, dims["images"])
    def _(b):
        size = (pixels_here.shape[1], IMAGE_PATCHES * 8)
        patch = lax.broadcasted_iota(jnp.int32, size, 0)
        at = lax.broadcasted_iota(jnp.int32, size, 1)
        wanted = patch * 8 + (group % 2) * dims["images"] + b
        choice = (at == wanted) & (patch < IMAGE_PATCHES)
        flat = eight[...].reshape(IMAGE_PATCHES * 8, pixels_wide)
        pixels_here[b] = dot(choice.astype(f32).astype(bf16), flat).astype(bf16)

    picture_copy = pltpu.make_async_copy(pixels_here, pictures, loaded.at[5])
    picture_copy.start()
    until(at_embed)
    embed_copy = load(0, PIX, embed)
    if ring:
        vec_copy = pltpu.make_async_copy(wholes[VEC], vec_parts, loaded.at[1])
        vec_copy.start()
        vec_copy.wait()
        vectors_all[...] = jnp.concatenate(
            [vec_parts[0, 0, k // 2, k % 2][:, :columns] for k in range(8)], axis=1
        )
    embed_copy.wait()
    assemble(PIX, embed)

    @pl.loop(0, dims["images"])
    def _(b):
        rows = pl.ds(pl.multiple_of(b * block, block), block)
        choice = (
            lax.broadcasted_iota(jnp.int32, (table.shape[0], block), 0) == codes[b][1:2, :block]
        )
        retained[rows] = dot_t(choice.astype(bf16), pixels_here[b]).astype(bf16)
        places = exact_pick(choice.astype(bf16), table[...], ((0,), (0,)))
        at = lax.broadcasted_iota(jnp.int32, (block, width), 0)
        start = dot(retained[rows], embed[...]) + places
        stream[rows] = jnp.where(at == CLASS_ROW, vectors[0:1, :], start)

    flush(0)
    until(at_in)
    load(2, EIN, w_in).wait()
    layer = layer_forward_rows(dims, stream, w_in, w_out, vectors, saved + work)
    next(layer)
    until(at_in + 1)
    next(layer)
    flush(4, 5, 6, 7, 8, 9)
    until(at_out)
    bridge_copy = load(1, BRI, bridge)
    load(3, EOUT, w_out).wait()
    assemble(EOUT, w_out)
    next(layer)
    flush(10, 11, 12)
    until(at_out + 1)
    for _ in layer:
        pass
    flush(13, 14)
    until(at_out + 2)
    norm_rows(stream, vectors[5:6, :], vectors[6:7, :], unit, inverse, low, dims["step"])
    flush(1, 2, 3)
    bridge_copy.wait()
    assemble(BRI, bridge)

    @pl.loop(0, dims["images"])
    def _(b):
        rows = pl.ds(pl.multiple_of(b * block, block), block)
        projected[b] = dot(low[rows], bridge[...])

    until(at_end + 1)
    picture_copy.wait()
    for copy in flushes:
        copy.wait()


def encode(images, indices, table, weights, vectors=None):
    dims = ENC
    ring = vectors is None
    count, width = dims["images"] * dims["block"], dims["width"]
    bridge_wide = weights[BRI].shape[-1]
    in_vmem = pl.BlockSpec(memory_space=pltpu.VMEM)
    anywhere = pl.BlockSpec(memory_space=pl.ANY)
    kept_shapes = [
        ((count, images.shape[2]), bf16),
        ((count, width), f32),
        ((count, 1), f32),
        ((count, width), bf16),
    ] + saved_shapes(dims)
    picture_shape = (dims["images"], DEC["block"], images.shape[2])
    outs = [((dims["images"], 8, 256), jnp.int32), (picture_shape, bf16)]
    outs += [((dims["images"], dims["block"], bridge_wide), f32)] + kept_shapes
    out_specs = [in_vmem, anywhere, in_vmem] + [anywhere] * len(kept_shapes)
    in_specs = [anywhere] + [in_vmem] * 5
    scratch = []
    if ring:
        shapes = []
        for array in range(6):
            rows, wide = weights[array].size // weights[array].shape[-1], weights[array].shape[-1]
            shapes.append((rows // 4 if array in SHARED else rows, wide))
        shapes.append((8, 256))
        types = [bf16] * 6 + [f32]
        operands = [images, *indices, table, *weights]
        in_specs += [in_vmem] * 7
        gathered = [(whole_shape(k, shape), types[k]) for k, shape in enumerate(shapes)]
        outs = gathered + [((8, shapes_total(weights[VEC])), f32)] + outs
        out_specs = [anywhere] * 7 + [in_vmem] + out_specs
        units = sum(len(step) for step in GATHER_STEPS)
        scratch += [pltpu.VMEM(shape, kind) for shape, kind in zip(shapes, types)]
        scratch += [
            pltpu.SemaphoreType.DMA((units, 6)),
            pltpu.SemaphoreType.DMA((units, 6)),
            pltpu.SemaphoreType.DMA((7,)),
            pltpu.VMEM(whole_shape(VEC, shapes[VEC]), f32),
        ]
        scratch += [
            pltpu.VMEM(whole_shape(array, shapes[array]), bf16) for array in (PIX, EOUT, BRI)
        ]
        params = dict(collective_id=0, has_side_effects=True)
        w_shapes = [
            (GROUPS, 8 * shapes[EIN][0], shapes[EIN][1]),
            (GROUPS, 8 * shapes[EOUT][0], shapes[EOUT][1]),
        ]
    else:
        operands = [images, *indices, table] + [weights[k] for k in (PIX, EIN, EOUT, BRI)] + [vectors]
        in_specs += [anywhere] * 4 + [in_vmem]
        params = {}
        w_shapes = [weights[EIN].shape, weights[EOUT].shape]
    scratch += [pltpu.SemaphoreType.DMA((8,)), pltpu.SemaphoreType.DMA((15,))]
    buffers = [
        ((images.shape[0], 8, images.shape[2]), bf16),
        (picture_shape, bf16),
        ((count, width), f32),
        (w_shapes[0], bf16),
        (w_shapes[1], bf16),
        ((PATCH_DIM, width), bf16),
        ((width, bridge_wide), bf16),
    ]
    buffers += kept_shapes + work_shapes(dims)
    scratch += [pltpu.VMEM(*buffer) for buffer in buffers]
    return pl.pallas_call(
        functools.partial(encode_kernel, ring),
        out_shape=[jax.ShapeDtypeStruct(shape, kind) for shape, kind in outs],
        in_specs=in_specs,
        out_specs=out_specs,
        scratch_shapes=scratch,
        compiler_params=pltpu.CompilerParams(vmem_limit_bytes=62 * 1024 * 1024, **params),
        name="gather_encode" if ring else "encode",
    )(*operands)


def shapes_total(vector_shard):
    return 8 * vector_shard.shape[1]


def encoder_backward_kernel(*refs):
    grad_projected = refs[0]
    sources = refs[1:18]
    bridge, vectors_all, grad_head, dec_sums = refs[18:22]
    grad_in_all, grad_out_all, grad_bridge, grad_pixel, packed = refs[22:27]
    given, spare, low, flow, sums, vec_all, turned = refs[27:34]
    held = refs[34:51]
    grad_in, grad_out, loaded, stored = refs[51:55]
    names = ("retained", "unit", "inverse", "low_end") + SAVED + ("w_in", "w_out")
    order = (3, 1, 2, 12, 13, 14, 16, 15, 10, 11, 9, 7, 8, 6, 4, 5, 0)
    need = loader(
        [names[k] for k in order], [sources[k] for k in order], [held[k] for k in order], loaded
    )
    ready, finish = storer((grad_in, grad_out), (grad_in_all, grad_out_all), stored)
    retained, unit, inverse, low_end = held[:4]
    saved = held[4:15] + refs[55:]
    w_in, w_out = held[15:17]
    dims = ENC
    vectors = token_gain(vectors_all, dims)
    count, width = given.shape
    block = dims["block"]
    sums[...] = jnp.zeros_like(sums)

    need("low_end", "unit", "inverse")
    flat = grad_projected[...].reshape(count, grad_projected.shape[-1])
    grad_bridge[...] = dot_t(low_end[...], flat).astype(bf16)
    given[...] = dot_nt(flat, bridge[...])
    norm_back_rows(given, unit, inverse, vectors[5:6, :], given, None, sums, 5, dims["step"])
    layer_backward_rows(
        dims, given, spare, w_in, w_out, vectors, saved, low, flow, turned, grad_in, grad_out, sums, need, ready
    )
    need("retained")
    grad_pixel[:PATCH_DIM] = dot_t(retained[...], given[...].astype(bf16)).astype(bf16)
    grad_pixel[PATCH_DIM:] = grad_head[...]

    def tokens(rows):
        at = lax.broadcasted_iota(jnp.int32, (block, width), 0)
        sums[0] = sums[0] + fold(jnp.where(at == CLASS_ROW, given[rows], 0.0))

    row_loop(count, block, tokens)
    for row in range(7):
        vec_all[row : row + 1, :width] = jnp.sum(sums[row], axis=0, keepdims=True)
    vec_all[7:8, :width] = jnp.zeros((1, width), f32)
    vec_all[:, width:] = dec_sums[...]
    columns = vec_all.shape[1] // 8
    packed[...] = jnp.zeros_like(packed)
    for k in range(8):
        packed[k, :, :columns] = vec_all[:, k * columns : (k + 1) * columns]
    finish()


def encoder_backward(grad_projected, kept_state, w_in, w_out, bridge, vectors, grad_head, dec_sums):
    dims = ENC
    count, width = dims["images"] * dims["block"], dims["width"]
    pixels_wide = kept_state[0].shape[1]
    outs = [
        jax.ShapeDtypeStruct(w_in.shape, bf16),
        jax.ShapeDtypeStruct(w_out.shape, bf16),
        jax.ShapeDtypeStruct(bridge.shape, bf16),
        jax.ShapeDtypeStruct((pixels_wide + grad_head.shape[0], width), bf16),
        jax.ShapeDtypeStruct((8, 8, 256), f32),
    ]
    scratch = [
        ((count, width), f32),
        ((count, width), f32),
        ((count, width), bf16),
        ((count, dims["hidden"]), bf16),
        ((7, 8, width), f32),
        (vectors.shape, f32),
        ((width, count), bf16),
    ]
    kept_shapes = [(member.shape, member.dtype) for member in kept_state]
    scratch += kept_shapes + [(w_in.shape, bf16), (w_out.shape, bf16)]
    scratch += [(w_in.shape, bf16), (w_out.shape, bf16), 17, 2] + work_shapes(dims)
    in_vmem = pl.BlockSpec(memory_space=pltpu.VMEM)
    anywhere = pl.BlockSpec(memory_space=pl.ANY)
    return pl.pallas_call(
        encoder_backward_kernel,
        out_shape=outs,
        in_specs=[in_vmem] + [anywhere] * 17 + [in_vmem] * 4,
        out_specs=[anywhere] * 2 + [in_vmem] * 3,
        scratch_shapes=[
            pltpu.SemaphoreType.DMA((shape,)) if isinstance(shape, int) else pltpu.VMEM(*shape)
            for shape in scratch
        ],
        compiler_params=pltpu.CompilerParams(vmem_limit_bytes=62 * 1024 * 1024),
        name="encoder_backward",
    )(grad_projected, *kept_state, w_in, w_out, bridge, vectors, grad_head, dec_sums)


def gather_grouped(part, groups):
    whole = lax.all_gather(part, GROUPED, axis=0, tiled=True)
    return whole.reshape(groups, -1, whole.shape[-1])


def scatter_grouped(gradient):
    flat = gradient.astype(f32).reshape(-1, gradient.shape[-1])
    return lax.psum_scatter(flat, GROUPED, scatter_dimension=0, tiled=True)


def ringed(tensor_count):
    return tensor_count == 4 and lax.axis_size("dp") == 8


def plain_gather(masters, counted):
    groups = lax.axis_size("tensor")
    wholes = {}
    for array, k in ((EIN, 0), (EOUT, 1), (DIN, 2), (DOUT, 3)):
        flat = masters[k].reshape(-1, masters[k].shape[-1]).astype(bf16)
        wholes[array] = gather_grouped(flat, groups)
    for array, k in ((PIX, 4), (BRI, 5)):
        wholes[array] = lax.all_gather(masters[k].astype(bf16), "dp", axis=0, tiled=True)
    low = masters[6].astype(bf16).astype(f32)
    vectors = lax.all_gather(low, "dp", axis=1, tiled=True)
    eighth = jnp.broadcast_to(lax.psum(counted, "dp") / 8, (1, vectors.shape[1]))
    return wholes, jnp.concatenate([vectors, eighth], axis=0)


def ring_finish(gradients, masters, firsts, seconds):
    grouped, grad_pixel, grad_bridge, packed = gradients
    tensor_count = lax.axis_size("tensor")
    order = (4, 0, 1, 5, 2, 3, 6)
    sources = (grad_pixel, grouped[0], grouped[1], grad_bridge, grouped[2], grouped[3])
    operands = []
    for array, source in enumerate(sources):
        master = masters[order[array]]
        rows, wide = master.size // master.shape[-1], master.shape[-1]
        if array in SHARED:
            rows = rows // tensor_count
        operands.append(source.reshape(whole_shape(array, (rows, wide))))
    operands.append(packed)
    states = [[members[k] for k in order] for members in (masters, firsts, seconds)]
    *sums, stats = scatter_gradients(operands, *states)
    for array in SHARED:
        sums[array] = sums[array].reshape(-1, sums[array].shape[-1])
    *results, loss_value, pairs = apply_update(sums, *states, stats)
    place_of = {k: at for at, k in enumerate(order)}
    results = [[members[place_of[k]] for k in range(7)] for members in results]
    return (loss_value, pairs, *results[0], *results[1], *results[2])


def plain_finish(gradients, masters, firsts, seconds):
    grouped, grad_pixel, grad_bridge, packed = gradients
    tensor_count = lax.axis_size("tensor")
    columns = masters[6].shape[1]

    def scatter_shared(gradient):
        part = lax.psum_scatter(gradient.astype(f32), EVERY, scatter_dimension=0, tiled=True)
        return lax.all_gather(part, "tensor", axis=0, tiled=True)

    reduced = [scatter_grouped(gradient) for gradient in grouped]
    reduced += [scatter_shared(grad_pixel), scatter_shared(grad_bridge)]
    whole = packed.shape[0] * (ENCODER_WIDTH + D_D) // 8
    packed = packed[:, :, : whole // packed.shape[0]].transpose(1, 0, 2).reshape(8, -1)
    vector_sum = lax.psum(packed, EVERY)
    own = lax.dynamic_slice_in_dim(
        vector_sum[:7], lax.axis_index("dp") * columns, columns, axis=1
    )
    reduced = [gradient.reshape(master.shape) for gradient, master in zip(reduced + [own], masters)]
    decays = (decay_matrix,) * 6 + (0.0,)
    share_counts = (1.0,) * 4 + (float(tensor_count),) * 3
    steps = [moments(*member) for member in zip(reduced, firsts, seconds, masters, decays)]
    new_firsts, new_seconds, updates = zip(*steps)

    def squares(members):
        return jnp.stack(
            [jnp.sum(member * member) / count for member, count in zip(members, share_counts)]
        )

    weight_norm, update_norm = map(
        jnp.sqrt, lax.psum((squares(masters), squares(updates)), EVERY)
    )
    ratio = learn_rate * weight_norm / update_norm
    news = [
        master - ratio[position] * update
        for position, (master, update) in enumerate(zip(masters, updates))
    ]
    return (vector_sum[7, -1], jnp.stack([weight_norm, update_norm]), *new_firsts, *new_seconds, *news)


def shards(
    images,
    keep_index,
    unshuffle,
    masked,
    image_valid,
    *state,
):
    masters, firsts, seconds = state[:7], state[7:14], state[14:21]
    tensor_count = lax.axis_size("tensor")
    enc_table, dec_table = (
        sinusoid_table(width, GRID_PATCHES, IMAGE_PATCHES, DEC["block"])
        for width in (ENCODER_WIDTH, D_D)
    )
    indices = (keep_index, unshuffle, masked, image_valid[None, :])
    by_patch = images.transpose(1, 0, 2)
    if ringed(tensor_count):
        order = (4, 0, 1, 5, 2, 3, 6)
        results = encode(by_patch, indices, enc_table, [masters[k] for k in order])
        wholes, results = results[:7], results[7:]
        vectors, codes, pictures, projected, *enc_state = results
        wholes = [
            whole.reshape(-1, whole.shape[-1])
            if array in SHARED
            else whole.reshape(tensor_count, -1, whole.shape[-1])
            for array, whole in enumerate(wholes)
        ]
    else:
        counted = jnp.sum(masked.astype(f32) * image_valid.astype(f32)[:, None])
        wholes, vectors = plain_gather(masters, counted)
        codes, pictures, projected, *enc_state = encode(
            by_patch, indices, enc_table, wholes, vectors=vectors
        )
    grad_dec_in, grad_dec_out, grad_head, grad_projected, dec_sums = decoder_step(
        projected, codes, pictures, dec_table, wholes[DIN], wholes[DOUT], wholes[PIX], vectors
    )
    grad_enc_in, grad_enc_out, grad_bridge, grad_pixel, packed = encoder_backward(
        grad_projected,
        enc_state,
        wholes[EIN],
        wholes[EOUT],
        wholes[BRI],
        vectors,
        grad_head,
        dec_sums,
    )
    finish = ring_finish if ringed(tensor_count) else plain_finish
    return finish(
        ([grad_enc_in, grad_enc_out, grad_dec_in, grad_dec_out], grad_pixel, grad_bridge, packed),
        masters,
        firsts,
        seconds,
    )


def solution(mesh):
    state_specs = (
        P("dp", "tensor", None),
        P("tensor", "dp", None),
        P("dp", "tensor", None),
        P("tensor", "dp", None),
        P("dp", None),
        P("dp", None),
        P(None, "dp"),
    )
    in_specs = (
        P("dp", None, None),
        P("dp", None),
        P("dp", None),
        P("dp", None),
        P("dp"),
    ) + state_specs * 3
    out_specs = (P(), P()) + state_specs * 3
    return jax.shard_map(shards, mesh=mesh, in_specs=in_specs, out_specs=out_specs, check_vma=False)
```

```python
import functools

import jax
import jax.numpy as jnp
from jax import lax
from jax.experimental import pallas as pl
from jax.experimental.pallas import tpu as pltpu
from jax.sharding import PartitionSpec as P
import numpy as np

ENCODER_WIDTH = 768
H_E = 12
HD_E = 64
D_D = 512
H_D = 16
HD_D = 32
PATCH_DIM = 768
GRID_PATCHES = 14
IMAGE_PATCHES = 196
KEEP = 49

eps_norm = 1e-06
beta_one = 0.9
beta_two = 0.999
step_count = 7.0
learn_rate = 0.3
decay_matrix = 0.05
eps_moment = 1e-06
f32 = jnp.float32
bf16 = jnp.bfloat16
EVERY = ("dp", "tensor")
GROUPED = ("tensor", "dp")


MESH_ID = pl.DeviceIdType.MESH
PIX, EIN, EOUT, BRI, DIN, DOUT, VEC = range(7)


def place():
    dp_at = lax.axis_index("dp")
    group = lax.axis_index("tensor")
    z, x = lax.div(dp_at, 2), lax.rem(dp_at, 2)
    y, c = lax.div(group, 2), lax.rem(group, 2)
    return z, x, y, c


def device(z, x, y, c):
    return (z * 2 + x, y * 2 + c)


def flip(z, m):
    low = lax.rem(z, 2)
    high = lax.div(z, 2)
    if m % 2:
        low = 1 - low
    if m // 2:
        high = 1 - high
    return high * 2 + low


def greet(z, x, y, c):
    barrier = pltpu.get_barrier_semaphore()
    peers = [device(flip(z, m), x, y, c) for m in (1, 2, 3)]
    for m in range(1, 8):
        peers.append(
            device(
                z,
                1 - x if m // 4 else x,
                1 - y if (m // 2) % 2 else y,
                1 - c if m % 2 else c,
            )
        )
    for peer in peers:
        pl.semaphore_signal(barrier, inc=1, device_id=peer, device_id_type=MESH_ID)
    pl.semaphore_wait(barrier, len(peers))


SHARED = (PIX, BRI)


def spot(array, y, c, z, x):
    return (z, x, y, c) if array in SHARED else (y, c, z, x)


def half_spot(array, y, z, x):
    return (z, x, y) if array in SHARED else (y, z, x)


def whole_shape(array, part):
    return ((4, 2, 2, 2) if array in SHARED else (2, 2, 4, 2)) + part


GATHER_STEPS = (
    ((VEC, 0, 8, 0), (PIX, 0, 24, 0), (PIX, 24, 16, 1)),
    ((EIN, 0, 16, 0), (EIN, 16, 16, 1)),
    ((EIN, 32, 16, 0), (EIN, 48, 16, 1)),
    ((EIN, 64, 16, 0), (EIN, 80, 16, 1)),
    ((EOUT, 0, 24, 0), (EOUT, 24, 24, 1)),
    ((EOUT, 48, 24, 0), (EOUT, 72, 24, 1)),
    ((EOUT, 96, 8, 0), (EOUT, 104, 16, 1), (BRI, 0, 16, 0), (BRI, 16, 8, 1)),
    ((DIN, 0, 16, 0), (DIN, 16, 16, 1)),
    ((DIN, 32, 16, 0), (DIN, 48, 16, 1)),
    ((DOUT, 0, 16, 0), (DOUT, 16, 32, 1)),
    ((DOUT, 48, 16, 0), (DOUT, 64, 16, 1)),
)
DEPTH = 4


def last_step(steps, array):
    return max(at for at, step in enumerate(steps) for unit in step if unit[0] == array)


def gather_ticks(parts, outs, send, recv, local):
    count = 7
    z, x, y, c = place()
    units = []
    for at, step in enumerate(GATHER_STEPS):
        for unit in step:
            units.append((at,) + unit)
    copies = {}

    def rows(array, region, first, size):
        ref = outs[array]
        return ref.at[region + (pl.ds(first, size),)]

    def plan(number, stage):
        at, array, first, size, turn = units[number]
        every = slice(None)
        if stage < 3:
            src = parts[array].at[pl.ds(first, size)]
            dst = rows(array, spot(array, y, c, z, x), first, size)
            peer = device(flip(z, stage + 1), x, y, c)
        else:
            if stage == 3:
                region = spot(array, y, c, every, x)
                peer = device(z, x, 1 - y, c) if turn == 0 else device(z, 1 - x, y, c)
            elif stage == 4 and turn == 0:
                region = spot(array, every, c, every, x)
                peer = device(z, 1 - x, y, c)
            elif stage == 4:
                region = spot(array, y, c, every, every)
                peer = device(z, x, 1 - y, c)
            else:
                region = spot(array, every, c, every, every)
                peer = device(z, x, y, 1 - c)
            src = dst = rows(array, region, first, size)
        return pltpu.make_async_remote_copy(
            src_ref=src,
            dst_ref=dst,
            send_sem=send.at[number, stage],
            recv_sem=recv.at[number, stage],
            device_id=peer,
            device_id_type=MESH_ID,
        )

    def start(number, stage):
        copies[number, stage] = plan(number, stage)
        copies[number, stage].start()

    own = []
    for array in range(count):
        own.append(
            pltpu.make_async_copy(parts[array], outs[array].at[spot(array, y, c, z, x)], local.at[array])
        )
        own[-1].start()
    greet(z, x, y, c)
    steps = len(GATHER_STEPS)
    waited = set()
    for tick in range(steps + 4):
        for number, unit in enumerate(units):
            if unit[0] == tick:
                for stage in range(3):
                    start(number, stage)
        for number, unit in enumerate(units):
            if unit[0] == tick - 1:
                if unit[1] not in waited:
                    waited.add(unit[1])
                    own[unit[1]].wait()
                for stage in range(3):
                    copies[number, stage].wait_recv()
                start(number, 3)
        for back in (2, 3):
            for number, unit in enumerate(units):
                if unit[0] == tick - back:
                    copies[number, back + 1].wait_recv()
                    start(number, back + 2)
        for number, unit in enumerate(units):
            if unit[0] == tick - 4:
                copies[number, 5].wait_recv()
        if tick < steps + 3:
            yield tick
    for key in copies:
        copies[key].wait_send()
    yield steps + 3
    yield None


SCATTER_STEPS = (
    ((BRI, 0, 8, 0), (BRI, 8, 16, 1)),
    ((PIX, 0, 24, 0), (PIX, 24, 16, 1)),
    ((EIN, 0, 16, 0), (EIN, 16, 16, 1)),
    ((EIN, 32, 16, 0), (EIN, 48, 16, 1)),
    ((EIN, 64, 16, 0), (EIN, 80, 16, 1)),
    ((EOUT, 0, 24, 0), (EOUT, 24, 24, 1)),
    ((EOUT, 48, 24, 0), (EOUT, 72, 24, 1)),
    ((EOUT, 96, 8, 0), (EOUT, 104, 16, 1)),
    ((DIN, 0, 16, 0), (DIN, 16, 16, 1)),
    ((DIN, 32, 16, 0), (DIN, 48, 16, 1)),
    ((DOUT, 0, 24, 0), (DOUT, 24, 24, 1)),
    ((DOUT, 48, 16, 0), (DOUT, 64, 16, 1)),
)


STAT_LANES = {EIN: 0, EOUT: 1, DIN: 2, DOUT: 3, PIX: 4, BRI: 5, VEC: 6}


def state_rows(ref, rows):
    if len(ref.shape) == 2:
        return ref[rows]
    return ref[rows, 0, :] if ref.shape[1] == 1 else ref[0, rows, :]


def put_rows(ref, rows, values):
    if len(ref.shape) == 2:
        ref[rows] = values
    elif ref.shape[1] == 1:
        ref[rows, 0, :] = values
    else:
        ref[0, rows, :] = values


def moments(gradient, moment_one, moment_two, master, decay):
    next_one = beta_one * moment_one + (1.0 - beta_one) * gradient
    next_two = beta_two * moment_two + (1.0 - beta_two) * gradient * gradient
    bias_one = 1.0 - beta_one**step_count
    bias_two = 1.0 - beta_two**step_count
    update = next_one / bias_one / (jnp.sqrt(next_two / bias_two) + eps_moment) + decay * master
    return next_one, next_two, update


def state_step(rows):
    return next(step for step in (32, 40, rows) if rows % step == 0)


def scatter_kernel(shapes, units, *refs):
    grads = refs[:7]
    sources, results = refs[7:28], refs[28:36]
    refs = refs[36:]
    n = len(units)
    own, one, two, three, four = (refs[k * n : (k + 1) * n] for k in range(5))
    vec_one, vec_two, vec_three, vec_four, vec_sum = refs[5 * n : 5 * n + 5]
    stats, stat_one, stat_four = refs[5 * n + 5 : 5 * n + 8]
    send, recv, local, vsend, vrecv, tsend, trecv, ssend, srecv = refs[5 * n + 8 : 5 * n + 17]
    refs = refs[5 * n + 17 :]
    held, outs, loaded, stored = refs[:21], refs[21:28] + results[7:], *refs[28:]
    masters, firsts, seconds = held[:7], held[7:14], held[14:]
    state_copies = [
        pltpu.make_async_copy(source, target, loaded.at[at])
        for at, (source, target) in enumerate(zip(sources, held))
    ]
    for copy in state_copies:
        copy.start()
    stores = []
    z, x, y, c = place()
    every = slice(None)
    copies = {}
    stat_row = lax.broadcasted_iota(jnp.int32, (8, 128), 0)
    stat_lane = lax.broadcasted_iota(jnp.int32, (8, 128), 1)

    def tally(array):
        stores.append(pltpu.make_async_copy(outs[array], results[array], stored.at[array]))
        stores[-1].start()
        for kind in range(3):
            state_copies[7 * kind + array].wait()
        if array == VEC:
            gradient = outs[VEC][:7, : masters[VEC].shape[1]]
            update = moments(
                gradient, firsts[VEC][...], seconds[VEC][...], masters[VEC][...], 0.0
            )[2]
            squares = [jnp.sum(v * v, axis=0, keepdims=True) for v in (masters[VEC][...], update)]
        else:
            flat = (array in SHARED) and outs[array].shape[0] == 4
            count = outs[array].shape[0] * outs[array].shape[1] if flat else outs[array].shape[0]
            columns = outs[array].shape[-1]
            step = outs[array].shape[1] if flat else state_step(count)

            def body(k, carry):
                rows = pl.ds(pl.multiple_of(k * step, 8), step)
                gradient = outs[array][k] if flat else outs[array][rows]
                master = state_rows(masters[array], rows)
                update = moments(
                    gradient,
                    state_rows(firsts[array], rows),
                    state_rows(seconds[array], rows),
                    master,
                    decay_matrix,
                )[2]
                return tuple(
                    total + jnp.sum((v * v).reshape(step // 8, 8, columns), axis=0)
                    for total, v in zip(carry, (master, update))
                )

            start = (jnp.zeros((8, columns), f32),) * 2
            squares = [
                jnp.sum(v, axis=0, keepdims=True)
                for v in lax.fori_loop(0, count // step, body, start)
            ]
        share = 0.25 if array in SHARED + (VEC,) else 1.0
        total = stats[...]
        for row, square in enumerate(squares):
            value = jnp.sum(square, axis=1, keepdims=True) * share
            total = total + jnp.where((stat_row == row) & (stat_lane == STAT_LANES[array]), value, 0.0)
        stats[...] = total

    def remote(src, dst, key, send_sem, recv_sem, peer):
        copies[key] = pltpu.make_async_remote_copy(
            src_ref=src,
            dst_ref=dst,
            send_sem=send_sem,
            recv_sem=recv_sem,
            device_id=peer,
            device_id_type=MESH_ID,
        )
        copies[key].start()

    def start(number, stage):
        at, array, first, size, turn = units[number]
        mine = own[number]
        if stage == 0:
            peer = device(z, x, y, 1 - c)
            src = grads[array].at[
                spot(array, every, 1 - c, every, every) + (pl.ds(first, size),)
            ]
            dst = one[number]
        elif stage == 1 and turn == 0:
            peer = device(z, 1 - x, y, c)
            src, dst = mine.at[half_spot(array, every, every, 1 - x)], two[number]
        elif stage == 1:
            peer = device(z, x, 1 - y, c)
            src, dst = mine.at[half_spot(array, 1 - y, every, every)], two[number]
        elif stage == 2 and turn == 0:
            peer = device(z, x, 1 - y, c)
            src, dst = mine.at[half_spot(array, 1 - y, every, x)], three[number]
        elif stage == 2:
            peer = device(z, 1 - x, y, c)
            src, dst = mine.at[half_spot(array, y, every, 1 - x)], three[number]
        else:
            other = flip(z, stage - 2)
            peer = device(other, x, y, c)
            src, dst = mine.at[half_spot(array, y, other, x)], four[number].at[stage - 3]
        remote(src, dst, (number, stage), send.at[number, stage], recv.at[number, stage], peer)

    def add(number, stage):
        at, array, first, size, turn = units[number]
        mine = own[number]

        def pair(here, there):
            mine[here] = (mine[here].astype(f32) + there.astype(f32)).astype(bf16)

        if stage == 0:

            @pl.loop(0, 16)
            def _(k):
                iy, iz, ix = k // 8, (k // 2) % 4, k % 2
                here = half_spot(array, iy, iz, ix)
                pair(here, one[number][here])

        elif stage == 1 and turn == 0:

            @pl.loop(0, 8)
            def _(k):
                iy, iz = k // 4, k % 4
                there = (iz, iy) if array in SHARED else (iy, iz)
                pair(half_spot(array, iy, iz, x), two[number][there])

        elif stage == 1:

            @pl.loop(0, 8)
            def _(k):
                iz, ix = k // 2, k % 2
                pair(half_spot(array, y, iz, ix), two[number][iz, ix])

        elif stage == 2:

            @pl.loop(0, 4)
            def _(k):
                pair(half_spot(array, y, k, x), three[number][k])

        else:
            total = mine[half_spot(array, y, z, x)].astype(f32)
            for slot in range(3):
                total = total + four[number][slot].astype(f32)
            if array in SHARED:
                outs[array][y * 2 + c, pl.ds(first, size)] = total
            else:
                outs[array][pl.ds(first, size)] = total

    loads = []
    for number, (at, array, first, size, turn) in enumerate(units):
        loads.append(
            pltpu.make_async_copy(
                grads[array].at[spot(array, every, c, every, every) + (pl.ds(first, size),)],
                own[number],
                local.at[number],
            )
        )
    stats[...] = jnp.zeros_like(stats)
    greet(z, x, y, c)
    steps = units[-1][0] + 1

    def step_units(tick):
        return [number for number in range(n) if units[number][0] == tick]

    vec_dst = (vec_one, vec_two, vec_three)
    vec_peer = (device(z, x, y, 1 - c), device(z, 1 - x, y, c), device(z, x, 1 - y, c))

    for tick in range(steps + 4):
        for number in step_units(tick):
            loads[number].start()
            start(number, 0)
        for number in step_units(tick - 1):
            loads[number].wait()
            copies[number, 0].wait_recv()
            add(number, 0)
            start(number, 1)
        for number in step_units(tick - 2):
            copies[number, 1].wait()
            add(number, 1)
            start(number, 2)
        for number in step_units(tick - 3):
            copies[number, 2].wait()
            add(number, 2)
            for stage in (3, 4, 5):
                start(number, stage)
        for number in step_units(tick - 4):
            for stage in (3, 4, 5):
                copies[number, stage].wait()
            add(number, 3)
        if tick == 0:
            vec_sum[...] = grads[6][...]
        if 1 <= tick <= 3:
            copies["v", tick - 1].wait()
            vec_sum[...] = vec_sum[...] + vec_dst[tick - 1][...]
        if tick < 3:
            remote(vec_sum, vec_dst[tick], ("v", tick), vsend.at[tick], vrecv.at[tick], vec_peer[tick])
        elif tick == 3:
            vec_four[z] = vec_sum[...]
            for m in (1, 2, 3):
                peer = device(flip(z, m), x, y, c)
                remote(vec_sum, vec_four.at[z], ("v", 2 + m), vsend.at[2 + m], vrecv.at[2 + m], peer)
        elif tick == 4:
            for m in (1, 2, 3):
                copies["v", 2 + m].wait()
            vec_sum[...] = (vec_four[0] + vec_four[1]) + (vec_four[2] + vec_four[3])
            outs[VEC][...] = vec_sum[z * 2 + x]
            tally(VEC)
        for array in range(6):
            last = max(units[number][0] for number in range(n) if units[number][1] == array)
            if array in SHARED and tick == last + 4:
                here = y * 2 + c
                peers = (
                    device(z, x, y, 1 - c),
                    device(z, x, 1 - y, c),
                    device(z, x, 1 - y, 1 - c),
                )
                for k, peer in enumerate(peers):
                    slot = SHARED.index(array) * 3 + k
                    piece = outs[array].at[here]
                    remote(piece, piece, ("t", slot), tsend.at[slot], trecv.at[slot], peer)
            elif array in SHARED and tick == last + 5:
                for k in range(3):
                    copies["t", SHARED.index(array) * 3 + k].wait()
                tally(array)
            elif array not in SHARED and tick == last + 4:
                tally(array)
    here = (x * 2 + y) * 2 + c
    stat_one[here] = stats[...]
    for m in range(1, 8):
        peer = device(
            z,
            1 - x if m // 4 else x,
            1 - y if (m // 2) % 2 else y,
            1 - c if m % 2 else c,
        )
        remote(stats, stat_one.at[here], ("p", m), ssend.at[m], srecv.at[m], peer)
    for m in range(1, 8):
        copies["p", m].wait()
    total = stat_one[0]
    for slot in range(1, 8):
        total = total + stat_one[slot]
    stats[...] = total
    stat_four[z] = total
    for m in (1, 2, 3):
        remote(
            stats,
            stat_four.at[z],
            ("s", 2 + m),
            ssend.at[7 + m],
            srecv.at[7 + m],
            device(flip(z, m), x, y, c),
        )
    for m in (1, 2, 3):
        copies["s", 2 + m].wait()
    norms = jnp.sqrt((stat_four[0] + stat_four[1]) + (stat_four[2] + stat_four[3]))
    loss = vec_sum[7, 7:8, 128:256][:, 31:32]
    outs[7][...] = jnp.where(stat_row == 2, loss, norms)
    for number in range(n):
        copies[number, 0].wait_send()
    for store in stores:
        store.wait()


def scatter_gradients(grads, masters, firsts, seconds):
    units = [(at,) + unit for at, step in enumerate(SCATTER_STEPS) for unit in step]
    n = len(units)
    shapes = [grad.shape for grad in grads]
    outs = []
    for array in range(6):
        rows, columns = shapes[array][4:]
        if array in SHARED:
            outs.append(jax.ShapeDtypeStruct((4, rows, columns), f32))
        else:
            outs.append(jax.ShapeDtypeStruct((rows, columns), f32))
    outs.append(jax.ShapeDtypeStruct(grads[6].shape[1:], f32))
    outs.append(jax.ShapeDtypeStruct((8, 128), f32))
    scratch = []
    for stage in range(5):
        for at, array, first, size, turn in units:
            shared = array in SHARED
            lead = ((4, 2, 2) if shared else (2, 4, 2), (4,), (3,))
            if stage < 2:
                lead = lead[0]
            elif stage == 2:
                lead = ((4, 2) if shared else (2, 4)) if turn == 0 else (4, 2)
            else:
                lead = lead[stage - 2]
            scratch.append(pltpu.VMEM(lead + (size, shapes[array][5]), bf16))
    vec = grads[6].shape
    scratch += [pltpu.VMEM(vec, f32)] * 3 + [pltpu.VMEM((4,) + vec, f32), pltpu.VMEM(vec, f32)]
    scratch += [pltpu.VMEM(lead + (8, 128), f32) for lead in ((), (8,), (4,))]
    scratch += [
        pltpu.SemaphoreType.DMA((n, 6)),
        pltpu.SemaphoreType.DMA((n, 6)),
        pltpu.SemaphoreType.DMA((n,)),
        pltpu.SemaphoreType.DMA((6,)),
        pltpu.SemaphoreType.DMA((6,)),
        pltpu.SemaphoreType.DMA((6,)),
        pltpu.SemaphoreType.DMA((6,)),
        pltpu.SemaphoreType.DMA((11,)),
        pltpu.SemaphoreType.DMA((11,)),
    ]
    states = [*masters, *firsts, *seconds]
    scratch += [pltpu.VMEM(member.shape, f32) for member in states + outs[:7]]
    scratch += [pltpu.SemaphoreType.DMA((21,)), pltpu.SemaphoreType.DMA((7,))]
    in_vmem = pl.BlockSpec(memory_space=pltpu.VMEM)
    anywhere = pl.BlockSpec(memory_space=pl.ANY)
    total = sum(int(grad.size) * grad.dtype.itemsize for grad in grads)
    return pl.pallas_call(
        functools.partial(scatter_kernel, shapes, units),
        out_shape=outs,
        in_specs=[anywhere] * 6 + [in_vmem] + [anywhere] * 21,
        out_specs=[anywhere] * 7 + [in_vmem],
        scratch_shapes=scratch,
        compiler_params=pltpu.CompilerParams(
            collective_id=1, has_side_effects=True, vmem_limit_bytes=60 * 1024 * 1024
        ),
        cost_estimate=pl.CostEstimate(flops=0, bytes_accessed=2 * total, transcendentals=0),
        name="scatter_gradients",
    )(*grads, *masters, *firsts, *seconds)


def apply_kernel(*refs):
    sources, stats = refs[:28], refs[28]
    targets = refs[29:50]
    loss, pairs = refs[50:52]
    held = refs[52:80]
    results = refs[80:101]
    loaded, stored = refs[101:]
    loads = [
        pltpu.make_async_copy(source, target, loaded.at[at])
        for at, (source, target) in enumerate(zip(sources, held))
    ]
    order = (EIN, EOUT, DIN, DOUT, PIX, BRI, VEC)
    for array in order:
        for kind in range(4):
            loads[7 * kind + array].start()
    grads, masters, firsts, seconds = (held[7 * k : 7 * k + 7] for k in range(4))
    next_firsts, next_seconds, news = (results[7 * k : 7 * k + 7] for k in range(3))
    stores = [
        pltpu.make_async_copy(source, target, stored.at[at])
        for at, (source, target) in enumerate(zip(results, targets))
    ]
    for array in order:
        lane = STAT_LANES[array]
        norms = [stats[row : row + 1, :][:, lane : lane + 1] for row in range(2)]
        ratio = learn_rate * norms[0] / norms[1]
        count = masters[array].shape[0]
        if len(masters[array].shape) == 3:
            count = count * masters[array].shape[1]
        decay = 0.0 if array == VEC else decay_matrix

        def body(rows, array=array, ratio=ratio, decay=decay):
            if array == VEC:
                gradient = grads[VEC][:7, : masters[VEC].shape[1]]
            else:
                gradient = grads[array][rows]
            master = state_rows(masters[array], rows)
            next_one, next_two, update = moments(
                gradient,
                state_rows(firsts[array], rows),
                state_rows(seconds[array], rows),
                master,
                decay,
            )
            put_rows(next_firsts[array], rows, next_one)
            put_rows(next_seconds[array], rows, next_two)
            put_rows(news[array], rows, master - ratio * update)

        for kind in range(4):
            loads[7 * kind + array].wait()
        if array == VEC:
            body(slice(None))
        else:
            row_loop(count, state_step(count), body)
        for kind in range(3):
            stores[7 * kind + array].start()
    pairs[...] = stats[:2, :][:, :7]
    loss[...] = stats[2:3, :][:, :1]
    for store in stores:
        store.wait()


def apply_update(reduced, masters, firsts, seconds, stats):
    shapes = [jax.ShapeDtypeStruct(master.shape, f32) for master in masters]
    operands = [*reduced, *masters, *firsts, *seconds]
    in_vmem = pl.BlockSpec(memory_space=pltpu.VMEM)
    anywhere = pl.BlockSpec(memory_space=pl.ANY)
    results = pl.pallas_call(
        apply_kernel,
        out_shape=shapes * 3
        + [jax.ShapeDtypeStruct((1, 1), f32), jax.ShapeDtypeStruct((2, 7), f32)],
        in_specs=[anywhere] * 28 + [in_vmem],
        out_specs=[anywhere] * 21 + [in_vmem] * 2,
        scratch_shapes=[pltpu.VMEM(member.shape, f32) for member in operands]
        + [pltpu.VMEM(master.shape, f32) for master in masters] * 3
        + [pltpu.SemaphoreType.DMA((28,)), pltpu.SemaphoreType.DMA((21,))],
        compiler_params=pltpu.CompilerParams(vmem_limit_bytes=60 * 1024 * 1024),
        name="apply_update",
    )(*operands, stats)
    return results[:7], results[7:14], results[14:21], results[21].reshape(()), results[22]


def sinusoid_table(feature_width, grid_side, patch_count, padded):
    position = np.arange(patch_count)
    quarter = feature_width // 4
    omegas = 1.0 / 10000.0 ** (np.arange(quarter) / quarter)
    parts = []
    for coords in (position % grid_side, position // grid_side):
        angles = coords[:, None] * omegas[None, :]
        parts += [np.sin(angles), np.cos(angles)]
    table = np.concatenate(parts, axis=1).astype(np.float32)
    return jnp.asarray(np.pad(table, ((0, padded - patch_count), (0, 0))))


GROUPS = 4
ENC = dict(step=128, first=0, images=4, block=64, tokens=50, width=768, heads=3, head=64, hidden=768, spans=1)
DEC = dict(step=208, first=768, images=4, block=208, tokens=197, width=512, heads=4, head=32, hidden=512, spans=4)
CLASS_ROW = 49
MASK_ROW = 50


def dot(left, right, dims=((1,), (0,)), precision=None):
    return lax.dot_general(
        left, right, (dims, ((), ())), preferred_element_type=f32, precision=precision
    )


def dot_t(left, right):
    return dot(left, right, ((0,), (0,)))


def dot_nt(left, right):
    return dot(left, right, ((1,), (1,)))


def exact_pick(choice, values, dims):
    total = None
    for _ in range(3):
        part = values.astype(bf16)
        values = values - part.astype(f32)
        product = dot(choice, part, dims)
        total = product if total is None else total + product
    return total


def row_loop(count, step, body):
    @pl.loop(0, count // step)
    def _(k):
        body(pl.ds(pl.multiple_of(k * step, step), step))


def fold(values):
    step, width = values.shape
    return jnp.sum(values.reshape(step // 8, 8, width), axis=0)


def norm_rows(source, gain, shift, unit, inverse, low, step):
    def body(rows):
        values = source[rows]
        centred = values - jnp.mean(values, axis=-1, keepdims=True)
        scale = lax.rsqrt(jnp.mean(centred * centred, axis=-1, keepdims=True) + eps_norm)
        normed = centred * scale
        unit[rows] = normed
        inverse[rows] = scale
        low[rows] = (normed * gain + shift).astype(bf16)

    row_loop(source.shape[0], step, body)


def norm_back_rows(incoming, unit, inverse, gain, result, residual, sums, at, step):
    width = incoming.shape[-1]

    def body(rows):
        given = incoming[rows]
        normed = unit[rows]
        scaled = given * gain
        inner = (
            scaled
            - jnp.mean(scaled, axis=-1, keepdims=True)
            - normed * jnp.mean(scaled * normed, axis=-1, keepdims=True)
        )
        value = inverse[rows] * inner
        if residual is not None:
            value = value + residual[rows]
        sums[at] = sums[at] + fold(given * normed)
        sums[at + 1] = sums[at + 1] + fold(given)
        result[rows] = value

    row_loop(incoming.shape[0], step, body)


def lane_chunks(size):
    return [slice(at, min(at + 128, size)) for at in range(0, size, 128)]


def attend_mask(dims, scores, start):
    if dims["spans"] == 1:
        key = lax.broadcasted_iota(jnp.int32, scores.shape, 0)
        query = lax.broadcasted_iota(jnp.int32, scores.shape, 1) + start
        allowed = ((key // dims["block"]) == (query // dims["block"])) & (
            (key % dims["block"]) < dims["tokens"]
        )
        return jnp.where(allowed, scores, -1e30)
    first = dims["tokens"] // 16 * 16
    tail = scores[first:]
    key = lax.broadcasted_iota(jnp.int32, tail.shape, 0) + first
    return jnp.concatenate([scores[:first], jnp.where(key < dims["tokens"], tail, -1e30)], axis=0)


def layer_forward_rows(dims, stream, w_in, w_out, vectors, saved):
    unit_one, inv_one, low_one, qkv, probs, mixed, unit_two, inv_two, low_two, active, slope, work, low_work, low_more = saved
    count, width = stream.shape
    inner = dims["heads"] * dims["head"]
    span = count // dims["spans"]
    norm_rows(stream, vectors[1:2, :], vectors[2:3, :], unit_one, inv_one, low_one, dims["step"])

    @pl.loop(0, GROUPS)
    def _(t):
        weights = w_in[t, :, : 3 * inner] if inner % 128 == 0 else w_in[t][:, : 3 * inner]

        def body(rows):
            qkv[t, rows] = dot(low_one[rows], weights).astype(bf16)

        body(slice(None))

    yield "projected"
    scale = dims["head"] ** (-0.5)

    @pl.loop(0, GROUPS * dims["spans"])
    def _(k):
        t = k // dims["spans"]
        b = k % dims["spans"]
        rows = pl.ds(pl.multiple_of(b * span, span), span)
        triple = qkv[t, rows]
        query_t = triple[:, :inner].T
        value_t = triple[:, 2 * inner :].T
        heads = range(dims["heads"])
        lanes = [slice(head * dims["head"], (head + 1) * dims["head"]) for head in heads]
        for head in heads:
            key = triple[:, inner : 2 * inner][:, lanes[head]]
            work[head] = dot(key, query_t[lanes[head]])
        for head in heads:
            for columns in lane_chunks(span):
                scores = attend_mask(dims, work[head, :, columns] * scale, columns.start)
                shifted = jnp.exp(scores - jnp.max(scores, axis=0, keepdims=True))
                share = shifted * (1.0 / jnp.sum(shifted, axis=0, keepdims=True))
                probs[k * dims["heads"] + head, :, columns] = share
                low_work[head, :, columns] = share.astype(bf16)
        results = [dot(value_t[lanes[head]], low_work[head]) for head in heads]
        mixed[t, rows] = jnp.concatenate(results, axis=0).T.astype(bf16)

    yield "attended"

    @pl.loop(0, GROUPS)
    def _(t):
        weights = w_out[t, :inner]

        def body(rows):
            stream[rows] = stream[rows] + dot(mixed[t, rows], weights)

        body(slice(None))

    norm_rows(stream, vectors[3:4, :], vectors[4:5, :], unit_two, inv_two, low_two, dims["step"])

    def feed(t):
        up = w_in[t, :, 3 * inner :] if inner % 128 == 0 else w_in[t][:, 3 * inner :]
        down = w_out[t, inner:]
        slope[t] = dot(low_two[...], up)

        def bend(rows):
            hidden = slope[t, rows]
            level = 0.5 + 0.5 * lax.erf(hidden * (0.5**0.5))
            active[t, rows] = (hidden * level).astype(bf16)
            slope[t, rows] = level + hidden * (
                jnp.exp(-0.5 * hidden * hidden) * (0.5 / np.pi) ** 0.5
            )

        row_loop(count, 32, bend)
        stream[...] = stream[...] + dot(active[t], down)

    half = GROUPS // 2 if dims["spans"] == 1 else GROUPS
    pl.loop(0, half)(feed)
    if half < GROUPS:
        yield "halfway"
        pl.loop(half, GROUPS)(feed)


def layer_backward_rows(
    dims, given, spare, w_in, w_out, vectors, saved, low, flow, turned, grad_in, grad_out, sums, need, ready
):
    unit_one, inv_one, low_one, qkv, probs, mixed, unit_two, inv_two, low_two, active, slope, work, low_work, low_more = saved
    count, width = given.shape
    inner = dims["heads"] * dims["head"]
    span = count // dims["spans"]
    aligned = inner % 128 == 0

    def lower(rows):
        low[rows] = given[rows].astype(bf16)
        spare[rows] = jnp.zeros_like(spare[rows])

    row_loop(count, 32, lower)
    need("low_two", "active", "slope", "w_out", "w_in")
    turned[...] = low_two[...].T

    @pl.loop(0, GROUPS)
    def _(t):
        down = w_out[t, inner:]
        up = w_in[t, :, 3 * inner :] if aligned else w_in[t][:, 3 * inner :]
        grad_out[t, inner:] = dot_t(active[t], low[...]).astype(bf16)

        def body(rows):
            flow[rows] = (slope[t, rows] * dot_nt(low[rows], down)).astype(bf16)
            spare[rows] = spare[rows] + dot_nt(flow[rows], up)

        body(slice(None))
        grad_up = dot(turned[...], flow[...]).astype(bf16)
        if aligned:
            grad_in[t, :, 3 * inner :] = grad_up
        else:
            grad_in[t] = jnp.concatenate([jnp.zeros((width, 3 * inner), bf16), grad_up], axis=1)

    need("unit_two", "inv_two", "mixed")
    norm_back_rows(spare, unit_two, inv_two, vectors[3:4, :], given, given, sums, 3, dims["step"])
    row_loop(count, 32, lower)

    @pl.loop(0, GROUPS)
    def _(t):
        weights = w_out[t, :inner]
        grad_out[t, :inner] = dot_t(mixed[t], low[...]).astype(bf16)

        mixed[t] = dot_nt(low[...], weights).astype(bf16)
        ready("out", t)

    need("qkv", "probs")

    scale = dims["head"] ** (-0.5)

    @pl.loop(0, GROUPS * dims["spans"])
    def _(k):
        t = k // dims["spans"]
        b = k % dims["spans"]
        rows = pl.ds(pl.multiple_of(b * span, span), span)
        triple = qkv[t, rows]
        back = mixed[t, rows]
        key_t = triple[:, inner : 2 * inner].T
        back_t = back.T
        heads = range(dims["heads"])
        lanes = [slice(head * dims["head"], (head + 1) * dims["head"]) for head in heads]
        for head in heads:
            work[head] = dot(triple[:, 2 * inner :][:, lanes[head]], back_t[lanes[head]])
        for head in heads:
            for columns in lane_chunks(span):
                share = probs[k * dims["heads"] + head, :, columns]
                grad_p = work[head, :, columns]
                grad_s = share * (grad_p - jnp.sum(share * grad_p, axis=0, keepdims=True))
                low_work[head, :, columns] = grad_s.astype(bf16)
                low_more[head, :, columns] = share.astype(bf16)
        parts = ([], [], [])
        for head in heads:
            parts[0].append(dot(key_t[lanes[head]], low_work[head]) * scale)
            parts[1].append(dot(low_work[head], triple[:, :inner][:, lanes[head]]) * scale)
            parts[2].append(dot(low_more[head], back[:, lanes[head]]))
        grad_query = jnp.concatenate(parts[0], axis=0).T
        qkv[t, rows] = jnp.concatenate([grad_query] + parts[1] + parts[2], axis=1).astype(bf16)

    need("low_one", "unit_one", "inv_one")
    turned[...] = low_one[...].T

    @pl.loop(0, GROUPS)
    def _(t):
        weights = w_in[t, :, : 3 * inner] if aligned else w_in[t][:, : 3 * inner]
        grad_triple = dot(turned[...], qkv[t]).astype(bf16)
        if aligned:
            grad_in[t, :, : 3 * inner] = grad_triple
        else:
            grad_in[t] = jnp.concatenate([grad_triple, grad_in[t][:, 3 * inner :]], axis=1)

        ready("in", t)
        spare[...] = spare[...] + dot_nt(qkv[t], weights)

    norm_back_rows(spare, unit_one, inv_one, vectors[1:2, :], given, given, sums, 1, dims["step"])


def saved_shapes(dims):
    count = dims["images"] * dims["block"]
    width, inner = dims["width"], dims["heads"] * dims["head"]
    span = count // dims["spans"]
    return [
        ((count, width), f32),
        ((count, 1), f32),
        ((count, width), bf16),
        ((GROUPS, count, 3 * inner), bf16),
        ((GROUPS * dims["spans"] * dims["heads"], span, span), f32),
        ((GROUPS, count, inner), bf16),
        ((count, width), f32),
        ((count, 1), f32),
        ((count, width), bf16),
        ((GROUPS, count, dims["hidden"]), bf16),
        ((GROUPS, count, dims["hidden"]), f32),
    ]


def work_shapes(dims):
    span = dims["images"] * dims["block"] // dims["spans"]
    shape = (dims["heads"], span, span)
    return [(shape, f32), (shape, bf16), (shape, bf16)]


SAVED = (
    "unit_one", "inv_one", "low_one", "qkv", "probs", "mixed",
    "unit_two", "inv_two", "low_two", "active", "slope",
)


def loader(names, sources, targets, semaphores):
    copies = {}
    for at, (name, source, target) in enumerate(zip(names, sources, targets)):
        copies[name] = pltpu.make_async_copy(source, target, semaphores.at[at])
        copies[name].start()

    def need(*wanted):
        for name in wanted:
            if name in copies:
                copies.pop(name).wait()

    return need


def storer(held, outs, semaphores):
    def ready(kind, t):
        at = ("in", "out").index(kind)
        pltpu.make_async_copy(held[at].at[t], outs[at].at[t], semaphores.at[at]).start()

    def finish():
        for at in range(2):
            pltpu.make_async_copy(held[at], outs[at], semaphores.at[at]).wait()

    return ready, finish


def token_gain(vectors, dims):
    return vectors.at[:, pl.ds(dims["first"], dims["width"])]


def decoder_kernel(*refs):
    projected, codes, images, table, w_in_all, w_out_all, pixel_w, vectors_all = refs[:8]
    grad_in_all, grad_out_all, grad_head, grad_projected, vec_out = refs[8:13]
    stream, given, unit, inverse, low, flow, sums, loss, head, pixels_here, head_sum = refs[13:24]
    w_in, w_out, grad_in, grad_out, turned, loaded, stored = refs[24:31]
    saved = refs[31:]
    dims = DEC
    vectors = token_gain(vectors_all, dims)
    count, width = stream.shape
    block = dims["block"]
    need = loader(
        ("w_in", "w_out", "head", "images"),
        (w_in_all, w_out_all, pixel_w.at[pl.ds(PATCH_DIM, width)], images),
        (w_in, w_out, head, pixels_here),
        loaded,
    )
    ready, finish = storer((grad_in, grad_out), (grad_in_all, grad_out_all), stored)
    sums[...] = jnp.zeros_like(sums)
    loss[...] = jnp.zeros_like(loss)

    def placer(b):
        return (
            lax.broadcasted_iota(jnp.int32, (64, block), 0) == codes[b][:1, :block]
        ).astype(bf16)

    def block_rows(b):
        return pl.ds(pl.multiple_of(b * block, block), block)

    @pl.loop(0, dims["images"])
    def _(b):
        at = lax.broadcasted_iota(jnp.int32, (64, width), 0)
        source = jnp.where(at == MASK_ROW, vectors[0:1, :], projected[b])
        source = jnp.where(at > MASK_ROW, 0.0, source)
        stream[block_rows(b)] = exact_pick(placer(b), source, ((0,), (0,))) + table[...]

    need("w_in", "w_out")
    for _ in layer_forward_rows(dims, stream, w_in, w_out, vectors, saved):
        pass
    norm_rows(stream, vectors[5:6, :], vectors[6:7, :], unit, inverse, low, dims["step"])
    need("head", "images")
    head_sum[...] = jnp.zeros_like(head_sum)
    pixels_wide = pixels_here.shape[-1]
    counted = vectors_all[7:8, :]
    patch_total = jnp.sum(counted, axis=1, keepdims=True) / (counted.shape[1] // 8)

    @pl.loop(0, dims["images"])
    def _(b):
        rows = block_rows(b)
        predicted = dot(low[rows], head[...])
        pixels = pixels_here[b].astype(f32)
        centred = pixels - jnp.mean(pixels, axis=-1, keepdims=True)
        variance = jnp.sum(centred * centred, axis=-1, keepdims=True) / (pixels_wide - 1)
        errors = predicted - centred * lax.rsqrt(variance + eps_norm)
        at = lax.broadcasted_iota(jnp.int32, (64, 128), 0)
        spread = jnp.where(at == MASK_ROW, codes[b][2:3, :128].astype(f32), 0.0)
        weight = dot_t(placer(b), spread.astype(bf16))[:, :1] / patch_total
        loss[...] = loss[...] + fold(errors * errors * weight)
        grad_low = (errors * (2.0 / pixels_wide) * weight).astype(bf16)
        head_sum[...] = head_sum[...] + dot_t(low[rows], grad_low)
        given[rows] = dot_nt(grad_low, head[...])

    grad_head[...] = head_sum[...].astype(bf16)
    norm_back_rows(given, unit, inverse, vectors[5:6, :], given, None, sums, 5, dims["step"])
    layer_backward_rows(
        dims, given, stream, w_in, w_out, vectors, saved, low, flow, turned, grad_in, grad_out, sums, need, ready
    )

    @pl.loop(0, dims["images"])
    def _(b):
        back = exact_pick(placer(b), given[block_rows(b)], ((1,), (0,)))
        at = lax.broadcasted_iota(jnp.int32, (64, width), 0)
        grad_projected[b] = jnp.where(at < MASK_ROW, back, 0.0).astype(bf16)
        sums[0] = sums[0] + fold(jnp.where(at == MASK_ROW, back, 0.0))

    for row in range(7):
        vec_out[row : row + 1, :] = jnp.sum(sums[row], axis=0, keepdims=True)
    total = jnp.sum(jnp.sum(loss[...], axis=0, keepdims=True), axis=1, keepdims=True)
    vec_out[7:8, :] = jnp.broadcast_to(total / pixels_wide, (1, width))
    finish()


def decoder_step(projected, codes, images, table, w_in, w_out, pixel_w, vectors):
    dims = DEC
    count, width = dims["images"] * dims["block"], dims["width"]
    wide = images.shape[-1]
    outs = [
        jax.ShapeDtypeStruct(w_in.shape, bf16),
        jax.ShapeDtypeStruct(w_out.shape, bf16),
        jax.ShapeDtypeStruct((width, wide), bf16),
        jax.ShapeDtypeStruct(projected.shape, bf16),
        jax.ShapeDtypeStruct((8, width), f32),
    ]
    scratch = [
        ((count, width), f32),
        ((count, width), f32),
        ((count, width), f32),
        ((count, 1), f32),
        ((count, width), bf16),
        ((count, dims["hidden"]), bf16),
        ((7, 8, width), f32),
        ((8, wide), f32),
        ((width, wide), bf16),
        (images.shape, bf16),
        ((width, wide), f32),
        (w_in.shape, bf16),
        (w_out.shape, bf16),
        (w_in.shape, bf16),
        (w_out.shape, bf16),
        ((width, count), bf16),
        4,
        2,
    ]
    scratch += saved_shapes(dims) + work_shapes(dims)
    in_vmem = pl.BlockSpec(memory_space=pltpu.VMEM)
    anywhere = pl.BlockSpec(memory_space=pl.ANY)
    return pl.pallas_call(
        decoder_kernel,
        out_shape=outs,
        in_specs=[in_vmem, in_vmem, anywhere, in_vmem, anywhere, anywhere, anywhere, in_vmem],
        out_specs=[anywhere, anywhere, in_vmem, in_vmem, in_vmem],
        scratch_shapes=[
            pltpu.SemaphoreType.DMA((shape,)) if isinstance(shape, int) else pltpu.VMEM(*shape)
            for shape in scratch
        ],
        compiler_params=pltpu.CompilerParams(vmem_limit_bytes=62 * 1024 * 1024),
        name="decoder_step",
    )(projected, codes, images, table, w_in, w_out, pixel_w, vectors)


def encode_kernel(ring, *refs):
    dims = ENC
    images, keep_index, unshuffle, masked, image_valid, table = refs[:6]
    refs = refs[6:]
    group = lax.axis_index("tensor")
    if ring:
        masters, refs = refs[:7], refs[7:]
        wholes, vectors_all, codes, pictures, projected = refs[:7], *refs[7:11]
        kept_state, refs = refs[11:26], refs[26:]
        parts, send, recv, local, vec_parts = refs[:7], *refs[7:11]
        raw = dict(zip((PIX, EOUT, BRI), refs[11:14]))
        refs = refs[14:]
    else:
        wholes, vectors_all = refs[:4], refs[4]
        codes, pictures, projected, kept_state = refs[5], refs[6], refs[7], refs[8:23]
        refs = refs[23:]
        wholes = dict(zip((PIX, EIN, EOUT, BRI), wholes))
    loaded, flushed = refs[:2]
    first_copies = []
    if ring:
        shards, states_loaded, refs = refs[2:9], refs[9], refs[:2] + refs[10:]
        for at, (source, target) in enumerate(zip(masters, shards)):
            first_copies.append(pltpu.make_async_copy(source, target, states_loaded.at[at]))
            first_copies[-1].start()
        masters = shards
    eight, pixels_here, stream, w_in, w_out, embed, bridge = refs[2:9]
    retained, unit, inverse, low = refs[9:13]
    saved = refs[13:24]
    work = refs[24:]
    held = (retained, unit, inverse, low) + tuple(saved)
    vectors = token_gain(vectors_all, dims)
    count, width = stream.shape
    block = dims["block"]

    first = pl.multiple_of((group // 2) * 8, 8)
    eight_copy = pltpu.make_async_copy(images.at[:, pl.ds(first, 8)], eight, loaded.at[4])
    eight_copy.start()
    lane = lax.broadcasted_iota(jnp.int32, (1, codes.shape[2]), 1)
    valid = image_valid[...]
    image_at = lax.broadcasted_iota(jnp.int32, valid.shape, 1)
    codes[...] = jnp.full(codes.shape, -1, jnp.int32)
    for b in range(dims["images"]):
        mine = group * dims["images"] + b
        row = pl.ds(mine, 1)
        codes[b, 0:1, :] = jnp.where(lane == IMAGE_PATCHES, CLASS_ROW, -1)
        codes[b, 0:1, :IMAGE_PATCHES] = jnp.where(masked[row] == 1, MASK_ROW, unshuffle[row])
        codes[b, 1:2, :KEEP] = keep_index[row]
        own_valid = jnp.sum(
            jnp.where(image_at == mine, valid, 0).astype(f32), axis=1, keepdims=True
        )
        codes[b, 2:3, :] = jnp.broadcast_to(own_valid, (1, codes.shape[2])).astype(jnp.int32)

    def load(slot, array, target):
        if not ring:
            source = wholes[array]
            if array == PIX:
                source = source.at[pl.ds(0, PATCH_DIM)]
            pltpu.make_async_copy(source, target, loaded.at[slot]).start()
            return pltpu.make_async_copy(source, target, loaded.at[slot])
        if array != EIN:
            pltpu.make_async_copy(wholes[array], raw[array], loaded.at[slot]).start()
            return pltpu.make_async_copy(wholes[array], raw[array], loaded.at[slot])
        rows = wholes[array].shape[4]

        @pl.loop(0, 32)
        def _(k):
            pltpu.make_async_copy(
                wholes[array].at[k // 16, (k // 8) % 2, (k // 2) % 4, k % 2],
                target.at[k // 8, pl.ds(pl.multiple_of((k % 8) * rows, rows), rows)],
                loaded.at[slot],
            ).start()

        return pltpu.make_async_copy(target, target, loaded.at[slot])

    def assemble(array, target):
        if ring and array in SHARED:
            count = -(-target.shape[0] // raw[array].shape[4])
            pieces = [
                raw[array][k // 8, (k // 4) % 2, (k // 2) % 2, k % 2] for k in range(count)
            ]
            target[...] = jnp.concatenate(pieces, axis=0)[: target.shape[0]]
        elif ring:

            @pl.loop(0, GROUPS)
            def _(t):
                pieces = [raw[array][t // 2, t % 2, k // 2, k % 2] for k in range(8)]
                target[t] = jnp.concatenate(pieces, axis=0)

    flushes = []

    def flush(*members):
        for member in members:
            copy = pltpu.make_async_copy(held[member], kept_state[member], flushed.at[member])
            copy.start()
            flushes.append(copy)

    for copy in first_copies:
        copy.wait()
    if ring:
        for array in range(6):
            if array in SHARED:
                rows = masters[array].shape[0] // 4
                rows = pl.ds(pl.multiple_of(group * rows, 8), rows)
                parts[array][...] = masters[array][rows].astype(bf16)
            else:
                parts[array][...] = state_rows(masters[array], slice(None)).astype(bf16)
        columns = masters[VEC].shape[1]
        parts[VEC][...] = jnp.zeros_like(parts[VEC])
        parts[VEC][:7, :columns] = masters[VEC][...].astype(bf16).astype(f32)
        counts = dot(valid.astype(bf16), masked[...].astype(f32).astype(bf16))
        counted = jnp.sum(counts, axis=1, keepdims=True)
        parts[VEC][7:8, :] = jnp.broadcast_to(counted, (1, parts[VEC].shape[1]))
        ticks = gather_ticks(parts, wholes, send, recv, local)

    done = [-1]

    def until(tick):
        while ring and done[0] < tick:
            next(ticks)
            done[0] += 1

    at_embed, at_in, at_out = (
        last_step(GATHER_STEPS, array) + DEPTH for array in (PIX, EIN, EOUT)
    )
    at_end = len(GATHER_STEPS) - 1 + DEPTH
    until(0)
    eight_copy.wait()
    pixels_wide = eight.shape[2]

    @pl.loop(0, dims["images"])
    def _(b):
        size = (pixels_here.shape[1], IMAGE_PATCHES * 8)
        patch = lax.broadcasted_iota(jnp.int32, size, 0)
        at = lax.broadcasted_iota(jnp.int32, size, 1)
        wanted = patch * 8 + (group % 2) * dims["images"] + b
        choice = (at == wanted) & (patch < IMAGE_PATCHES)
        flat = eight[...].reshape(IMAGE_PATCHES * 8, pixels_wide)
        pixels_here[b] = dot(choice.astype(f32).astype(bf16), flat).astype(bf16)

    picture_copy = pltpu.make_async_copy(pixels_here, pictures, loaded.at[5])
    picture_copy.start()
    until(at_embed)
    embed_copy = load(0, PIX, embed)
    if ring:
        vec_copy = pltpu.make_async_copy(wholes[VEC], vec_parts, loaded.at[1])
        vec_copy.start()
        vec_copy.wait()
        vectors_all[...] = jnp.concatenate(
            [vec_parts[0, 0, k // 2, k % 2][:, :columns] for k in range(8)], axis=1
        )
    embed_copy.wait()
    assemble(PIX, embed)

    @pl.loop(0, dims["images"])
    def _(b):
        rows = pl.ds(pl.multiple_of(b * block, block), block)
        choice = (
            lax.broadcasted_iota(jnp.int32, (table.shape[0], block), 0) == codes[b][1:2, :block]
        )
        retained[rows] = dot_t(choice.astype(bf16), pixels_here[b]).astype(bf16)
        places = exact_pick(choice.astype(bf16), table[...], ((0,), (0,)))
        at = lax.broadcasted_iota(jnp.int32, (block, width), 0)
        start = dot(retained[rows], embed[...]) + places
        stream[rows] = jnp.where(at == CLASS_ROW, vectors[0:1, :], start)

    flush(0)
    until(at_in)
    load(2, EIN, w_in).wait()
    layer = layer_forward_rows(dims, stream, w_in, w_out, vectors, saved + work)
    next(layer)
    until(at_in + 1)
    next(layer)
    flush(4, 5, 6, 7, 8, 9)
    until(at_out)
    bridge_copy = load(1, BRI, bridge)
    load(3, EOUT, w_out).wait()
    assemble(EOUT, w_out)
    next(layer)
    flush(10, 11, 12)
    until(at_out + 1)
    for _ in layer:
        pass
    flush(13, 14)
    until(at_out + 2)
    norm_rows(stream, vectors[5:6, :], vectors[6:7, :], unit, inverse, low, dims["step"])
    flush(1, 2, 3)
    bridge_copy.wait()
    assemble(BRI, bridge)

    @pl.loop(0, dims["images"])
    def _(b):
        rows = pl.ds(pl.multiple_of(b * block, block), block)
        projected[b] = dot(low[rows], bridge[...])

    until(at_end + 1)
    picture_copy.wait()
    for copy in flushes:
        copy.wait()


def encode(images, indices, table, weights, vectors=None):
    dims = ENC
    ring = vectors is None
    count, width = dims["images"] * dims["block"], dims["width"]
    bridge_wide = weights[BRI].shape[-1]
    in_vmem = pl.BlockSpec(memory_space=pltpu.VMEM)
    anywhere = pl.BlockSpec(memory_space=pl.ANY)
    kept_shapes = [
        ((count, images.shape[2]), bf16),
        ((count, width), f32),
        ((count, 1), f32),
        ((count, width), bf16),
    ] + saved_shapes(dims)
    picture_shape = (dims["images"], DEC["block"], images.shape[2])
    outs = [((dims["images"], 8, 256), jnp.int32), (picture_shape, bf16)]
    outs += [((dims["images"], dims["block"], bridge_wide), f32)] + kept_shapes
    out_specs = [in_vmem, anywhere, in_vmem] + [anywhere] * len(kept_shapes)
    in_specs = [anywhere] + [in_vmem] * 5
    scratch = []
    if ring:
        shapes = []
        for array in range(6):
            rows, wide = weights[array].size // weights[array].shape[-1], weights[array].shape[-1]
            shapes.append((rows // 4 if array in SHARED else rows, wide))
        shapes.append((8, 256))
        types = [bf16] * 6 + [f32]
        operands = [images, *indices, table, *weights]
        in_specs += [anywhere] * 7
        gathered = [(whole_shape(k, shape), types[k]) for k, shape in enumerate(shapes)]
        outs = gathered + [((8, shapes_total(weights[VEC])), f32)] + outs
        out_specs = [anywhere] * 7 + [in_vmem] + out_specs
        units = sum(len(step) for step in GATHER_STEPS)
        scratch += [pltpu.VMEM(shape, kind) for shape, kind in zip(shapes, types)]
        scratch += [
            pltpu.SemaphoreType.DMA((units, 6)),
            pltpu.SemaphoreType.DMA((units, 6)),
            pltpu.SemaphoreType.DMA((7,)),
            pltpu.VMEM(whole_shape(VEC, shapes[VEC]), f32),
        ]
        scratch += [
            pltpu.VMEM(whole_shape(array, shapes[array]), bf16) for array in (PIX, EOUT, BRI)
        ]
        params = dict(collective_id=0, has_side_effects=True)
        w_shapes = [
            (GROUPS, 8 * shapes[EIN][0], shapes[EIN][1]),
            (GROUPS, 8 * shapes[EOUT][0], shapes[EOUT][1]),
        ]
    else:
        operands = [images, *indices, table] + [weights[k] for k in (PIX, EIN, EOUT, BRI)] + [vectors]
        in_specs += [anywhere] * 4 + [in_vmem]
        params = {}
        w_shapes = [weights[EIN].shape, weights[EOUT].shape]
    scratch += [pltpu.SemaphoreType.DMA((8,)), pltpu.SemaphoreType.DMA((15,))]
    if ring:
        scratch += [pltpu.VMEM(member.shape, f32) for member in weights]
        scratch += [pltpu.SemaphoreType.DMA((7,))]
    buffers = [
        ((images.shape[0], 8, images.shape[2]), bf16),
        (picture_shape, bf16),
        ((count, width), f32),
        (w_shapes[0], bf16),
        (w_shapes[1], bf16),
        ((PATCH_DIM, width), bf16),
        ((width, bridge_wide), bf16),
    ]
    buffers += kept_shapes + work_shapes(dims)
    scratch += [pltpu.VMEM(*buffer) for buffer in buffers]
    return pl.pallas_call(
        functools.partial(encode_kernel, ring),
        out_shape=[jax.ShapeDtypeStruct(shape, kind) for shape, kind in outs],
        in_specs=in_specs,
        out_specs=out_specs,
        scratch_shapes=scratch,
        compiler_params=pltpu.CompilerParams(vmem_limit_bytes=62 * 1024 * 1024, **params),
        name="gather_encode" if ring else "encode",
    )(*operands)


def shapes_total(vector_shard):
    return 8 * vector_shard.shape[1]


def encoder_backward_kernel(*refs):
    grad_projected = refs[0]
    sources = refs[1:18]
    bridge, vectors_all, grad_head, dec_sums = refs[18:22]
    grad_in_all, grad_out_all, grad_bridge, grad_pixel, packed = refs[22:27]
    given, spare, low, flow, sums, vec_all, turned = refs[27:34]
    held = refs[34:51]
    grad_in, grad_out, loaded, stored = refs[51:55]
    names = ("retained", "unit", "inverse", "low_end") + SAVED + ("w_in", "w_out")
    order = (3, 1, 2, 12, 13, 14, 16, 15, 10, 11, 9, 7, 8, 6, 4, 5, 0)
    need = loader(
        [names[k] for k in order], [sources[k] for k in order], [held[k] for k in order], loaded
    )
    ready, finish = storer((grad_in, grad_out), (grad_in_all, grad_out_all), stored)
    retained, unit, inverse, low_end = held[:4]
    saved = held[4:15] + refs[55:]
    w_in, w_out = held[15:17]
    dims = ENC
    vectors = token_gain(vectors_all, dims)
    count, width = given.shape
    block = dims["block"]
    sums[...] = jnp.zeros_like(sums)

    need("low_end", "unit", "inverse")
    flat = grad_projected[...].reshape(count, grad_projected.shape[-1])
    grad_bridge[...] = dot_t(low_end[...], flat).astype(bf16)
    given[...] = dot_nt(flat, bridge[...])
    norm_back_rows(given, unit, inverse, vectors[5:6, :], given, None, sums, 5, dims["step"])
    layer_backward_rows(
        dims, given, spare, w_in, w_out, vectors, saved, low, flow, turned, grad_in, grad_out, sums, need, ready
    )
    need("retained")
    grad_pixel[:PATCH_DIM] = dot_t(retained[...], given[...].astype(bf16)).astype(bf16)
    grad_pixel[PATCH_DIM:] = grad_head[...]

    def tokens(rows):
        at = lax.broadcasted_iota(jnp.int32, (block, width), 0)
        sums[0] = sums[0] + fold(jnp.where(at == CLASS_ROW, given[rows], 0.0))

    row_loop(count, block, tokens)
    for row in range(7):
        vec_all[row : row + 1, :width] = jnp.sum(sums[row], axis=0, keepdims=True)
    vec_all[7:8, :width] = jnp.zeros((1, width), f32)
    vec_all[:, width:] = dec_sums[...]
    columns = vec_all.shape[1] // 8
    packed[...] = jnp.zeros_like(packed)
    for k in range(8):
        packed[k, :, :columns] = vec_all[:, k * columns : (k + 1) * columns]
    finish()


def encoder_backward(grad_projected, kept_state, w_in, w_out, bridge, vectors, grad_head, dec_sums):
    dims = ENC
    count, width = dims["images"] * dims["block"], dims["width"]
    pixels_wide = kept_state[0].shape[1]
    outs = [
        jax.ShapeDtypeStruct(w_in.shape, bf16),
        jax.ShapeDtypeStruct(w_out.shape, bf16),
        jax.ShapeDtypeStruct(bridge.shape, bf16),
        jax.ShapeDtypeStruct((pixels_wide + grad_head.shape[0], width), bf16),
        jax.ShapeDtypeStruct((8, 8, 256), f32),
    ]
    scratch = [
        ((count, width), f32),
        ((count, width), f32),
        ((count, width), bf16),
        ((count, dims["hidden"]), bf16),
        ((7, 8, width), f32),
        (vectors.shape, f32),
        ((width, count), bf16),
    ]
    kept_shapes = [(member.shape, member.dtype) for member in kept_state]
    scratch += kept_shapes + [(w_in.shape, bf16), (w_out.shape, bf16)]
    scratch += [(w_in.shape, bf16), (w_out.shape, bf16), 17, 2] + work_shapes(dims)
    in_vmem = pl.BlockSpec(memory_space=pltpu.VMEM)
    anywhere = pl.BlockSpec(memory_space=pl.ANY)
    return pl.pallas_call(
        encoder_backward_kernel,
        out_shape=outs,
        in_specs=[in_vmem] + [anywhere] * 17 + [in_vmem] * 4,
        out_specs=[anywhere] * 2 + [in_vmem] * 3,
        scratch_shapes=[
            pltpu.SemaphoreType.DMA((shape,)) if isinstance(shape, int) else pltpu.VMEM(*shape)
            for shape in scratch
        ],
        compiler_params=pltpu.CompilerParams(vmem_limit_bytes=62 * 1024 * 1024),
        name="encoder_backward",
    )(grad_projected, *kept_state, w_in, w_out, bridge, vectors, grad_head, dec_sums)


def gather_grouped(part, groups):
    whole = lax.all_gather(part, GROUPED, axis=0, tiled=True)
    return whole.reshape(groups, -1, whole.shape[-1])


def scatter_grouped(gradient):
    flat = gradient.astype(f32).reshape(-1, gradient.shape[-1])
    return lax.psum_scatter(flat, GROUPED, scatter_dimension=0, tiled=True)


def ringed(tensor_count):
    return tensor_count == 4 and lax.axis_size("dp") == 8


def plain_gather(masters, counted):
    groups = lax.axis_size("tensor")
    wholes = {}
    for array, k in ((EIN, 0), (EOUT, 1), (DIN, 2), (DOUT, 3)):
        flat = masters[k].reshape(-1, masters[k].shape[-1]).astype(bf16)
        wholes[array] = gather_grouped(flat, groups)
    for array, k in ((PIX, 4), (BRI, 5)):
        wholes[array] = lax.all_gather(masters[k].astype(bf16), "dp", axis=0, tiled=True)
    low = masters[6].astype(bf16).astype(f32)
    vectors = lax.all_gather(low, "dp", axis=1, tiled=True)
    eighth = jnp.broadcast_to(lax.psum(counted, "dp") / 8, (1, vectors.shape[1]))
    return wholes, jnp.concatenate([vectors, eighth], axis=0)


def ring_finish(gradients, masters, firsts, seconds):
    grouped, grad_pixel, grad_bridge, packed = gradients
    tensor_count = lax.axis_size("tensor")
    order = (4, 0, 1, 5, 2, 3, 6)
    sources = (grad_pixel, grouped[0], grouped[1], grad_bridge, grouped[2], grouped[3])
    operands = []
    for array, source in enumerate(sources):
        master = masters[order[array]]
        rows, wide = master.size // master.shape[-1], master.shape[-1]
        if array in SHARED:
            rows = rows // tensor_count
        operands.append(source.reshape(whole_shape(array, (rows, wide))))
    operands.append(packed)
    states = [[members[k] for k in order] for members in (masters, firsts, seconds)]
    *sums, stats = scatter_gradients(operands, *states)
    for array in SHARED:
        sums[array] = sums[array].reshape(-1, sums[array].shape[-1])
    *results, loss_value, pairs = apply_update(sums, *states, stats)
    place_of = {k: at for at, k in enumerate(order)}
    results = [[members[place_of[k]] for k in range(7)] for members in results]
    return (loss_value, pairs, *results[0], *results[1], *results[2])


def plain_finish(gradients, masters, firsts, seconds):
    grouped, grad_pixel, grad_bridge, packed = gradients
    tensor_count = lax.axis_size("tensor")
    columns = masters[6].shape[1]

    def scatter_shared(gradient):
        part = lax.psum_scatter(gradient.astype(f32), EVERY, scatter_dimension=0, tiled=True)
        return lax.all_gather(part, "tensor", axis=0, tiled=True)

    reduced = [scatter_grouped(gradient) for gradient in grouped]
    reduced += [scatter_shared(grad_pixel), scatter_shared(grad_bridge)]
    whole = packed.shape[0] * (ENCODER_WIDTH + D_D) // 8
    packed = packed[:, :, : whole // packed.shape[0]].transpose(1, 0, 2).reshape(8, -1)
    vector_sum = lax.psum(packed, EVERY)
    own = lax.dynamic_slice_in_dim(
        vector_sum[:7], lax.axis_index("dp") * columns, columns, axis=1
    )
    reduced = [gradient.reshape(master.shape) for gradient, master in zip(reduced + [own], masters)]
    decays = (decay_matrix,) * 6 + (0.0,)
    share_counts = (1.0,) * 4 + (float(tensor_count),) * 3
    steps = [moments(*member) for member in zip(reduced, firsts, seconds, masters, decays)]
    new_firsts, new_seconds, updates = zip(*steps)

    def squares(members):
        return jnp.stack(
            [jnp.sum(member * member) / count for member, count in zip(members, share_counts)]
        )

    weight_norm, update_norm = map(
        jnp.sqrt, lax.psum((squares(masters), squares(updates)), EVERY)
    )
    ratio = learn_rate * weight_norm / update_norm
    news = [
        master - ratio[position] * update
        for position, (master, update) in enumerate(zip(masters, updates))
    ]
    return (vector_sum[7, -1], jnp.stack([weight_norm, update_norm]), *new_firsts, *new_seconds, *news)


def shards(
    images,
    keep_index,
    unshuffle,
    masked,
    image_valid,
    *state,
):
    masters, firsts, seconds = state[:7], state[7:14], state[14:21]
    tensor_count = lax.axis_size("tensor")
    enc_table, dec_table = (
        sinusoid_table(width, GRID_PATCHES, IMAGE_PATCHES, DEC["block"])
        for width in (ENCODER_WIDTH, D_D)
    )
    indices = (keep_index, unshuffle, masked, image_valid[None, :])
    by_patch = images.transpose(1, 0, 2)
    if ringed(tensor_count):
        order = (4, 0, 1, 5, 2, 3, 6)
        results = encode(by_patch, indices, enc_table, [masters[k] for k in order])
        wholes, results = results[:7], results[7:]
        vectors, codes, pictures, projected, *enc_state = results
        wholes = [
            whole.reshape(-1, whole.shape[-1])
            if array in SHARED
            else whole.reshape(tensor_count, -1, whole.shape[-1])
            for array, whole in enumerate(wholes)
        ]
    else:
        counted = jnp.sum(masked.astype(f32) * image_valid.astype(f32)[:, None])
        wholes, vectors = plain_gather(masters, counted)
        codes, pictures, projected, *enc_state = encode(
            by_patch, indices, enc_table, wholes, vectors=vectors
        )
    grad_dec_in, grad_dec_out, grad_head, grad_projected, dec_sums = decoder_step(
        projected, codes, pictures, dec_table, wholes[DIN], wholes[DOUT], wholes[PIX], vectors
    )
    grad_enc_in, grad_enc_out, grad_bridge, grad_pixel, packed = encoder_backward(
        grad_projected,
        enc_state,
        wholes[EIN],
        wholes[EOUT],
        wholes[BRI],
        vectors,
        grad_head,
        dec_sums,
    )
    finish = ring_finish if ringed(tensor_count) else plain_finish
    return finish(
        ([grad_enc_in, grad_enc_out, grad_dec_in, grad_dec_out], grad_pixel, grad_bridge, packed),
        masters,
        firsts,
        seconds,
    )


def solution(mesh):
    state_specs = (
        P("dp", "tensor", None),
        P("tensor", "dp", None),
        P("dp", "tensor", None),
        P("tensor", "dp", None),
        P("dp", None),
        P("dp", None),
        P(None, "dp"),
    )
    in_specs = (
        P("dp", None, None),
        P("dp", None),
        P("dp", None),
        P("dp", None),
        P("dp"),
    ) + state_specs * 3
    out_specs = (P(), P()) + state_specs * 3
    return jax.shard_map(shards, mesh=mesh, in_specs=in_specs, out_specs=out_specs, check_vma=False)
```

```python
import functools

import jax
import jax.numpy as jnp
from jax import lax
from jax.experimental import pallas as pl
from jax.experimental.pallas import tpu as pltpu
from jax.sharding import PartitionSpec as P
import numpy as np

ENCODER_WIDTH = 768
H_E = 12
HD_E = 64
D_D = 512
H_D = 16
HD_D = 32
PATCH_DIM = 768
GRID_PATCHES = 14
IMAGE_PATCHES = 196
KEEP = 49

eps_norm = 1e-06
beta_one = 0.9
beta_two = 0.999
step_count = 7.0
learn_rate = 0.3
decay_matrix = 0.05
eps_moment = 1e-06
f32 = jnp.float32
bf16 = jnp.bfloat16
EVERY = ("dp", "tensor")
GROUPED = ("tensor", "dp")


MESH_ID = pl.DeviceIdType.MESH
PIX, EIN, EOUT, BRI, DIN, DOUT, VEC = range(7)


def place():
    dp_at = lax.axis_index("dp")
    group = lax.axis_index("tensor")
    z, x = lax.div(dp_at, 2), lax.rem(dp_at, 2)
    y, c = lax.div(group, 2), lax.rem(group, 2)
    return z, x, y, c


def device(z, x, y, c):
    return (z * 2 + x, y * 2 + c)


def flip(z, m):
    low = lax.rem(z, 2)
    high = lax.div(z, 2)
    if m % 2:
        low = 1 - low
    if m // 2:
        high = 1 - high
    return high * 2 + low


def greet(z, x, y, c):
    barrier = pltpu.get_barrier_semaphore()
    peers = [device(flip(z, m), x, y, c) for m in (1, 2, 3)]
    for m in range(1, 8):
        peers.append(
            device(
                z,
                1 - x if m // 4 else x,
                1 - y if (m // 2) % 2 else y,
                1 - c if m % 2 else c,
            )
        )
    for peer in peers:
        pl.semaphore_signal(barrier, inc=1, device_id=peer, device_id_type=MESH_ID)
    pl.semaphore_wait(barrier, len(peers))


SHARED = (PIX, BRI)


def spot(array, y, c, z, x):
    return (z, x, y, c) if array in SHARED else (y, c, z, x)


def half_spot(array, y, z, x):
    return (z, x, y) if array in SHARED else (y, z, x)


def whole_shape(array, part):
    return ((4, 2, 2, 2) if array in SHARED else (2, 2, 4, 2)) + part


GATHER_STEPS = (
    ((VEC, 0, 8, 0), (PIX, 0, 24, 0), (PIX, 24, 16, 1)),
    ((EIN, 0, 16, 0), (EIN, 16, 16, 1)),
    ((EIN, 32, 16, 0), (EIN, 48, 16, 1)),
    ((EIN, 64, 16, 0), (EIN, 80, 16, 1)),
    ((EOUT, 0, 24, 0), (EOUT, 24, 24, 1)),
    ((EOUT, 48, 24, 0), (EOUT, 72, 24, 1)),
    ((EOUT, 96, 8, 0), (EOUT, 104, 16, 1), (BRI, 0, 16, 0), (BRI, 16, 8, 1)),
    ((DIN, 0, 16, 0), (DIN, 16, 16, 1)),
    ((DIN, 32, 16, 0), (DIN, 48, 16, 1)),
    ((DOUT, 0, 16, 0), (DOUT, 16, 32, 1)),
    ((DOUT, 48, 16, 0), (DOUT, 64, 16, 1)),
)
DEPTH = 4


def last_step(steps, array):
    return max(at for at, step in enumerate(steps) for unit in step if unit[0] == array)


def gather_ticks(parts, outs, send, recv, local):
    count = 7
    z, x, y, c = place()
    units = []
    for at, step in enumerate(GATHER_STEPS):
        for unit in step:
            units.append((at,) + unit)
    copies = {}

    def rows(array, region, first, size):
        ref = outs[array]
        return ref.at[region + (pl.ds(first, size),)]

    def plan(number, stage):
        at, array, first, size, turn = units[number]
        every = slice(None)
        if stage < 3:
            src = parts[array].at[pl.ds(first, size)]
            dst = rows(array, spot(array, y, c, z, x), first, size)
            peer = device(flip(z, stage + 1), x, y, c)
        else:
            if stage == 3:
                region = spot(array, y, c, every, x)
                peer = device(z, x, 1 - y, c) if turn == 0 else device(z, 1 - x, y, c)
            elif stage == 4 and turn == 0:
                region = spot(array, every, c, every, x)
                peer = device(z, 1 - x, y, c)
            elif stage == 4:
                region = spot(array, y, c, every, every)
                peer = device(z, x, 1 - y, c)
            else:
                region = spot(array, every, c, every, every)
                peer = device(z, x, y, 1 - c)
            src = dst = rows(array, region, first, size)
        return pltpu.make_async_remote_copy(
            src_ref=src,
            dst_ref=dst,
            send_sem=send.at[number, stage],
            recv_sem=recv.at[number, stage],
            device_id=peer,
            device_id_type=MESH_ID,
        )

    def start(number, stage):
        copies[number, stage] = plan(number, stage)
        copies[number, stage].start()

    own = []
    for array in range(count):
        own.append(
            pltpu.make_async_copy(parts[array], outs[array].at[spot(array, y, c, z, x)], local.at[array])
        )
        own[-1].start()
    greet(z, x, y, c)
    steps = len(GATHER_STEPS)
    waited = set()
    for tick in range(steps + 4):
        for number, unit in enumerate(units):
            if unit[0] == tick:
                for stage in range(3):
                    start(number, stage)
        for number, unit in enumerate(units):
            if unit[0] == tick - 1:
                if unit[1] not in waited:
                    waited.add(unit[1])
                    own[unit[1]].wait()
                for stage in range(3):
                    copies[number, stage].wait_recv()
                start(number, 3)
        for back in (2, 3):
            for number, unit in enumerate(units):
                if unit[0] == tick - back:
                    copies[number, back + 1].wait_recv()
                    start(number, back + 2)
        for number, unit in enumerate(units):
            if unit[0] == tick - 4:
                copies[number, 5].wait_recv()
        if tick < steps + 3:
            yield tick
    for key in copies:
        copies[key].wait_send()
    yield steps + 3
    yield None


SCATTER_STEPS = (
    ((BRI, 0, 8, 0), (BRI, 8, 16, 1)),
    ((PIX, 0, 24, 0), (PIX, 24, 16, 1)),
    ((EIN, 0, 16, 0), (EIN, 16, 16, 1)),
    ((EIN, 32, 16, 0), (EIN, 48, 16, 1)),
    ((EIN, 64, 16, 0), (EIN, 80, 16, 1)),
    ((EOUT, 0, 24, 0), (EOUT, 24, 24, 1)),
    ((EOUT, 48, 24, 0), (EOUT, 72, 24, 1)),
    ((EOUT, 96, 8, 0), (EOUT, 104, 16, 1)),
    ((DIN, 0, 16, 0), (DIN, 16, 16, 1)),
    ((DIN, 32, 16, 0), (DIN, 48, 16, 1)),
    ((DOUT, 0, 24, 0), (DOUT, 24, 24, 1)),
    ((DOUT, 48, 16, 0), (DOUT, 64, 16, 1)),
)


STAT_LANES = {EIN: 0, EOUT: 1, DIN: 2, DOUT: 3, PIX: 4, BRI: 5, VEC: 6}


def state_rows(ref, rows):
    if len(ref.shape) == 2:
        return ref[rows]
    return ref[rows, 0, :] if ref.shape[1] == 1 else ref[0, rows, :]


def put_rows(ref, rows, values):
    if len(ref.shape) == 2:
        ref[rows] = values
    elif ref.shape[1] == 1:
        ref[rows, 0, :] = values
    else:
        ref[0, rows, :] = values


def moments(gradient, moment_one, moment_two, master, decay):
    next_one = beta_one * moment_one + (1.0 - beta_one) * gradient
    next_two = beta_two * moment_two + (1.0 - beta_two) * gradient * gradient
    bias_one = 1.0 - beta_one**step_count
    bias_two = 1.0 - beta_two**step_count
    update = next_one / bias_one / (jnp.sqrt(next_two / bias_two) + eps_moment) + decay * master
    return next_one, next_two, update


def state_step(rows):
    return next(step for step in (32, 40, rows) if rows % step == 0)


def scatter_kernel(shapes, units, *refs):
    grads = refs[:7]
    sources, results = refs[7:28], refs[28:36]
    refs = refs[36:]
    n = len(units)
    own, one, two, three, four = (refs[k * n : (k + 1) * n] for k in range(5))
    vec_one, vec_two, vec_three, vec_four, vec_sum = refs[5 * n : 5 * n + 5]
    stats, stat_one, stat_four = refs[5 * n + 5 : 5 * n + 8]
    send, recv, local, vsend, vrecv, tsend, trecv, ssend, srecv = refs[5 * n + 8 : 5 * n + 17]
    refs = refs[5 * n + 17 :]
    held, outs, loaded, stored = refs[:21], refs[21:28] + results[7:], *refs[28:]
    masters, firsts, seconds = held[:7], held[7:14], held[14:]
    state_copies = [
        pltpu.make_async_copy(source, target, loaded.at[at])
        for at, (source, target) in enumerate(zip(sources, held))
    ]
    for copy in state_copies:
        copy.start()
    stores = []
    z, x, y, c = place()
    every = slice(None)
    copies = {}
    stat_row = lax.broadcasted_iota(jnp.int32, (8, 128), 0)
    stat_lane = lax.broadcasted_iota(jnp.int32, (8, 128), 1)

    def tally(array):
        stores.append(pltpu.make_async_copy(outs[array], results[array], stored.at[array]))
        stores[-1].start()
        for kind in range(3):
            state_copies[7 * kind + array].wait()
        if array == VEC:
            gradient = outs[VEC][:7, : masters[VEC].shape[1]]
            update = moments(
                gradient, firsts[VEC][...], seconds[VEC][...], masters[VEC][...], 0.0
            )[2]
            squares = [jnp.sum(v * v, axis=0, keepdims=True) for v in (masters[VEC][...], update)]
        else:
            flat = (array in SHARED) and outs[array].shape[0] == 4
            count = outs[array].shape[0] * outs[array].shape[1] if flat else outs[array].shape[0]
            columns = outs[array].shape[-1]
            step = outs[array].shape[1] if flat else state_step(count)

            def body(k, carry):
                rows = pl.ds(pl.multiple_of(k * step, 8), step)
                gradient = outs[array][k] if flat else outs[array][rows]
                master = state_rows(masters[array], rows)
                update = moments(
                    gradient,
                    state_rows(firsts[array], rows),
                    state_rows(seconds[array], rows),
                    master,
                    decay_matrix,
                )[2]
                return tuple(
                    total + jnp.sum((v * v).reshape(step // 8, 8, columns), axis=0)
                    for total, v in zip(carry, (master, update))
                )

            start = (jnp.zeros((8, columns), f32),) * 2
            squares = [
                jnp.sum(v, axis=0, keepdims=True)
                for v in lax.fori_loop(0, count // step, body, start)
            ]
        share = 0.25 if array in SHARED + (VEC,) else 1.0
        total = stats[...]
        for row, square in enumerate(squares):
            value = jnp.sum(square, axis=1, keepdims=True) * share
            total = total + jnp.where((stat_row == row) & (stat_lane == STAT_LANES[array]), value, 0.0)
        stats[...] = total

    def remote(src, dst, key, send_sem, recv_sem, peer):
        copies[key] = pltpu.make_async_remote_copy(
            src_ref=src,
            dst_ref=dst,
            send_sem=send_sem,
            recv_sem=recv_sem,
            device_id=peer,
            device_id_type=MESH_ID,
        )
        copies[key].start()

    def start(number, stage):
        at, array, first, size, turn = units[number]
        mine = own[number]
        if stage == 0:
            peer = device(z, x, y, 1 - c)
            src = grads[array].at[
                spot(array, every, 1 - c, every, every) + (pl.ds(first, size),)
            ]
            dst = one[number]
        elif stage == 1 and turn == 0:
            peer = device(z, 1 - x, y, c)
            src, dst = mine.at[half_spot(array, every, every, 1 - x)], two[number]
        elif stage == 1:
            peer = device(z, x, 1 - y, c)
            src, dst = mine.at[half_spot(array, 1 - y, every, every)], two[number]
        elif stage == 2 and turn == 0:
            peer = device(z, x, 1 - y, c)
            src, dst = mine.at[half_spot(array, 1 - y, every, x)], three[number]
        elif stage == 2:
            peer = device(z, 1 - x, y, c)
            src, dst = mine.at[half_spot(array, y, every, 1 - x)], three[number]
        else:
            other = flip(z, stage - 2)
            peer = device(other, x, y, c)
            src, dst = mine.at[half_spot(array, y, other, x)], four[number].at[stage - 3]
        remote(src, dst, (number, stage), send.at[number, stage], recv.at[number, stage], peer)

    def add(number, stage):
        at, array, first, size, turn = units[number]
        mine = own[number]

        def pair(here, there):
            mine[here] = (mine[here].astype(f32) + there.astype(f32)).astype(bf16)

        if stage == 0:

            @pl.loop(0, 16)
            def _(k):
                iy, iz, ix = k // 8, (k // 2) % 4, k % 2
                here = half_spot(array, iy, iz, ix)
                pair(here, one[number][here])

        elif stage == 1 and turn == 0:

            @pl.loop(0, 8)
            def _(k):
                iy, iz = k // 4, k % 4
                there = (iz, iy) if array in SHARED else (iy, iz)
                pair(half_spot(array, iy, iz, x), two[number][there])

        elif stage == 1:

            @pl.loop(0, 8)
            def _(k):
                iz, ix = k // 2, k % 2
                pair(half_spot(array, y, iz, ix), two[number][iz, ix])

        elif stage == 2:

            @pl.loop(0, 4)
            def _(k):
                pair(half_spot(array, y, k, x), three[number][k])

        else:
            total = mine[half_spot(array, y, z, x)].astype(f32)
            for slot in range(3):
                total = total + four[number][slot].astype(f32)
            if array in SHARED:
                outs[array][y * 2 + c, pl.ds(first, size)] = total
            else:
                outs[array][pl.ds(first, size)] = total

    loads = []
    for number, (at, array, first, size, turn) in enumerate(units):
        loads.append(
            pltpu.make_async_copy(
                grads[array].at[spot(array, every, c, every, every) + (pl.ds(first, size),)],
                own[number],
                local.at[number],
            )
        )
    stats[...] = jnp.zeros_like(stats)
    greet(z, x, y, c)
    steps = units[-1][0] + 1

    def step_units(tick):
        return [number for number in range(n) if units[number][0] == tick]

    vec_dst = (vec_one, vec_two, vec_three)
    vec_peer = (device(z, x, y, 1 - c), device(z, 1 - x, y, c), device(z, x, 1 - y, c))

    for tick in range(steps + 4):
        for number in step_units(tick):
            loads[number].start()
            start(number, 0)
        for number in step_units(tick - 1):
            loads[number].wait()
            copies[number, 0].wait_recv()
            add(number, 0)
            start(number, 1)
        for number in step_units(tick - 2):
            copies[number, 1].wait()
            add(number, 1)
            start(number, 2)
        for number in step_units(tick - 3):
            copies[number, 2].wait()
            add(number, 2)
            for stage in (5, 4, 3):
                start(number, stage)
        for number in step_units(tick - 4):
            for stage in (3, 4, 5):
                copies[number, stage].wait()
            add(number, 3)
        if tick == 0:
            vec_sum[...] = grads[6][...]
        if 1 <= tick <= 3:
            copies["v", tick - 1].wait()
            vec_sum[...] = vec_sum[...] + vec_dst[tick - 1][...]
        if tick < 3:
            remote(vec_sum, vec_dst[tick], ("v", tick), vsend.at[tick], vrecv.at[tick], vec_peer[tick])
        elif tick == 3:
            vec_four[z] = vec_sum[...]
            for m in (1, 2, 3):
                peer = device(flip(z, m), x, y, c)
                remote(vec_sum, vec_four.at[z], ("v", 2 + m), vsend.at[2 + m], vrecv.at[2 + m], peer)
        elif tick == 4:
            for m in (1, 2, 3):
                copies["v", 2 + m].wait()
            vec_sum[...] = (vec_four[0] + vec_four[1]) + (vec_four[2] + vec_four[3])
            outs[VEC][...] = vec_sum[z * 2 + x]
            tally(VEC)
        for array in range(6):
            last = max(units[number][0] for number in range(n) if units[number][1] == array)
            if array in SHARED and tick == last + 4:
                here = y * 2 + c
                peers = (
                    device(z, x, y, 1 - c),
                    device(z, x, 1 - y, c),
                    device(z, x, 1 - y, 1 - c),
                )
                for k, peer in enumerate(peers):
                    slot = SHARED.index(array) * 3 + k
                    piece = outs[array].at[here]
                    remote(piece, piece, ("t", slot), tsend.at[slot], trecv.at[slot], peer)
            elif array in SHARED and tick == last + 5:
                for k in range(3):
                    copies["t", SHARED.index(array) * 3 + k].wait()
                tally(array)
            elif array not in SHARED and tick == last + 4:
                tally(array)
    here = (x * 2 + y) * 2 + c
    stat_one[here] = stats[...]
    for m in range(1, 8):
        peer = device(
            z,
            1 - x if m // 4 else x,
            1 - y if (m // 2) % 2 else y,
            1 - c if m % 2 else c,
        )
        remote(stats, stat_one.at[here], ("p", m), ssend.at[m], srecv.at[m], peer)
    for m in range(1, 8):
        copies["p", m].wait()
    total = stat_one[0]
    for slot in range(1, 8):
        total = total + stat_one[slot]
    stats[...] = total
    stat_four[z] = total
    for m in (1, 2, 3):
        remote(
            stats,
            stat_four.at[z],
            ("s", 2 + m),
            ssend.at[7 + m],
            srecv.at[7 + m],
            device(flip(z, m), x, y, c),
        )
    for m in (1, 2, 3):
        copies["s", 2 + m].wait()
    norms = jnp.sqrt((stat_four[0] + stat_four[1]) + (stat_four[2] + stat_four[3]))
    loss = vec_sum[7, 7:8, 128:256][:, 31:32]
    outs[7][...] = jnp.where(stat_row == 2, loss, norms)
    for number in range(n):
        copies[number, 0].wait_send()
    for store in stores:
        store.wait()


def scatter_gradients(grads, masters, firsts, seconds):
    units = [(at,) + unit for at, step in enumerate(SCATTER_STEPS) for unit in step]
    n = len(units)
    shapes = [grad.shape for grad in grads]
    outs = []
    for array in range(6):
        rows, columns = shapes[array][4:]
        if array in SHARED:
            outs.append(jax.ShapeDtypeStruct((4, rows, columns), f32))
        else:
            outs.append(jax.ShapeDtypeStruct((rows, columns), f32))
    outs.append(jax.ShapeDtypeStruct(grads[6].shape[1:], f32))
    outs.append(jax.ShapeDtypeStruct((8, 128), f32))
    scratch = []
    for stage in range(5):
        for at, array, first, size, turn in units:
            shared = array in SHARED
            lead = ((4, 2, 2) if shared else (2, 4, 2), (4,), (3,))
            if stage < 2:
                lead = lead[0]
            elif stage == 2:
                lead = ((4, 2) if shared else (2, 4)) if turn == 0 else (4, 2)
            else:
                lead = lead[stage - 2]
            scratch.append(pltpu.VMEM(lead + (size, shapes[array][5]), bf16))
    vec = grads[6].shape
    scratch += [pltpu.VMEM(vec, f32)] * 3 + [pltpu.VMEM((4,) + vec, f32), pltpu.VMEM(vec, f32)]
    scratch += [pltpu.VMEM(lead + (8, 128), f32) for lead in ((), (8,), (4,))]
    scratch += [
        pltpu.SemaphoreType.DMA((n, 6)),
        pltpu.SemaphoreType.DMA((n, 6)),
        pltpu.SemaphoreType.DMA((n,)),
        pltpu.SemaphoreType.DMA((6,)),
        pltpu.SemaphoreType.DMA((6,)),
        pltpu.SemaphoreType.DMA((6,)),
        pltpu.SemaphoreType.DMA((6,)),
        pltpu.SemaphoreType.DMA((11,)),
        pltpu.SemaphoreType.DMA((11,)),
    ]
    states = [*masters, *firsts, *seconds]
    scratch += [pltpu.VMEM(member.shape, f32) for member in states + outs[:7]]
    scratch += [pltpu.SemaphoreType.DMA((21,)), pltpu.SemaphoreType.DMA((7,))]
    in_vmem = pl.BlockSpec(memory_space=pltpu.VMEM)
    anywhere = pl.BlockSpec(memory_space=pl.ANY)
    total = sum(int(grad.size) * grad.dtype.itemsize for grad in grads)
    return pl.pallas_call(
        functools.partial(scatter_kernel, shapes, units),
        out_shape=outs,
        in_specs=[anywhere] * 6 + [in_vmem] + [anywhere] * 21,
        out_specs=[anywhere] * 7 + [in_vmem],
        scratch_shapes=scratch,
        compiler_params=pltpu.CompilerParams(
            collective_id=1, has_side_effects=True, vmem_limit_bytes=60 * 1024 * 1024
        ),
        cost_estimate=pl.CostEstimate(flops=0, bytes_accessed=2 * total, transcendentals=0),
        name="scatter_gradients",
    )(*grads, *masters, *firsts, *seconds)


def apply_kernel(*refs):
    sources, stats = refs[:28], refs[28]
    targets = refs[29:50]
    loss, pairs = refs[50:52]
    held = refs[52:80]
    results = refs[80:101]
    loaded, stored = refs[101:]
    loads = [
        pltpu.make_async_copy(source, target, loaded.at[at])
        for at, (source, target) in enumerate(zip(sources, held))
    ]
    order = (EIN, EOUT, DIN, DOUT, PIX, BRI, VEC)
    for array in order:
        for kind in range(4):
            loads[7 * kind + array].start()
    grads, masters, firsts, seconds = (held[7 * k : 7 * k + 7] for k in range(4))
    next_firsts, next_seconds, news = (results[7 * k : 7 * k + 7] for k in range(3))
    stores = [
        pltpu.make_async_copy(source, target, stored.at[at])
        for at, (source, target) in enumerate(zip(results, targets))
    ]
    for array in order:
        lane = STAT_LANES[array]
        norms = [stats[row : row + 1, :][:, lane : lane + 1] for row in range(2)]
        ratio = learn_rate * norms[0] / norms[1]
        count = masters[array].shape[0]
        if len(masters[array].shape) == 3:
            count = count * masters[array].shape[1]
        decay = 0.0 if array == VEC else decay_matrix

        def body(rows, array=array, ratio=ratio, decay=decay):
            if array == VEC:
                gradient = grads[VEC][:7, : masters[VEC].shape[1]]
            else:
                gradient = grads[array][rows]
            master = state_rows(masters[array], rows)
            next_one, next_two, update = moments(
                gradient,
                state_rows(firsts[array], rows),
                state_rows(seconds[array], rows),
                master,
                decay,
            )
            put_rows(next_firsts[array], rows, next_one)
            put_rows(next_seconds[array], rows, next_two)
            put_rows(news[array], rows, master - ratio * update)

        for kind in range(4):
            loads[7 * kind + array].wait()
        if array == VEC:
            body(slice(None))
        else:
            row_loop(count, state_step(count), body)
        for kind in range(3):
            stores[7 * kind + array].start()
    pairs[...] = stats[:2, :][:, :7]
    loss[...] = stats[2:3, :][:, :1]
    for store in stores:
        store.wait()


def apply_update(reduced, masters, firsts, seconds, stats):
    shapes = [jax.ShapeDtypeStruct(master.shape, f32) for master in masters]
    operands = [*reduced, *masters, *firsts, *seconds]
    in_vmem = pl.BlockSpec(memory_space=pltpu.VMEM)
    anywhere = pl.BlockSpec(memory_space=pl.ANY)
    results = pl.pallas_call(
        apply_kernel,
        out_shape=shapes * 3
        + [jax.ShapeDtypeStruct((1, 1), f32), jax.ShapeDtypeStruct((2, 7), f32)],
        in_specs=[anywhere] * 28 + [in_vmem],
        out_specs=[anywhere] * 21 + [in_vmem] * 2,
        scratch_shapes=[pltpu.VMEM(member.shape, f32) for member in operands]
        + [pltpu.VMEM(master.shape, f32) for master in masters] * 3
        + [pltpu.SemaphoreType.DMA((28,)), pltpu.SemaphoreType.DMA((21,))],
        compiler_params=pltpu.CompilerParams(vmem_limit_bytes=60 * 1024 * 1024),
        name="apply_update",
    )(*operands, stats)
    return results[:7], results[7:14], results[14:21], results[21].reshape(()), results[22]


def sinusoid_table(feature_width, grid_side, patch_count, padded):
    position = np.arange(patch_count)
    quarter = feature_width // 4
    omegas = 1.0 / 10000.0 ** (np.arange(quarter) / quarter)
    parts = []
    for coords in (position % grid_side, position // grid_side):
        angles = coords[:, None] * omegas[None, :]
        parts += [np.sin(angles), np.cos(angles)]
    table = np.concatenate(parts, axis=1).astype(np.float32)
    return jnp.asarray(np.pad(table, ((0, padded - patch_count), (0, 0))))


GROUPS = 4
ENC = dict(step=128, first=0, images=4, block=64, tokens=50, width=768, heads=3, head=64, hidden=768, spans=1)
DEC = dict(step=208, first=768, images=4, block=208, tokens=197, width=512, heads=4, head=32, hidden=512, spans=4)
CLASS_ROW = 49
MASK_ROW = 50


def dot(left, right, dims=((1,), (0,)), precision=None):
    return lax.dot_general(
        left, right, (dims, ((), ())), preferred_element_type=f32, precision=precision
    )


def dot_t(left, right):
    return dot(left, right, ((0,), (0,)))


def dot_nt(left, right):
    return dot(left, right, ((1,), (1,)))


def exact_pick(choice, values, dims):
    total = None
    for _ in range(3):
        part = values.astype(bf16)
        values = values - part.astype(f32)
        product = dot(choice, part, dims)
        total = product if total is None else total + product
    return total


def row_loop(count, step, body):
    @pl.loop(0, count // step)
    def _(k):
        body(pl.ds(pl.multiple_of(k * step, step), step))


def fold(values):
    step, width = values.shape
    return jnp.sum(values.reshape(step // 8, 8, width), axis=0)


def norm_rows(source, gain, shift, unit, inverse, low, step):
    def body(rows):
        values = source[rows]
        centred = values - jnp.mean(values, axis=-1, keepdims=True)
        scale = lax.rsqrt(jnp.mean(centred * centred, axis=-1, keepdims=True) + eps_norm)
        normed = centred * scale
        unit[rows] = normed
        inverse[rows] = scale
        low[rows] = (normed * gain + shift).astype(bf16)

    row_loop(source.shape[0], step, body)


def norm_back_rows(incoming, unit, inverse, gain, result, residual, sums, at, step):
    width = incoming.shape[-1]

    def body(rows):
        given = incoming[rows]
        normed = unit[rows]
        scaled = given * gain
        inner = (
            scaled
            - jnp.mean(scaled, axis=-1, keepdims=True)
            - normed * jnp.mean(scaled * normed, axis=-1, keepdims=True)
        )
        value = inverse[rows] * inner
        if residual is not None:
            value = value + residual[rows]
        sums[at] = sums[at] + fold(given * normed)
        sums[at + 1] = sums[at + 1] + fold(given)
        result[rows] = value

    row_loop(incoming.shape[0], step, body)


def lane_chunks(size):
    return [slice(at, min(at + 128, size)) for at in range(0, size, 128)]


def attend_mask(dims, scores, start):
    if dims["spans"] == 1:
        key = lax.broadcasted_iota(jnp.int32, scores.shape, 0)
        query = lax.broadcasted_iota(jnp.int32, scores.shape, 1) + start
        allowed = ((key // dims["block"]) == (query // dims["block"])) & (
            (key % dims["block"]) < dims["tokens"]
        )
        return jnp.where(allowed, scores, -1e30)
    first = dims["tokens"] // 16 * 16
    tail = scores[first:]
    key = lax.broadcasted_iota(jnp.int32, tail.shape, 0) + first
    return jnp.concatenate([scores[:first], jnp.where(key < dims["tokens"], tail, -1e30)], axis=0)


def layer_forward_rows(dims, stream, w_in, w_out, vectors, saved):
    unit_one, inv_one, low_one, qkv, probs, mixed, unit_two, inv_two, low_two, active, slope, work, low_work, low_more = saved
    count, width = stream.shape
    inner = dims["heads"] * dims["head"]
    span = count // dims["spans"]
    norm_rows(stream, vectors[1:2, :], vectors[2:3, :], unit_one, inv_one, low_one, dims["step"])

    @pl.loop(0, GROUPS)
    def _(t):
        weights = w_in[t, :, : 3 * inner] if inner % 128 == 0 else w_in[t][:, : 3 * inner]

        def body(rows):
            qkv[t, rows] = dot(low_one[rows], weights).astype(bf16)

        body(slice(None))

    yield "projected"
    scale = dims["head"] ** (-0.5)

    @pl.loop(0, GROUPS * dims["spans"])
    def _(k):
        t = k // dims["spans"]
        b = k % dims["spans"]
        rows = pl.ds(pl.multiple_of(b * span, span), span)
        triple = qkv[t, rows]
        query_t = triple[:, :inner].T
        value_t = triple[:, 2 * inner :].T
        heads = range(dims["heads"])
        lanes = [slice(head * dims["head"], (head + 1) * dims["head"]) for head in heads]
        for head in heads:
            key = triple[:, inner : 2 * inner][:, lanes[head]]
            work[head] = dot(key, query_t[lanes[head]])
        for head in heads:
            for columns in lane_chunks(span):
                scores = attend_mask(dims, work[head, :, columns] * scale, columns.start)
                shifted = jnp.exp(scores - jnp.max(scores, axis=0, keepdims=True))
                share = shifted * (1.0 / jnp.sum(shifted, axis=0, keepdims=True))
                probs[k * dims["heads"] + head, :, columns] = share
                low_work[head, :, columns] = share.astype(bf16)
        results = [dot(value_t[lanes[head]], low_work[head]) for head in heads]
        mixed[t, rows] = jnp.concatenate(results, axis=0).T.astype(bf16)

    yield "attended"

    @pl.loop(0, GROUPS)
    def _(t):
        weights = w_out[t, :inner]

        def body(rows):
            stream[rows] = stream[rows] + dot(mixed[t, rows], weights)

        body(slice(None))

    norm_rows(stream, vectors[3:4, :], vectors[4:5, :], unit_two, inv_two, low_two, dims["step"])

    def feed(t):
        up = w_in[t, :, 3 * inner :] if inner % 128 == 0 else w_in[t][:, 3 * inner :]
        down = w_out[t, inner:]
        slope[t] = dot(low_two[...], up)

        def bend(rows):
            hidden = slope[t, rows]
            level = 0.5 + 0.5 * lax.erf(hidden * (0.5**0.5))
            active[t, rows] = (hidden * level).astype(bf16)
            slope[t, rows] = level + hidden * (
                jnp.exp(-0.5 * hidden * hidden) * (0.5 / np.pi) ** 0.5
            )

        row_loop(count, 64, bend)
        stream[...] = stream[...] + dot(active[t], down)

    half = GROUPS // 2 if dims["spans"] == 1 else GROUPS
    pl.loop(0, half)(feed)
    if half < GROUPS:
        yield "halfway"
        pl.loop(half, GROUPS)(feed)


def layer_backward_rows(
    dims, given, spare, w_in, w_out, vectors, saved, low, flow, turned, grad_in, grad_out, sums, need, ready
):
    unit_one, inv_one, low_one, qkv, probs, mixed, unit_two, inv_two, low_two, active, slope, work, low_work, low_more = saved
    count, width = given.shape
    inner = dims["heads"] * dims["head"]
    span = count // dims["spans"]
    aligned = inner % 128 == 0

    def lower(rows):
        low[rows] = given[rows].astype(bf16)
        spare[rows] = jnp.zeros_like(spare[rows])

    row_loop(count, 32, lower)
    need("low_two", "active", "slope", "w_out", "w_in")
    turned[...] = low_two[...].T

    @pl.loop(0, GROUPS)
    def _(t):
        down = w_out[t, inner:]
        up = w_in[t, :, 3 * inner :] if aligned else w_in[t][:, 3 * inner :]
        grad_out[t, inner:] = dot_t(active[t], low[...]).astype(bf16)

        def body(rows):
            flow[rows] = (slope[t, rows] * dot_nt(low[rows], down)).astype(bf16)
            spare[rows] = spare[rows] + dot_nt(flow[rows], up)

        body(slice(None))
        grad_up = dot(turned[...], flow[...]).astype(bf16)
        if aligned:
            grad_in[t, :, 3 * inner :] = grad_up
        else:
            grad_in[t] = jnp.concatenate([jnp.zeros((width, 3 * inner), bf16), grad_up], axis=1)

    need("unit_two", "inv_two", "mixed")
    norm_back_rows(spare, unit_two, inv_two, vectors[3:4, :], given, given, sums, 3, dims["step"])
    row_loop(count, 32, lower)

    @pl.loop(0, GROUPS)
    def _(t):
        weights = w_out[t, :inner]
        grad_out[t, :inner] = dot_t(mixed[t], low[...]).astype(bf16)

        mixed[t] = dot_nt(low[...], weights).astype(bf16)
        ready("out", t)

    need("qkv", "probs")

    scale = dims["head"] ** (-0.5)

    @pl.loop(0, GROUPS * dims["spans"])
    def _(k):
        t = k // dims["spans"]
        b = k % dims["spans"]
        rows = pl.ds(pl.multiple_of(b * span, span), span)
        triple = qkv[t, rows]
        back = mixed[t, rows]
        key_t = triple[:, inner : 2 * inner].T
        back_t = back.T
        heads = range(dims["heads"])
        lanes = [slice(head * dims["head"], (head + 1) * dims["head"]) for head in heads]
        for head in heads:
            work[head] = dot(triple[:, 2 * inner :][:, lanes[head]], back_t[lanes[head]])
        for head in heads:
            for columns in lane_chunks(span):
                share = probs[k * dims["heads"] + head, :, columns]
                grad_p = work[head, :, columns]
                grad_s = share * (grad_p - jnp.sum(share * grad_p, axis=0, keepdims=True))
                low_work[head, :, columns] = grad_s.astype(bf16)
                low_more[head, :, columns] = share.astype(bf16)
        parts = ([], [], [])
        for head in heads:
            parts[0].append(dot(key_t[lanes[head]], low_work[head]) * scale)
            parts[1].append(dot(low_work[head], triple[:, :inner][:, lanes[head]]) * scale)
            parts[2].append(dot(low_more[head], back[:, lanes[head]]))
        grad_query = jnp.concatenate(parts[0], axis=0).T
        qkv[t, rows] = jnp.concatenate([grad_query] + parts[1] + parts[2], axis=1).astype(bf16)

    need("low_one", "unit_one", "inv_one")
    turned[...] = low_one[...].T

    @pl.loop(0, GROUPS)
    def _(t):
        weights = w_in[t, :, : 3 * inner] if aligned else w_in[t][:, : 3 * inner]
        grad_triple = dot(turned[...], qkv[t]).astype(bf16)
        if aligned:
            grad_in[t, :, : 3 * inner] = grad_triple
        else:
            grad_in[t] = jnp.concatenate([grad_triple, grad_in[t][:, 3 * inner :]], axis=1)

        ready("in", t)
        spare[...] = spare[...] + dot_nt(qkv[t], weights)

    norm_back_rows(spare, unit_one, inv_one, vectors[1:2, :], given, given, sums, 1, dims["step"])


def saved_shapes(dims):
    count = dims["images"] * dims["block"]
    width, inner = dims["width"], dims["heads"] * dims["head"]
    span = count // dims["spans"]
    return [
        ((count, width), f32),
        ((count, 1), f32),
        ((count, width), bf16),
        ((GROUPS, count, 3 * inner), bf16),
        ((GROUPS * dims["spans"] * dims["heads"], span, span), f32),
        ((GROUPS, count, inner), bf16),
        ((count, width), f32),
        ((count, 1), f32),
        ((count, width), bf16),
        ((GROUPS, count, dims["hidden"]), bf16),
        ((GROUPS, count, dims["hidden"]), f32),
    ]


def work_shapes(dims):
    span = dims["images"] * dims["block"] // dims["spans"]
    shape = (dims["heads"], span, span)
    return [(shape, f32), (shape, bf16), (shape, bf16)]


SAVED = (
    "unit_one", "inv_one", "low_one", "qkv", "probs", "mixed",
    "unit_two", "inv_two", "low_two", "active", "slope",
)


def loader(names, sources, targets, semaphores):
    copies = {}
    for at, (name, source, target) in enumerate(zip(names, sources, targets)):
        copies[name] = pltpu.make_async_copy(source, target, semaphores.at[at])
        copies[name].start()

    def need(*wanted):
        for name in wanted:
            if name in copies:
                copies.pop(name).wait()

    return need


def storer(held, outs, semaphores):
    def ready(kind, t):
        at = ("in", "out").index(kind)
        pltpu.make_async_copy(held[at].at[t], outs[at].at[t], semaphores.at[at]).start()

    def finish():
        for at in range(2):
            pltpu.make_async_copy(held[at], outs[at], semaphores.at[at]).wait()

    return ready, finish


def token_gain(vectors, dims):
    return vectors.at[:, pl.ds(dims["first"], dims["width"])]


def decoder_kernel(*refs):
    projected, codes, images, table, w_in_all, w_out_all, pixel_w, vectors_all = refs[:8]
    grad_in_all, grad_out_all, grad_head, grad_projected, vec_out = refs[8:13]
    stream, given, unit, inverse, low, flow, sums, loss, head, pixels_here, head_sum = refs[13:24]
    w_in, w_out, grad_in, grad_out, turned, loaded, stored = refs[24:31]
    saved = refs[31:]
    dims = DEC
    vectors = token_gain(vectors_all, dims)
    count, width = stream.shape
    block = dims["block"]
    need = loader(
        ("w_in", "w_out", "head", "images"),
        (w_in_all, w_out_all, pixel_w.at[pl.ds(PATCH_DIM, width)], images),
        (w_in, w_out, head, pixels_here),
        loaded,
    )
    ready, finish = storer((grad_in, grad_out), (grad_in_all, grad_out_all), stored)
    sums[...] = jnp.zeros_like(sums)
    loss[...] = jnp.zeros_like(loss)

    def placer(b):
        return (
            lax.broadcasted_iota(jnp.int32, (64, block), 0) == codes[b][:1, :block]
        ).astype(bf16)

    def block_rows(b):
        return pl.ds(pl.multiple_of(b * block, block), block)

    @pl.loop(0, dims["images"])
    def _(b):
        at = lax.broadcasted_iota(jnp.int32, (64, width), 0)
        source = jnp.where(at == MASK_ROW, vectors[0:1, :], projected[b])
        source = jnp.where(at > MASK_ROW, 0.0, source)
        stream[block_rows(b)] = exact_pick(placer(b), source, ((0,), (0,))) + table[...]

    need("w_in", "w_out")
    for _ in layer_forward_rows(dims, stream, w_in, w_out, vectors, saved):
        pass
    norm_rows(stream, vectors[5:6, :], vectors[6:7, :], unit, inverse, low, dims["step"])
    need("head", "images")
    head_sum[...] = jnp.zeros_like(head_sum)
    pixels_wide = pixels_here.shape[-1]
    counted = vectors_all[7:8, :]
    patch_total = jnp.sum(counted, axis=1, keepdims=True) / (counted.shape[1] // 8)

    @pl.loop(0, dims["images"])
    def _(b):
        rows = block_rows(b)
        predicted = dot(low[rows], head[...])
        pixels = pixels_here[b].astype(f32)
        centred = pixels - jnp.mean(pixels, axis=-1, keepdims=True)
        variance = jnp.sum(centred * centred, axis=-1, keepdims=True) / (pixels_wide - 1)
        errors = predicted - centred * lax.rsqrt(variance + eps_norm)
        at = lax.broadcasted_iota(jnp.int32, (64, 128), 0)
        spread = jnp.where(at == MASK_ROW, codes[b][2:3, :128].astype(f32), 0.0)
        weight = dot_t(placer(b), spread.astype(bf16))[:, :1] / patch_total
        loss[...] = loss[...] + fold(errors * errors * weight)
        grad_low = (errors * (2.0 / pixels_wide) * weight).astype(bf16)
        head_sum[...] = head_sum[...] + dot_t(low[rows], grad_low)
        given[rows] = dot_nt(grad_low, head[...])

    grad_head[...] = head_sum[...].astype(bf16)
    norm_back_rows(given, unit, inverse, vectors[5:6, :], given, None, sums, 5, dims["step"])
    layer_backward_rows(
        dims, given, stream, w_in, w_out, vectors, saved, low, flow, turned, grad_in, grad_out, sums, need, ready
    )

    @pl.loop(0, dims["images"])
    def _(b):
        back = exact_pick(placer(b), given[block_rows(b)], ((1,), (0,)))
        at = lax.broadcasted_iota(jnp.int32, (64, width), 0)
        grad_projected[b] = jnp.where(at < MASK_ROW, back, 0.0).astype(bf16)
        sums[0] = sums[0] + fold(jnp.where(at == MASK_ROW, back, 0.0))

    for row in range(7):
        vec_out[row : row + 1, :] = jnp.sum(sums[row], axis=0, keepdims=True)
    total = jnp.sum(jnp.sum(loss[...], axis=0, keepdims=True), axis=1, keepdims=True)
    vec_out[7:8, :] = jnp.broadcast_to(total / pixels_wide, (1, width))
    finish()


def decoder_step(projected, codes, images, table, w_in, w_out, pixel_w, vectors):
    dims = DEC
    count, width = dims["images"] * dims["block"], dims["width"]
    wide = images.shape[-1]
    outs = [
        jax.ShapeDtypeStruct(w_in.shape, bf16),
        jax.ShapeDtypeStruct(w_out.shape, bf16),
        jax.ShapeDtypeStruct((width, wide), bf16),
        jax.ShapeDtypeStruct(projected.shape, bf16),
        jax.ShapeDtypeStruct((8, width), f32),
    ]
    scratch = [
        ((count, width), f32),
        ((count, width), f32),
        ((count, width), f32),
        ((count, 1), f32),
        ((count, width), bf16),
        ((count, dims["hidden"]), bf16),
        ((7, 8, width), f32),
        ((8, wide), f32),
        ((width, wide), bf16),
        (images.shape, bf16),
        ((width, wide), f32),
        (w_in.shape, bf16),
        (w_out.shape, bf16),
        (w_in.shape, bf16),
        (w_out.shape, bf16),
        ((width, count), bf16),
        4,
        2,
    ]
    scratch += saved_shapes(dims) + work_shapes(dims)
    in_vmem = pl.BlockSpec(memory_space=pltpu.VMEM)
    anywhere = pl.BlockSpec(memory_space=pl.ANY)
    return pl.pallas_call(
        decoder_kernel,
        out_shape=outs,
        in_specs=[in_vmem, in_vmem, anywhere, in_vmem, anywhere, anywhere, anywhere, in_vmem],
        out_specs=[anywhere, anywhere, in_vmem, in_vmem, in_vmem],
        scratch_shapes=[
            pltpu.SemaphoreType.DMA((shape,)) if isinstance(shape, int) else pltpu.VMEM(*shape)
            for shape in scratch
        ],
        compiler_params=pltpu.CompilerParams(vmem_limit_bytes=62 * 1024 * 1024),
        name="decoder_step",
    )(projected, codes, images, table, w_in, w_out, pixel_w, vectors)


def encode_kernel(ring, *refs):
    dims = ENC
    images, keep_index, unshuffle, masked, image_valid, table = refs[:6]
    refs = refs[6:]
    group = lax.axis_index("tensor")
    if ring:
        masters, refs = refs[:7], refs[7:]
        wholes, vectors_all, codes, pictures, projected = refs[:7], *refs[7:11]
        kept_state, refs = refs[11:26], refs[26:]
        parts, send, recv, local, vec_parts = refs[:7], *refs[7:11]
        raw = dict(zip((PIX, EOUT, BRI), refs[11:14]))
        refs = refs[14:]
    else:
        wholes, vectors_all = refs[:4], refs[4]
        codes, pictures, projected, kept_state = refs[5], refs[6], refs[7], refs[8:23]
        refs = refs[23:]
        wholes = dict(zip((PIX, EIN, EOUT, BRI), wholes))
    loaded, flushed = refs[:2]
    first_copies = []
    if ring:
        shards, states_loaded, refs = refs[2:9], refs[9], refs[:2] + refs[10:]
        for at, (source, target) in enumerate(zip(masters, shards)):
            first_copies.append(pltpu.make_async_copy(source, target, states_loaded.at[at]))
            first_copies[-1].start()
        masters = shards
    eight, pixels_here, stream, w_in, w_out, embed, bridge = refs[2:9]
    retained, unit, inverse, low = refs[9:13]
    saved = refs[13:24]
    work = refs[24:]
    held = (retained, unit, inverse, low) + tuple(saved)
    vectors = token_gain(vectors_all, dims)
    count, width = stream.shape
    block = dims["block"]

    first = pl.multiple_of((group // 2) * 8, 8)
    eight_copy = pltpu.make_async_copy(images.at[:, pl.ds(first, 8)], eight, loaded.at[4])
    eight_copy.start()
    lane = lax.broadcasted_iota(jnp.int32, (1, codes.shape[2]), 1)
    valid = image_valid[...]
    image_at = lax.broadcasted_iota(jnp.int32, valid.shape, 1)
    codes[...] = jnp.full(codes.shape, -1, jnp.int32)
    for b in range(dims["images"]):
        mine = group * dims["images"] + b
        row = pl.ds(mine, 1)
        codes[b, 0:1, :] = jnp.where(lane == IMAGE_PATCHES, CLASS_ROW, -1)
        codes[b, 0:1, :IMAGE_PATCHES] = jnp.where(masked[row] == 1, MASK_ROW, unshuffle[row])
        codes[b, 1:2, :KEEP] = keep_index[row]
        own_valid = jnp.sum(
            jnp.where(image_at == mine, valid, 0).astype(f32), axis=1, keepdims=True
        )
        codes[b, 2:3, :] = jnp.broadcast_to(own_valid, (1, codes.shape[2])).astype(jnp.int32)

    def load(slot, array, target):
        if not ring:
            source = wholes[array]
            if array == PIX:
                source = source.at[pl.ds(0, PATCH_DIM)]
            pltpu.make_async_copy(source, target, loaded.at[slot]).start()
            return pltpu.make_async_copy(source, target, loaded.at[slot])
        if array != EIN:
            pltpu.make_async_copy(wholes[array], raw[array], loaded.at[slot]).start()
            return pltpu.make_async_copy(wholes[array], raw[array], loaded.at[slot])
        rows = wholes[array].shape[4]

        @pl.loop(0, 32)
        def _(k):
            pltpu.make_async_copy(
                wholes[array].at[k // 16, (k // 8) % 2, (k // 2) % 4, k % 2],
                target.at[k // 8, pl.ds(pl.multiple_of((k % 8) * rows, rows), rows)],
                loaded.at[slot],
            ).start()

        return pltpu.make_async_copy(target, target, loaded.at[slot])

    def assemble(array, target):
        if ring and array in SHARED:
            count = -(-target.shape[0] // raw[array].shape[4])
            pieces = [
                raw[array][k // 8, (k // 4) % 2, (k // 2) % 2, k % 2] for k in range(count)
            ]
            target[...] = jnp.concatenate(pieces, axis=0)[: target.shape[0]]
        elif ring:

            @pl.loop(0, GROUPS)
            def _(t):
                pieces = [raw[array][t // 2, t % 2, k // 2, k % 2] for k in range(8)]
                target[t] = jnp.concatenate(pieces, axis=0)

    flushes = []

    def flush(*members):
        for member in members:
            copy = pltpu.make_async_copy(held[member], kept_state[member], flushed.at[member])
            copy.start()
            flushes.append(copy)

    for copy in first_copies:
        copy.wait()
    if ring:
        for array in range(6):
            if array in SHARED:
                rows = masters[array].shape[0] // 4
                rows = pl.ds(pl.multiple_of(group * rows, 8), rows)
                parts[array][...] = masters[array][rows].astype(bf16)
            else:
                parts[array][...] = state_rows(masters[array], slice(None)).astype(bf16)
        columns = masters[VEC].shape[1]
        parts[VEC][...] = jnp.zeros_like(parts[VEC])
        parts[VEC][:7, :columns] = masters[VEC][...].astype(bf16).astype(f32)
        counts = dot(valid.astype(bf16), masked[...].astype(f32).astype(bf16))
        counted = jnp.sum(counts, axis=1, keepdims=True)
        parts[VEC][7:8, :] = jnp.broadcast_to(counted, (1, parts[VEC].shape[1]))
        ticks = gather_ticks(parts, wholes, send, recv, local)

    done = [-1]

    def until(tick):
        while ring and done[0] < tick:
            next(ticks)
            done[0] += 1

    at_embed, at_in, at_out = (
        last_step(GATHER_STEPS, array) + DEPTH for array in (PIX, EIN, EOUT)
    )
    at_end = len(GATHER_STEPS) - 1 + DEPTH
    until(0)
    eight_copy.wait()
    pixels_wide = eight.shape[2]

    @pl.loop(0, dims["images"])
    def _(b):
        size = (pixels_here.shape[1], IMAGE_PATCHES * 8)
        patch = lax.broadcasted_iota(jnp.int32, size, 0)
        at = lax.broadcasted_iota(jnp.int32, size, 1)
        wanted = patch * 8 + (group % 2) * dims["images"] + b
        choice = (at == wanted) & (patch < IMAGE_PATCHES)
        flat = eight[...].reshape(IMAGE_PATCHES * 8, pixels_wide)
        pixels_here[b] = dot(choice.astype(f32).astype(bf16), flat).astype(bf16)

    picture_copy = pltpu.make_async_copy(pixels_here, pictures, loaded.at[5])
    picture_copy.start()
    until(at_embed)
    embed_copy = load(0, PIX, embed)
    if ring:
        vec_copy = pltpu.make_async_copy(wholes[VEC], vec_parts, loaded.at[1])
        vec_copy.start()
        vec_copy.wait()
        vectors_all[...] = jnp.concatenate(
            [vec_parts[0, 0, k // 2, k % 2][:, :columns] for k in range(8)], axis=1
        )
    embed_copy.wait()
    assemble(PIX, embed)

    @pl.loop(0, dims["images"])
    def _(b):
        rows = pl.ds(pl.multiple_of(b * block, block), block)
        choice = (
            lax.broadcasted_iota(jnp.int32, (table.shape[0], block), 0) == codes[b][1:2, :block]
        )
        retained[rows] = dot_t(choice.astype(bf16), pixels_here[b]).astype(bf16)
        places = exact_pick(choice.astype(bf16), table[...], ((0,), (0,)))
        at = lax.broadcasted_iota(jnp.int32, (block, width), 0)
        start = dot(retained[rows], embed[...]) + places
        stream[rows] = jnp.where(at == CLASS_ROW, vectors[0:1, :], start)

    flush(0)
    until(at_in)
    load(2, EIN, w_in).wait()
    layer = layer_forward_rows(dims, stream, w_in, w_out, vectors, saved + work)
    next(layer)
    until(at_in + 1)
    next(layer)
    flush(4, 5, 6, 7, 8, 9)
    until(at_out)
    bridge_copy = load(1, BRI, bridge)
    load(3, EOUT, w_out).wait()
    assemble(EOUT, w_out)
    next(layer)
    flush(10, 11, 12)
    until(at_out + 1)
    for _ in layer:
        pass
    flush(13, 14)
    until(at_out + 2)
    norm_rows(stream, vectors[5:6, :], vectors[6:7, :], unit, inverse, low, dims["step"])
    flush(1, 2, 3)
    bridge_copy.wait()
    assemble(BRI, bridge)

    @pl.loop(0, dims["images"])
    def _(b):
        rows = pl.ds(pl.multiple_of(b * block, block), block)
        projected[b] = dot(low[rows], bridge[...])

    until(at_end + 1)
    picture_copy.wait()
    for copy in flushes:
        copy.wait()


def encode(images, indices, table, weights, vectors=None):
    dims = ENC
    ring = vectors is None
    count, width = dims["images"] * dims["block"], dims["width"]
    bridge_wide = weights[BRI].shape[-1]
    in_vmem = pl.BlockSpec(memory_space=pltpu.VMEM)
    anywhere = pl.BlockSpec(memory_space=pl.ANY)
    kept_shapes = [
        ((count, images.shape[2]), bf16),
        ((count, width), f32),
        ((count, 1), f32),
        ((count, width), bf16),
    ] + saved_shapes(dims)
    picture_shape = (dims["images"], DEC["block"], images.shape[2])
    outs = [((dims["images"], 8, 256), jnp.int32), (picture_shape, bf16)]
    outs += [((dims["images"], dims["block"], bridge_wide), f32)] + kept_shapes
    out_specs = [in_vmem, anywhere, in_vmem] + [anywhere] * len(kept_shapes)
    in_specs = [anywhere] + [in_vmem] * 5
    scratch = []
    if ring:
        shapes = []
        for array in range(6):
            rows, wide = weights[array].size // weights[array].shape[-1], weights[array].shape[-1]
            shapes.append((rows // 4 if array in SHARED else rows, wide))
        shapes.append((8, 256))
        types = [bf16] * 6 + [f32]
        operands = [images, *indices, table, *weights]
        in_specs += [anywhere] * 7
        gathered = [(whole_shape(k, shape), types[k]) for k, shape in enumerate(shapes)]
        outs = gathered + [((8, shapes_total(weights[VEC])), f32)] + outs
        out_specs = [anywhere] * 7 + [in_vmem] + out_specs
        units = sum(len(step) for step in GATHER_STEPS)
        scratch += [pltpu.VMEM(shape, kind) for shape, kind in zip(shapes, types)]
        scratch += [
            pltpu.SemaphoreType.DMA((units, 6)),
            pltpu.SemaphoreType.DMA((units, 6)),
            pltpu.SemaphoreType.DMA((7,)),
            pltpu.VMEM(whole_shape(VEC, shapes[VEC]), f32),
        ]
        scratch += [
            pltpu.VMEM(whole_shape(array, shapes[array]), bf16) for array in (PIX, EOUT, BRI)
        ]
        params = dict(collective_id=0, has_side_effects=True)
        w_shapes = [
            (GROUPS, 8 * shapes[EIN][0], shapes[EIN][1]),
            (GROUPS, 8 * shapes[EOUT][0], shapes[EOUT][1]),
        ]
    else:
        operands = [images, *indices, table] + [weights[k] for k in (PIX, EIN, EOUT, BRI)] + [vectors]
        in_specs += [anywhere] * 4 + [in_vmem]
        params = {}
        w_shapes = [weights[EIN].shape, weights[EOUT].shape]
    scratch += [pltpu.SemaphoreType.DMA((8,)), pltpu.SemaphoreType.DMA((15,))]
    if ring:
        scratch += [pltpu.VMEM(member.shape, f32) for member in weights]
        scratch += [pltpu.SemaphoreType.DMA((7,))]
    buffers = [
        ((images.shape[0], 8, images.shape[2]), bf16),
        (picture_shape, bf16),
        ((count, width), f32),
        (w_shapes[0], bf16),
        (w_shapes[1], bf16),
        ((PATCH_DIM, width), bf16),
        ((width, bridge_wide), bf16),
    ]
    buffers += kept_shapes + work_shapes(dims)
    scratch += [pltpu.VMEM(*buffer) for buffer in buffers]
    return pl.pallas_call(
        functools.partial(encode_kernel, ring),
        out_shape=[jax.ShapeDtypeStruct(shape, kind) for shape, kind in outs],
        in_specs=in_specs,
        out_specs=out_specs,
        scratch_shapes=scratch,
        compiler_params=pltpu.CompilerParams(vmem_limit_bytes=62 * 1024 * 1024, **params),
        name="gather_encode" if ring else "encode",
    )(*operands)


def shapes_total(vector_shard):
    return 8 * vector_shard.shape[1]


def encoder_backward_kernel(*refs):
    grad_projected = refs[0]
    sources = refs[1:18]
    bridge, vectors_all, grad_head, dec_sums = refs[18:22]
    grad_in_all, grad_out_all, grad_bridge, grad_pixel, packed = refs[22:27]
    given, spare, low, flow, sums, vec_all, turned = refs[27:34]
    held = refs[34:51]
    grad_in, grad_out, loaded, stored = refs[51:55]
    names = ("retained", "unit", "inverse", "low_end") + SAVED + ("w_in", "w_out")
    order = (3, 1, 2, 12, 13, 14, 16, 15, 10, 11, 9, 7, 8, 6, 4, 5, 0)
    need = loader(
        [names[k] for k in order], [sources[k] for k in order], [held[k] for k in order], loaded
    )
    ready, finish = storer((grad_in, grad_out), (grad_in_all, grad_out_all), stored)
    retained, unit, inverse, low_end = held[:4]
    saved = held[4:15] + refs[55:]
    w_in, w_out = held[15:17]
    dims = ENC
    vectors = token_gain(vectors_all, dims)
    count, width = given.shape
    block = dims["block"]
    sums[...] = jnp.zeros_like(sums)

    need("low_end", "unit", "inverse")
    flat = grad_projected[...].reshape(count, grad_projected.shape[-1])
    grad_bridge[...] = dot_t(low_end[...], flat).astype(bf16)
    given[...] = dot_nt(flat, bridge[...])
    norm_back_rows(given, unit, inverse, vectors[5:6, :], given, None, sums, 5, dims["step"])
    layer_backward_rows(
        dims, given, spare, w_in, w_out, vectors, saved, low, flow, turned, grad_in, grad_out, sums, need, ready
    )
    need("retained")
    grad_pixel[:PATCH_DIM] = dot_t(retained[...], given[...].astype(bf16)).astype(bf16)
    grad_pixel[PATCH_DIM:] = grad_head[...]

    def tokens(rows):
        at = lax.broadcasted_iota(jnp.int32, (block, width), 0)
        sums[0] = sums[0] + fold(jnp.where(at == CLASS_ROW, given[rows], 0.0))

    row_loop(count, block, tokens)
    for row in range(7):
        vec_all[row : row + 1, :width] = jnp.sum(sums[row], axis=0, keepdims=True)
    vec_all[7:8, :width] = jnp.zeros((1, width), f32)
    vec_all[:, width:] = dec_sums[...]
    columns = vec_all.shape[1] // 8
    packed[...] = jnp.zeros_like(packed)
    for k in range(8):
        packed[k, :, :columns] = vec_all[:, k * columns : (k + 1) * columns]
    finish()


def encoder_backward(grad_projected, kept_state, w_in, w_out, bridge, vectors, grad_head, dec_sums):
    dims = ENC
    count, width = dims["images"] * dims["block"], dims["width"]
    pixels_wide = kept_state[0].shape[1]
    outs = [
        jax.ShapeDtypeStruct(w_in.shape, bf16),
        jax.ShapeDtypeStruct(w_out.shape, bf16),
        jax.ShapeDtypeStruct(bridge.shape, bf16),
        jax.ShapeDtypeStruct((pixels_wide + grad_head.shape[0], width), bf16),
        jax.ShapeDtypeStruct((8, 8, 256), f32),
    ]
    scratch = [
        ((count, width), f32),
        ((count, width), f32),
        ((count, width), bf16),
        ((count, dims["hidden"]), bf16),
        ((7, 8, width), f32),
        (vectors.shape, f32),
        ((width, count), bf16),
    ]
    kept_shapes = [(member.shape, member.dtype) for member in kept_state]
    scratch += kept_shapes + [(w_in.shape, bf16), (w_out.shape, bf16)]
    scratch += [(w_in.shape, bf16), (w_out.shape, bf16), 17, 2] + work_shapes(dims)
    in_vmem = pl.BlockSpec(memory_space=pltpu.VMEM)
    anywhere = pl.BlockSpec(memory_space=pl.ANY)
    return pl.pallas_call(
        encoder_backward_kernel,
        out_shape=outs,
        in_specs=[in_vmem] + [anywhere] * 17 + [in_vmem] * 4,
        out_specs=[anywhere] * 2 + [in_vmem] * 3,
        scratch_shapes=[
            pltpu.SemaphoreType.DMA((shape,)) if isinstance(shape, int) else pltpu.VMEM(*shape)
            for shape in scratch
        ],
        compiler_params=pltpu.CompilerParams(vmem_limit_bytes=62 * 1024 * 1024),
        name="encoder_backward",
    )(grad_projected, *kept_state, w_in, w_out, bridge, vectors, grad_head, dec_sums)


def gather_grouped(part, groups):
    whole = lax.all_gather(part, GROUPED, axis=0, tiled=True)
    return whole.reshape(groups, -1, whole.shape[-1])


def scatter_grouped(gradient):
    flat = gradient.astype(f32).reshape(-1, gradient.shape[-1])
    return lax.psum_scatter(flat, GROUPED, scatter_dimension=0, tiled=True)


def ringed(tensor_count):
    return tensor_count == 4 and lax.axis_size("dp") == 8


def plain_gather(masters, counted):
    groups = lax.axis_size("tensor")
    wholes = {}
    for array, k in ((EIN, 0), (EOUT, 1), (DIN, 2), (DOUT, 3)):
        flat = masters[k].reshape(-1, masters[k].shape[-1]).astype(bf16)
        wholes[array] = gather_grouped(flat, groups)
    for array, k in ((PIX, 4), (BRI, 5)):
        wholes[array] = lax.all_gather(masters[k].astype(bf16), "dp", axis=0, tiled=True)
    low = masters[6].astype(bf16).astype(f32)
    vectors = lax.all_gather(low, "dp", axis=1, tiled=True)
    eighth = jnp.broadcast_to(lax.psum(counted, "dp") / 8, (1, vectors.shape[1]))
    return wholes, jnp.concatenate([vectors, eighth], axis=0)


def ring_finish(gradients, masters, firsts, seconds):
    grouped, grad_pixel, grad_bridge, packed = gradients
    tensor_count = lax.axis_size("tensor")
    order = (4, 0, 1, 5, 2, 3, 6)
    sources = (grad_pixel, grouped[0], grouped[1], grad_bridge, grouped[2], grouped[3])
    operands = []
    for array, source in enumerate(sources):
        master = masters[order[array]]
        rows, wide = master.size // master.shape[-1], master.shape[-1]
        if array in SHARED:
            rows = rows // tensor_count
        operands.append(source.reshape(whole_shape(array, (rows, wide))))
    operands.append(packed)
    states = [[members[k] for k in order] for members in (masters, firsts, seconds)]
    *sums, stats = scatter_gradients(operands, *states)
    for array in SHARED:
        sums[array] = sums[array].reshape(-1, sums[array].shape[-1])
    *results, loss_value, pairs = apply_update(sums, *states, stats)
    place_of = {k: at for at, k in enumerate(order)}
    results = [[members[place_of[k]] for k in range(7)] for members in results]
    return (loss_value, pairs, *results[0], *results[1], *results[2])


def plain_finish(gradients, masters, firsts, seconds):
    grouped, grad_pixel, grad_bridge, packed = gradients
    tensor_count = lax.axis_size("tensor")
    columns = masters[6].shape[1]

    def scatter_shared(gradient):
        part = lax.psum_scatter(gradient.astype(f32), EVERY, scatter_dimension=0, tiled=True)
        return lax.all_gather(part, "tensor", axis=0, tiled=True)

    reduced = [scatter_grouped(gradient) for gradient in grouped]
    reduced += [scatter_shared(grad_pixel), scatter_shared(grad_bridge)]
    whole = packed.shape[0] * (ENCODER_WIDTH + D_D) // 8
    packed = packed[:, :, : whole // packed.shape[0]].transpose(1, 0, 2).reshape(8, -1)
    vector_sum = lax.psum(packed, EVERY)
    own = lax.dynamic_slice_in_dim(
        vector_sum[:7], lax.axis_index("dp") * columns, columns, axis=1
    )
    reduced = [gradient.reshape(master.shape) for gradient, master in zip(reduced + [own], masters)]
    decays = (decay_matrix,) * 6 + (0.0,)
    share_counts = (1.0,) * 4 + (float(tensor_count),) * 3
    steps = [moments(*member) for member in zip(reduced, firsts, seconds, masters, decays)]
    new_firsts, new_seconds, updates = zip(*steps)

    def squares(members):
        return jnp.stack(
            [jnp.sum(member * member) / count for member, count in zip(members, share_counts)]
        )

    weight_norm, update_norm = map(
        jnp.sqrt, lax.psum((squares(masters), squares(updates)), EVERY)
    )
    ratio = learn_rate * weight_norm / update_norm
    news = [
        master - ratio[position] * update
        for position, (master, update) in enumerate(zip(masters, updates))
    ]
    return (vector_sum[7, -1], jnp.stack([weight_norm, update_norm]), *new_firsts, *new_seconds, *news)


def shards(
    images,
    keep_index,
    unshuffle,
    masked,
    image_valid,
    *state,
):
    masters, firsts, seconds = state[:7], state[7:14], state[14:21]
    tensor_count = lax.axis_size("tensor")
    enc_table, dec_table = (
        sinusoid_table(width, GRID_PATCHES, IMAGE_PATCHES, DEC["block"])
        for width in (ENCODER_WIDTH, D_D)
    )
    indices = (keep_index, unshuffle, masked, image_valid[None, :])
    by_patch = images.transpose(1, 0, 2)
    if ringed(tensor_count):
        order = (4, 0, 1, 5, 2, 3, 6)
        results = encode(by_patch, indices, enc_table, [masters[k] for k in order])
        wholes, results = results[:7], results[7:]
        vectors, codes, pictures, projected, *enc_state = results
        wholes = [
            whole.reshape(-1, whole.shape[-1])
            if array in SHARED
            else whole.reshape(tensor_count, -1, whole.shape[-1])
            for array, whole in enumerate(wholes)
        ]
    else:
        counted = jnp.sum(masked.astype(f32) * image_valid.astype(f32)[:, None])
        wholes, vectors = plain_gather(masters, counted)
        codes, pictures, projected, *enc_state = encode(
            by_patch, indices, enc_table, wholes, vectors=vectors
        )
    grad_dec_in, grad_dec_out, grad_head, grad_projected, dec_sums = decoder_step(
        projected, codes, pictures, dec_table, wholes[DIN], wholes[DOUT], wholes[PIX], vectors
    )
    grad_enc_in, grad_enc_out, grad_bridge, grad_pixel, packed = encoder_backward(
        grad_projected,
        enc_state,
        wholes[EIN],
        wholes[EOUT],
        wholes[BRI],
        vectors,
        grad_head,
        dec_sums,
    )
    finish = ring_finish if ringed(tensor_count) else plain_finish
    return finish(
        ([grad_enc_in, grad_enc_out, grad_dec_in, grad_dec_out], grad_pixel, grad_bridge, packed),
        masters,
        firsts,
        seconds,
    )


def solution(mesh):
    state_specs = (
        P("dp", "tensor", None),
        P("tensor", "dp", None),
        P("dp", "tensor", None),
        P("tensor", "dp", None),
        P("dp", None),
        P("dp", None),
        P(None, "dp"),
    )
    in_specs = (
        P("dp", None, None),
        P("dp", None),
        P("dp", None),
        P("dp", None),
        P("dp"),
    ) + state_specs * 3
    out_specs = (P(), P()) + state_specs * 3
    return jax.shard_map(shards, mesh=mesh, in_specs=in_specs, out_specs=out_specs, check_vma=False)
```

```python
import functools

import jax
import jax.numpy as jnp
from jax import lax
from jax.experimental import pallas as pl
from jax.experimental.pallas import tpu as pltpu
from jax.sharding import PartitionSpec as P
import numpy as np

ENCODER_WIDTH = 768
H_E = 12
HD_E = 64
D_D = 512
H_D = 16
HD_D = 32
PATCH_DIM = 768
GRID_PATCHES = 14
IMAGE_PATCHES = 196
KEEP = 49

eps_norm = 1e-06
beta_one = 0.9
beta_two = 0.999
step_count = 7.0
learn_rate = 0.3
decay_matrix = 0.05
eps_moment = 1e-06
f32 = jnp.float32
bf16 = jnp.bfloat16
EVERY = ("dp", "tensor")
GROUPED = ("tensor", "dp")


MESH_ID = pl.DeviceIdType.MESH
PIX, EIN, EOUT, BRI, DIN, DOUT, VEC = range(7)


def place():
    dp_at = lax.axis_index("dp")
    group = lax.axis_index("tensor")
    z, x = lax.div(dp_at, 2), lax.rem(dp_at, 2)
    y, c = lax.div(group, 2), lax.rem(group, 2)
    return z, x, y, c


def device(z, x, y, c):
    return (z * 2 + x, y * 2 + c)


def flip(z, m):
    low = lax.rem(z, 2)
    high = lax.div(z, 2)
    if m % 2:
        low = 1 - low
    if m // 2:
        high = 1 - high
    return high * 2 + low


def greet(z, x, y, c):
    barrier = pltpu.get_barrier_semaphore()
    peers = [device(flip(z, m), x, y, c) for m in (1, 2, 3)]
    for m in range(1, 8):
        peers.append(
            device(
                z,
                1 - x if m // 4 else x,
                1 - y if (m // 2) % 2 else y,
                1 - c if m % 2 else c,
            )
        )
    for peer in peers:
        pl.semaphore_signal(barrier, inc=1, device_id=peer, device_id_type=MESH_ID)
    pl.semaphore_wait(barrier, len(peers))


SHARED = (PIX, BRI)


def spot(array, y, c, z, x):
    return (z, x, y, c) if array in SHARED else (y, c, z, x)


def half_spot(array, y, z, x):
    return (z, x, y) if array in SHARED else (y, z, x)


def whole_shape(array, part):
    return ((4, 2, 2, 2) if array in SHARED else (2, 2, 4, 2)) + part


GATHER_STEPS = (
    ((VEC, 0, 8, 0), (PIX, 0, 24, 0), (PIX, 24, 16, 1)),
    ((EIN, 0, 16, 0), (EIN, 16, 16, 1)),
    ((EIN, 32, 16, 0), (EIN, 48, 16, 1)),
    ((EIN, 64, 16, 0), (EIN, 80, 16, 1)),
    ((EOUT, 0, 24, 0), (EOUT, 24, 24, 1)),
    ((EOUT, 48, 24, 0), (EOUT, 72, 24, 1)),
    ((EOUT, 96, 8, 0), (EOUT, 104, 16, 1), (BRI, 0, 16, 0), (BRI, 16, 8, 1)),
    ((DIN, 0, 16, 0), (DIN, 16, 16, 1)),
    ((DIN, 32, 16, 0), (DIN, 48, 16, 1)),
    ((DOUT, 0, 16, 0), (DOUT, 16, 32, 1)),
    ((DOUT, 48, 16, 0), (DOUT, 64, 16, 1)),
)
DEPTH = 4


def last_step(steps, array):
    return max(at for at, step in enumerate(steps) for unit in step if unit[0] == array)


def gather_ticks(parts, outs, send, recv, local):
    count = 7
    z, x, y, c = place()
    units = []
    for at, step in enumerate(GATHER_STEPS):
        for unit in step:
            units.append((at,) + unit)
    copies = {}

    def rows(array, region, first, size):
        ref = outs[array]
        return ref.at[region + (pl.ds(first, size),)]

    def plan(number, stage):
        at, array, first, size, turn = units[number]
        every = slice(None)
        if stage < 3:
            src = parts[array].at[pl.ds(first, size)]
            dst = rows(array, spot(array, y, c, z, x), first, size)
            peer = device(flip(z, stage + 1), x, y, c)
        else:
            if stage == 3:
                region = spot(array, y, c, every, x)
                peer = device(z, x, 1 - y, c) if turn == 0 else device(z, 1 - x, y, c)
            elif stage == 4 and turn == 0:
                region = spot(array, every, c, every, x)
                peer = device(z, 1 - x, y, c)
            elif stage == 4:
                region = spot(array, y, c, every, every)
                peer = device(z, x, 1 - y, c)
            else:
                region = spot(array, every, c, every, every)
                peer = device(z, x, y, 1 - c)
            src = dst = rows(array, region, first, size)
        return pltpu.make_async_remote_copy(
            src_ref=src,
            dst_ref=dst,
            send_sem=send.at[number, stage],
            recv_sem=recv.at[number, stage],
            device_id=peer,
            device_id_type=MESH_ID,
        )

    def start(number, stage):
        copies[number, stage] = plan(number, stage)
        copies[number, stage].start()

    own = []
    for array in range(count):
        own.append(
            pltpu.make_async_copy(parts[array], outs[array].at[spot(array, y, c, z, x)], local.at[array])
        )
        own[-1].start()
    greet(z, x, y, c)
    steps = len(GATHER_STEPS)
    waited = set()
    for tick in range(steps + 4):
        for number, unit in enumerate(units):
            if unit[0] == tick:
                for stage in range(3):
                    start(number, stage)
        for number, unit in enumerate(units):
            if unit[0] == tick - 1:
                if unit[1] not in waited:
                    waited.add(unit[1])
                    own[unit[1]].wait()
                for stage in range(3):
                    copies[number, stage].wait_recv()
                start(number, 3)
        for back in (2, 3):
            for number, unit in enumerate(units):
                if unit[0] == tick - back:
                    copies[number, back + 1].wait_recv()
                    start(number, back + 2)
        for number, unit in enumerate(units):
            if unit[0] == tick - 4:
                copies[number, 5].wait_recv()
        if tick < steps + 3:
            yield tick
    for key in copies:
        copies[key].wait_send()
    yield steps + 3
    yield None


SCATTER_STEPS = (
    ((BRI, 0, 8, 0), (BRI, 8, 16, 1)),
    ((PIX, 0, 24, 0), (PIX, 24, 16, 1)),
    ((EIN, 0, 16, 0), (EIN, 16, 16, 1)),
    ((EIN, 32, 16, 0), (EIN, 48, 16, 1)),
    ((EIN, 64, 16, 0), (EIN, 80, 16, 1)),
    ((EOUT, 0, 24, 0), (EOUT, 24, 24, 1)),
    ((EOUT, 48, 24, 0), (EOUT, 72, 24, 1)),
    ((EOUT, 96, 8, 0), (EOUT, 104, 16, 1)),
    ((DIN, 0, 16, 0), (DIN, 16, 16, 1)),
    ((DIN, 32, 16, 0), (DIN, 48, 16, 1)),
    ((DOUT, 0, 24, 0), (DOUT, 24, 24, 1)),
    ((DOUT, 48, 16, 0), (DOUT, 64, 16, 1)),
)


STAT_LANES = {EIN: 0, EOUT: 1, DIN: 2, DOUT: 3, PIX: 4, BRI: 5, VEC: 6}


def state_rows(ref, rows):
    if len(ref.shape) == 2:
        return ref[rows]
    return ref[rows, 0, :] if ref.shape[1] == 1 else ref[0, rows, :]


def put_rows(ref, rows, values):
    if len(ref.shape) == 2:
        ref[rows] = values
    elif ref.shape[1] == 1:
        ref[rows, 0, :] = values
    else:
        ref[0, rows, :] = values


def moments(gradient, moment_one, moment_two, master, decay):
    next_one = beta_one * moment_one + (1.0 - beta_one) * gradient
    next_two = beta_two * moment_two + (1.0 - beta_two) * gradient * gradient
    bias_one = 1.0 - beta_one**step_count
    bias_two = 1.0 - beta_two**step_count
    update = next_one / bias_one / (jnp.sqrt(next_two / bias_two) + eps_moment) + decay * master
    return next_one, next_two, update


def state_step(rows):
    return next(step for step in (32, 40, rows) if rows % step == 0)


def scatter_kernel(shapes, units, *refs):
    grads = refs[:7]
    sources, results = refs[7:28], refs[28:36]
    refs = refs[36:]
    n = len(units)
    own, one, two, three, four = (refs[k * n : (k + 1) * n] for k in range(5))
    vec_one, vec_two, vec_three, vec_four, vec_sum = refs[5 * n : 5 * n + 5]
    stats, stat_one, stat_four = refs[5 * n + 5 : 5 * n + 8]
    send, recv, local, vsend, vrecv, tsend, trecv, ssend, srecv = refs[5 * n + 8 : 5 * n + 17]
    refs = refs[5 * n + 17 :]
    held, outs, loaded, stored = refs[:21], refs[21:28] + results[7:], *refs[28:]
    masters, firsts, seconds = held[:7], held[7:14], held[14:]
    state_copies = [
        pltpu.make_async_copy(source, target, loaded.at[at])
        for at, (source, target) in enumerate(zip(sources, held))
    ]
    for copy in state_copies:
        copy.start()
    stores = []
    z, x, y, c = place()
    every = slice(None)
    copies = {}
    stat_row = lax.broadcasted_iota(jnp.int32, (8, 128), 0)
    stat_lane = lax.broadcasted_iota(jnp.int32, (8, 128), 1)

    def tally(array):
        stores.append(pltpu.make_async_copy(outs[array], results[array], stored.at[array]))
        stores[-1].start()
        for kind in range(3):
            state_copies[7 * kind + array].wait()
        if array == VEC:
            gradient = outs[VEC][:7, : masters[VEC].shape[1]]
            update = moments(
                gradient, firsts[VEC][...], seconds[VEC][...], masters[VEC][...], 0.0
            )[2]
            squares = [jnp.sum(v * v, axis=0, keepdims=True) for v in (masters[VEC][...], update)]
        else:
            flat = (array in SHARED) and outs[array].shape[0] == 4
            count = outs[array].shape[0] * outs[array].shape[1] if flat else outs[array].shape[0]
            columns = outs[array].shape[-1]
            step = outs[array].shape[1] if flat else state_step(count)

            def body(k, carry):
                rows = pl.ds(pl.multiple_of(k * step, 8), step)
                gradient = outs[array][k] if flat else outs[array][rows]
                master = state_rows(masters[array], rows)
                update = moments(
                    gradient,
                    state_rows(firsts[array], rows),
                    state_rows(seconds[array], rows),
                    master,
                    decay_matrix,
                )[2]
                return tuple(
                    total + jnp.sum((v * v).reshape(step // 8, 8, columns), axis=0)
                    for total, v in zip(carry, (master, update))
                )

            start = (jnp.zeros((8, columns), f32),) * 2
            squares = [
                jnp.sum(v, axis=0, keepdims=True)
                for v in lax.fori_loop(0, count // step, body, start)
            ]
        share = 0.25 if array in SHARED + (VEC,) else 1.0
        total = stats[...]
        for row, square in enumerate(squares):
            value = jnp.sum(square, axis=1, keepdims=True) * share
            total = total + jnp.where((stat_row == row) & (stat_lane == STAT_LANES[array]), value, 0.0)
        stats[...] = total

    def remote(src, dst, key, send_sem, recv_sem, peer):
        copies[key] = pltpu.make_async_remote_copy(
            src_ref=src,
            dst_ref=dst,
            send_sem=send_sem,
            recv_sem=recv_sem,
            device_id=peer,
            device_id_type=MESH_ID,
        )
        copies[key].start()

    def start(number, stage):
        at, array, first, size, turn = units[number]
        mine = own[number]
        if stage == 0:
            peer = device(z, x, y, 1 - c)
            src = grads[array].at[
                spot(array, every, 1 - c, every, every) + (pl.ds(first, size),)
            ]
            dst = one[number]
        elif stage == 1 and turn == 0:
            peer = device(z, 1 - x, y, c)
            src, dst = mine.at[half_spot(array, every, every, 1 - x)], two[number]
        elif stage == 1:
            peer = device(z, x, 1 - y, c)
            src, dst = mine.at[half_spot(array, 1 - y, every, every)], two[number]
        elif stage == 2 and turn == 0:
            peer = device(z, x, 1 - y, c)
            src, dst = mine.at[half_spot(array, 1 - y, every, x)], three[number]
        elif stage == 2:
            peer = device(z, 1 - x, y, c)
            src, dst = mine.at[half_spot(array, y, every, 1 - x)], three[number]
        else:
            other = flip(z, stage - 2)
            peer = device(other, x, y, c)
            src, dst = mine.at[half_spot(array, y, other, x)], four[number].at[stage - 3]
        remote(src, dst, (number, stage), send.at[number, stage], recv.at[number, stage], peer)

    def add(number, stage):
        at, array, first, size, turn = units[number]
        mine = own[number]

        def pair(here, there):
            mine[here] = (mine[here].astype(f32) + there.astype(f32)).astype(bf16)

        if stage == 0:

            @pl.loop(0, 16)
            def _(k):
                iy, iz, ix = k // 8, (k // 2) % 4, k % 2
                here = half_spot(array, iy, iz, ix)
                pair(here, one[number][here])

        elif stage == 1 and turn == 0:

            @pl.loop(0, 8)
            def _(k):
                iy, iz = k // 4, k % 4
                there = (iz, iy) if array in SHARED else (iy, iz)
                pair(half_spot(array, iy, iz, x), two[number][there])

        elif stage == 1:

            @pl.loop(0, 8)
            def _(k):
                iz, ix = k // 2, k % 2
                pair(half_spot(array, y, iz, ix), two[number][iz, ix])

        elif stage == 2:

            @pl.loop(0, 4)
            def _(k):
                pair(half_spot(array, y, k, x), three[number][k])

        else:
            total = mine[half_spot(array, y, z, x)].astype(f32)
            for slot in range(3):
                total = total + four[number][slot].astype(f32)
            if array in SHARED:
                outs[array][y * 2 + c, pl.ds(first, size)] = total
            else:
                outs[array][pl.ds(first, size)] = total

    loads = []
    for number, (at, array, first, size, turn) in enumerate(units):
        loads.append(
            pltpu.make_async_copy(
                grads[array].at[spot(array, every, c, every, every) + (pl.ds(first, size),)],
                own[number],
                local.at[number],
            )
        )
    stats[...] = jnp.zeros_like(stats)
    greet(z, x, y, c)
    steps = units[-1][0] + 1

    def step_units(tick):
        return [number for number in range(n) if units[number][0] == tick]

    vec_dst = (vec_one, vec_two, vec_three)
    vec_peer = (device(z, x, y, 1 - c), device(z, 1 - x, y, c), device(z, x, 1 - y, c))

    for tick in range(steps + 4):
        for number in step_units(tick):
            loads[number].start()
            start(number, 0)
        for number in step_units(tick - 1):
            loads[number].wait()
            copies[number, 0].wait_recv()
            add(number, 0)
            start(number, 1)
        for number in step_units(tick - 2):
            copies[number, 1].wait()
            add(number, 1)
            start(number, 2)
        for number in step_units(tick - 3):
            copies[number, 2].wait()
            add(number, 2)
            for stage in (3, 4, 5):
                start(number, stage)
        for number in step_units(tick - 4):
            for stage in (3, 4, 5):
                copies[number, stage].wait()
            add(number, 3)
        if tick == 0:
            vec_sum[...] = grads[6][...]
        if 1 <= tick <= 3:
            copies["v", tick - 1].wait()
            vec_sum[...] = vec_sum[...] + vec_dst[tick - 1][...]
        if tick < 3:
            remote(vec_sum, vec_dst[tick], ("v", tick), vsend.at[tick], vrecv.at[tick], vec_peer[tick])
        elif tick == 3:
            vec_four[z] = vec_sum[...]
            for m in (1, 2, 3):
                peer = device(flip(z, m), x, y, c)
                remote(vec_sum, vec_four.at[z], ("v", 2 + m), vsend.at[2 + m], vrecv.at[2 + m], peer)
        elif tick == 4:
            for m in (1, 2, 3):
                copies["v", 2 + m].wait()
            vec_sum[...] = (vec_four[0] + vec_four[1]) + (vec_four[2] + vec_four[3])
            outs[VEC][...] = vec_sum[z * 2 + x]
            tally(VEC)
        for array in range(6):
            last = max(units[number][0] for number in range(n) if units[number][1] == array)
            if array in SHARED and tick == last + 4:
                here = y * 2 + c
                peers = (
                    device(z, x, y, 1 - c),
                    device(z, x, 1 - y, c),
                    device(z, x, 1 - y, 1 - c),
                )
                for k, peer in enumerate(peers):
                    slot = SHARED.index(array) * 3 + k
                    piece = outs[array].at[here]
                    remote(piece, piece, ("t", slot), tsend.at[slot], trecv.at[slot], peer)
            elif array in SHARED and tick == last + 5:
                for k in range(3):
                    copies["t", SHARED.index(array) * 3 + k].wait()
                tally(array)
            elif array not in SHARED and tick == last + 4:
                tally(array)
    here = (x * 2 + y) * 2 + c
    stat_one[here] = stats[...]
    for m in range(1, 8):
        peer = device(
            z,
            1 - x if m // 4 else x,
            1 - y if (m // 2) % 2 else y,
            1 - c if m % 2 else c,
        )
        remote(stats, stat_one.at[here], ("p", m), ssend.at[m], srecv.at[m], peer)
    for m in range(1, 8):
        copies["p", m].wait()
    total = stat_one[0]
    for slot in range(1, 8):
        total = total + stat_one[slot]
    stats[...] = total
    stat_four[z] = total
    for m in (1, 2, 3):
        remote(
            stats,
            stat_four.at[z],
            ("s", 2 + m),
            ssend.at[7 + m],
            srecv.at[7 + m],
            device(flip(z, m), x, y, c),
        )
    for m in (1, 2, 3):
        copies["s", 2 + m].wait()
    norms = jnp.sqrt((stat_four[0] + stat_four[1]) + (stat_four[2] + stat_four[3]))
    loss = vec_sum[7, 7:8, 128:256][:, 31:32]
    outs[7][...] = jnp.where(stat_row == 2, loss, norms)
    for number in range(n):
        copies[number, 0].wait_send()
    for store in stores:
        store.wait()


def scatter_gradients(grads, masters, firsts, seconds):
    units = [(at,) + unit for at, step in enumerate(SCATTER_STEPS) for unit in step]
    n = len(units)
    shapes = [grad.shape for grad in grads]
    outs = []
    for array in range(6):
        rows, columns = shapes[array][4:]
        if array in SHARED:
            outs.append(jax.ShapeDtypeStruct((4, rows, columns), f32))
        else:
            outs.append(jax.ShapeDtypeStruct((rows, columns), f32))
    outs.append(jax.ShapeDtypeStruct(grads[6].shape[1:], f32))
    outs.append(jax.ShapeDtypeStruct((8, 128), f32))
    scratch = []
    for stage in range(5):
        for at, array, first, size, turn in units:
            shared = array in SHARED
            lead = ((4, 2, 2) if shared else (2, 4, 2), (4,), (3,))
            if stage < 2:
                lead = lead[0]
            elif stage == 2:
                lead = ((4, 2) if shared else (2, 4)) if turn == 0 else (4, 2)
            else:
                lead = lead[stage - 2]
            scratch.append(pltpu.VMEM(lead + (size, shapes[array][5]), bf16))
    vec = grads[6].shape
    scratch += [pltpu.VMEM(vec, f32)] * 3 + [pltpu.VMEM((4,) + vec, f32), pltpu.VMEM(vec, f32)]
    scratch += [pltpu.VMEM(lead + (8, 128), f32) for lead in ((), (8,), (4,))]
    scratch += [
        pltpu.SemaphoreType.DMA((n, 6)),
        pltpu.SemaphoreType.DMA((n, 6)),
        pltpu.SemaphoreType.DMA((n,)),
        pltpu.SemaphoreType.DMA((6,)),
        pltpu.SemaphoreType.DMA((6,)),
        pltpu.SemaphoreType.DMA((6,)),
        pltpu.SemaphoreType.DMA((6,)),
        pltpu.SemaphoreType.DMA((11,)),
        pltpu.SemaphoreType.DMA((11,)),
    ]
    states = [*masters, *firsts, *seconds]
    scratch += [pltpu.VMEM(member.shape, f32) for member in states + outs[:7]]
    scratch += [pltpu.SemaphoreType.DMA((21,)), pltpu.SemaphoreType.DMA((7,))]
    in_vmem = pl.BlockSpec(memory_space=pltpu.VMEM)
    anywhere = pl.BlockSpec(memory_space=pl.ANY)
    total = sum(int(grad.size) * grad.dtype.itemsize for grad in grads)
    return pl.pallas_call(
        functools.partial(scatter_kernel, shapes, units),
        out_shape=outs,
        in_specs=[anywhere] * 6 + [in_vmem] + [anywhere] * 21,
        out_specs=[anywhere] * 7 + [in_vmem],
        scratch_shapes=scratch,
        compiler_params=pltpu.CompilerParams(
            collective_id=1, has_side_effects=True, vmem_limit_bytes=60 * 1024 * 1024
        ),
        cost_estimate=pl.CostEstimate(flops=0, bytes_accessed=2 * total, transcendentals=0),
        name="scatter_gradients",
    )(*grads, *masters, *firsts, *seconds)


def apply_kernel(*refs):
    sources, stats = refs[:28], refs[28]
    targets = refs[29:50]
    loss, pairs = refs[50:52]
    held = refs[52:80]
    results = refs[80:101]
    loaded, stored = refs[101:]
    loads = [
        pltpu.make_async_copy(source, target, loaded.at[at])
        for at, (source, target) in enumerate(zip(sources, held))
    ]
    order = (EIN, EOUT, DIN, DOUT, PIX, BRI, VEC)
    for array in order:
        for kind in range(4):
            loads[7 * kind + array].start()
    grads, masters, firsts, seconds = (held[7 * k : 7 * k + 7] for k in range(4))
    next_firsts, next_seconds, news = (results[7 * k : 7 * k + 7] for k in range(3))
    stores = [
        pltpu.make_async_copy(source, target, stored.at[at])
        for at, (source, target) in enumerate(zip(results, targets))
    ]
    for array in order:
        lane = STAT_LANES[array]
        norms = [stats[row : row + 1, :][:, lane : lane + 1] for row in range(2)]
        ratio = learn_rate * norms[0] / norms[1]
        count = masters[array].shape[0]
        if len(masters[array].shape) == 3:
            count = count * masters[array].shape[1]
        decay = 0.0 if array == VEC else decay_matrix

        def body(rows, array=array, ratio=ratio, decay=decay):
            if array == VEC:
                gradient = grads[VEC][:7, : masters[VEC].shape[1]]
            else:
                gradient = grads[array][rows]
            master = state_rows(masters[array], rows)
            next_one, next_two, update = moments(
                gradient,
                state_rows(firsts[array], rows),
                state_rows(seconds[array], rows),
                master,
                decay,
            )
            put_rows(next_firsts[array], rows, next_one)
            put_rows(next_seconds[array], rows, next_two)
            put_rows(news[array], rows, master - ratio * update)

        for kind in range(4):
            loads[7 * kind + array].wait()
        if array == VEC:
            body(slice(None))
        else:
            row_loop(count, state_step(count), body)
        for kind in range(3):
            stores[7 * kind + array].start()
    pairs[...] = stats[:2, :][:, :7]
    loss[...] = stats[2:3, :][:, :1]
    for store in stores:
        store.wait()


def apply_update(reduced, masters, firsts, seconds, stats):
    shapes = [jax.ShapeDtypeStruct(master.shape, f32) for master in masters]
    operands = [*reduced, *masters, *firsts, *seconds]
    in_vmem = pl.BlockSpec(memory_space=pltpu.VMEM)
    anywhere = pl.BlockSpec(memory_space=pl.ANY)
    results = pl.pallas_call(
        apply_kernel,
        out_shape=shapes * 3
        + [jax.ShapeDtypeStruct((1, 1), f32), jax.ShapeDtypeStruct((2, 7), f32)],
        in_specs=[anywhere] * 28 + [in_vmem],
        out_specs=[anywhere] * 21 + [in_vmem] * 2,
        scratch_shapes=[pltpu.VMEM(member.shape, f32) for member in operands]
        + [pltpu.VMEM(master.shape, f32) for master in masters] * 3
        + [pltpu.SemaphoreType.DMA((28,)), pltpu.SemaphoreType.DMA((21,))],
        compiler_params=pltpu.CompilerParams(vmem_limit_bytes=60 * 1024 * 1024),
        name="apply_update",
    )(*operands, stats)
    return results[:7], results[7:14], results[14:21], results[21].reshape(()), results[22]


def sinusoid_table(feature_width, grid_side, patch_count, padded):
    position = np.arange(patch_count)
    quarter = feature_width // 4
    omegas = 1.0 / 10000.0 ** (np.arange(quarter) / quarter)
    parts = []
    for coords in (position % grid_side, position // grid_side):
        angles = coords[:, None] * omegas[None, :]
        parts += [np.sin(angles), np.cos(angles)]
    table = np.concatenate(parts, axis=1).astype(np.float32)
    return jnp.asarray(np.pad(table, ((0, padded - patch_count), (0, 0))))


GROUPS = 4
ENC = dict(step=128, first=0, images=4, block=64, tokens=50, width=768, heads=3, head=64, hidden=768, spans=1)
DEC = dict(step=416, first=768, images=4, block=208, tokens=197, width=512, heads=4, head=32, hidden=512, spans=4)
CLASS_ROW = 49
MASK_ROW = 50


def dot(left, right, dims=((1,), (0,)), precision=None):
    return lax.dot_general(
        left, right, (dims, ((), ())), preferred_element_type=f32, precision=precision
    )


def dot_t(left, right):
    return dot(left, right, ((0,), (0,)))


def dot_nt(left, right):
    return dot(left, right, ((1,), (1,)))


def exact_pick(choice, values, dims):
    total = None
    for _ in range(3):
        part = values.astype(bf16)
        values = values - part.astype(f32)
        product = dot(choice, part, dims)
        total = product if total is None else total + product
    return total


def row_loop(count, step, body):
    @pl.loop(0, count // step)
    def _(k):
        body(pl.ds(pl.multiple_of(k * step, step), step))


def fold(values):
    step, width = values.shape
    return jnp.sum(values.reshape(step // 8, 8, width), axis=0)


def norm_rows(source, gain, shift, unit, inverse, low, step):
    def body(rows):
        values = source[rows]
        centred = values - jnp.mean(values, axis=-1, keepdims=True)
        scale = lax.rsqrt(jnp.mean(centred * centred, axis=-1, keepdims=True) + eps_norm)
        normed = centred * scale
        unit[rows] = normed
        inverse[rows] = scale
        low[rows] = (normed * gain + shift).astype(bf16)

    row_loop(source.shape[0], step, body)


def norm_back_rows(incoming, unit, inverse, gain, result, residual, sums, at, step):
    width = incoming.shape[-1]

    def body(rows):
        given = incoming[rows]
        normed = unit[rows]
        scaled = given * gain
        inner = (
            scaled
            - jnp.mean(scaled, axis=-1, keepdims=True)
            - normed * jnp.mean(scaled * normed, axis=-1, keepdims=True)
        )
        value = inverse[rows] * inner
        if residual is not None:
            value = value + residual[rows]
        sums[at] = sums[at] + fold(given * normed)
        sums[at + 1] = sums[at + 1] + fold(given)
        result[rows] = value

    row_loop(incoming.shape[0], step, body)


def lane_chunks(size):
    return [slice(at, min(at + 128, size)) for at in range(0, size, 128)]


def attend_mask(dims, scores, start):
    if dims["spans"] == 1:
        key = lax.broadcasted_iota(jnp.int32, scores.shape, 0)
        query = lax.broadcasted_iota(jnp.int32, scores.shape, 1) + start
        allowed = ((key // dims["block"]) == (query // dims["block"])) & (
            (key % dims["block"]) < dims["tokens"]
        )
        return jnp.where(allowed, scores, -1e30)
    first = dims["tokens"] // 16 * 16
    tail = scores[first:]
    key = lax.broadcasted_iota(jnp.int32, tail.shape, 0) + first
    return jnp.concatenate([scores[:first], jnp.where(key < dims["tokens"], tail, -1e30)], axis=0)


def layer_forward_rows(dims, stream, w_in, w_out, vectors, saved):
    unit_one, inv_one, low_one, qkv, probs, mixed, unit_two, inv_two, low_two, active, slope, work, low_work, low_more = saved
    count, width = stream.shape
    inner = dims["heads"] * dims["head"]
    span = count // dims["spans"]
    norm_rows(stream, vectors[1:2, :], vectors[2:3, :], unit_one, inv_one, low_one, dims["step"])

    @pl.loop(0, GROUPS)
    def _(t):
        weights = w_in[t, :, : 3 * inner] if inner % 128 == 0 else w_in[t][:, : 3 * inner]

        def body(rows):
            qkv[t, rows] = dot(low_one[rows], weights).astype(bf16)

        body(slice(None))

    yield "projected"
    scale = dims["head"] ** (-0.5)

    @pl.loop(0, GROUPS * dims["spans"])
    def _(k):
        t = k // dims["spans"]
        b = k % dims["spans"]
        rows = pl.ds(pl.multiple_of(b * span, span), span)
        triple = qkv[t, rows]
        query_t = triple[:, :inner].T
        value_t = triple[:, 2 * inner :].T
        heads = range(dims["heads"])
        lanes = [slice(head * dims["head"], (head + 1) * dims["head"]) for head in heads]
        for head in heads:
            key = triple[:, inner : 2 * inner][:, lanes[head]]
            work[head] = dot(key, query_t[lanes[head]])
        for head in heads:
            for columns in lane_chunks(span):
                scores = attend_mask(dims, work[head, :, columns] * scale, columns.start)
                shifted = jnp.exp(scores - jnp.max(scores, axis=0, keepdims=True))
                share = shifted * (1.0 / jnp.sum(shifted, axis=0, keepdims=True))
                probs[k * dims["heads"] + head, :, columns] = share
                low_work[head, :, columns] = share.astype(bf16)
        results = [dot(value_t[lanes[head]], low_work[head]) for head in heads]
        mixed[t, rows] = jnp.concatenate(results, axis=0).T.astype(bf16)

    yield "attended"

    @pl.loop(0, GROUPS)
    def _(t):
        weights = w_out[t, :inner]

        def body(rows):
            stream[rows] = stream[rows] + dot(mixed[t, rows], weights)

        body(slice(None))

    norm_rows(stream, vectors[3:4, :], vectors[4:5, :], unit_two, inv_two, low_two, dims["step"])

    def feed(t):
        up = w_in[t, :, 3 * inner :] if inner % 128 == 0 else w_in[t][:, 3 * inner :]
        down = w_out[t, inner:]
        slope[t] = dot(low_two[...], up)

        def bend(rows):
            hidden = slope[t, rows]
            level = 0.5 + 0.5 * lax.erf(hidden * (0.5**0.5))
            active[t, rows] = (hidden * level).astype(bf16)
            slope[t, rows] = level + hidden * (
                jnp.exp(-0.5 * hidden * hidden) * (0.5 / np.pi) ** 0.5
            )

        row_loop(count, 32, bend)
        stream[...] = stream[...] + dot(active[t], down)

    half = GROUPS // 2 if dims["spans"] == 1 else GROUPS
    pl.loop(0, half)(feed)
    if half < GROUPS:
        yield "halfway"
        pl.loop(half, GROUPS)(feed)


def layer_backward_rows(
    dims, given, spare, w_in, w_out, vectors, saved, low, flow, turned, grad_in, grad_out, sums, need, ready
):
    unit_one, inv_one, low_one, qkv, probs, mixed, unit_two, inv_two, low_two, active, slope, work, low_work, low_more = saved
    count, width = given.shape
    inner = dims["heads"] * dims["head"]
    span = count // dims["spans"]
    aligned = inner % 128 == 0

    def lower(rows):
        low[rows] = given[rows].astype(bf16)
        spare[rows] = jnp.zeros_like(spare[rows])

    row_loop(count, 32, lower)
    need("low_two", "active", "slope", "w_out", "w_in")
    turned[...] = low_two[...].T

    @pl.loop(0, GROUPS)
    def _(t):
        down = w_out[t, inner:]
        up = w_in[t, :, 3 * inner :] if aligned else w_in[t][:, 3 * inner :]
        grad_out[t, inner:] = dot_t(active[t], low[...]).astype(bf16)

        def body(rows):
            flow[rows] = (slope[t, rows] * dot_nt(low[rows], down)).astype(bf16)
            spare[rows] = spare[rows] + dot_nt(flow[rows], up)

        body(slice(None))
        grad_up = dot(turned[...], flow[...]).astype(bf16)
        if aligned:
            grad_in[t, :, 3 * inner :] = grad_up
        else:
            grad_in[t] = jnp.concatenate([jnp.zeros((width, 3 * inner), bf16), grad_up], axis=1)

    need("unit_two", "inv_two", "mixed")
    norm_back_rows(spare, unit_two, inv_two, vectors[3:4, :], given, given, sums, 3, dims["step"])
    row_loop(count, 32, lower)

    @pl.loop(0, GROUPS)
    def _(t):
        weights = w_out[t, :inner]
        grad_out[t, :inner] = dot_t(mixed[t], low[...]).astype(bf16)

        mixed[t] = dot_nt(low[...], weights).astype(bf16)
        ready("out", t)

    need("qkv", "probs")

    scale = dims["head"] ** (-0.5)

    @pl.loop(0, GROUPS * dims["spans"])
    def _(k):
        t = k // dims["spans"]
        b = k % dims["spans"]
        rows = pl.ds(pl.multiple_of(b * span, span), span)
        triple = qkv[t, rows]
        back = mixed[t, rows]
        key_t = triple[:, inner : 2 * inner].T
        back_t = back.T
        heads = range(dims["heads"])
        lanes = [slice(head * dims["head"], (head + 1) * dims["head"]) for head in heads]
        for head in heads:
            work[head] = dot(triple[:, 2 * inner :][:, lanes[head]], back_t[lanes[head]])
        for head in heads:
            for columns in lane_chunks(span):
                share = probs[k * dims["heads"] + head, :, columns]
                grad_p = work[head, :, columns]
                grad_s = share * (grad_p - jnp.sum(share * grad_p, axis=0, keepdims=True))
                low_work[head, :, columns] = grad_s.astype(bf16)
                low_more[head, :, columns] = share.astype(bf16)
        parts = ([], [], [])
        for head in heads:
            parts[0].append(dot(key_t[lanes[head]], low_work[head]) * scale)
            parts[1].append(dot(low_work[head], triple[:, :inner][:, lanes[head]]) * scale)
            parts[2].append(dot(low_more[head], back[:, lanes[head]]))
        grad_query = jnp.concatenate(parts[0], axis=0).T
        qkv[t, rows] = jnp.concatenate([grad_query] + parts[1] + parts[2], axis=1).astype(bf16)

    need("low_one", "unit_one", "inv_one")
    turned[...] = low_one[...].T

    @pl.loop(0, GROUPS)
    def _(t):
        weights = w_in[t, :, : 3 * inner] if aligned else w_in[t][:, : 3 * inner]
        grad_triple = dot(turned[...], qkv[t]).astype(bf16)
        if aligned:
            grad_in[t, :, : 3 * inner] = grad_triple
        else:
            grad_in[t] = jnp.concatenate([grad_triple, grad_in[t][:, 3 * inner :]], axis=1)

        ready("in", t)
        spare[...] = spare[...] + dot_nt(qkv[t], weights)

    norm_back_rows(spare, unit_one, inv_one, vectors[1:2, :], given, given, sums, 1, dims["step"])


def saved_shapes(dims):
    count = dims["images"] * dims["block"]
    width, inner = dims["width"], dims["heads"] * dims["head"]
    span = count // dims["spans"]
    return [
        ((count, width), f32),
        ((count, 1), f32),
        ((count, width), bf16),
        ((GROUPS, count, 3 * inner), bf16),
        ((GROUPS * dims["spans"] * dims["heads"], span, span), f32),
        ((GROUPS, count, inner), bf16),
        ((count, width), f32),
        ((count, 1), f32),
        ((count, width), bf16),
        ((GROUPS, count, dims["hidden"]), bf16),
        ((GROUPS, count, dims["hidden"]), f32),
    ]


def work_shapes(dims):
    span = dims["images"] * dims["block"] // dims["spans"]
    shape = (dims["heads"], span, span)
    return [(shape, f32), (shape, bf16), (shape, bf16)]


SAVED = (
    "unit_one", "inv_one", "low_one", "qkv", "probs", "mixed",
    "unit_two", "inv_two", "low_two", "active", "slope",
)


def loader(names, sources, targets, semaphores):
    copies = {}
    for at, (name, source, target) in enumerate(zip(names, sources, targets)):
        copies[name] = pltpu.make_async_copy(source, target, semaphores.at[at])
        copies[name].start()

    def need(*wanted):
        for name in wanted:
            if name in copies:
                copies.pop(name).wait()

    return need


def storer(held, outs, semaphores):
    def ready(kind, t):
        at = ("in", "out").index(kind)
        pltpu.make_async_copy(held[at].at[t], outs[at].at[t], semaphores.at[at]).start()

    def finish():
        for at in range(2):
            pltpu.make_async_copy(held[at], outs[at], semaphores.at[at]).wait()

    return ready, finish


def token_gain(vectors, dims):
    return vectors.at[:, pl.ds(dims["first"], dims["width"])]


def decoder_kernel(*refs):
    projected, codes, images, table, w_in_all, w_out_all, pixel_w, vectors_all = refs[:8]
    grad_in_all, grad_out_all, grad_head, grad_projected, vec_out = refs[8:13]
    stream, given, unit, inverse, low, flow, sums, loss, head, pixels_here, head_sum = refs[13:24]
    w_in, w_out, grad_in, grad_out, turned, loaded, stored = refs[24:31]
    saved = refs[31:]
    dims = DEC
    vectors = token_gain(vectors_all, dims)
    count, width = stream.shape
    block = dims["block"]
    need = loader(
        ("w_in", "w_out", "head", "images"),
        (w_in_all, w_out_all, pixel_w.at[pl.ds(PATCH_DIM, width)], images),
        (w_in, w_out, head, pixels_here),
        loaded,
    )
    ready, finish = storer((grad_in, grad_out), (grad_in_all, grad_out_all), stored)
    sums[...] = jnp.zeros_like(sums)
    loss[...] = jnp.zeros_like(loss)

    def placer(b):
        return (
            lax.broadcasted_iota(jnp.int32, (64, block), 0) == codes[b][:1, :block]
        ).astype(bf16)

    def block_rows(b):
        return pl.ds(pl.multiple_of(b * block, block), block)

    @pl.loop(0, dims["images"])
    def _(b):
        at = lax.broadcasted_iota(jnp.int32, (64, width), 0)
        source = jnp.where(at == MASK_ROW, vectors[0:1, :], projected[b])
        source = jnp.where(at > MASK_ROW, 0.0, source)
        stream[block_rows(b)] = exact_pick(placer(b), source, ((0,), (0,))) + table[...]

    need("w_in", "w_out")
    for _ in layer_forward_rows(dims, stream, w_in, w_out, vectors, saved):
        pass
    norm_rows(stream, vectors[5:6, :], vectors[6:7, :], unit, inverse, low, dims["step"])
    need("head", "images")
    head_sum[...] = jnp.zeros_like(head_sum)
    pixels_wide = pixels_here.shape[-1]
    counted = vectors_all[7:8, :]
    patch_total = jnp.sum(counted, axis=1, keepdims=True) / (counted.shape[1] // 8)

    @pl.loop(0, dims["images"])
    def _(b):
        rows = block_rows(b)
        predicted = dot(low[rows], head[...])
        pixels = pixels_here[b].astype(f32)
        centred = pixels - jnp.mean(pixels, axis=-1, keepdims=True)
        variance = jnp.sum(centred * centred, axis=-1, keepdims=True) / (pixels_wide - 1)
        errors = predicted - centred * lax.rsqrt(variance + eps_norm)
        at = lax.broadcasted_iota(jnp.int32, (64, 128), 0)
        spread = jnp.where(at == MASK_ROW, codes[b][2:3, :128].astype(f32), 0.0)
        weight = dot_t(placer(b), spread.astype(bf16))[:, :1] / patch_total
        loss[...] = loss[...] + fold(errors * errors * weight)
        grad_low = (errors * (2.0 / pixels_wide) * weight).astype(bf16)
        head_sum[...] = head_sum[...] + dot_t(low[rows], grad_low)
        given[rows] = dot_nt(grad_low, head[...])

    grad_head[...] = head_sum[...].astype(bf16)
    norm_back_rows(given, unit, inverse, vectors[5:6, :], given, None, sums, 5, dims["step"])
    layer_backward_rows(
        dims, given, stream, w_in, w_out, vectors, saved, low, flow, turned, grad_in, grad_out, sums, need, ready
    )

    @pl.loop(0, dims["images"])
    def _(b):
        back = exact_pick(placer(b), given[block_rows(b)], ((1,), (0,)))
        at = lax.broadcasted_iota(jnp.int32, (64, width), 0)
        grad_projected[b] = jnp.where(at < MASK_ROW, back, 0.0).astype(bf16)
        sums[0] = sums[0] + fold(jnp.where(at == MASK_ROW, back, 0.0))

    for row in range(7):
        vec_out[row : row + 1, :] = jnp.sum(sums[row], axis=0, keepdims=True)
    total = jnp.sum(jnp.sum(loss[...], axis=0, keepdims=True), axis=1, keepdims=True)
    vec_out[7:8, :] = jnp.broadcast_to(total / pixels_wide, (1, width))
    finish()


def decoder_step(projected, codes, images, table, w_in, w_out, pixel_w, vectors):
    dims = DEC
    count, width = dims["images"] * dims["block"], dims["width"]
    wide = images.shape[-1]
    outs = [
        jax.ShapeDtypeStruct(w_in.shape, bf16),
        jax.ShapeDtypeStruct(w_out.shape, bf16),
        jax.ShapeDtypeStruct((width, wide), bf16),
        jax.ShapeDtypeStruct(projected.shape, bf16),
        jax.ShapeDtypeStruct((8, width), f32),
    ]
    scratch = [
        ((count, width), f32),
        ((count, width), f32),
        ((count, width), f32),
        ((count, 1), f32),
        ((count, width), bf16),
        ((count, dims["hidden"]), bf16),
        ((7, 8, width), f32),
        ((8, wide), f32),
        ((width, wide), bf16),
        (images.shape, bf16),
        ((width, wide), f32),
        (w_in.shape, bf16),
        (w_out.shape, bf16),
        (w_in.shape, bf16),
        (w_out.shape, bf16),
        ((width, count), bf16),
        4,
        2,
    ]
    scratch += saved_shapes(dims) + work_shapes(dims)
    in_vmem = pl.BlockSpec(memory_space=pltpu.VMEM)
    anywhere = pl.BlockSpec(memory_space=pl.ANY)
    return pl.pallas_call(
        decoder_kernel,
        out_shape=outs,
        in_specs=[in_vmem, in_vmem, anywhere, in_vmem, anywhere, anywhere, anywhere, in_vmem],
        out_specs=[anywhere, anywhere, in_vmem, in_vmem, in_vmem],
        scratch_shapes=[
            pltpu.SemaphoreType.DMA((shape,)) if isinstance(shape, int) else pltpu.VMEM(*shape)
            for shape in scratch
        ],
        compiler_params=pltpu.CompilerParams(vmem_limit_bytes=62 * 1024 * 1024),
        name="decoder_step",
    )(projected, codes, images, table, w_in, w_out, pixel_w, vectors)


def encode_kernel(ring, *refs):
    dims = ENC
    images, keep_index, unshuffle, masked, image_valid, table = refs[:6]
    refs = refs[6:]
    group = lax.axis_index("tensor")
    if ring:
        masters, refs = refs[:7], refs[7:]
        wholes, vectors_all, codes, pictures, projected = refs[:7], *refs[7:11]
        kept_state, refs = refs[11:26], refs[26:]
        parts, send, recv, local, vec_parts = refs[:7], *refs[7:11]
        raw = dict(zip((PIX, EOUT, BRI), refs[11:14]))
        refs = refs[14:]
    else:
        wholes, vectors_all = refs[:4], refs[4]
        codes, pictures, projected, kept_state = refs[5], refs[6], refs[7], refs[8:23]
        refs = refs[23:]
        wholes = dict(zip((PIX, EIN, EOUT, BRI), wholes))
    loaded, flushed = refs[:2]
    first_copies = []
    if ring:
        shards, states_loaded, refs = refs[2:9], refs[9], refs[:2] + refs[10:]
        for at, (source, target) in enumerate(zip(masters, shards)):
            first_copies.append(pltpu.make_async_copy(source, target, states_loaded.at[at]))
            first_copies[-1].start()
        masters = shards
    eight, pixels_here, stream, w_in, w_out, embed, bridge = refs[2:9]
    retained, unit, inverse, low = refs[9:13]
    saved = refs[13:24]
    work = refs[24:]
    held = (retained, unit, inverse, low) + tuple(saved)
    vectors = token_gain(vectors_all, dims)
    count, width = stream.shape
    block = dims["block"]

    first = pl.multiple_of((group // 2) * 8, 8)
    eight_copy = pltpu.make_async_copy(images.at[:, pl.ds(first, 8)], eight, loaded.at[4])
    eight_copy.start()
    lane = lax.broadcasted_iota(jnp.int32, (1, codes.shape[2]), 1)
    valid = image_valid[...]
    image_at = lax.broadcasted_iota(jnp.int32, valid.shape, 1)
    codes[...] = jnp.full(codes.shape, -1, jnp.int32)
    for b in range(dims["images"]):
        mine = group * dims["images"] + b
        row = pl.ds(mine, 1)
        codes[b, 0:1, :] = jnp.where(lane == IMAGE_PATCHES, CLASS_ROW, -1)
        codes[b, 0:1, :IMAGE_PATCHES] = jnp.where(masked[row] == 1, MASK_ROW, unshuffle[row])
        codes[b, 1:2, :KEEP] = keep_index[row]
        own_valid = jnp.sum(
            jnp.where(image_at == mine, valid, 0).astype(f32), axis=1, keepdims=True
        )
        codes[b, 2:3, :] = jnp.broadcast_to(own_valid, (1, codes.shape[2])).astype(jnp.int32)

    def load(slot, array, target):
        if not ring:
            source = wholes[array]
            if array == PIX:
                source = source.at[pl.ds(0, PATCH_DIM)]
            pltpu.make_async_copy(source, target, loaded.at[slot]).start()
            return pltpu.make_async_copy(source, target, loaded.at[slot])
        if array != EIN:
            pltpu.make_async_copy(wholes[array], raw[array], loaded.at[slot]).start()
            return pltpu.make_async_copy(wholes[array], raw[array], loaded.at[slot])
        rows = wholes[array].shape[4]

        @pl.loop(0, 32)
        def _(k):
            pltpu.make_async_copy(
                wholes[array].at[k // 16, (k // 8) % 2, (k // 2) % 4, k % 2],
                target.at[k // 8, pl.ds(pl.multiple_of((k % 8) * rows, rows), rows)],
                loaded.at[slot],
            ).start()

        return pltpu.make_async_copy(target, target, loaded.at[slot])

    def assemble(array, target):
        if ring and array in SHARED:
            count = -(-target.shape[0] // raw[array].shape[4])
            pieces = [
                raw[array][k // 8, (k // 4) % 2, (k // 2) % 2, k % 2] for k in range(count)
            ]
            target[...] = jnp.concatenate(pieces, axis=0)[: target.shape[0]]
        elif ring:

            @pl.loop(0, GROUPS)
            def _(t):
                pieces = [raw[array][t // 2, t % 2, k // 2, k % 2] for k in range(8)]
                target[t] = jnp.concatenate(pieces, axis=0)

    flushes = []

    def flush(*members):
        for member in members:
            copy = pltpu.make_async_copy(held[member], kept_state[member], flushed.at[member])
            copy.start()
            flushes.append(copy)

    for copy in first_copies:
        copy.wait()
    if ring:
        for array in range(6):
            if array in SHARED:
                rows = masters[array].shape[0] // 4
                rows = pl.ds(pl.multiple_of(group * rows, 8), rows)
                parts[array][...] = masters[array][rows].astype(bf16)
            else:
                parts[array][...] = state_rows(masters[array], slice(None)).astype(bf16)
        columns = masters[VEC].shape[1]
        parts[VEC][...] = jnp.zeros_like(parts[VEC])
        parts[VEC][:7, :columns] = masters[VEC][...].astype(bf16).astype(f32)
        counts = dot(valid.astype(bf16), masked[...].astype(f32).astype(bf16))
        counted = jnp.sum(counts, axis=1, keepdims=True)
        parts[VEC][7:8, :] = jnp.broadcast_to(counted, (1, parts[VEC].shape[1]))
        ticks = gather_ticks(parts, wholes, send, recv, local)

    done = [-1]

    def until(tick):
        while ring and done[0] < tick:
            next(ticks)
            done[0] += 1

    at_embed, at_in, at_out = (
        last_step(GATHER_STEPS, array) + DEPTH for array in (PIX, EIN, EOUT)
    )
    at_end = len(GATHER_STEPS) - 1 + DEPTH
    until(0)
    eight_copy.wait()
    pixels_wide = eight.shape[2]

    @pl.loop(0, dims["images"])
    def _(b):
        size = (pixels_here.shape[1], IMAGE_PATCHES * 8)
        patch = lax.broadcasted_iota(jnp.int32, size, 0)
        at = lax.broadcasted_iota(jnp.int32, size, 1)
        wanted = patch * 8 + (group % 2) * dims["images"] + b
        choice = (at == wanted) & (patch < IMAGE_PATCHES)
        flat = eight[...].reshape(IMAGE_PATCHES * 8, pixels_wide)
        pixels_here[b] = dot(choice.astype(f32).astype(bf16), flat).astype(bf16)

    picture_copy = pltpu.make_async_copy(pixels_here, pictures, loaded.at[5])
    picture_copy.start()
    until(at_embed)
    embed_copy = load(0, PIX, embed)
    if ring:
        vec_copy = pltpu.make_async_copy(wholes[VEC], vec_parts, loaded.at[1])
        vec_copy.start()
        vec_copy.wait()
        vectors_all[...] = jnp.concatenate(
            [vec_parts[0, 0, k // 2, k % 2][:, :columns] for k in range(8)], axis=1
        )
    embed_copy.wait()
    assemble(PIX, embed)

    @pl.loop(0, dims["images"])
    def _(b):
        rows = pl.ds(pl.multiple_of(b * block, block), block)
        choice = (
            lax.broadcasted_iota(jnp.int32, (table.shape[0], block), 0) == codes[b][1:2, :block]
        )
        retained[rows] = dot_t(choice.astype(bf16), pixels_here[b]).astype(bf16)
        places = exact_pick(choice.astype(bf16), table[...], ((0,), (0,)))
        at = lax.broadcasted_iota(jnp.int32, (block, width), 0)
        start = dot(retained[rows], embed[...]) + places
        stream[rows] = jnp.where(at == CLASS_ROW, vectors[0:1, :], start)

    flush(0)
    until(at_in)
    load(2, EIN, w_in).wait()
    layer = layer_forward_rows(dims, stream, w_in, w_out, vectors, saved + work)
    next(layer)
    until(at_in + 1)
    next(layer)
    flush(4, 5, 6, 7, 8, 9)
    until(at_out)
    bridge_copy = load(1, BRI, bridge)
    load(3, EOUT, w_out).wait()
    assemble(EOUT, w_out)
    next(layer)
    flush(10, 11, 12)
    until(at_out + 1)
    for _ in layer:
        pass
    flush(13, 14)
    until(at_out + 2)
    norm_rows(stream, vectors[5:6, :], vectors[6:7, :], unit, inverse, low, dims["step"])
    flush(1, 2, 3)
    bridge_copy.wait()
    assemble(BRI, bridge)

    @pl.loop(0, dims["images"])
    def _(b):
        rows = pl.ds(pl.multiple_of(b * block, block), block)
        projected[b] = dot(low[rows], bridge[...])

    until(at_end + 1)
    picture_copy.wait()
    for copy in flushes:
        copy.wait()


def encode(images, indices, table, weights, vectors=None):
    dims = ENC
    ring = vectors is None
    count, width = dims["images"] * dims["block"], dims["width"]
    bridge_wide = weights[BRI].shape[-1]
    in_vmem = pl.BlockSpec(memory_space=pltpu.VMEM)
    anywhere = pl.BlockSpec(memory_space=pl.ANY)
    kept_shapes = [
        ((count, images.shape[2]), bf16),
        ((count, width), f32),
        ((count, 1), f32),
        ((count, width), bf16),
    ] + saved_shapes(dims)
    picture_shape = (dims["images"], DEC["block"], images.shape[2])
    outs = [((dims["images"], 8, 256), jnp.int32), (picture_shape, bf16)]
    outs += [((dims["images"], dims["block"], bridge_wide), f32)] + kept_shapes
    out_specs = [in_vmem, anywhere, in_vmem] + [anywhere] * len(kept_shapes)
    in_specs = [anywhere] + [in_vmem] * 5
    scratch = []
    if ring:
        shapes = []
        for array in range(6):
            rows, wide = weights[array].size // weights[array].shape[-1], weights[array].shape[-1]
            shapes.append((rows // 4 if array in SHARED else rows, wide))
        shapes.append((8, 256))
        types = [bf16] * 6 + [f32]
        operands = [images, *indices, table, *weights]
        in_specs += [anywhere] * 7
        gathered = [(whole_shape(k, shape), types[k]) for k, shape in enumerate(shapes)]
        outs = gathered + [((8, shapes_total(weights[VEC])), f32)] + outs
        out_specs = [anywhere] * 7 + [in_vmem] + out_specs
        units = sum(len(step) for step in GATHER_STEPS)
        scratch += [pltpu.VMEM(shape, kind) for shape, kind in zip(shapes, types)]
        scratch += [
            pltpu.SemaphoreType.DMA((units, 6)),
            pltpu.SemaphoreType.DMA((units, 6)),
            pltpu.SemaphoreType.DMA((7,)),
            pltpu.VMEM(whole_shape(VEC, shapes[VEC]), f32),
        ]
        scratch += [
            pltpu.VMEM(whole_shape(array, shapes[array]), bf16) for array in (PIX, EOUT, BRI)
        ]
        params = dict(collective_id=0, has_side_effects=True)
        w_shapes = [
            (GROUPS, 8 * shapes[EIN][0], shapes[EIN][1]),
            (GROUPS, 8 * shapes[EOUT][0], shapes[EOUT][1]),
        ]
    else:
        operands = [images, *indices, table] + [weights[k] for k in (PIX, EIN, EOUT, BRI)] + [vectors]
        in_specs += [anywhere] * 4 + [in_vmem]
        params = {}
        w_shapes = [weights[EIN].shape, weights[EOUT].shape]
    scratch += [pltpu.SemaphoreType.DMA((8,)), pltpu.SemaphoreType.DMA((15,))]
    if ring:
        scratch += [pltpu.VMEM(member.shape, f32) for member in weights]
        scratch += [pltpu.SemaphoreType.DMA((7,))]
    buffers = [
        ((images.shape[0], 8, images.shape[2]), bf16),
        (picture_shape, bf16),
        ((count, width), f32),
        (w_shapes[0], bf16),
        (w_shapes[1], bf16),
        ((PATCH_DIM, width), bf16),
        ((width, bridge_wide), bf16),
    ]
    buffers += kept_shapes + work_shapes(dims)
    scratch += [pltpu.VMEM(*buffer) for buffer in buffers]
    return pl.pallas_call(
        functools.partial(encode_kernel, ring),
        out_shape=[jax.ShapeDtypeStruct(shape, kind) for shape, kind in outs],
        in_specs=in_specs,
        out_specs=out_specs,
        scratch_shapes=scratch,
        compiler_params=pltpu.CompilerParams(vmem_limit_bytes=62 * 1024 * 1024, **params),
        name="gather_encode" if ring else "encode",
    )(*operands)


def shapes_total(vector_shard):
    return 8 * vector_shard.shape[1]


def encoder_backward_kernel(*refs):
    grad_projected = refs[0]
    sources = refs[1:18]
    bridge, vectors_all, grad_head, dec_sums = refs[18:22]
    grad_in_all, grad_out_all, grad_bridge, grad_pixel, packed = refs[22:27]
    given, spare, low, flow, sums, vec_all, turned = refs[27:34]
    held = refs[34:51]
    grad_in, grad_out, loaded, stored = refs[51:55]
    names = ("retained", "unit", "inverse", "low_end") + SAVED + ("w_in", "w_out")
    order = (3, 1, 2, 12, 13, 14, 16, 15, 10, 11, 9, 7, 8, 6, 4, 5, 0)
    need = loader(
        [names[k] for k in order], [sources[k] for k in order], [held[k] for k in order], loaded
    )
    ready, finish = storer((grad_in, grad_out), (grad_in_all, grad_out_all), stored)
    retained, unit, inverse, low_end = held[:4]
    saved = held[4:15] + refs[55:]
    w_in, w_out = held[15:17]
    dims = ENC
    vectors = token_gain(vectors_all, dims)
    count, width = given.shape
    block = dims["block"]
    sums[...] = jnp.zeros_like(sums)

    need("low_end", "unit", "inverse")
    flat = grad_projected[...].reshape(count, grad_projected.shape[-1])
    grad_bridge[...] = dot_t(low_end[...], flat).astype(bf16)
    given[...] = dot_nt(flat, bridge[...])
    norm_back_rows(given, unit, inverse, vectors[5:6, :], given, None, sums, 5, dims["step"])
    layer_backward_rows(
        dims, given, spare, w_in, w_out, vectors, saved, low, flow, turned, grad_in, grad_out, sums, need, ready
    )
    need("retained")
    grad_pixel[:PATCH_DIM] = dot_t(retained[...], given[...].astype(bf16)).astype(bf16)
    grad_pixel[PATCH_DIM:] = grad_head[...]

    def tokens(rows):
        at = lax.broadcasted_iota(jnp.int32, (block, width), 0)
        sums[0] = sums[0] + fold(jnp.where(at == CLASS_ROW, given[rows], 0.0))

    row_loop(count, block, tokens)
    for row in range(7):
        vec_all[row : row + 1, :width] = jnp.sum(sums[row], axis=0, keepdims=True)
    vec_all[7:8, :width] = jnp.zeros((1, width), f32)
    vec_all[:, width:] = dec_sums[...]
    columns = vec_all.shape[1] // 8
    packed[...] = jnp.zeros_like(packed)
    for k in range(8):
        packed[k, :, :columns] = vec_all[:, k * columns : (k + 1) * columns]
    finish()


def encoder_backward(grad_projected, kept_state, w_in, w_out, bridge, vectors, grad_head, dec_sums):
    dims = ENC
    count, width = dims["images"] * dims["block"], dims["width"]
    pixels_wide = kept_state[0].shape[1]
    outs = [
        jax.ShapeDtypeStruct(w_in.shape, bf16),
        jax.ShapeDtypeStruct(w_out.shape, bf16),
        jax.ShapeDtypeStruct(bridge.shape, bf16),
        jax.ShapeDtypeStruct((pixels_wide + grad_head.shape[0], width), bf16),
        jax.ShapeDtypeStruct((8, 8, 256), f32),
    ]
    scratch = [
        ((count, width), f32),
        ((count, width), f32),
        ((count, width), bf16),
        ((count, dims["hidden"]), bf16),
        ((7, 8, width), f32),
        (vectors.shape, f32),
        ((width, count), bf16),
    ]
    kept_shapes = [(member.shape, member.dtype) for member in kept_state]
    scratch += kept_shapes + [(w_in.shape, bf16), (w_out.shape, bf16)]
    scratch += [(w_in.shape, bf16), (w_out.shape, bf16), 17, 2] + work_shapes(dims)
    in_vmem = pl.BlockSpec(memory_space=pltpu.VMEM)
    anywhere = pl.BlockSpec(memory_space=pl.ANY)
    return pl.pallas_call(
        encoder_backward_kernel,
        out_shape=outs,
        in_specs=[in_vmem] + [anywhere] * 17 + [in_vmem] * 4,
        out_specs=[anywhere] * 2 + [in_vmem] * 3,
        scratch_shapes=[
            pltpu.SemaphoreType.DMA((shape,)) if isinstance(shape, int) else pltpu.VMEM(*shape)
            for shape in scratch
        ],
        compiler_params=pltpu.CompilerParams(vmem_limit_bytes=62 * 1024 * 1024),
        name="encoder_backward",
    )(grad_projected, *kept_state, w_in, w_out, bridge, vectors, grad_head, dec_sums)


def gather_grouped(part, groups):
    whole = lax.all_gather(part, GROUPED, axis=0, tiled=True)
    return whole.reshape(groups, -1, whole.shape[-1])


def scatter_grouped(gradient):
    flat = gradient.astype(f32).reshape(-1, gradient.shape[-1])
    return lax.psum_scatter(flat, GROUPED, scatter_dimension=0, tiled=True)


def ringed(tensor_count):
    return tensor_count == 4 and lax.axis_size("dp") == 8


def plain_gather(masters, counted):
    groups = lax.axis_size("tensor")
    wholes = {}
    for array, k in ((EIN, 0), (EOUT, 1), (DIN, 2), (DOUT, 3)):
        flat = masters[k].reshape(-1, masters[k].shape[-1]).astype(bf16)
        wholes[array] = gather_grouped(flat, groups)
    for array, k in ((PIX, 4), (BRI, 5)):
        wholes[array] = lax.all_gather(masters[k].astype(bf16), "dp", axis=0, tiled=True)
    low = masters[6].astype(bf16).astype(f32)
    vectors = lax.all_gather(low, "dp", axis=1, tiled=True)
    eighth = jnp.broadcast_to(lax.psum(counted, "dp") / 8, (1, vectors.shape[1]))
    return wholes, jnp.concatenate([vectors, eighth], axis=0)


def ring_finish(gradients, masters, firsts, seconds):
    grouped, grad_pixel, grad_bridge, packed = gradients
    tensor_count = lax.axis_size("tensor")
    order = (4, 0, 1, 5, 2, 3, 6)
    sources = (grad_pixel, grouped[0], grouped[1], grad_bridge, grouped[2], grouped[3])
    operands = []
    for array, source in enumerate(sources):
        master = masters[order[array]]
        rows, wide = master.size // master.shape[-1], master.shape[-1]
        if array in SHARED:
            rows = rows // tensor_count
        operands.append(source.reshape(whole_shape(array, (rows, wide))))
    operands.append(packed)
    states = [[members[k] for k in order] for members in (masters, firsts, seconds)]
    *sums, stats = scatter_gradients(operands, *states)
    for array in SHARED:
        sums[array] = sums[array].reshape(-1, sums[array].shape[-1])
    *results, loss_value, pairs = apply_update(sums, *states, stats)
    place_of = {k: at for at, k in enumerate(order)}
    results = [[members[place_of[k]] for k in range(7)] for members in results]
    return (loss_value, pairs, *results[0], *results[1], *results[2])


def plain_finish(gradients, masters, firsts, seconds):
    grouped, grad_pixel, grad_bridge, packed = gradients
    tensor_count = lax.axis_size("tensor")
    columns = masters[6].shape[1]

    def scatter_shared(gradient):
        part = lax.psum_scatter(gradient.astype(f32), EVERY, scatter_dimension=0, tiled=True)
        return lax.all_gather(part, "tensor", axis=0, tiled=True)

    reduced = [scatter_grouped(gradient) for gradient in grouped]
    reduced += [scatter_shared(grad_pixel), scatter_shared(grad_bridge)]
    whole = packed.shape[0] * (ENCODER_WIDTH + D_D) // 8
    packed = packed[:, :, : whole // packed.shape[0]].transpose(1, 0, 2).reshape(8, -1)
    vector_sum = lax.psum(packed, EVERY)
    own = lax.dynamic_slice_in_dim(
        vector_sum[:7], lax.axis_index("dp") * columns, columns, axis=1
    )
    reduced = [gradient.reshape(master.shape) for gradient, master in zip(reduced + [own], masters)]
    decays = (decay_matrix,) * 6 + (0.0,)
    share_counts = (1.0,) * 4 + (float(tensor_count),) * 3
    steps = [moments(*member) for member in zip(reduced, firsts, seconds, masters, decays)]
    new_firsts, new_seconds, updates = zip(*steps)

    def squares(members):
        return jnp.stack(
            [jnp.sum(member * member) / count for member, count in zip(members, share_counts)]
        )

    weight_norm, update_norm = map(
        jnp.sqrt, lax.psum((squares(masters), squares(updates)), EVERY)
    )
    ratio = learn_rate * weight_norm / update_norm
    news = [
        master - ratio[position] * update
        for position, (master, update) in enumerate(zip(masters, updates))
    ]
    return (vector_sum[7, -1], jnp.stack([weight_norm, update_norm]), *new_firsts, *new_seconds, *news)


def shards(
    images,
    keep_index,
    unshuffle,
    masked,
    image_valid,
    *state,
):
    masters, firsts, seconds = state[:7], state[7:14], state[14:21]
    tensor_count = lax.axis_size("tensor")
    enc_table, dec_table = (
        sinusoid_table(width, GRID_PATCHES, IMAGE_PATCHES, DEC["block"])
        for width in (ENCODER_WIDTH, D_D)
    )
    indices = (keep_index, unshuffle, masked, image_valid[None, :])
    by_patch = images.transpose(1, 0, 2)
    if ringed(tensor_count):
        order = (4, 0, 1, 5, 2, 3, 6)
        results = encode(by_patch, indices, enc_table, [masters[k] for k in order])
        wholes, results = results[:7], results[7:]
        vectors, codes, pictures, projected, *enc_state = results
        wholes = [
            whole.reshape(-1, whole.shape[-1])
            if array in SHARED
            else whole.reshape(tensor_count, -1, whole.shape[-1])
            for array, whole in enumerate(wholes)
        ]
    else:
        counted = jnp.sum(masked.astype(f32) * image_valid.astype(f32)[:, None])
        wholes, vectors = plain_gather(masters, counted)
        codes, pictures, projected, *enc_state = encode(
            by_patch, indices, enc_table, wholes, vectors=vectors
        )
    grad_dec_in, grad_dec_out, grad_head, grad_projected, dec_sums = decoder_step(
        projected, codes, pictures, dec_table, wholes[DIN], wholes[DOUT], wholes[PIX], vectors
    )
    grad_enc_in, grad_enc_out, grad_bridge, grad_pixel, packed = encoder_backward(
        grad_projected,
        enc_state,
        wholes[EIN],
        wholes[EOUT],
        wholes[BRI],
        vectors,
        grad_head,
        dec_sums,
    )
    finish = ring_finish if ringed(tensor_count) else plain_finish
    return finish(
        ([grad_enc_in, grad_enc_out, grad_dec_in, grad_dec_out], grad_pixel, grad_bridge, packed),
        masters,
        firsts,
        seconds,
    )


def solution(mesh):
    state_specs = (
        P("dp", "tensor", None),
        P("tensor", "dp", None),
        P("dp", "tensor", None),
        P("tensor", "dp", None),
        P("dp", None),
        P("dp", None),
        P(None, "dp"),
    )
    in_specs = (
        P("dp", None, None),
        P("dp", None),
        P("dp", None),
        P("dp", None),
        P("dp"),
    ) + state_specs * 3
    out_specs = (P(), P()) + state_specs * 3
    return jax.shard_map(shards, mesh=mesh, in_specs=in_specs, out_specs=out_specs, check_vma=False)
```
